32 devices in a mesh: dp: 2 (over x), zero: 16 (over z, y, core).
Axes of the slice: x: 2, y: 2, z: 4, core: 2. Of those that a mesh axis runs over, the one named last changes fastest.
Arguments:
- token_ids: int32 [128, 2, 128], P(('dp', 'zero')), may hold values from 0 to 30527
- lengths: int32 [128, 2], P(('dp', 'zero')), may hold values from 32 to 128
- false_neg: int32 [128, 128], P(('dp', 'zero')), may hold values 0 or 1
- pair_index: int32 [128], P(('dp', 'zero')), may hold values from -1 to 127, as said below
- word_table: float32 [30528, 512], P('zero'), may hold values from -0.3125 to 0.3125
- vectors: float32 [78848], P('zero'), may hold values from -0.4 to 1.4, as said below
- attn_w: float32 [2, 512, 2048], P(None, 'zero'), may hold values from -0.25 to 0.25
- ffn_w: float32 [2, 512, 4096], P(None, 'zero'), may hold values from -0.25 to 0.25
- word_first: float32 [30528, 512], P('zero'), may hold values from -0.0012207031 to 0.0012207031
- vector_first: float32 [78848], P('zero'), may hold values from -0.0012207031 to 0.0012207031
- attn_first: float32 [2, 512, 2048], P(None, 'zero'), may hold values from -0.0012207031 to 0.0012207031
- ffn_first: float32 [2, 512, 4096], P(None, 'zero'), may hold values from -0.0012207031 to 0.0012207031
- word_second: float32 [30528, 512], P('zero'), may hold values from 4.5453223e-08 to 1.818129e-07
- vector_second: float32 [78848], P('zero'), may hold values from 2.272661e-06 to 3.6362577e-05
- attn_second: float32 [2, 512, 2048], P(None, 'zero'), may hold values from 4.5453223e-08 to 1.818129e-07
- ffn_second: float32 [2, 512, 4096], P(None, 'zero'), may hold values from 4.5453223e-08 to 1.818129e-07
Outputs:
- loss: float32 [], replicated
- grad_norm: float32 [], replicated
- word_new: float32 [30528, 512], P('zero')
- vector_new: float32 [78848], P('zero')
- attn_new: float32 [2, 512, 2048], P(None, 'zero')
- ffn_new: float32 [2, 512, 4096], P(None, 'zero')
- word_low: bfloat16 [30528, 512], P('zero')
- vector_low: bfloat16 [78848], P('zero')
- attn_low: bfloat16 [2, 512, 2048], P(None, 'zero')
- ffn_low: bfloat16 [2, 512, 4096], P(None, 'zero')
- word_first_new: float32 [30528, 512], P('zero')
- vector_first_new: float32 [78848], P('zero')
- attn_first_new: float32 [2, 512, 2048], P(None, 'zero')
- ffn_first_new: float32 [2, 512, 4096], P(None, 'zero')
- word_second_new: float32 [30528, 512], P('zero')
- vector_second_new: float32 [78848], P('zero')
- attn_second_new: float32 [2, 512, 2048], P(None, 'zero')
- ffn_second_new: float32 [2, 512, 4096], P(None, 'zero')
- down_bias_grad: float32 [2, 512], P(None, 'zero')
The draws below stay inside these ranges and needn't reach their ends.
Inputs may be any that keep to these rules, and one draw needn't show every extreme that they name: `pair_index`: each positive row is named by at most one anchor; anchor 0 always counts. `vectors`: gains lie near 1; biases, shifts and positions near 0.
All inputs are finite; a program needn't handle non-finite values. No bound on the sum of `false_neg` on one device may be relied on, other than what follows from the above.
Results may differ from the reference program's by a relative error of at most 0.015.
The reference program's roundings to bfloat16 on the way count: a program that leaves them out, or rounds other values in their place, can miss the bound.
Values may be sent and summed in bfloat16 or wider, within the bound.
A program may use at most 320 MiB of HBM per device.

```python
import math
import jax
import jax.numpy as jnp
import numpy as np
from jax import lax

D = 512
HEADS = 8
HD = 64
FF = 2048
VOCAB = 30528
SEQ = 128
LAYERS = 2
ADAM_STEP = 5
PAIRS = 128
VEC = 78848
NPARAMS = 22000640


def draw_pair_index(key, part):
    order = jax.random.permutation(jax.random.fold_in(key, 11), PAIRS).astype(jnp.int32)
    places = jnp.arange(PAIRS, dtype=jnp.int32)
    dropped = (jax.random.randint(jax.random.fold_in(key, 12), (PAIRS,), 0, 8) == 0) | (places == 1)
    dropped = dropped & (order < PAIRS - 1) & (places > 0)
    return jnp.where(dropped, -1, order).astype(jnp.int32)


def draw_vectors(key, part):

    def segment(index, length_now, kind):
        sub_key = jax.random.fold_in(key, index)
        noise = jnp.clip(jax.random.normal(sub_key, (length_now,), jnp.float32), -3.5, 3.5)
        if kind == 'gain':
            return 1.0 + 0.1 * noise
        if kind == 'position':
            return 0.05 * noise
        return 0.1 * noise
    pieces = [segment(0, SEQ * D, 'position'), segment(1, D, 'gain'), segment(2, D, 'shift')]
    for layer_index in range(LAYERS):
        base = 10 + 10 * layer_index
        kinds = ('shift', 'shift', 'shift', 'gain', 'shift', 'shift', 'shift', 'gain', 'shift')
        for place, kind in enumerate(kinds):
            length_now = FF if place == 5 else D
            pieces.append(segment(base + place, length_now, kind))
    return jnp.concatenate(pieces).astype(jnp.float32)


def set_ends(array, own_key, smallest, largest):
    longest = array.shape.index(max(array.shape))
    spots = []
    for shift in (0, 1):
        where = [jax.random.randint(jax.random.fold_in(own_key, axis), (), 0, length) for axis, length in enumerate(array.shape)]
        where[longest] = (where[longest] + shift) % array.shape[longest]
        spots.append(tuple(where))
    return array.at[spots[0]].set(smallest).at[spots[1]].set(largest)


def steps_of(own_key, shape, split, smallest, top_value):
    loudness, own = 1.0, jax.random.fold_in(own_key, 6)
    for dim, shards_of in split:
        steps = jnp.exp(jax.random.uniform(jax.random.fold_in(own, dim), (shards_of,), jnp.float32, smallest / len(split), top_value / len(split)))
        loudness = loudness * jnp.repeat(steps, shape[dim] // shards_of).reshape([-1 if axis == dim else 1 for axis in range(len(shape))])
    return loudness


def rank_table(amount, skew):
    weights = [(1 << 20) // math.isqrt(standing ** skew) + 1 for standing in range(1, amount + 1)]
    scale = 1 + sum(weights) // (1 << 30)
    return np.cumsum(np.array([max(1, weight // scale) for weight in weights]))


def ranked(rng, dims, number_of, slope):
    listing = rank_table(number_of, slope)
    ticket = jax.random.randint(jax.random.fold_in(rng, 1), dims, 0, int(listing[number_of - 1]))
    rank = jnp.searchsorted(jnp.asarray(listing, jnp.int32), ticket, side="right")
    return jax.random.permutation(jax.random.fold_in(rng, 2), number_of)[rank].astype(jnp.int32)


def gaussian(rng, extent, width, limit, cuts=(), held_as=jnp.bfloat16):
    factor_of = steps_of(rng, extent, cuts, -0.22, 0.18) if cuts else 1.0
    result = jax.random.normal(rng, extent, jnp.float32) * width * factor_of
    return jnp.minimum(jnp.maximum(result, -limit), limit).astype(held_as)


def setup_inputs(seed: int = 0) -> dict:
    key_of = jax.random.split(jax.random.key(seed), 17)
    return {
        "token_ids": set_ends(ranked(key_of[0], (PAIRS, 2, SEQ), VOCAB, 2), jax.random.fold_in(key_of[0], 3), 0, VOCAB - 1).astype(jnp.int32),
        "lengths": set_ends(jax.random.randint(key_of[1], (PAIRS, 2), SEQ // 4, SEQ + 1), jax.random.fold_in(key_of[1], 1), SEQ // 4, SEQ).astype(jnp.int32),
        "false_neg": set_ends((jax.random.randint(key_of[2], (PAIRS, PAIRS), 0, 8) < 1).astype(jnp.int32), jax.random.fold_in(key_of[2], 1), 0, 1),
        "pair_index": draw_pair_index(jax.random.fold_in(key_of[16], 71), 0),
        "word_table": gaussian(key_of[4], (VOCAB, D), 0.05, 0.3125, ((0, 16),), jnp.float32),
        "vectors": draw_vectors(jax.random.fold_in(key_of[16], 71), 0),
        "attn_w": gaussian(key_of[6], (LAYERS, D, 4 * D), D ** -0.5, 0.25, ((1, 16),), jnp.float32),
        "ffn_w": gaussian(key_of[7], (LAYERS, D, 2 * FF), D ** -0.5, 0.25, ((1, 16),), jnp.float32),
        "word_first": gaussian(key_of[8], (VOCAB, D), (NPARAMS ** -0.5), 0.0012207031, ((0, 16),), jnp.float32),
        "vector_first": gaussian(key_of[9], (VEC,), (NPARAMS ** -0.5), 0.0012207031, ((0, 16),), jnp.float32),
        "attn_first": gaussian(key_of[10], (LAYERS, D, 4 * D), (NPARAMS ** -0.5), 0.0012207031, ((1, 16),), jnp.float32),
        "ffn_first": gaussian(key_of[11], (LAYERS, D, 2 * FF), (NPARAMS ** -0.5), 0.0012207031, ((1, 16),), jnp.float32),
        "word_second": jnp.clip(jnp.exp(math.log(1.818128936292851e-07) - 1.3862944 * jax.random.uniform(key_of[12], (VOCAB, D), jnp.float32) ** steps_of(key_of[12], (VOCAB, D), ((0, 16),), -0.2, 0.2)), 4.5453223407321275e-08, 1.818128936292851e-07),
        "vector_second": jnp.clip(jnp.exp(math.log(3.636257679318078e-05) - 2.7725887 * jax.random.uniform(key_of[13], (VEC,), jnp.float32) ** steps_of(key_of[13], (VEC,), ((0, 16),), -0.2, 0.2)), 2.2726610495737987e-06, 3.636257679318078e-05),
        "attn_second": jnp.clip(jnp.exp(math.log(1.818128936292851e-07) - 1.3862944 * jax.random.uniform(key_of[14], (LAYERS, D, 4 * D), jnp.float32) ** steps_of(key_of[14], (LAYERS, D, 4 * D), ((1, 16),), -0.2, 0.2)), 4.5453223407321275e-08, 1.818128936292851e-07),
        "ffn_second": jnp.clip(jnp.exp(math.log(1.818128936292851e-07) - 1.3862944 * jax.random.uniform(key_of[15], (LAYERS, D, 2 * FF), jnp.float32) ** steps_of(key_of[15], (LAYERS, D, 2 * FF), ((1, 16),), -0.2, 0.2)), 4.5453223407321275e-08, 1.818128936292851e-07),
    }


SOFTMAX_TEMP = 0.05
CLIP_NORM = 1.0
LEARN_RATE = 0.02
VECTOR_RATE = 0.15
BETA_ONE = 0.5
BETA_TWO = 0.5
WEIGHT_DECAY = 0.01
ADAM_EPS = 1e-08
NORM_EPS = 1e-06
MASKED = -1000000000.0

@jax.custom_vjp
def low(v):
    return lax.optimization_barrier(v.astype(jnp.bfloat16)).astype(jnp.float32)

@jax.custom_vjp
def low_back(v):
    return v

def low_keep(v):
    return (low(v), None)

def low_pass(kept, grad):
    return (grad,)

def back_keep(v):
    return (v, None)

def back_low(kept, grad):
    return (low(grad),)
low.defvjp(low_keep, low_pass)
low_back.defvjp(back_keep, back_low)

def rounded(value):
    return low(low_back(value))

def matmul(left, right):
    return jnp.dot(left, right, precision=lax.Precision.HIGHEST)

def einsum_high(form, left, right):
    return jnp.einsum(form, left, right, precision=lax.Precision.HIGHEST)

def split_vectors(vec_all):
    offset = SEQ * D
    position = vec_all[:offset].reshape(SEQ, D)
    emb_gain = vec_all[offset:offset + D]
    emb_shift = vec_all[offset + D:offset + 2 * D]
    offset = offset + 2 * D
    layer_parts = []
    for layer_index in range(LAYERS):
        pieces = []
        for length_now in (D, D, D, D, D, FF, D, D, D):
            pieces.append(vec_all[offset:offset + length_now])
            offset = offset + length_now
        layer_parts.append(pieces)
    return (position, emb_gain, emb_shift, layer_parts)

def layer_norm(values, gain, shift):
    center = values - lax.optimization_barrier(jnp.mean(values, axis=-1, keepdims=True))
    spread = lax.optimization_barrier(jnp.mean(center * center, axis=-1, keepdims=True))
    return center * lax.rsqrt(spread + NORM_EPS) * gain + shift

def embed_tokens(rows, vec_all):
    position, emb_gain, emb_shift, layer_parts = split_vectors(vec_all)
    return layer_norm(low_back(rows) + position[None], emb_gain, emb_shift)

def encoder_layer(hidden, attn_weights, ffn_weights, vec_all, key_mask, layer_index):
    q_bias, v_bias, o_bias, gain_one, shift_one, up_bias, down_bias, gain_two, second_shift = split_vectors(vec_all)[3][layer_index]
    sequence_count = hidden.shape[0]
    packed = matmul(low(hidden), attn_weights[:, :3 * D])
    packed = rounded(packed + jnp.concatenate([q_bias, jnp.zeros_like(q_bias), v_bias]))
    heads_shape = (sequence_count, SEQ, HEADS, HD)
    queries = packed[..., :D].reshape(heads_shape)
    key_rows = packed[..., D:2 * D].reshape(heads_shape)
    value_rows = packed[..., 2 * D:].reshape(heads_shape)
    scores = low_back(einsum_high('nqhd,nkhd->nhqk', queries, key_rows) * HD ** (-0.5))
    scores = jnp.where(key_mask[:, None, None, :], scores, MASKED)
    attention = low(jax.nn.softmax(scores, axis=-1))
    context = rounded(einsum_high('nhqk,nkhd->nqhd', attention, value_rows).reshape(sequence_count, SEQ, D))
    attended = low_back(matmul(context, attn_weights[:, 3 * D:]) + o_bias)
    first_out = layer_norm(hidden + attended, gain_one, shift_one)
    upward = low_back(matmul(low(first_out), ffn_weights[:, :FF]) + up_bias)
    active = rounded(jax.nn.gelu(upward, approximate=True))
    downward = low_back(einsum_high('nsf,df->nsd', active, ffn_weights[:, FF:]) + down_bias)
    return layer_norm(first_out + downward, gain_two, second_shift)

def pool_rows(hidden, key_mask, seq_lengths):
    share = key_mask.astype(jnp.float32) / seq_lengths.astype(jnp.float32)[:, None]
    return lax.optimization_barrier(jnp.sum(hidden * share[:, :, None], axis=1))

def normalized_rows(rows):
    return rows * lax.rsqrt(lax.optimization_barrier(jnp.sum(rows * rows, axis=-1, keepdims=True)) + NORM_EPS)

def contrastive_terms(shallow_anchor, deep_anchor, shallow_pos, deep_pos, false_neg, pair_index):
    columns = lax.broadcasted_iota(jnp.int32, false_neg.shape, 1)
    hit = columns == pair_index[:, None]
    kept_cols = (false_neg == 0) | hit
    valid_rows = (pair_index >= 0).astype(jnp.float32)
    totals = jnp.zeros(pair_index.shape, jnp.float32)
    for current_width in (D, D * 2 // 3, D // 3, D // 6, D // 12):
        log_probs = []
        for anchor_vectors, positive_rows in ((shallow_anchor, shallow_pos), (deep_anchor, deep_pos)):
            similarity_scores = jnp.dot(normalized_rows(anchor_vectors[:, :current_width]), normalized_rows(positive_rows[:, :current_width]).T, precision=lax.Precision.HIGHEST) / SOFTMAX_TEMP
            similarity_scores = jnp.where(kept_cols, similarity_scores, MASKED)
            log_probs.append(jax.nn.log_softmax(similarity_scores, axis=-1))
        for log_now in log_probs:
            totals = totals - lax.optimization_barrier(jnp.sum(jnp.where(hit, log_now, 0.0), axis=-1))
        totals = totals + lax.optimization_barrier(jnp.sum(jnp.exp(log_probs[1]) * (log_probs[1] - log_probs[0]), axis=-1))
    return jnp.sum(totals * valid_rows)

def adam_update(master, gradient, first, second, step_rate):
    first_new = BETA_ONE * first + (1.0 - BETA_ONE) * gradient
    second_new = BETA_TWO * second + (1.0 - BETA_TWO) * gradient * gradient
    first_hat = first_new / (1.0 - BETA_ONE ** ADAM_STEP)
    second_hat = second_new / (1.0 - BETA_TWO ** ADAM_STEP)
    master_new = master - step_rate * (first_hat / (jnp.sqrt(second_hat) + ADAM_EPS) + WEIGHT_DECAY * master)
    return (master_new, first_new, second_new)

def encode_block(token_ids, lengths, word_copy, vec_copy, attn_copy, ffn_copy):
    flat_ids = token_ids.reshape(-1, SEQ)
    seq_lengths = lengths.reshape(-1)
    key_mask = lax.broadcasted_iota(jnp.int32, flat_ids.shape, 1) < seq_lengths[:, None]
    hidden = embed_tokens(word_copy[flat_ids], vec_copy)
    pooled = []
    for layer_index in range(LAYERS):
        hidden = encoder_layer(hidden, attn_copy[layer_index], ffn_copy[layer_index], vec_copy, key_mask, layer_index)
        if layer_index == 0 or layer_index == LAYERS - 1:
            pooled.append(low(pool_rows(hidden, key_mask, seq_lengths)))
    return (pooled[0].reshape(-1, 2, D), pooled[-1].reshape(-1, 2, D))

def reference(token_ids, lengths, false_neg, pair_index, word_table, vectors, attn_w, ffn_w, word_first, vector_first, attn_first, ffn_first, word_second, vector_second, attn_second, ffn_second):
    block_pairs = math.gcd(PAIRS, max(1, 4096 // (2 * SEQ)))
    block_count = PAIRS // block_pairs
    ids_blocks = token_ids.reshape(block_count, block_pairs, 2, SEQ)
    len_blocks = lengths.reshape(block_count, block_pairs, 2)

    def total_loss(word_copy, vec_copy, attn_copy, ffn_copy):

        def one_block(block_args):
            return encode_block(block_args[0], block_args[1], word_copy, vec_copy, attn_copy, ffn_copy)
        shallow, deep = lax.map(jax.checkpoint(one_block), (ids_blocks, len_blocks))
        shallow = shallow.reshape(PAIRS, 2, D)
        deep = deep.reshape(PAIRS, 2, D)
        summed = contrastive_terms(shallow[:, 0], deep[:, 0], shallow[:, 1], deep[:, 1], false_neg, pair_index)
        valid_count = jnp.sum((pair_index >= 0).astype(jnp.float32))
        return summed / jnp.maximum(valid_count, 1.0)
    loss, backward = jax.vjp(total_loss, low(word_table), low(vectors), low(attn_w), low(ffn_w))
    word_grad, vec_grad, attn_grad, ffn_grad = backward(jnp.ones_like(loss))
    square_total = jnp.sum(word_grad * word_grad) + jnp.sum(vec_grad * vec_grad)
    square_total = square_total + jnp.sum(attn_grad * attn_grad) + jnp.sum(ffn_grad * ffn_grad)
    grad_norm = jnp.sqrt(square_total)
    factor = jnp.minimum(1.0, CLIP_NORM / (grad_norm + 1e-06))
    down_bias_grad = jnp.stack([split_vectors(vec_grad)[3][layer_index][6] for layer_index in range(LAYERS)]) * factor
    word_new, word_first_new, word_second_new = adam_update(word_table, word_grad * factor, word_first, word_second, LEARN_RATE)
    vector_new, vector_first_new, vector_second_new = adam_update(vectors, vec_grad * factor, vector_first, vector_second, VECTOR_RATE)
    attn_new, attn_first_new, attn_second_new = adam_update(attn_w, attn_grad * factor, attn_first, attn_second, LEARN_RATE)
    ffn_new, ffn_first_new, ffn_second_new = adam_update(ffn_w, ffn_grad * factor, ffn_first, ffn_second, LEARN_RATE)
    return (loss, grad_norm, word_new, vector_new, attn_new, ffn_new, word_new.astype(jnp.bfloat16), vector_new.astype(jnp.bfloat16), attn_new.astype(jnp.bfloat16), ffn_new.astype(jnp.bfloat16), word_first_new, vector_first_new, attn_first_new, ffn_first_new, word_second_new, vector_second_new, attn_second_new, ffn_second_new, down_bias_grad)
```

```python
import functools

import jax
import jax.numpy as jnp
from jax import lax
from jax.experimental import pallas as pl
from jax.experimental.pallas import tpu as pltpu
from jax.sharding import PartitionSpec as P

D = 512
HEADS = 8
HD = 64
FF = 2048
SEQ = 128
LAYERS = 2
ADAM_STEP = 5


SOFTMAX_TEMP = 0.05
CLIP_NORM = 1.0
LEARN_RATE = 0.02
VECTOR_RATE = 0.15
BETA_ONE = 0.5
BETA_TWO = 0.5
WEIGHT_DECAY = 0.01
ADAM_EPS = 1e-08
NORM_EPS = 1e-06
MASKED = -1000000000.0

MESH = pl.DeviceIdType.MESH


def build_low():

    def rounder(value):
        return lax.optimization_barrier(value.astype(jnp.bfloat16)).astype(jnp.float32)

    def keep_fwd(value):
        return (rounder(value), None)

    def pass_bwd(kept, grad):
        return (grad,)

    wrapped = jax.custom_vjp(rounder)
    wrapped.defvjp(keep_fwd, pass_bwd)
    return wrapped


def build_low_back():

    def identity_fn(value):
        return value

    def keep_fwd(value):
        return (value, None)

    def round_bwd(kept, grad):
        return (low(grad),)

    wrapped = jax.custom_vjp(identity_fn)
    wrapped.defvjp(keep_fwd, round_bwd)
    return wrapped


def low(value):
    return build_low()(value)


def low_back(value):
    return build_low_back()(value)


def rounded(value):
    return low(low_back(value))


def matmul(left, right):
    return jnp.dot(left, right, preferred_element_type=jnp.float32)


def einsum_plain(form, left, right):
    return jnp.einsum(form, left, right, preferred_element_type=jnp.float32)


def exchange_kernel(modes, ndp, nz, *refs):
    count = len(modes)
    ins = refs[:count]
    outs = refs[count : 2 * count]
    sems = refs[2 * count :]
    d = lax.axis_index("dp")
    z = lax.axis_index("zero")
    me = d * nz + z
    n = ndp * nz

    def peer_of(group, k):
        if group == "dp":
            pd = lax.rem(d + k, ndp)
            return pd, z, pd
        if group == "zero":
            pz = lax.rem(z + k, nz)
            return d, pz, pz
        p = lax.rem(me + k, n)
        return p // nz, lax.rem(p, nz), p

    groups = {m.split("_")[0] for m in modes}
    sizes = {"all": n, "zero": nz, "dp": ndp}
    mine = {"all": me, "zero": z, "dp": d}
    barrier = pltpu.get_barrier_semaphore()
    meet = ["all"] if "all" in groups else sorted(groups)
    total = 0
    for group in meet:
        total += sizes[group] - 1

        def greet(k, carry, group=group):
            pd, pz, _ = peer_of(group, k)
            pl.semaphore_signal(barrier, inc=1, device_id=(pd, pz), device_id_type=MESH)
            return carry

        lax.fori_loop(1, sizes[group], greet, 0)
    pl.semaphore_wait(barrier, total)

    def make(a, k):
        mode = modes[a]
        group = mode.split("_")[0]
        pd, pz, _ = peer_of(group, k)
        src = ins[a].at[pz] if mode.endswith("_p") else ins[a]
        return pltpu.make_async_remote_copy(
            src_ref=src,
            dst_ref=outs[a].at[mine[group]],
            send_sem=sems[2 * a].at[k],
            recv_sem=sems[2 * a + 1].at[k],
            device_id=(pd, pz),
            device_id_type=MESH,
        )

    for a, mode in enumerate(modes):
        group = mode.split("_")[0]

        def begin(k, carry, a=a):
            make(a, k).start()
            return carry

        lax.fori_loop(1, sizes[group], begin, 0)
    for a, mode in enumerate(modes):
        group = mode.split("_")[0]
        if mode.endswith("_p"):
            outs[a][mine[group]] = ins[a][z]
        else:
            outs[a][mine[group]] = ins[a][...]
    for a, mode in enumerate(modes):
        group = mode.split("_")[0]

        def finish(k, carry, a=a):
            make(a, k).wait()
            return carry

        lax.fori_loop(1, sizes[group], finish, 0)


def exchange(arrays, modes, ndp, nz, collective_id, name):
    sizes = {"all": ndp * nz, "zero": nz, "dp": ndp}
    outs = []
    scratch = []
    moved = 0
    for array, mode in zip(arrays, modes):
        size = sizes[mode.split("_")[0]]
        block = array.shape[1:] if mode.endswith("_p") else array.shape
        outs.append(jax.ShapeDtypeStruct((size,) + block, array.dtype))
        scratch += [pltpu.SemaphoreType.DMA((size,)), pltpu.SemaphoreType.DMA((size,))]
        one = array.dtype.itemsize
        for s in block:
            one *= s
        moved += one * size
    vmem = pl.BlockSpec(memory_space=pltpu.VMEM)
    return pl.pallas_call(
        functools.partial(exchange_kernel, tuple(modes), ndp, nz),
        out_shape=tuple(outs),
        in_specs=[vmem] * len(arrays),
        out_specs=tuple([vmem] * len(arrays)),
        scratch_shapes=scratch,
        compiler_params=pltpu.CompilerParams(
            collective_id=collective_id, has_side_effects=True, vmem_limit_bytes=48 * 1024 * 1024
        ),
        cost_estimate=pl.CostEstimate(flops=0, bytes_accessed=20 * moved, transcendentals=0),
        name=name,
    )(*arrays)


def split_vectors(vec_all):
    offset = SEQ * D
    position = vec_all[:offset].reshape(SEQ, D)
    emb_gain = vec_all[offset : offset + D]
    emb_shift = vec_all[offset + D : offset + 2 * D]
    offset = offset + 2 * D
    layer_parts = []
    for layer_index in range(LAYERS):
        pieces = []
        for length_now in (D, D, D, D, D, FF, D, D, D):
            pieces.append(vec_all[offset : offset + length_now])
            offset = offset + length_now
        layer_parts.append(pieces)
    return (position, emb_gain, emb_shift, layer_parts)


def layer_norm(values, gain, shift):
    center = values - jnp.mean(values, axis=-1, keepdims=True)
    spread = jnp.mean(center * center, axis=-1, keepdims=True)
    return center * lax.rsqrt(spread + NORM_EPS) * gain + shift


def embed_tokens(rows, vec_all):
    position, emb_gain, emb_shift, layer_parts = split_vectors(vec_all)
    return layer_norm(low_back(rows) + position[None], emb_gain, emb_shift)


def encoder_layer(hidden, attn_weights, ffn_weights, vec_all, key_mask, layer_index):
    q_bias, v_bias, o_bias, gain_one, shift_one, up_bias, down_bias, gain_two, second_shift = (
        split_vectors(vec_all)[3][layer_index]
    )
    sequence_count = hidden.shape[0]
    packed = matmul(low(hidden), attn_weights[:, : 3 * D])
    packed = rounded(packed + jnp.concatenate([q_bias, jnp.zeros_like(q_bias), v_bias]))
    heads_shape = (sequence_count, SEQ, HEADS, HD)
    queries = packed[..., :D].reshape(heads_shape)
    key_rows = packed[..., D : 2 * D].reshape(heads_shape)
    value_rows = packed[..., 2 * D :].reshape(heads_shape)
    scores = low_back(einsum_plain("nqhd,nkhd->nhqk", queries, key_rows) * HD ** (-0.5))
    scores = jnp.where(key_mask[:, None, None, :], scores, MASKED)
    attention = low(jax.nn.softmax(scores, axis=-1))
    context = rounded(
        einsum_plain("nhqk,nkhd->nqhd", attention, value_rows).reshape(sequence_count, SEQ, D)
    )
    attended = low_back(matmul(context, attn_weights[:, 3 * D :]) + o_bias)
    first_out = layer_norm(hidden + attended, gain_one, shift_one)
    upward = low_back(matmul(low(first_out), ffn_weights[:, :FF]) + up_bias)
    active = rounded(jax.nn.gelu(upward, approximate=True))
    downward = low_back(einsum_plain("nsf,df->nsd", active, ffn_weights[:, FF:]) + down_bias)
    return layer_norm(first_out + downward, gain_two, second_shift)


def pool_rows(hidden, key_mask, seq_lengths):
    share = key_mask.astype(jnp.float32) / seq_lengths.astype(jnp.float32)[:, None]
    return jnp.sum(hidden * share[:, :, None], axis=1)


def normalized_rows(rows):
    return rows * lax.rsqrt(jnp.sum(rows * rows, axis=-1, keepdims=True) + NORM_EPS)


def contrastive_terms(shallow_anchor, deep_anchor, shallow_pos, deep_pos, false_neg, pair_index):
    columns = lax.broadcasted_iota(jnp.int32, false_neg.shape, 1)
    hit = columns == pair_index[:, None]
    kept_cols = (false_neg == 0) | hit
    valid_rows = (pair_index >= 0).astype(jnp.float32)
    totals = jnp.zeros(pair_index.shape, jnp.float32)
    for current_width in (D, D * 2 // 3, D // 3, D // 6, D // 12):
        log_probs = []
        for anchor_vectors, positive_rows in (
            (shallow_anchor, shallow_pos),
            (deep_anchor, deep_pos),
        ):
            similarity_scores = (
                jnp.dot(
                    normalized_rows(anchor_vectors[:, :current_width]),
                    normalized_rows(positive_rows[:, :current_width]).T,
                    precision=lax.Precision.HIGHEST,
                )
                / SOFTMAX_TEMP
            )
            similarity_scores = jnp.where(kept_cols, similarity_scores, MASKED)
            log_probs.append(jax.nn.log_softmax(similarity_scores, axis=-1))
        for log_now in log_probs:
            totals = totals - jnp.sum(jnp.where(hit, log_now, 0.0), axis=-1)
        totals = totals + jnp.sum(jnp.exp(log_probs[1]) * (log_probs[1] - log_probs[0]), axis=-1)
    return jnp.sum(totals * valid_rows)


def adam_update(master, gradient, first, second, step_rate):
    first_new = BETA_ONE * first + (1.0 - BETA_ONE) * gradient
    second_new = BETA_TWO * second + (1.0 - BETA_TWO) * gradient * gradient
    first_hat = first_new / (1.0 - BETA_ONE**ADAM_STEP)
    second_hat = second_new / (1.0 - BETA_TWO**ADAM_STEP)
    master_new = master - step_rate * (
        first_hat / (jnp.sqrt(second_hat) + ADAM_EPS) + WEIGHT_DECAY * master
    )
    return (master_new, first_new, second_new)


def pad_rows(flat, multiple):
    rows = -(-flat.shape[0] // (128 * multiple)) * multiple
    return jnp.pad(flat, (0, rows * 128 - flat.shape[0])).reshape(rows, 128)


def one_hot(index, size, dtype=jnp.bfloat16):
    return (index[:, None] == lax.broadcasted_iota(jnp.int32, (1, size), 1)).astype(dtype)


def token_plan(ids, shard_rows):
    places = lax.broadcasted_iota(jnp.int32, ids.shape, 0)
    same = ids[:, None] == ids[None, :]
    leader = jnp.min(jnp.where(same, places[None, :], ids.shape[0]), axis=1)
    leads = leader == places
    owner = ids // shard_rows
    low_id = owner * shard_rows
    ahead = leads[None, :] & (ids[None, :] >= low_id[:, None]) & (ids[None, :] < ids[:, None])
    place = jnp.sum(ahead.astype(jnp.int32), axis=1)
    return owner, place, ids - low_id


def round_slots(owner, place, local_row, round_index, room, nz):
    inside = (place >= round_index * room) & (place < (round_index + 1) * room)
    slot = jnp.where(inside, owner * room + place - round_index * room, -1)
    slots = lax.broadcasted_iota(jnp.int32, (1, nz * room), 1)
    asked = jnp.max(jnp.where(slot[:, None] == slots, local_row[:, None], -1), axis=0)
    return slot, asked


def body(
    token_ids,
    lengths,
    false_neg,
    pair_index,
    word_table,
    vectors,
    attn_w,
    ffn_w,
    word_first,
    vector_first,
    attn_first,
    ffn_first,
    word_second,
    vector_second,
    attn_second,
    ffn_second,
):
    ndp = lax.axis_size("dp")
    nz = lax.axis_size("zero")
    n = ndp * nz
    my_dp = lax.axis_index("dp")
    my_zero = lax.axis_index("zero")
    me = my_dp * nz + my_zero
    pair_rows = token_ids.shape[0]
    total_pairs = pair_rows * n
    flat_ids = token_ids.reshape(-1, SEQ)
    seq_rows = flat_ids.shape[0]
    tokens = seq_rows * SEQ
    seq_lengths = lengths.reshape(-1)
    key_mask = lax.broadcasted_iota(jnp.int32, flat_ids.shape, 1) < seq_lengths[:, None]
    shard_rows = word_table.shape[0]
    vec_len = vectors.shape[0]

    room = -(-(tokens * 5 // 4) // (nz * 16)) * 16
    owner, place, local_row = token_plan(flat_ids.reshape(-1), shard_rows)
    slot, asked = round_slots(owner, place, local_row, 0, room, nz)
    rounds_here = jnp.max(place) // room + 1
    packet = jnp.concatenate(
        [asked, false_neg.reshape(-1), pair_index, rounds_here[None].astype(jnp.int32)]
    )
    packets, vec_parts = exchange(
        [pad_rows(packet, 8), pad_rows(vectors.astype(jnp.bfloat16), 16)],
        ["all", "zero"],
        ndp,
        nz,
        0,
        "gather_requests",
    )
    packets = packets.reshape(n, -1)
    asked_all = packets[:, : nz * room].reshape(n, nz, room)
    at = nz * room
    false_all = packets[:, at : at + pair_rows * total_pairs].reshape(total_pairs, total_pairs)
    at = at + pair_rows * total_pairs
    pair_all = packets[:, at : at + pair_rows].reshape(total_pairs)
    rounds = jnp.max(packets[:, at + pair_rows])
    vec_all = vec_parts.reshape(nz, -1)[:, :vec_len].reshape(-1).astype(jnp.float32)

    layer_weights = []
    for layer_index in range(LAYERS):
        both = jnp.concatenate(
            [attn_w[layer_index].astype(jnp.bfloat16), ffn_w[layer_index].astype(jnp.bfloat16)],
            axis=1,
        )
        layer_weights.append(lax.all_gather(both, "zero", axis=0, tiled=True))

    word_half = word_table.astype(jnp.bfloat16)
    asked_mine = lax.dynamic_index_in_dim(asked_all, my_zero, 1, keepdims=False)
    asked_near = lax.dynamic_slice_in_dim(asked_mine, my_dp * nz, nz, 0)

    def rows_for(wanted):
        return matmul(one_hot(wanted.reshape(-1), shard_rows), word_half).astype(jnp.bfloat16)

    def rows_from(slot_now, received):
        return matmul(one_hot(slot_now, nz * room), received.reshape(nz * room, D)).astype(
            jnp.bfloat16
        )

    (received,) = exchange(
        [rows_for(asked_near).reshape(nz, room, D)], ["zero_p"], ndp, nz, 1, "send_rows"
    )
    rows = rows_from(slot, received)

    def more_rows(state):
        round_index, rows_now = state
        slot_now, asked_now = round_slots(owner, place, local_row, round_index, room, nz)
        wanted = lax.all_to_all(asked_now.reshape(nz, room), "zero", 0, 0, tiled=True)
        got = lax.all_to_all(rows_for(wanted).reshape(nz, room, D), "zero", 0, 0, tiled=True)
        return round_index + 1, rows_now + rows_from(slot_now, got)

    _, rows = lax.while_loop(lambda state: state[0] < rounds, more_rows, (jnp.int32(1), rows))
    rows = rows.reshape(seq_rows, SEQ, D).astype(jnp.float32)

    embedded, embed_back = jax.vjp(embed_tokens, rows, vec_all)
    hidden = embedded
    saved = []
    pooled = []
    for layer_index in range(LAYERS):
        layer_fn = functools.partial(encoder_layer, key_mask=key_mask, layer_index=layer_index)
        weights = layer_weights[layer_index]
        output, layer_back = jax.vjp(
            layer_fn,
            hidden,
            weights[:, : 4 * D].astype(jnp.float32),
            weights[:, 4 * D :].astype(jnp.float32),
            vec_all,
        )
        saved.append(layer_back)
        hidden = output
        pooled.append(pool_rows(hidden, key_mask, seq_lengths).astype(jnp.bfloat16))

    (pooled_all,) = exchange(
        [jnp.stack(pooled).reshape(-1, 128)], ["all"], ndp, nz, 2, "gather_pooled"
    )
    pooled_all = pooled_all.reshape(n, 2, pair_rows, 2, D).astype(jnp.float32)
    pooled_all = pooled_all.transpose(1, 3, 0, 2, 4).reshape(2, 2, total_pairs, D)

    def whole_loss(shallow_anchor, deep_anchor, shallow_pos, deep_pos):
        return contrastive_terms(
            shallow_anchor, deep_anchor, shallow_pos, deep_pos, false_all, pair_all
        )

    loss_total, loss_back = jax.vjp(
        whole_loss, pooled_all[0, 0], pooled_all[1, 0], pooled_all[0, 1], pooled_all[1, 1]
    )
    valid_total = jnp.sum((pair_all >= 0).astype(jnp.float32))
    inverse = 1.0 / jnp.maximum(valid_total, 1.0)
    loss = loss_total * inverse
    shallow_anchor_grad, deep_anchor_grad, shallow_pos_grad, deep_pos_grad = [
        lax.dynamic_slice_in_dim(part, me * pair_rows, pair_rows, 0) for part in loss_back(inverse)
    ]
    share = key_mask.astype(jnp.float32) / seq_lengths.astype(jnp.float32)[:, None]
    shallow_back = jnp.stack([shallow_anchor_grad, shallow_pos_grad], axis=1).reshape(seq_rows, D)
    deep_back = jnp.stack([deep_anchor_grad, deep_pos_grad], axis=1).reshape(seq_rows, D)
    grad_hidden = jnp.zeros_like(embedded)
    weight_parts = []
    vec_grad = jnp.zeros_like(vec_all)
    for layer_index in range(LAYERS - 1, -1, -1):
        if layer_index == LAYERS - 1:
            grad_hidden = grad_hidden + deep_back[:, None, :] * share[:, :, None]
        if layer_index == 0:
            grad_hidden = grad_hidden + shallow_back[:, None, :] * share[:, :, None]
        layer_back = saved[layer_index]
        grad_hidden, attn_grad, ffn_grad, vec_layer_grad = layer_back(grad_hidden)
        both = jnp.concatenate(
            [attn_grad.astype(jnp.bfloat16), ffn_grad.astype(jnp.bfloat16)], axis=1
        )
        weight_parts.insert(0, lax.psum_scatter(both, "zero", scatter_dimension=0, tiled=True))
        vec_grad = vec_grad + vec_layer_grad
    rows_grad, vec_embed_grad = embed_back(grad_hidden)
    vec_grad = vec_grad + vec_embed_grad
    down_local = jnp.stack(
        [split_vectors(vec_grad)[3][layer_index][6] for layer_index in range(LAYERS)]
    )

    rows_grad = rows_grad.reshape(tokens, D).astype(jnp.bfloat16)

    def slot_sums(slot_now):
        picked = one_hot(slot_now, nz * room)
        return lax.dot_general(
            picked, rows_grad, (((0,), (0,)), ((), ())), preferred_element_type=jnp.float32
        ).astype(jnp.bfloat16)

    def into_rows(wanted, sums):
        return lax.dot_general(
            one_hot(wanted.reshape(-1), shard_rows),
            sums.reshape(-1, D),
            (((0,), (0,)), ((), ())),
            preferred_element_type=jnp.float32,
        )

    down_each = down_local.reshape(LAYERS, nz, -1).transpose(1, 0, 2).reshape(nz, -1)
    down_len = down_each.shape[1]
    vec_blocks = jnp.concatenate([vec_grad.reshape(nz, vec_len), down_each], axis=1)
    lines = -(-vec_blocks.shape[1] // 1024) * 8
    vec_blocks = jnp.pad(vec_blocks, ((0, 0), (0, lines * 128 - vec_blocks.shape[1])))
    sums_all, vec_shares = exchange(
        [slot_sums(slot).reshape(nz, room, D), vec_blocks.reshape(nz, lines, 128)],
        ["all_p", "all_p"],
        ndp,
        nz,
        3,
        "send_gradients",
    )
    word_grad = into_rows(asked_mine, sums_all)

    def more_sums(state):
        round_index, grad_now = state
        slot_now, asked_now = round_slots(owner, place, local_row, round_index, room, nz)
        wanted = lax.all_to_all(asked_now.reshape(nz, room), "zero", 0, 0, tiled=True)
        got = lax.all_to_all(slot_sums(slot_now).reshape(nz, room, D), "zero", 0, 0, tiled=True)
        wanted = lax.all_gather(wanted, "dp", axis=0, tiled=True)
        got = lax.all_gather(got, "dp", axis=0, tiled=True)
        return round_index + 1, grad_now + into_rows(wanted, got)

    _, word_grad = lax.while_loop(
        lambda state: state[0] < rounds, more_sums, (jnp.int32(1), word_grad)
    )
    vec_sum = jnp.sum(vec_shares.reshape(n, -1), axis=0)
    vec_shard = vec_sum[:vec_len]
    down_shard = vec_sum[vec_len : vec_len + down_len].reshape(LAYERS, -1)

    (weight_all,) = exchange([jnp.stack(weight_parts)], ["dp"], ndp, nz, 4, "sum_replicas")
    weight_sum = jnp.sum(weight_all.astype(jnp.float32), axis=0)
    attn_shard = weight_sum[:, :, : 4 * D]
    ffn_shard = weight_sum[:, :, 4 * D :]

    square_local = jnp.sum(word_grad * word_grad) + jnp.sum(vec_shard * vec_shard)
    square_local = square_local + jnp.sum(attn_shard * attn_shard) + jnp.sum(ffn_shard * ffn_shard)
    (squares,) = exchange(
        [jnp.broadcast_to(square_local, (8, 128))], ["zero"], ndp, nz, 5, "gather_squares"
    )
    square_total = jnp.sum(squares[:, 0, 0])
    grad_norm = jnp.sqrt(square_total)
    factor = jnp.minimum(1.0, CLIP_NORM / (grad_norm + 1e-06))
    word_new, word_first_new, word_second_new = adam_update(
        word_table, word_grad * factor, word_first, word_second, LEARN_RATE
    )
    vector_new, vector_first_new, vector_second_new = adam_update(
        vectors, vec_shard * factor, vector_first, vector_second, VECTOR_RATE
    )
    attn_new, attn_first_new, attn_second_new = adam_update(
        attn_w, attn_shard * factor, attn_first, attn_second, LEARN_RATE
    )
    ffn_new, ffn_first_new, ffn_second_new = adam_update(
        ffn_w, ffn_shard * factor, ffn_first, ffn_second, LEARN_RATE
    )
    return (
        loss,
        grad_norm,
        word_new,
        vector_new,
        attn_new,
        ffn_new,
        word_new.astype(jnp.bfloat16),
        vector_new.astype(jnp.bfloat16),
        attn_new.astype(jnp.bfloat16),
        ffn_new.astype(jnp.bfloat16),
        word_first_new,
        vector_first_new,
        attn_first_new,
        ffn_first_new,
        word_second_new,
        vector_second_new,
        attn_second_new,
        ffn_second_new,
        down_shard * factor,
    )


def solution(mesh):
    placed = (
        P(("dp", "zero"), None, None),
        P(("dp", "zero"), None),
        P(("dp", "zero"), None),
        P(("dp", "zero")),
        P("zero", None),
        P("zero"),
        P(None, "zero", None),
        P(None, "zero", None),
        P("zero", None),
        P("zero"),
        P(None, "zero", None),
        P(None, "zero", None),
        P("zero", None),
        P("zero"),
        P(None, "zero", None),
        P(None, "zero", None),
    )
    return jax.shard_map(
        body,
        mesh=mesh,
        in_specs=placed,
        out_specs=(
            P(),
            P(),
            P("zero", None),
            P("zero"),
            P(None, "zero", None),
            P(None, "zero", None),
            P("zero", None),
            P("zero"),
            P(None, "zero", None),
            P(None, "zero", None),
            P("zero", None),
            P("zero"),
            P(None, "zero", None),
            P(None, "zero", None),
            P("zero", None),
            P("zero"),
            P(None, "zero", None),
            P(None, "zero", None),
            P(None, "zero"),
        ),
        check_vma=False,
    )
```

```python
import functools

import jax
import jax.numpy as jnp
from jax import lax
from jax.experimental import pallas as pl
from jax.experimental.pallas import tpu as pltpu
from jax.sharding import PartitionSpec as P

D = 512
HEADS = 8
HD = 64
FF = 2048
SEQ = 128
LAYERS = 2
ADAM_STEP = 5


SOFTMAX_TEMP = 0.05
CLIP_NORM = 1.0
LEARN_RATE = 0.02
VECTOR_RATE = 0.15
BETA_ONE = 0.5
BETA_TWO = 0.5
WEIGHT_DECAY = 0.01
ADAM_EPS = 1e-08
NORM_EPS = 1e-06
MASKED = -1000000000.0

MESH = pl.DeviceIdType.MESH


def build_low():

    def rounder(value):
        return lax.optimization_barrier(value.astype(jnp.bfloat16)).astype(jnp.float32)

    def keep_fwd(value):
        return (rounder(value), None)

    def pass_bwd(kept, grad):
        return (grad,)

    wrapped = jax.custom_vjp(rounder)
    wrapped.defvjp(keep_fwd, pass_bwd)
    return wrapped


def build_low_back():

    def identity_fn(value):
        return value

    def keep_fwd(value):
        return (value, None)

    def round_bwd(kept, grad):
        return (low(grad),)

    wrapped = jax.custom_vjp(identity_fn)
    wrapped.defvjp(keep_fwd, round_bwd)
    return wrapped


def low(value):
    return build_low()(value)


def low_back(value):
    return build_low_back()(value)


def rounded(value):
    return low(low_back(value))


def matmul(left, right):
    return jnp.dot(left, right, preferred_element_type=jnp.float32)


def einsum_plain(form, left, right):
    return jnp.einsum(form, left, right, preferred_element_type=jnp.float32)


def exchange_kernel(modes, ndp, nz, *refs):
    count = len(modes)
    ins = refs[:count]
    outs = refs[count : 2 * count]
    sems = refs[2 * count :]
    d = lax.axis_index("dp")
    z = lax.axis_index("zero")
    me = d * nz + z
    n = ndp * nz

    def peer_of(group, k):
        if group == "dp":
            pd = lax.rem(d + k, ndp)
            return pd, z, pd
        if group == "zero":
            pz = lax.rem(z + k, nz)
            return d, pz, pz
        p = lax.rem(me + k, n)
        return p // nz, lax.rem(p, nz), p

    groups = {m.split("_")[0] for m in modes}
    sizes = {"all": n, "zero": nz, "dp": ndp}
    mine = {"all": me, "zero": z, "dp": d}
    barrier = pltpu.get_barrier_semaphore()
    meet = ["all"] if "all" in groups else sorted(groups)
    total = 0
    for group in meet:
        total += sizes[group] - 1

        def greet(k, carry, group=group):
            pd, pz, _ = peer_of(group, k)
            pl.semaphore_signal(barrier, inc=1, device_id=(pd, pz), device_id_type=MESH)
            return carry

        lax.fori_loop(1, sizes[group], greet, 0)
    pl.semaphore_wait(barrier, total)

    def make(a, k):
        mode = modes[a]
        group = mode.split("_")[0]
        pd, pz, _ = peer_of(group, k)
        src = ins[a].at[pz] if mode.endswith("_p") else ins[a]
        return pltpu.make_async_remote_copy(
            src_ref=src,
            dst_ref=outs[a].at[mine[group]],
            send_sem=sems[2 * a].at[k],
            recv_sem=sems[2 * a + 1].at[k],
            device_id=(pd, pz),
            device_id_type=MESH,
        )

    for a, mode in enumerate(modes):
        group = mode.split("_")[0]

        def begin(k, carry, a=a):
            make(a, k).start()
            return carry

        lax.fori_loop(1, sizes[group], begin, 0)
    for a, mode in enumerate(modes):
        group = mode.split("_")[0]
        if mode.endswith("_p"):
            outs[a][mine[group]] = ins[a][z]
        else:
            outs[a][mine[group]] = ins[a][...]
    for a, mode in enumerate(modes):
        group = mode.split("_")[0]

        def finish(k, carry, a=a):
            make(a, k).wait()
            return carry

        lax.fori_loop(1, sizes[group], finish, 0)


def exchange(arrays, modes, ndp, nz, collective_id, name):
    sizes = {"all": ndp * nz, "zero": nz, "dp": ndp}
    outs = []
    scratch = []
    moved = 0
    for array, mode in zip(arrays, modes):
        size = sizes[mode.split("_")[0]]
        block = array.shape[1:] if mode.endswith("_p") else array.shape
        outs.append(jax.ShapeDtypeStruct((size,) + block, array.dtype))
        scratch += [pltpu.SemaphoreType.DMA((size,)), pltpu.SemaphoreType.DMA((size,))]
        one = array.dtype.itemsize
        for s in block:
            one *= s
        moved += one * size
    vmem = pl.BlockSpec(memory_space=pltpu.VMEM)
    return pl.pallas_call(
        functools.partial(exchange_kernel, tuple(modes), ndp, nz),
        out_shape=tuple(outs),
        in_specs=[vmem] * len(arrays),
        out_specs=tuple([vmem] * len(arrays)),
        scratch_shapes=scratch,
        compiler_params=pltpu.CompilerParams(
            collective_id=collective_id, has_side_effects=True, vmem_limit_bytes=48 * 1024 * 1024
        ),
        cost_estimate=pl.CostEstimate(flops=0, bytes_accessed=20 * moved, transcendentals=0),
        name=name,
    )(*arrays)


def gradient_kernel(chunks, count, *refs):
    take = iter(refs)
    parts = [next(take) for _ in range(count)]
    sums_ref, near_ref = next(take), next(take)
    totals = [next(take) for _ in range(count)]
    rows_ref, near_out = next(take), next(take)
    bufs = [[next(take) for _ in range(5)] for _ in chunks]
    near_buf = next(take)
    send_a, recv_a, send_y, recv_y, send_z, recv_z, send_x, recv_x = [next(take) for _ in range(8)]
    row_send, row_recv, pass_send, pass_recv, near_sem = [next(take) for _ in range(5)]

    d = lax.axis_index("dp")
    z = lax.axis_index("zero")
    core = lax.rem(z, 2)
    col = lax.rem(z // 2, 2)
    line = z // 4
    sibling = z + 1 - 2 * core
    across = z + 2 - 4 * col

    def along(k):
        return lax.rem(line + k, 4) * 4 + lax.rem(z, 4)

    barrier = pltpu.get_barrier_semaphore()

    def greet(k, carry):
        pl.semaphore_signal(
            barrier, inc=1, device_id=(d, lax.rem(z + k, 16)), device_id_type=MESH
        )
        return carry

    lax.fori_loop(1, 16, greet, 0)
    pl.semaphore_signal(barrier, inc=1, device_id=(1 - d, z), device_id_type=MESH)
    pl.semaphore_wait(barrier, 16)

    def remote(src, dst, send, recv, to):
        return pltpu.make_async_remote_copy(
            src_ref=src,
            dst_ref=dst,
            send_sem=send,
            recv_sem=recv,
            device_id=to,
            device_id_type=MESH,
        )

    def copy_a(i):
        part, start, width = chunks[i]
        src = parts[part].at[:, :, 1 - core, :, pl.ds(start, width)]
        return remote(src, bufs[i][0], send_a.at[i], recv_a.at[i], (d, sibling))

    def copy_y(i):
        src = bufs[i][0].at[:, 1 - col]
        return remote(src, bufs[i][1], send_y.at[i], recv_y.at[i], (d, across))

    def copy_z(i, k):
        src = bufs[i][1].at[lax.rem(line + k, 4)]
        return remote(
            src, bufs[i][2].at[k - 1], send_z.at[i, k - 1], recv_z.at[i, k - 1], (d, along(k))
        )

    def copy_x(i):
        return remote(bufs[i][3], bufs[i][4], send_x.at[i], recv_x.at[i], (1 - d, z))

    def row_push(k):
        to = lax.rem(z + k, 16)
        return remote(sums_ref.at[to], rows_ref.at[d, z], row_send.at[k], row_recv.at[k], (d, to))

    def row_pass(k):
        at = lax.rem(z + 16 - k, 16)
        return remote(
            rows_ref.at[d, at], rows_ref.at[d, at], pass_send.at[k], pass_recv.at[k], (1 - d, z)
        )

    near = remote(near_ref, near_buf, near_sem.at[0], near_sem.at[1], (1 - d, z))

    total = len(chunks)
    for i in range(total):
        copy_a(i).start()

    def push(k, carry):
        row_push(k).start()
        return carry

    lax.fori_loop(1, 16, push, 0)
    near.start()
    rows_ref[d, z] = sums_ref[z]
    row_pass(0).start()

    def stage_a(i):
        part, start, width = chunks[i]
        copy_a(i).wait_recv()

        buf = bufs[i][0]

        def add_block(b, carry):
            line_at, col_at = b // 2, lax.rem(b, 2)
            mine = parts[part][line_at, col_at, core, :, pl.ds(start, width)].astype(jnp.float32)
            got = buf[line_at, col_at].astype(jnp.float32)
            buf[line_at, col_at] = (mine + got).astype(jnp.bfloat16)
            return carry

        lax.fori_loop(0, 8, add_block, 0)
        copy_y(i).start()

    def stage_y(i):
        copy_y(i).wait_recv()
        buf = bufs[i][1]

        def add_block(b, carry):
            mine = bufs[i][0][b, col].astype(jnp.float32)
            buf[b] = (mine + buf[b].astype(jnp.float32)).astype(jnp.bfloat16)
            return carry

        lax.fori_loop(0, 4, add_block, 0)
        for k in range(1, 4):
            copy_z(i, k).start()

    def stage_z(i):
        for k in range(1, 4):
            copy_z(i, k).wait_recv()
        value = bufs[i][1][line].astype(jnp.float32)
        for k in range(3):
            value = value + bufs[i][2][k].astype(jnp.float32)
        bufs[i][3][...] = value.astype(jnp.bfloat16)
        copy_x(i).start()

    def stage_x(i):
        part, start, width = chunks[i]
        copy_x(i).wait_recv()
        totals[part][:, pl.ds(start, width)] = bufs[i][3][...].astype(jnp.float32) + bufs[i][4][
            ...
        ].astype(jnp.float32)

    def pass_on(k):
        row_push(k).wait_recv()
        row_pass(k).start()

    passed = 1
    for t in range(total + 3):
        if t < total:
            stage_a(t)
        if 0 <= t - 1 < total:
            stage_y(t - 1)
        if 0 <= t - 2 < total:
            stage_z(t - 2)
        if 0 <= t - 3 < total:
            stage_x(t - 3)
        until = min(16, 1 + (t + 1) * 15 // (total + 3))
        for k in range(passed, until):
            pass_on(k)
        passed = until
    for k in range(passed, 16):
        pass_on(k)

    near.wait()
    near_out[...] = near_ref[...].astype(jnp.float32) + near_buf[...].astype(jnp.float32)

    for i in range(total):
        copy_a(i).wait_send()
        copy_y(i).wait_send()
        for k in range(1, 4):
            copy_z(i, k).wait_send()
        copy_x(i).wait_send()

    def finish(k, carry):
        row_push(k).wait_send()
        return carry

    lax.fori_loop(1, 16, finish, 0)

    def finish_pass(k, carry):
        row_pass(k).wait_send()
        at = lax.rem(z + 16 - k, 16)
        remote(
            rows_ref.at[1 - d, at], rows_ref.at[1 - d, at], pass_send.at[k], pass_recv.at[k], (1 - d, z)
        ).wait_recv()
        return carry

    lax.fori_loop(0, 16, finish_pass, 0)


def exchange_gradients(parts, sums, near, collective_id):
    chunks = []
    for index, part in enumerate(parts):
        width = min(part.shape[4], 1024)
        for start in range(0, part.shape[4], width):
            chunks.append((index, start, width))
    half = jnp.bfloat16
    scratch = []
    for index, start, width in chunks:
        r = parts[index].shape[3]
        scratch += [
            pltpu.VMEM((4, 2, r, width), half),
            pltpu.VMEM((4, r, width), half),
            pltpu.VMEM((3, r, width), half),
            pltpu.VMEM((r, width), half),
            pltpu.VMEM((r, width), half),
        ]
    scratch += [pltpu.VMEM(near.shape, half)]
    dma = pltpu.SemaphoreType.DMA
    count = len(chunks)
    scratch += [dma((count,)) for _ in range(4)] + [dma((count, 3)) for _ in range(2)]
    scratch += [dma((count,)) for _ in range(2)]
    scratch += [dma((16,)) for _ in range(4)] + [dma((2,))]
    outs = [jax.ShapeDtypeStruct(part.shape[3:], jnp.float32) for part in parts]
    outs += [jax.ShapeDtypeStruct((2,) + sums.shape, sums.dtype)]
    outs += [jax.ShapeDtypeStruct(near.shape, jnp.float32)]
    vmem = pl.BlockSpec(memory_space=pltpu.VMEM)
    return pl.pallas_call(
        functools.partial(gradient_kernel, tuple(chunks), len(parts)),
        out_shape=tuple(outs),
        in_specs=[vmem] * (len(parts) + 2),
        out_specs=tuple([vmem] * len(outs)),
        scratch_shapes=scratch,
        compiler_params=pltpu.CompilerParams(
            collective_id=collective_id, has_side_effects=True, vmem_limit_bytes=48 * 1024 * 1024
        ),
        cost_estimate=pl.CostEstimate(flops=0, bytes_accessed=200_000_000, transcendentals=0),
        name="exchange_gradients",
    )(*parts, sums, near)


def split_vectors(vec_all):
    offset = SEQ * D
    position = vec_all[:offset].reshape(SEQ, D)
    emb_gain = vec_all[offset : offset + D]
    emb_shift = vec_all[offset + D : offset + 2 * D]
    offset = offset + 2 * D
    layer_parts = []
    for layer_index in range(LAYERS):
        pieces = []
        for length_now in (D, D, D, D, D, FF, D, D, D):
            pieces.append(vec_all[offset : offset + length_now])
            offset = offset + length_now
        layer_parts.append(pieces)
    return (position, emb_gain, emb_shift, layer_parts)


def layer_norm(values, gain, shift):
    center = values - jnp.mean(values, axis=-1, keepdims=True)
    spread = jnp.mean(center * center, axis=-1, keepdims=True)
    return center * lax.rsqrt(spread + NORM_EPS) * gain + shift


def embed_tokens(rows, vec_all):
    position, emb_gain, emb_shift, layer_parts = split_vectors(vec_all)
    return layer_norm(low_back(rows) + position[None], emb_gain, emb_shift)


def encoder_layer(hidden, attn_weights, ffn_weights, vec_all, key_mask, layer_index):
    q_bias, v_bias, o_bias, gain_one, shift_one, up_bias, down_bias, gain_two, second_shift = (
        split_vectors(vec_all)[3][layer_index]
    )
    sequence_count = hidden.shape[0]
    packed = matmul(low(hidden), attn_weights[:, : 3 * D])
    packed = rounded(packed + jnp.concatenate([q_bias, jnp.zeros_like(q_bias), v_bias]))
    heads_shape = (sequence_count, SEQ, HEADS, HD)
    queries = packed[..., :D].reshape(heads_shape)
    key_rows = packed[..., D : 2 * D].reshape(heads_shape)
    value_rows = packed[..., 2 * D :].reshape(heads_shape)
    scores = low_back(einsum_plain("nqhd,nkhd->nhqk", queries, key_rows) * HD ** (-0.5))
    scores = jnp.where(key_mask[:, None, None, :], scores, MASKED)
    attention = low(jax.nn.softmax(scores, axis=-1))
    context = rounded(
        einsum_plain("nhqk,nkhd->nqhd", attention, value_rows).reshape(sequence_count, SEQ, D)
    )
    attended = low_back(matmul(context, attn_weights[:, 3 * D :]) + o_bias)
    first_out = layer_norm(hidden + attended, gain_one, shift_one)
    upward = low_back(matmul(low(first_out), ffn_weights[:, :FF]) + up_bias)
    active = rounded(jax.nn.gelu(upward, approximate=True))
    downward = low_back(einsum_plain("nsf,df->nsd", active, ffn_weights[:, FF:]) + down_bias)
    return layer_norm(first_out + downward, gain_two, second_shift)


def pool_rows(hidden, key_mask, seq_lengths):
    share = key_mask.astype(jnp.float32) / seq_lengths.astype(jnp.float32)[:, None]
    return jnp.sum(hidden * share[:, :, None], axis=1)


def normalized_rows(rows):
    return rows * lax.rsqrt(jnp.sum(rows * rows, axis=-1, keepdims=True) + NORM_EPS)


def contrastive_terms(shallow_anchor, deep_anchor, shallow_pos, deep_pos, false_neg, pair_index):
    columns = lax.broadcasted_iota(jnp.int32, false_neg.shape, 1)
    hit = columns == pair_index[:, None]
    kept_cols = (false_neg == 0) | hit
    valid_rows = (pair_index >= 0).astype(jnp.float32)
    totals = jnp.zeros(pair_index.shape, jnp.float32)
    for current_width in (D, D * 2 // 3, D // 3, D // 6, D // 12):
        log_probs = []
        for anchor_vectors, positive_rows in (
            (shallow_anchor, shallow_pos),
            (deep_anchor, deep_pos),
        ):
            similarity_scores = (
                jnp.dot(
                    normalized_rows(anchor_vectors[:, :current_width]),
                    normalized_rows(positive_rows[:, :current_width]).T,
                    precision=lax.Precision.HIGHEST,
                )
                / SOFTMAX_TEMP
            )
            similarity_scores = jnp.where(kept_cols, similarity_scores, MASKED)
            log_probs.append(jax.nn.log_softmax(similarity_scores, axis=-1))
        for log_now in log_probs:
            totals = totals - jnp.sum(jnp.where(hit, log_now, 0.0), axis=-1)
        totals = totals + jnp.sum(jnp.exp(log_probs[1]) * (log_probs[1] - log_probs[0]), axis=-1)
    return jnp.sum(totals * valid_rows)


def adam_update(master, gradient, first, second, step_rate):
    first_new = BETA_ONE * first + (1.0 - BETA_ONE) * gradient
    second_new = BETA_TWO * second + (1.0 - BETA_TWO) * gradient * gradient
    first_hat = first_new / (1.0 - BETA_ONE**ADAM_STEP)
    second_hat = second_new / (1.0 - BETA_TWO**ADAM_STEP)
    master_new = master - step_rate * (
        first_hat / (jnp.sqrt(second_hat) + ADAM_EPS) + WEIGHT_DECAY * master
    )
    return (master_new, first_new, second_new)


def pad_rows(flat, multiple):
    rows = -(-flat.shape[0] // (128 * multiple)) * multiple
    return jnp.pad(flat, (0, rows * 128 - flat.shape[0])).reshape(rows, 128)


def one_hot(index, size, dtype=jnp.bfloat16):
    return (index[:, None] == lax.broadcasted_iota(jnp.int32, (1, size), 1)).astype(dtype)


def token_plan(ids, shard_rows):
    places = lax.broadcasted_iota(jnp.int32, ids.shape, 0)
    same = ids[:, None] == ids[None, :]
    leader = jnp.min(jnp.where(same, places[None, :], ids.shape[0]), axis=1)
    leads = leader == places
    owner = ids // shard_rows
    low_id = owner * shard_rows
    ahead = leads[None, :] & (ids[None, :] >= low_id[:, None]) & (ids[None, :] < ids[:, None])
    place = jnp.sum(ahead.astype(jnp.int32), axis=1)
    return owner, place, ids - low_id


def round_slots(owner, place, local_row, round_index, room, nz):
    inside = (place >= round_index * room) & (place < (round_index + 1) * room)
    slot = jnp.where(inside, owner * room + place - round_index * room, -1)
    slots = lax.broadcasted_iota(jnp.int32, (1, nz * room), 1)
    asked = jnp.max(jnp.where(slot[:, None] == slots, local_row[:, None], -1), axis=0)
    return slot, asked


def body(
    token_ids,
    lengths,
    false_neg,
    pair_index,
    word_table,
    vectors,
    attn_w,
    ffn_w,
    word_first,
    vector_first,
    attn_first,
    ffn_first,
    word_second,
    vector_second,
    attn_second,
    ffn_second,
):
    ndp = lax.axis_size("dp")
    nz = lax.axis_size("zero")
    n = ndp * nz
    my_dp = lax.axis_index("dp")
    my_zero = lax.axis_index("zero")
    me = my_dp * nz + my_zero
    pair_rows = token_ids.shape[0]
    total_pairs = pair_rows * n
    flat_ids = token_ids.reshape(-1, SEQ)
    seq_rows = flat_ids.shape[0]
    tokens = seq_rows * SEQ
    seq_lengths = lengths.reshape(-1)
    key_mask = lax.broadcasted_iota(jnp.int32, flat_ids.shape, 1) < seq_lengths[:, None]
    shard_rows = word_table.shape[0]
    vec_len = vectors.shape[0]

    room = -(-(tokens * 9 // 8) // (nz * 8)) * 8
    owner, place, local_row = token_plan(flat_ids.reshape(-1), shard_rows)
    slot, asked = round_slots(owner, place, local_row, 0, room, nz)
    rounds_here = jnp.max(place) // room + 1
    packet = jnp.concatenate(
        [asked, false_neg.reshape(-1), pair_index, rounds_here[None].astype(jnp.int32)]
    )
    packets, vec_parts = exchange(
        [pad_rows(packet, 8), pad_rows(vectors.astype(jnp.bfloat16), 16)],
        ["all", "zero"],
        ndp,
        nz,
        0,
        "gather_requests",
    )
    packets = packets.reshape(n, -1)
    asked_all = packets[:, : nz * room].reshape(n, nz, room)
    at = nz * room
    false_all = packets[:, at : at + pair_rows * total_pairs].reshape(total_pairs, total_pairs)
    at = at + pair_rows * total_pairs
    pair_all = packets[:, at : at + pair_rows].reshape(total_pairs)
    rounds = jnp.max(packets[:, at + pair_rows])
    vec_all = vec_parts.reshape(nz, -1)[:, :vec_len].reshape(-1).astype(jnp.float32)

    layer_weights = []
    for layer_index in range(LAYERS):
        both = jnp.concatenate(
            [attn_w[layer_index].astype(jnp.bfloat16), ffn_w[layer_index].astype(jnp.bfloat16)],
            axis=1,
        )
        layer_weights.append(lax.all_gather(both, "zero", axis=0, tiled=True))

    word_half = word_table.astype(jnp.bfloat16)
    asked_mine = lax.dynamic_index_in_dim(asked_all, my_zero, 1, keepdims=False)
    asked_near = lax.dynamic_slice_in_dim(asked_mine, my_dp * nz, nz, 0)

    def rows_for(wanted):
        return matmul(one_hot(wanted.reshape(-1), shard_rows), word_half).astype(jnp.bfloat16)

    def rows_from(slot_now, received):
        return matmul(one_hot(slot_now, nz * room), received.reshape(nz * room, D)).astype(
            jnp.bfloat16
        )

    (received,) = exchange(
        [rows_for(asked_near).reshape(nz, room, D)], ["zero_p"], ndp, nz, 1, "send_rows"
    )
    rows = rows_from(slot, received)

    def more_rows(state):
        round_index, rows_now = state
        slot_now, asked_now = round_slots(owner, place, local_row, round_index, room, nz)
        wanted = lax.all_to_all(asked_now.reshape(nz, room), "zero", 0, 0, tiled=True)
        got = lax.all_to_all(rows_for(wanted).reshape(nz, room, D), "zero", 0, 0, tiled=True)
        return round_index + 1, rows_now + rows_from(slot_now, got)

    _, rows = lax.while_loop(lambda state: state[0] < rounds, more_rows, (jnp.int32(1), rows))
    rows = rows.reshape(seq_rows, SEQ, D).astype(jnp.float32)

    embedded, embed_back = jax.vjp(embed_tokens, rows, vec_all)
    hidden = embedded
    saved = []
    pooled = []
    for layer_index in range(LAYERS):
        layer_fn = functools.partial(encoder_layer, key_mask=key_mask, layer_index=layer_index)
        weights = layer_weights[layer_index]
        output, layer_back = jax.vjp(
            layer_fn,
            hidden,
            weights[:, : 4 * D].astype(jnp.float32),
            weights[:, 4 * D :].astype(jnp.float32),
            vec_all,
        )
        saved.append(layer_back)
        hidden = output
        pooled.append(pool_rows(hidden, key_mask, seq_lengths).astype(jnp.bfloat16))

    (pooled_all,) = exchange(
        [jnp.stack(pooled).reshape(-1, 128)], ["all"], ndp, nz, 2, "gather_pooled"
    )
    pooled_all = pooled_all.reshape(n, 2, pair_rows, 2, D).astype(jnp.float32)
    pooled_all = pooled_all.transpose(1, 3, 0, 2, 4).reshape(2, 2, total_pairs, D)

    def whole_loss(shallow_anchor, deep_anchor, shallow_pos, deep_pos):
        return contrastive_terms(
            shallow_anchor, deep_anchor, shallow_pos, deep_pos, false_all, pair_all
        )

    loss_total, loss_back = jax.vjp(
        whole_loss, pooled_all[0, 0], pooled_all[1, 0], pooled_all[0, 1], pooled_all[1, 1]
    )
    valid_total = jnp.sum((pair_all >= 0).astype(jnp.float32))
    inverse = 1.0 / jnp.maximum(valid_total, 1.0)
    loss = loss_total * inverse
    shallow_anchor_grad, deep_anchor_grad, shallow_pos_grad, deep_pos_grad = [
        lax.dynamic_slice_in_dim(part, me * pair_rows, pair_rows, 0) for part in loss_back(inverse)
    ]
    share = key_mask.astype(jnp.float32) / seq_lengths.astype(jnp.float32)[:, None]
    shallow_back = jnp.stack([shallow_anchor_grad, shallow_pos_grad], axis=1).reshape(seq_rows, D)
    deep_back = jnp.stack([deep_anchor_grad, deep_pos_grad], axis=1).reshape(seq_rows, D)
    grad_hidden = jnp.zeros_like(embedded)
    weight_parts = []
    by_hand = (ndp, nz) == (2, 16)
    vec_grad = jnp.zeros_like(vec_all)
    for layer_index in range(LAYERS - 1, -1, -1):
        if layer_index == LAYERS - 1:
            grad_hidden = grad_hidden + deep_back[:, None, :] * share[:, :, None]
        if layer_index == 0:
            grad_hidden = grad_hidden + shallow_back[:, None, :] * share[:, :, None]
        layer_back = saved[layer_index]
        grad_hidden, attn_grad, ffn_grad, vec_layer_grad = layer_back(grad_hidden)
        if by_hand and layer_index == 0:
            weight_parts.insert(0, (attn_grad.astype(jnp.bfloat16), ffn_grad.astype(jnp.bfloat16)))
        else:
            both = jnp.concatenate(
                [attn_grad.astype(jnp.bfloat16), ffn_grad.astype(jnp.bfloat16)], axis=1
            )
            both, grad_hidden = lax.optimization_barrier((both, grad_hidden))
            weight_parts.insert(0, lax.psum_scatter(both, "zero", scatter_dimension=0, tiled=True))
        vec_grad = vec_grad + vec_layer_grad
    rows_grad, vec_embed_grad = embed_back(grad_hidden)
    vec_grad = vec_grad + vec_embed_grad
    down_local = jnp.stack(
        [split_vectors(vec_grad)[3][layer_index][6] for layer_index in range(LAYERS)]
    )

    rows_grad = rows_grad.reshape(tokens, D).astype(jnp.bfloat16)

    def slot_sums(slot_now):
        picked = one_hot(slot_now, nz * room)
        return lax.dot_general(
            picked, rows_grad, (((0,), (0,)), ((), ())), preferred_element_type=jnp.float32
        ).astype(jnp.bfloat16)

    def into_rows(wanted, sums):
        return lax.dot_general(
            one_hot(wanted.reshape(-1), shard_rows),
            sums.reshape(-1, D),
            (((0,), (0,)), ((), ())),
            preferred_element_type=jnp.float32,
        )

    down_each = down_local.reshape(LAYERS, nz, -1).transpose(1, 0, 2).reshape(nz, -1)
    down_len = down_each.shape[1]
    vec_blocks = jnp.concatenate([vec_grad.reshape(nz, vec_len), down_each], axis=1)
    lines = -(-vec_blocks.shape[1] // 1024) * 8
    vec_blocks = jnp.pad(vec_blocks, ((0, 0), (0, lines * 128 - vec_blocks.shape[1])))
    sums = slot_sums(slot).reshape(nz, room, D)
    if by_hand:
        attn_part, ffn_part = weight_parts[0]
        attn_near, ffn_near, vec_near, sums_all, other_near = exchange_gradients(
            [
                attn_part.reshape(4, 2, 2, -1, 4 * D),
                ffn_part.reshape(4, 2, 2, -1, 2 * FF),
                vec_blocks.astype(jnp.bfloat16).reshape(4, 2, 2, lines, 128),
            ],
            sums,
            weight_parts[1],
            3,
        )
        attn_shard = jnp.stack([attn_near, other_near[:, : 4 * D]])
        ffn_shard = jnp.stack([ffn_near, other_near[:, 4 * D :]])
        vec_sum = vec_near.reshape(-1)
    else:
        sums_all, vec_shares = exchange(
            [sums, vec_blocks.reshape(nz, lines, 128)],
            ["all_p", "all_p"],
            ndp,
            nz,
            3,
            "send_gradients",
        )
        vec_sum = jnp.sum(vec_shares.reshape(n, -1), axis=0)
        (weight_all,) = exchange([jnp.stack(weight_parts)], ["dp"], ndp, nz, 4, "sum_replicas")
        weight_sum = jnp.sum(weight_all.astype(jnp.float32), axis=0)
        attn_shard = weight_sum[:, :, : 4 * D]
        ffn_shard = weight_sum[:, :, 4 * D :]
    word_grad = into_rows(asked_mine, sums_all)

    def more_sums(state):
        round_index, grad_now = state
        slot_now, asked_now = round_slots(owner, place, local_row, round_index, room, nz)
        wanted = lax.all_to_all(asked_now.reshape(nz, room), "zero", 0, 0, tiled=True)
        got = lax.all_to_all(slot_sums(slot_now).reshape(nz, room, D), "zero", 0, 0, tiled=True)
        wanted = lax.all_gather(wanted, "dp", axis=0, tiled=True)
        got = lax.all_gather(got, "dp", axis=0, tiled=True)
        return round_index + 1, grad_now + into_rows(wanted, got)

    _, word_grad = lax.while_loop(
        lambda state: state[0] < rounds, more_sums, (jnp.int32(1), word_grad)
    )
    vec_shard = vec_sum[:vec_len]
    down_shard = vec_sum[vec_len : vec_len + down_len].reshape(LAYERS, -1)

    square_local = jnp.sum(word_grad * word_grad) + jnp.sum(vec_shard * vec_shard)
    square_local = square_local + jnp.sum(attn_shard * attn_shard) + jnp.sum(ffn_shard * ffn_shard)
    (squares,) = exchange(
        [jnp.broadcast_to(square_local, (8, 128))], ["zero"], ndp, nz, 5, "gather_squares"
    )
    square_total = jnp.sum(squares[:, 0, 0])
    grad_norm = jnp.sqrt(square_total)
    factor = jnp.minimum(1.0, CLIP_NORM / (grad_norm + 1e-06))
    word_new, word_first_new, word_second_new = adam_update(
        word_table, word_grad * factor, word_first, word_second, LEARN_RATE
    )
    vector_new, vector_first_new, vector_second_new = adam_update(
        vectors, vec_shard * factor, vector_first, vector_second, VECTOR_RATE
    )
    attn_new, attn_first_new, attn_second_new = adam_update(
        attn_w, attn_shard * factor, attn_first, attn_second, LEARN_RATE
    )
    ffn_new, ffn_first_new, ffn_second_new = adam_update(
        ffn_w, ffn_shard * factor, ffn_first, ffn_second, LEARN_RATE
    )
    return (
        loss,
        grad_norm,
        word_new,
        vector_new,
        attn_new,
        ffn_new,
        word_new.astype(jnp.bfloat16),
        vector_new.astype(jnp.bfloat16),
        attn_new.astype(jnp.bfloat16),
        ffn_new.astype(jnp.bfloat16),
        word_first_new,
        vector_first_new,
        attn_first_new,
        ffn_first_new,
        word_second_new,
        vector_second_new,
        attn_second_new,
        ffn_second_new,
        down_shard * factor,
    )


def solution(mesh):
    placed = (
        P(("dp", "zero"), None, None),
        P(("dp", "zero"), None),
        P(("dp", "zero"), None),
        P(("dp", "zero")),
        P("zero", None),
        P("zero"),
        P(None, "zero", None),
        P(None, "zero", None),
        P("zero", None),
        P("zero"),
        P(None, "zero", None),
        P(None, "zero", None),
        P("zero", None),
        P("zero"),
        P(None, "zero", None),
        P(None, "zero", None),
    )
    return jax.shard_map(
        body,
        mesh=mesh,
        in_specs=placed,
        out_specs=(
            P(),
            P(),
            P("zero", None),
            P("zero"),
            P(None, "zero", None),
            P(None, "zero", None),
            P("zero", None),
            P("zero"),
            P(None, "zero", None),
            P(None, "zero", None),
            P("zero", None),
            P("zero"),
            P(None, "zero", None),
            P(None, "zero", None),
            P("zero", None),
            P("zero"),
            P(None, "zero", None),
            P(None, "zero", None),
            P(None, "zero"),
        ),
        check_vma=False,
    )
```

```python
import functools

import jax
import jax.numpy as jnp
from jax import lax
from jax.experimental import pallas as pl
from jax.experimental.pallas import tpu as pltpu
from jax.sharding import PartitionSpec as P

D = 512
HEADS = 8
HD = 64
FF = 2048
SEQ = 128
LAYERS = 2
ADAM_STEP = 5


SOFTMAX_TEMP = 0.05
CLIP_NORM = 1.0
LEARN_RATE = 0.02
VECTOR_RATE = 0.15
BETA_ONE = 0.5
BETA_TWO = 0.5
WEIGHT_DECAY = 0.01
ADAM_EPS = 1e-08
NORM_EPS = 1e-06
MASKED = -1000000000.0

MESH = pl.DeviceIdType.MESH


def build_low():

    def rounder(value):
        return lax.optimization_barrier(value.astype(jnp.bfloat16)).astype(jnp.float32)

    def keep_fwd(value):
        return (rounder(value), None)

    def pass_bwd(kept, grad):
        return (grad,)

    wrapped = jax.custom_vjp(rounder)
    wrapped.defvjp(keep_fwd, pass_bwd)
    return wrapped


def build_low_back():

    def identity_fn(value):
        return value

    def keep_fwd(value):
        return (value, None)

    def round_bwd(kept, grad):
        return (low(grad),)

    wrapped = jax.custom_vjp(identity_fn)
    wrapped.defvjp(keep_fwd, round_bwd)
    return wrapped


def low(value):
    return build_low()(value)


def low_back(value):
    return build_low_back()(value)


def rounded(value):
    return low(low_back(value))


def matmul(left, right):
    return jnp.dot(left, right, preferred_element_type=jnp.float32)


def einsum_plain(form, left, right):
    return jnp.einsum(form, left, right, preferred_element_type=jnp.float32)


def exchange_kernel(modes, ndp, nz, *refs):
    count = len(modes)
    ins = refs[:count]
    outs = refs[count : 2 * count]
    sems = refs[2 * count :]
    d = lax.axis_index("dp")
    z = lax.axis_index("zero")
    me = d * nz + z
    n = ndp * nz

    def peer_of(group, k):
        if group == "dp":
            pd = lax.rem(d + k, ndp)
            return pd, z, pd
        if group == "zero":
            pz = lax.rem(z + k, nz)
            return d, pz, pz
        p = lax.rem(me + k, n)
        return p // nz, lax.rem(p, nz), p

    groups = {m.split("_")[0] for m in modes}
    sizes = {"all": n, "zero": nz, "dp": ndp}
    mine = {"all": me, "zero": z, "dp": d}
    barrier = pltpu.get_barrier_semaphore()
    meet = ["all"] if "all" in groups else sorted(groups)
    total = 0
    for group in meet:
        total += sizes[group] - 1

        def greet(k, carry, group=group):
            pd, pz, _ = peer_of(group, k)
            pl.semaphore_signal(barrier, inc=1, device_id=(pd, pz), device_id_type=MESH)
            return carry

        lax.fori_loop(1, sizes[group], greet, 0)
    pl.semaphore_wait(barrier, total)

    def make(a, k):
        mode = modes[a]
        group = mode.split("_")[0]
        pd, pz, _ = peer_of(group, k)
        src = ins[a].at[pz] if mode.endswith("_p") else ins[a]
        return pltpu.make_async_remote_copy(
            src_ref=src,
            dst_ref=outs[a].at[mine[group]],
            send_sem=sems[2 * a].at[k],
            recv_sem=sems[2 * a + 1].at[k],
            device_id=(pd, pz),
            device_id_type=MESH,
        )

    for a, mode in enumerate(modes):
        group = mode.split("_")[0]

        def begin(k, carry, a=a):
            make(a, k).start()
            return carry

        lax.fori_loop(1, sizes[group], begin, 0)
    for a, mode in enumerate(modes):
        group = mode.split("_")[0]
        if mode.endswith("_p"):
            outs[a][mine[group]] = ins[a][z]
        else:
            outs[a][mine[group]] = ins[a][...]
    for a, mode in enumerate(modes):
        group = mode.split("_")[0]

        def finish(k, carry, a=a):
            make(a, k).wait()
            return carry

        lax.fori_loop(1, sizes[group], finish, 0)


def exchange(arrays, modes, ndp, nz, collective_id, name):
    sizes = {"all": ndp * nz, "zero": nz, "dp": ndp}
    outs = []
    scratch = []
    moved = 0
    for array, mode in zip(arrays, modes):
        size = sizes[mode.split("_")[0]]
        block = array.shape[1:] if mode.endswith("_p") else array.shape
        outs.append(jax.ShapeDtypeStruct((size,) + block, array.dtype))
        scratch += [pltpu.SemaphoreType.DMA((size,)), pltpu.SemaphoreType.DMA((size,))]
        one = array.dtype.itemsize
        for s in block:
            one *= s
        moved += one * size
    vmem = pl.BlockSpec(memory_space=pltpu.VMEM)
    return pl.pallas_call(
        functools.partial(exchange_kernel, tuple(modes), ndp, nz),
        out_shape=tuple(outs),
        in_specs=[vmem] * len(arrays),
        out_specs=tuple([vmem] * len(arrays)),
        scratch_shapes=scratch,
        compiler_params=pltpu.CompilerParams(
            collective_id=collective_id, has_side_effects=True, vmem_limit_bytes=48 * 1024 * 1024
        ),
        cost_estimate=pl.CostEstimate(flops=0, bytes_accessed=20 * moved, transcendentals=0),
        name=name,
    )(*arrays)


def gradient_kernel(chunks, count, *refs):
    take = iter(refs)
    parts = [next(take) for _ in range(count)]
    sums_ref, near_ref = next(take), next(take)
    totals = [next(take) for _ in range(count)]
    rows_ref, near_out = next(take), next(take)
    bufs = [[next(take) for _ in range(5)] for _ in chunks]
    near_buf = next(take)
    send_a, recv_a, send_y, recv_y, send_z, recv_z, send_x, recv_x = [next(take) for _ in range(8)]
    row_send, row_recv, pass_send, pass_recv, near_sem = [next(take) for _ in range(5)]

    d = lax.axis_index("dp")
    z = lax.axis_index("zero")
    core = lax.rem(z, 2)
    col = lax.rem(z // 2, 2)
    line = z // 4
    sibling = z + 1 - 2 * core
    across = z + 2 - 4 * col

    def along(k):
        return lax.rem(line + k, 4) * 4 + lax.rem(z, 4)

    barrier = pltpu.get_barrier_semaphore()

    def greet(k, carry):
        pl.semaphore_signal(
            barrier, inc=1, device_id=(d, lax.rem(z + k, 16)), device_id_type=MESH
        )
        return carry

    lax.fori_loop(1, 16, greet, 0)
    pl.semaphore_signal(barrier, inc=1, device_id=(1 - d, z), device_id_type=MESH)
    pl.semaphore_wait(barrier, 16)

    def remote(src, dst, send, recv, to):
        return pltpu.make_async_remote_copy(
            src_ref=src,
            dst_ref=dst,
            send_sem=send,
            recv_sem=recv,
            device_id=to,
            device_id_type=MESH,
        )

    def copy_a(i):
        part, start, width = chunks[i]
        src = parts[part].at[:, :, 1 - core, :, pl.ds(start, width)]
        return remote(src, bufs[i][0], send_a.at[i], recv_a.at[i], (d, sibling))

    def copy_y(i):
        src = bufs[i][0].at[:, 1 - col]
        return remote(src, bufs[i][1], send_y.at[i], recv_y.at[i], (d, across))

    def copy_z(i, k):
        src = bufs[i][1].at[lax.rem(line + k, 4)]
        return remote(
            src, bufs[i][2].at[k - 1], send_z.at[i, k - 1], recv_z.at[i, k - 1], (d, along(k))
        )

    def copy_x(i):
        return remote(bufs[i][3], bufs[i][4], send_x.at[i], recv_x.at[i], (1 - d, z))

    def row_push(k):
        to = lax.rem(z + k, 16)
        return remote(sums_ref.at[to], rows_ref.at[d, z], row_send.at[k], row_recv.at[k], (d, to))

    def row_pass(k):
        at = lax.rem(z + 16 - k, 16)
        return remote(
            rows_ref.at[d, at], rows_ref.at[d, at], pass_send.at[k], pass_recv.at[k], (1 - d, z)
        )

    near = remote(near_ref, near_buf, near_sem.at[0], near_sem.at[1], (1 - d, z))

    total = len(chunks)
    for i in range(total):
        copy_a(i).start()

    def push(k, carry):
        row_push(k).start()
        return carry

    lax.fori_loop(1, 16, push, 0)
    near.start()
    rows_ref[d, z] = sums_ref[z]
    row_pass(0).start()

    def stage_a(i):
        part, start, width = chunks[i]
        copy_a(i).wait_recv()

        buf = bufs[i][0]

        def add_block(b, carry):
            line_at, col_at = b // 2, lax.rem(b, 2)
            mine = parts[part][line_at, col_at, core, :, pl.ds(start, width)].astype(jnp.float32)
            got = buf[line_at, col_at].astype(jnp.float32)
            buf[line_at, col_at] = (mine + got).astype(buf.dtype)
            return carry

        lax.fori_loop(0, 8, add_block, 0)
        copy_y(i).start()

    def stage_y(i):
        copy_y(i).wait_recv()
        buf = bufs[i][1]

        def add_block(b, carry):
            mine = bufs[i][0][b, col].astype(jnp.float32)
            buf[b] = (mine + buf[b].astype(jnp.float32)).astype(buf.dtype)
            return carry

        lax.fori_loop(0, 4, add_block, 0)
        for k in range(1, 4):
            copy_z(i, k).start()

    def stage_z(i):
        for k in range(1, 4):
            copy_z(i, k).wait_recv()
        value = bufs[i][1][line].astype(jnp.float32)
        for k in range(3):
            value = value + bufs[i][2][k].astype(jnp.float32)
        bufs[i][3][...] = value.astype(bufs[i][3].dtype)
        copy_x(i).start()

    def stage_x(i):
        part, start, width = chunks[i]
        copy_x(i).wait_recv()
        totals[part][:, pl.ds(start, width)] = bufs[i][3][...].astype(jnp.float32) + bufs[i][4][
            ...
        ].astype(jnp.float32)

    def pass_on(k):
        row_push(k).wait_recv()
        row_pass(k).start()

    passed = 1
    for t in range(total + 3):
        if t < total:
            stage_a(t)
        if 0 <= t - 1 < total:
            stage_y(t - 1)
        if 0 <= t - 2 < total:
            stage_z(t - 2)
        if 0 <= t - 3 < total:
            stage_x(t - 3)
        until = min(16, 1 + (t + 1) * 15 // (total + 3))
        for k in range(passed, until):
            pass_on(k)
        passed = until
    for k in range(passed, 16):
        pass_on(k)

    near.wait()
    near_out[...] = near_ref[...].astype(jnp.float32) + near_buf[...].astype(jnp.float32)

    for i in range(total):
        copy_a(i).wait_send()
        copy_y(i).wait_send()
        for k in range(1, 4):
            copy_z(i, k).wait_send()
        copy_x(i).wait_send()

    def finish(k, carry):
        row_push(k).wait_send()
        return carry

    lax.fori_loop(1, 16, finish, 0)

    def finish_pass(k, carry):
        row_pass(k).wait_send()
        at = lax.rem(z + 16 - k, 16)
        remote(
            rows_ref.at[1 - d, at], rows_ref.at[1 - d, at], pass_send.at[k], pass_recv.at[k], (1 - d, z)
        ).wait_recv()
        return carry

    lax.fori_loop(0, 16, finish_pass, 0)


def exchange_gradients(parts, sums, near, collective_id):
    chunks = []
    for index, part in enumerate(parts):
        width = min(part.shape[4], 1024)
        for start in range(0, part.shape[4], width):
            chunks.append((index, start, width))
    half = jnp.bfloat16
    scratch = []
    for index, start, width in chunks:
        r = parts[index].shape[3]
        scratch += [
            pltpu.VMEM((4, 2, r, width), parts[index].dtype),
            pltpu.VMEM((4, r, width), parts[index].dtype),
            pltpu.VMEM((3, r, width), parts[index].dtype),
            pltpu.VMEM((r, width), parts[index].dtype),
            pltpu.VMEM((r, width), parts[index].dtype),
        ]
    scratch += [pltpu.VMEM(near.shape, half)]
    dma = pltpu.SemaphoreType.DMA
    count = len(chunks)
    scratch += [dma((count,)) for _ in range(4)] + [dma((count, 3)) for _ in range(2)]
    scratch += [dma((count,)) for _ in range(2)]
    scratch += [dma((16,)) for _ in range(4)] + [dma((2,))]
    outs = [jax.ShapeDtypeStruct(part.shape[3:], jnp.float32) for part in parts]
    outs += [jax.ShapeDtypeStruct((2,) + sums.shape, sums.dtype)]
    outs += [jax.ShapeDtypeStruct(near.shape, jnp.float32)]
    vmem = pl.BlockSpec(memory_space=pltpu.VMEM)
    return pl.pallas_call(
        functools.partial(gradient_kernel, tuple(chunks), len(parts)),
        out_shape=tuple(outs),
        in_specs=[vmem] * (len(parts) + 2),
        out_specs=tuple([vmem] * len(outs)),
        scratch_shapes=scratch,
        compiler_params=pltpu.CompilerParams(
            collective_id=collective_id, has_side_effects=True, vmem_limit_bytes=48 * 1024 * 1024
        ),
        cost_estimate=pl.CostEstimate(flops=0, bytes_accessed=200_000_000, transcendentals=0),
        name="exchange_gradients",
    )(*parts, sums, near)


SPLITS = 4


def start_kernel(shard_rows, room, *refs):
    packet_ref, vec_ref, attn_ref, ffn_ref, word_ref = refs[:5]
    packet_out, vec_out, weight_out, rows_out = refs[5:9]
    table, rows_held = refs[9:11]
    packet_sem, vec_sem, row_sem, z_sem, y_sem, x_sem, d_sem = refs[11:]

    d = lax.axis_index("dp")
    z = lax.axis_index("zero")
    me = d * 16 + z
    core = lax.rem(z, 2)
    col = lax.rem(z // 2, 2)
    line = z // 4
    sibling = z + 1 - 2 * core
    across = z + 2 - 4 * col
    width = attn_ref.shape[1]
    part = width // SPLITS

    def everyone(k):
        p = lax.rem(me + k, 32)
        return (p // 16, lax.rem(p, 16))

    barrier = pltpu.get_barrier_semaphore()

    def greet(k, carry):
        pl.semaphore_signal(barrier, inc=1, device_id=everyone(k), device_id_type=MESH)
        return carry

    lax.fori_loop(1, 32, greet, 0)
    weight_out[z, :, 0:width] = attn_ref[...].astype(jnp.bfloat16)
    weight_out[z, :, width : 3 * width] = ffn_ref[...].astype(jnp.bfloat16)
    pl.semaphore_wait(barrier, 31)

    def remote(src, dst, sems, at, to):
        return pltpu.make_async_remote_copy(
            src_ref=src,
            dst_ref=dst,
            send_sem=sems.at[(0,) + at],
            recv_sem=sems.at[(1,) + at],
            device_id=to,
            device_id_type=MESH,
        )

    def packet_copy(k, slot):
        return remote(packet_ref, packet_out.at[slot], packet_sem, (k,), everyone(k))

    def vec_copy(k, slot):
        return remote(vec_ref, vec_out.at[slot], vec_sem, (k,), (d, lax.rem(z + k, 16)))

    def row_copy(k, slot):
        to = lax.rem(z + k, 16)
        return remote(rows_held.at[to], rows_out.at[slot], row_sem, (k,), (d, to))

    def send_packets(k, carry):
        packet_copy(k, me).start()
        return carry

    lax.fori_loop(1, 32, send_packets, 0)

    def shard(i):
        at = lax.rem(line + i % 4, 4) * 4 + lax.rem(z, 4)
        return at if i < 4 else at + 2 - 4 * col

    columns = (
        pl.multiple_of(d * width, width),
        2 * width,
        pl.multiple_of((1 - d) * width, width),
    )

    def block(at, s, g):
        first = pl.multiple_of(columns[g] + s * part, 128)
        return weight_out.at[at, :, pl.ds(first, part)]

    def z_copy(s, k, g, at):
        to = lax.rem(line + k, 4) * 4 + lax.rem(z, 4)
        return remote(block(at, s, g), block(at, s, g), z_sem, (s, k - 1, g), (d, to))

    def y_copy(s, j, g, at):
        return remote(block(at, s, g), block(at, s, g), y_sem, (s, j, g), (d, across))

    def x_copy(s, i, g, at):
        return remote(block(at, s, g), block(at, s, g), x_sem, (s, i), (1 - d, z))

    def d_copy(s, i, g, at):
        return remote(block(at, s, g), block(at, s, g), d_sem, (s, i, g), (d, sibling))

    def spread(s, i):
        at = shard(i)
        if i < 4:
            y_copy(s, i, 0, at).start()
            y_copy(s, i, 1, at).start()
        if i > 0:
            x_copy(s, i, 0, at).start()
        for g in range(2 if i > 0 else 3):
            d_copy(s, i, g, at).start()

    for s in range(SPLITS):
        for k in range(1, 4):
            for g in range(2):
                z_copy(s, k, g, z).start()
        spread(s, 0)

    def send_vec(k, carry):
        vec_copy(k, z).start()
        return carry

    lax.fori_loop(1, 16, send_vec, 0)
    packet_out[me] = packet_ref[...]
    vec_out[z] = vec_ref[...]

    body_rows = shard_rows // 16 * 16
    step = 112 if body_rows % 112 == 0 else 16

    def to_half(i, carry):
        at = pl.multiple_of(i * step, 16)
        table[pl.ds(at, step), :] = word_ref[pl.ds(at, step), :].astype(jnp.bfloat16)
        return carry

    lax.fori_loop(0, body_rows // step, to_half, 0)
    padded = table.shape[0]
    table[body_rows:padded, :] = jnp.zeros((padded - body_rows, table.shape[1]), jnp.bfloat16)
    if shard_rows > body_rows:
        table[body_rows:shard_rows, :] = word_ref[body_rows:shard_rows, :].astype(jnp.bfloat16)

    def answer(k):
        src = lax.rem(z + k, 16)
        asked = packet_out[d * 16 + src, pl.ds(z, 1), :]
        rows_at = lax.broadcasted_iota(jnp.int32, (padded, 128), 0)
        picked = (rows_at == asked).astype(jnp.bfloat16)
        found = lax.dot_general(
            picked, table[...], (((0,), (0,)), ((), ())), preferred_element_type=jnp.float32
        )
        return src, found[:room, :].astype(jnp.bfloat16)

    def packet_in(k, carry):
        packet_copy(k, lax.rem(me + 32 - k, 32)).wait_recv()
        return carry

    def answer_one(k, carry):
        src, found = answer(k)
        rows_held[src] = found
        row_copy(k, z).start()
        return carry

    def z_phase(s):
        for k in range(1, 4):
            at = shard(4 - k)
            for g in range(2):
                z_copy(s, k, g, at).wait_recv()
            spread(s, 4 - k)

    def y_phase(s):
        for j in range(4):
            at = shard(4 + j)
            for g in range(2):
                y_copy(s, j, g, at).wait_recv()
            spread(s, 4 + j)

    def x_phase(s):
        for i in range(1, 8):
            at = shard(i)
            x_copy(s, i, 2, at).wait_recv()
            d_copy(s, i, 2, at).start()

    lax.fori_loop(1, 32, packet_in, 0)
    done = 1
    for t in range(SPLITS + 2):
        until = min(16, 1 + (t + 1) * 15 // SPLITS)
        if until > done:
            lax.fori_loop(done, until, answer_one, 0)
        done = max(done, until)
        if t < SPLITS:
            z_phase(t)
        if 0 <= t - 1 < SPLITS:
            y_phase(t - 1)
        if 0 <= t - 2 < SPLITS:
            x_phase(t - 2)
    _, found = answer(0)
    rows_out[z] = found

    for s in range(SPLITS):
        for i in range(8):
            at = shard(i)
            there = at + 1 - 2 * core
            for g in range(3):
                d_copy(s, i, g, there).wait_recv()
    for s in range(SPLITS):
        for k in range(1, 4):
            for g in range(2):
                z_copy(s, k, g, z).wait_send()
        for i in range(8):
            at = shard(i)
            if i < 4:
                y_copy(s, i, 0, at).wait_send()
                y_copy(s, i, 1, at).wait_send()
            if i > 0:
                x_copy(s, i, 0, at).wait_send()
            for g in range(3):
                d_copy(s, i, g, at).wait_send()

    def finish(k, carry):
        back = lax.rem(z + 16 - k, 16)
        row_copy(k, back).wait_recv()
        row_copy(k, z).wait_send()
        vec_copy(k, back).wait_recv()
        vec_copy(k, z).wait_send()
        return carry

    lax.fori_loop(1, 16, finish, 0)

    def finish_packets(k, carry):
        packet_copy(k, me).wait_send()
        return carry

    lax.fori_loop(1, 32, finish_packets, 0)


def exchange_start(packet, vec_rows, attn, ffn, word_table, room, collective_id):
    half = jnp.bfloat16
    shard_rows, features = word_table.shape
    padded = -(-shard_rows // 128) * 128
    rows, width = attn.shape
    dma = pltpu.SemaphoreType.DMA
    vmem = pl.BlockSpec(memory_space=pltpu.VMEM)
    return pl.pallas_call(
        functools.partial(start_kernel, shard_rows, room),
        out_shape=(
            jax.ShapeDtypeStruct((32,) + packet.shape, packet.dtype),
            jax.ShapeDtypeStruct((16,) + vec_rows.shape, vec_rows.dtype),
            jax.ShapeDtypeStruct((16, rows, 3 * width), half),
            jax.ShapeDtypeStruct((16, room, features), half),
        ),
        in_specs=[vmem] * 5,
        out_specs=tuple([vmem] * 4),
        scratch_shapes=[
            pltpu.VMEM((padded, features), half),
            pltpu.VMEM((16, room, features), half),
            dma((2, 32)),
            dma((2, 16)),
            dma((2, 16)),
            dma((2, SPLITS, 3, 2)),
            dma((2, SPLITS, 4, 2)),
            dma((2, SPLITS, 8)),
            dma((2, SPLITS, 8, 3)),
        ],
        compiler_params=pltpu.CompilerParams(
            collective_id=collective_id, has_side_effects=True, vmem_limit_bytes=48 * 1024 * 1024
        ),
        cost_estimate=pl.CostEstimate(flops=0, bytes_accessed=150_000_000, transcendentals=0),
        name="exchange_start",
    )(packet, vec_rows, attn, ffn, word_table)


def split_vectors(vec_all):
    offset = SEQ * D
    position = vec_all[:offset].reshape(SEQ, D)
    emb_gain = vec_all[offset : offset + D]
    emb_shift = vec_all[offset + D : offset + 2 * D]
    offset = offset + 2 * D
    layer_parts = []
    for layer_index in range(LAYERS):
        pieces = []
        for length_now in (D, D, D, D, D, FF, D, D, D):
            pieces.append(vec_all[offset : offset + length_now])
            offset = offset + length_now
        layer_parts.append(pieces)
    return (position, emb_gain, emb_shift, layer_parts)


def layer_norm(values, gain, shift):
    center = values - jnp.mean(values, axis=-1, keepdims=True)
    spread = jnp.mean(center * center, axis=-1, keepdims=True)
    return center * lax.rsqrt(spread + NORM_EPS) * gain + shift


def embed_tokens(rows, vec_all):
    position, emb_gain, emb_shift, layer_parts = split_vectors(vec_all)
    return layer_norm(low_back(rows) + position[None], emb_gain, emb_shift)


def encoder_layer(hidden, attn_weights, ffn_weights, vec_all, key_mask, layer_index):
    q_bias, v_bias, o_bias, gain_one, shift_one, up_bias, down_bias, gain_two, second_shift = (
        split_vectors(vec_all)[3][layer_index]
    )
    sequence_count = hidden.shape[0]
    packed = matmul(low(hidden), attn_weights[:, : 3 * D])
    packed = rounded(packed + jnp.concatenate([q_bias, jnp.zeros_like(q_bias), v_bias]))
    heads_shape = (sequence_count, SEQ, HEADS, HD)
    queries = packed[..., :D].reshape(heads_shape)
    key_rows = packed[..., D : 2 * D].reshape(heads_shape)
    value_rows = packed[..., 2 * D :].reshape(heads_shape)
    scores = low_back(einsum_plain("nqhd,nkhd->nhqk", queries, key_rows) * HD ** (-0.5))
    scores = jnp.where(key_mask[:, None, None, :], scores, MASKED)
    attention = low(jax.nn.softmax(scores, axis=-1))
    context = rounded(
        einsum_plain("nhqk,nkhd->nqhd", attention, value_rows).reshape(sequence_count, SEQ, D)
    )
    attended = low_back(matmul(context, attn_weights[:, 3 * D :]) + o_bias)
    first_out = layer_norm(hidden + attended, gain_one, shift_one)
    upward = low_back(matmul(low(first_out), ffn_weights[:, :FF]) + up_bias)
    active = rounded(jax.nn.gelu(upward, approximate=True))
    downward = low_back(einsum_plain("nsf,df->nsd", active, ffn_weights[:, FF:]) + down_bias)
    return layer_norm(first_out + downward, gain_two, second_shift)


def pool_rows(hidden, key_mask, seq_lengths):
    share = key_mask.astype(jnp.float32) / seq_lengths.astype(jnp.float32)[:, None]
    return jnp.sum(hidden * share[:, :, None], axis=1)


def normalized_rows(rows):
    return rows * lax.rsqrt(jnp.sum(rows * rows, axis=-1, keepdims=True) + NORM_EPS)


def contrastive_terms(shallow_anchor, deep_anchor, shallow_pos, deep_pos, false_neg, pair_index):
    columns = lax.broadcasted_iota(jnp.int32, false_neg.shape, 1)
    hit = columns == pair_index[:, None]
    kept_cols = (false_neg == 0) | hit
    valid_rows = (pair_index >= 0).astype(jnp.float32)
    totals = jnp.zeros(pair_index.shape, jnp.float32)
    for current_width in (D, D * 2 // 3, D // 3, D // 6, D // 12):
        log_probs = []
        for anchor_vectors, positive_rows in (
            (shallow_anchor, shallow_pos),
            (deep_anchor, deep_pos),
        ):
            similarity_scores = (
                jnp.dot(
                    normalized_rows(anchor_vectors[:, :current_width]),
                    normalized_rows(positive_rows[:, :current_width]).T,
                    precision=lax.Precision.HIGHEST,
                )
                / SOFTMAX_TEMP
            )
            similarity_scores = jnp.where(kept_cols, similarity_scores, MASKED)
            log_probs.append(jax.nn.log_softmax(similarity_scores, axis=-1))
        for log_now in log_probs:
            totals = totals - jnp.sum(jnp.where(hit, log_now, 0.0), axis=-1)
        totals = totals + jnp.sum(jnp.exp(log_probs[1]) * (log_probs[1] - log_probs[0]), axis=-1)
    return jnp.sum(totals * valid_rows)


def adam_update(master, gradient, first, second, step_rate):
    first_new = BETA_ONE * first + (1.0 - BETA_ONE) * gradient
    second_new = BETA_TWO * second + (1.0 - BETA_TWO) * gradient * gradient
    first_hat = first_new / (1.0 - BETA_ONE**ADAM_STEP)
    second_hat = second_new / (1.0 - BETA_TWO**ADAM_STEP)
    master_new = master - step_rate * (
        first_hat / (jnp.sqrt(second_hat) + ADAM_EPS) + WEIGHT_DECAY * master
    )
    return (master_new, first_new, second_new)


def pad_rows(flat, multiple):
    rows = -(-flat.shape[0] // (128 * multiple)) * multiple
    return jnp.pad(flat, (0, rows * 128 - flat.shape[0])).reshape(rows, 128)


def one_hot(index, size, dtype=jnp.bfloat16):
    return (index[:, None] == lax.broadcasted_iota(jnp.int32, (1, size), 1)).astype(dtype)


def token_plan(ids, shard_rows):
    places = lax.broadcasted_iota(jnp.int32, ids.shape, 0)
    same = ids[:, None] == ids[None, :]
    leader = jnp.min(jnp.where(same, places[None, :], ids.shape[0]), axis=1)
    leads = leader == places
    owner = ids // shard_rows
    low_id = owner * shard_rows
    ahead = leads[None, :] & (ids[None, :] >= low_id[:, None]) & (ids[None, :] < ids[:, None])
    place = jnp.sum(ahead.astype(jnp.int32), axis=1)
    return owner, place, ids - low_id


def round_slots(owner, place, local_row, round_index, room, nz):
    inside = (place >= round_index * room) & (place < (round_index + 1) * room)
    slot = jnp.where(inside, owner * room + place - round_index * room, -1)
    slots = lax.broadcasted_iota(jnp.int32, (1, nz * room), 1)
    asked = jnp.max(jnp.where(slot[:, None] == slots, local_row[:, None], -1), axis=0)
    return slot, asked


def body(
    token_ids,
    lengths,
    false_neg,
    pair_index,
    word_table,
    vectors,
    attn_w,
    ffn_w,
    word_first,
    vector_first,
    attn_first,
    ffn_first,
    word_second,
    vector_second,
    attn_second,
    ffn_second,
):
    ndp = lax.axis_size("dp")
    nz = lax.axis_size("zero")
    n = ndp * nz
    by_hand = (ndp, nz) == (2, 16)
    my_dp = lax.axis_index("dp")
    my_zero = lax.axis_index("zero")
    me = my_dp * nz + my_zero
    pair_rows = token_ids.shape[0]
    total_pairs = pair_rows * n
    flat_ids = token_ids.reshape(-1, SEQ)
    seq_rows = flat_ids.shape[0]
    tokens = seq_rows * SEQ
    seq_lengths = lengths.reshape(-1)
    key_mask = lax.broadcasted_iota(jnp.int32, flat_ids.shape, 1) < seq_lengths[:, None]
    shard_rows = word_table.shape[0]
    vec_len = vectors.shape[0]

    room = -(-(tokens * 9 // 8) // (nz * 8)) * 8
    owner, place, local_row = token_plan(flat_ids.reshape(-1), shard_rows)
    slot, asked = round_slots(owner, place, local_row, 0, room, nz)
    rounds_here = jnp.max(place) // room + 1
    last = jnp.concatenate([pair_index, rounds_here[None].astype(jnp.int32)])
    packet = jnp.concatenate(
        [
            jnp.pad(asked.reshape(nz, room), ((0, 0), (0, 128 - room)), constant_values=-1),
            false_neg.reshape(-1, 128),
            jnp.pad(last, (0, 128 - last.shape[0]))[None],
        ]
    )
    packet = jnp.pad(packet, ((0, -packet.shape[0] % 8), (0, 0)))
    vec_rows = pad_rows(vectors.astype(jnp.bfloat16), 16)

    def gather_layer(layer_index):
        both = jnp.concatenate(
            [attn_w[layer_index].astype(jnp.bfloat16), ffn_w[layer_index].astype(jnp.bfloat16)],
            axis=1,
        )
        return lax.all_gather(both, "zero", axis=0, tiled=True)

    if by_hand:
        packets, vec_parts, first_weights, received = exchange_start(
            packet, vec_rows, attn_w[0], ffn_w[0], word_table, room, 0
        )
        layer_weights = [first_weights.reshape(-1, 4 * D + 2 * FF)]
    else:
        packets, vec_parts = exchange(
            [packet, vec_rows], ["all", "zero"], ndp, nz, 0, "gather_requests"
        )
        layer_weights = [gather_layer(0)]
    for layer_index in range(1, LAYERS):
        layer_weights.append(gather_layer(layer_index))
    asked_all = packets[:, :nz, :room]
    at = nz + pair_rows * total_pairs // 128
    false_all = packets[:, nz:at].reshape(total_pairs, total_pairs)
    pair_all = packets[:, at, :pair_rows].reshape(total_pairs)
    rounds = jnp.max(packets[:, at, pair_rows])
    vec_all = vec_parts.reshape(nz, -1)[:, :vec_len].reshape(-1).astype(jnp.float32)

    word_half = word_table.astype(jnp.bfloat16)
    asked_mine = lax.dynamic_index_in_dim(asked_all, my_zero, 1, keepdims=False)
    asked_near = lax.dynamic_slice_in_dim(asked_mine, my_dp * nz, nz, 0)

    def rows_for(wanted):
        return matmul(one_hot(wanted.reshape(-1), shard_rows), word_half).astype(jnp.bfloat16)

    def rows_from(slot_now, received):
        return matmul(one_hot(slot_now, nz * room), received.reshape(nz * room, D)).astype(
            jnp.bfloat16
        )

    if not by_hand:
        (received,) = exchange(
            [rows_for(asked_near).reshape(nz, room, D)], ["zero_p"], ndp, nz, 1, "send_rows"
        )
    rows = rows_from(slot, received)

    def more_rows(state):
        round_index, rows_now = state
        slot_now, asked_now = round_slots(owner, place, local_row, round_index, room, nz)
        wanted = lax.all_to_all(asked_now.reshape(nz, room), "zero", 0, 0, tiled=True)
        got = lax.all_to_all(rows_for(wanted).reshape(nz, room, D), "zero", 0, 0, tiled=True)
        return round_index + 1, rows_now + rows_from(slot_now, got)

    _, rows = lax.while_loop(lambda state: state[0] < rounds, more_rows, (jnp.int32(1), rows))
    rows = rows.reshape(seq_rows, SEQ, D).astype(jnp.float32)

    embedded, embed_back = jax.vjp(embed_tokens, rows, vec_all)
    hidden = embedded
    saved = []
    pooled = []
    for layer_index in range(LAYERS):
        layer_fn = functools.partial(encoder_layer, key_mask=key_mask, layer_index=layer_index)
        weights = layer_weights[layer_index]
        output, layer_back = jax.vjp(
            layer_fn,
            hidden,
            weights[:, : 4 * D].astype(jnp.float32),
            weights[:, 4 * D :].astype(jnp.float32),
            vec_all,
        )
        saved.append(layer_back)
        hidden = output
        pooled.append(pool_rows(hidden, key_mask, seq_lengths).astype(jnp.bfloat16))

    (pooled_all,) = exchange(
        [jnp.stack(pooled).reshape(-1, 128)], ["all"], ndp, nz, 2, "gather_pooled"
    )
    pooled_all = pooled_all.reshape(n, 2, pair_rows, 2, D).astype(jnp.float32)
    pooled_all = pooled_all.transpose(1, 3, 0, 2, 4).reshape(2, 2, total_pairs, D)

    def whole_loss(shallow_anchor, deep_anchor, shallow_pos, deep_pos):
        return contrastive_terms(
            shallow_anchor, deep_anchor, shallow_pos, deep_pos, false_all, pair_all
        )

    loss_total, loss_back = jax.vjp(
        whole_loss, pooled_all[0, 0], pooled_all[1, 0], pooled_all[0, 1], pooled_all[1, 1]
    )
    valid_total = jnp.sum((pair_all >= 0).astype(jnp.float32))
    inverse = 1.0 / jnp.maximum(valid_total, 1.0)
    loss = loss_total * inverse
    shallow_anchor_grad, deep_anchor_grad, shallow_pos_grad, deep_pos_grad = [
        lax.dynamic_slice_in_dim(part, me * pair_rows, pair_rows, 0) for part in loss_back(inverse)
    ]
    share = key_mask.astype(jnp.float32) / seq_lengths.astype(jnp.float32)[:, None]
    shallow_back = jnp.stack([shallow_anchor_grad, shallow_pos_grad], axis=1).reshape(seq_rows, D)
    deep_back = jnp.stack([deep_anchor_grad, deep_pos_grad], axis=1).reshape(seq_rows, D)
    grad_hidden = jnp.zeros_like(embedded)
    weight_parts = []
    vec_grad = jnp.zeros_like(vec_all)
    for layer_index in range(LAYERS - 1, -1, -1):
        if layer_index == LAYERS - 1:
            grad_hidden = grad_hidden + deep_back[:, None, :] * share[:, :, None]
        if layer_index == 0:
            grad_hidden = grad_hidden + shallow_back[:, None, :] * share[:, :, None]
        layer_back = saved[layer_index]
        grad_hidden, attn_grad, ffn_grad, vec_layer_grad = layer_back(grad_hidden)
        if by_hand and layer_index == 0:
            weight_parts.insert(0, (attn_grad.astype(jnp.bfloat16), ffn_grad.astype(jnp.bfloat16)))
        else:
            both = jnp.concatenate(
                [attn_grad.astype(jnp.bfloat16), ffn_grad.astype(jnp.bfloat16)], axis=1
            )
            both, grad_hidden = lax.optimization_barrier((both, grad_hidden))
            weight_parts.insert(0, lax.psum_scatter(both, "zero", scatter_dimension=0, tiled=True))
        vec_grad = vec_grad + vec_layer_grad
    rows_grad, vec_embed_grad = embed_back(grad_hidden)
    vec_grad = vec_grad + vec_embed_grad
    down_local = jnp.stack(
        [split_vectors(vec_grad)[3][layer_index][6] for layer_index in range(LAYERS)]
    )

    rows_grad = rows_grad.reshape(tokens, D).astype(jnp.bfloat16)

    def slot_sums(slot_now):
        picked = one_hot(slot_now, nz * room)
        return lax.dot_general(
            picked, rows_grad, (((0,), (0,)), ((), ())), preferred_element_type=jnp.float32
        ).astype(jnp.bfloat16)

    def into_rows(wanted, sums):
        return lax.dot_general(
            one_hot(wanted.reshape(-1), shard_rows),
            sums.reshape(-1, D),
            (((0,), (0,)), ((), ())),
            preferred_element_type=jnp.float32,
        )

    down_each = down_local.reshape(LAYERS, nz, -1).transpose(1, 0, 2).reshape(nz, -1)
    down_len = down_each.shape[1]
    vec_blocks = jnp.concatenate([vec_grad.reshape(nz, vec_len), down_each], axis=1)
    lines = -(-vec_blocks.shape[1] // 1024) * 8
    vec_blocks = jnp.pad(vec_blocks, ((0, 0), (0, lines * 128 - vec_blocks.shape[1])))
    sums = slot_sums(slot).reshape(nz, room, D)
    if by_hand:
        attn_part, ffn_part = weight_parts[0]
        attn_near, ffn_near, vec_near, sums_all, other_near = exchange_gradients(
            [
                attn_part.reshape(4, 2, 2, -1, 4 * D),
                ffn_part.reshape(4, 2, 2, -1, 2 * FF),
                vec_blocks.reshape(4, 2, 2, lines, 128),
            ],
            sums,
            weight_parts[1],
            3,
        )
        attn_shard = jnp.stack([attn_near, other_near[:, : 4 * D]])
        ffn_shard = jnp.stack([ffn_near, other_near[:, 4 * D :]])
        vec_sum = vec_near.reshape(-1)
    else:
        sums_all, vec_shares = exchange(
            [sums, vec_blocks.reshape(nz, lines, 128)],
            ["all_p", "all_p"],
            ndp,
            nz,
            3,
            "send_gradients",
        )
        vec_sum = jnp.sum(vec_shares.reshape(n, -1), axis=0)
        (weight_all,) = exchange([jnp.stack(weight_parts)], ["dp"], ndp, nz, 4, "sum_replicas")
        weight_sum = jnp.sum(weight_all.astype(jnp.float32), axis=0)
        attn_shard = weight_sum[:, :, : 4 * D]
        ffn_shard = weight_sum[:, :, 4 * D :]
    word_grad = into_rows(asked_mine, sums_all)

    def more_sums(state):
        round_index, grad_now = state
        slot_now, asked_now = round_slots(owner, place, local_row, round_index, room, nz)
        wanted = lax.all_to_all(asked_now.reshape(nz, room), "zero", 0, 0, tiled=True)
        got = lax.all_to_all(slot_sums(slot_now).reshape(nz, room, D), "zero", 0, 0, tiled=True)
        wanted = lax.all_gather(wanted, "dp", axis=0, tiled=True)
        got = lax.all_gather(got, "dp", axis=0, tiled=True)
        return round_index + 1, grad_now + into_rows(wanted, got)

    _, word_grad = lax.while_loop(
        lambda state: state[0] < rounds, more_sums, (jnp.int32(1), word_grad)
    )
    vec_shard = vec_sum[:vec_len]
    down_shard = vec_sum[vec_len : vec_len + down_len].reshape(LAYERS, -1)

    square_local = jnp.sum(word_grad * word_grad) + jnp.sum(vec_shard * vec_shard)
    square_local = square_local + jnp.sum(attn_shard * attn_shard) + jnp.sum(ffn_shard * ffn_shard)
    (squares,) = exchange(
        [jnp.broadcast_to(square_local, (8, 128))], ["zero"], ndp, nz, 5, "gather_squares"
    )
    square_total = jnp.sum(squares[:, 0, 0])
    grad_norm = jnp.sqrt(square_total)
    factor = jnp.minimum(1.0, CLIP_NORM / (grad_norm + 1e-06))
    word_new, word_first_new, word_second_new = adam_update(
        word_table, word_grad * factor, word_first, word_second, LEARN_RATE
    )
    vector_new, vector_first_new, vector_second_new = adam_update(
        vectors, vec_shard * factor, vector_first, vector_second, VECTOR_RATE
    )
    attn_new, attn_first_new, attn_second_new = adam_update(
        attn_w, attn_shard * factor, attn_first, attn_second, LEARN_RATE
    )
    ffn_new, ffn_first_new, ffn_second_new = adam_update(
        ffn_w, ffn_shard * factor, ffn_first, ffn_second, LEARN_RATE
    )
    return (
        loss,
        grad_norm,
        word_new,
        vector_new,
        attn_new,
        ffn_new,
        word_new.astype(jnp.bfloat16),
        vector_new.astype(jnp.bfloat16),
        attn_new.astype(jnp.bfloat16),
        ffn_new.astype(jnp.bfloat16),
        word_first_new,
        vector_first_new,
        attn_first_new,
        ffn_first_new,
        word_second_new,
        vector_second_new,
        attn_second_new,
        ffn_second_new,
        down_shard * factor,
    )


def solution(mesh):
    placed = (
        P(("dp", "zero"), None, None),
        P(("dp", "zero"), None),
        P(("dp", "zero"), None),
        P(("dp", "zero")),
        P("zero", None),
        P("zero"),
        P(None, "zero", None),
        P(None, "zero", None),
        P("zero", None),
        P("zero"),
        P(None, "zero", None),
        P(None, "zero", None),
        P("zero", None),
        P("zero"),
        P(None, "zero", None),
        P(None, "zero", None),
    )
    return jax.shard_map(
        body,
        mesh=mesh,
        in_specs=placed,
        out_specs=(
            P(),
            P(),
            P("zero", None),
            P("zero"),
            P(None, "zero", None),
            P(None, "zero", None),
            P("zero", None),
            P("zero"),
            P(None, "zero", None),
            P(None, "zero", None),
            P("zero", None),
            P("zero"),
            P(None, "zero", None),
            P(None, "zero", None),
            P("zero", None),
            P("zero"),
            P(None, "zero", None),
            P(None, "zero", None),
            P(None, "zero"),
        ),
        check_vma=False,
    )
```

```python
import functools

import jax
import jax.numpy as jnp
from jax import lax
from jax.experimental import pallas as pl
from jax.experimental.pallas import tpu as pltpu
from jax.sharding import PartitionSpec as P

D = 512
HEADS = 8
HD = 64
FF = 2048
SEQ = 128
LAYERS = 2
ADAM_STEP = 5


SOFTMAX_TEMP = 0.05
CLIP_NORM = 1.0
LEARN_RATE = 0.02
VECTOR_RATE = 0.15
BETA_ONE = 0.5
BETA_TWO = 0.5
WEIGHT_DECAY = 0.01
ADAM_EPS = 1e-08
NORM_EPS = 1e-06
MASKED = -1000000000.0

MESH = pl.DeviceIdType.MESH


def build_low():

    def rounder(value):
        return lax.optimization_barrier(value.astype(jnp.bfloat16)).astype(jnp.float32)

    def keep_fwd(value):
        return (rounder(value), None)

    def pass_bwd(kept, grad):
        return (grad,)

    wrapped = jax.custom_vjp(rounder)
    wrapped.defvjp(keep_fwd, pass_bwd)
    return wrapped


def build_low_back():

    def identity_fn(value):
        return value

    def keep_fwd(value):
        return (value, None)

    def round_bwd(kept, grad):
        return (low(grad),)

    wrapped = jax.custom_vjp(identity_fn)
    wrapped.defvjp(keep_fwd, round_bwd)
    return wrapped


def low(value):
    return build_low()(value)


def low_back(value):
    return build_low_back()(value)


def rounded(value):
    return low(low_back(value))


def matmul(left, right):
    return jnp.dot(left, right, preferred_element_type=jnp.float32)


def einsum_plain(form, left, right):
    return jnp.einsum(form, left, right, preferred_element_type=jnp.float32)


def exchange_kernel(modes, ndp, nz, *refs):
    count = len(modes)
    ins = refs[:count]
    outs = refs[count : 2 * count]
    sems = refs[2 * count :]
    d = lax.axis_index("dp")
    z = lax.axis_index("zero")
    me = d * nz + z
    n = ndp * nz

    def peer_of(group, k):
        if group == "dp":
            pd = lax.rem(d + k, ndp)
            return pd, z, pd
        if group == "zero":
            pz = lax.rem(z + k, nz)
            return d, pz, pz
        p = lax.rem(me + k, n)
        return p // nz, lax.rem(p, nz), p

    groups = {m.split("_")[0] for m in modes}
    sizes = {"all": n, "zero": nz, "dp": ndp}
    mine = {"all": me, "zero": z, "dp": d}
    barrier = pltpu.get_barrier_semaphore()
    meet = ["all"] if "all" in groups else sorted(groups)
    total = 0
    for group in meet:
        total += sizes[group] - 1

        def greet(k, carry, group=group):
            pd, pz, _ = peer_of(group, k)
            pl.semaphore_signal(barrier, inc=1, device_id=(pd, pz), device_id_type=MESH)
            return carry

        lax.fori_loop(1, sizes[group], greet, 0)
    pl.semaphore_wait(barrier, total)

    def make(a, k):
        mode = modes[a]
        group = mode.split("_")[0]
        pd, pz, _ = peer_of(group, k)
        src = ins[a].at[pz] if mode.endswith("_p") else ins[a]
        return pltpu.make_async_remote_copy(
            src_ref=src,
            dst_ref=outs[a].at[mine[group]],
            send_sem=sems[2 * a].at[k],
            recv_sem=sems[2 * a + 1].at[k],
            device_id=(pd, pz),
            device_id_type=MESH,
        )

    for a, mode in enumerate(modes):
        group = mode.split("_")[0]

        def begin(k, carry, a=a):
            make(a, k).start()
            return carry

        lax.fori_loop(1, sizes[group], begin, 0)
    for a, mode in enumerate(modes):
        group = mode.split("_")[0]
        if mode.endswith("_p"):
            outs[a][mine[group]] = ins[a][z]
        else:
            outs[a][mine[group]] = ins[a][...]
    for a, mode in enumerate(modes):
        group = mode.split("_")[0]

        def finish(k, carry, a=a):
            make(a, k).wait()
            return carry

        lax.fori_loop(1, sizes[group], finish, 0)


def exchange(arrays, modes, ndp, nz, collective_id, name):
    sizes = {"all": ndp * nz, "zero": nz, "dp": ndp}
    outs = []
    scratch = []
    moved = 0
    for array, mode in zip(arrays, modes):
        size = sizes[mode.split("_")[0]]
        block = array.shape[1:] if mode.endswith("_p") else array.shape
        outs.append(jax.ShapeDtypeStruct((size,) + block, array.dtype))
        scratch += [pltpu.SemaphoreType.DMA((size,)), pltpu.SemaphoreType.DMA((size,))]
        one = array.dtype.itemsize
        for s in block:
            one *= s
        moved += one * size
    vmem = pl.BlockSpec(memory_space=pltpu.VMEM)
    return pl.pallas_call(
        functools.partial(exchange_kernel, tuple(modes), ndp, nz),
        out_shape=tuple(outs),
        in_specs=[vmem] * len(arrays),
        out_specs=tuple([vmem] * len(arrays)),
        scratch_shapes=scratch,
        compiler_params=pltpu.CompilerParams(
            collective_id=collective_id, has_side_effects=True, vmem_limit_bytes=48 * 1024 * 1024
        ),
        cost_estimate=pl.CostEstimate(flops=0, bytes_accessed=20 * moved, transcendentals=0),
        name=name,
    )(*arrays)


def gradient_kernel(chunks, count, *refs):
    take = iter(refs)
    parts = [next(take) for _ in range(count)]
    sums_ref, near_ref = next(take), next(take)
    totals = [next(take) for _ in range(count)]
    rows_ref, near_out = next(take), next(take)
    bufs = [[next(take) for _ in range(5)] for _ in chunks]
    near_buf = next(take)
    send_a, recv_a, send_y, recv_y, send_z, recv_z, send_x, recv_x = [next(take) for _ in range(8)]
    row_send, row_recv, pass_send, pass_recv, near_sem = [next(take) for _ in range(5)]

    d = lax.axis_index("dp")
    z = lax.axis_index("zero")
    core = lax.rem(z, 2)
    col = lax.rem(z // 2, 2)
    line = z // 4
    sibling = z + 1 - 2 * core
    across = z + 2 - 4 * col

    def along(k):
        return lax.rem(line + k, 4) * 4 + lax.rem(z, 4)

    barrier = pltpu.get_barrier_semaphore()

    def greet(k, carry):
        pl.semaphore_signal(
            barrier, inc=1, device_id=(d, lax.rem(z + k, 16)), device_id_type=MESH
        )
        return carry

    lax.fori_loop(1, 16, greet, 0)
    pl.semaphore_signal(barrier, inc=1, device_id=(1 - d, z), device_id_type=MESH)
    pl.semaphore_wait(barrier, 16)

    def remote(src, dst, send, recv, to):
        return pltpu.make_async_remote_copy(
            src_ref=src,
            dst_ref=dst,
            send_sem=send,
            recv_sem=recv,
            device_id=to,
            device_id_type=MESH,
        )

    def copy_a(i):
        part, start, width = chunks[i]
        src = parts[part].at[:, :, 1 - core, :, pl.ds(start, width)]
        return remote(src, bufs[i][0], send_a.at[i], recv_a.at[i], (d, sibling))

    def copy_y(i):
        src = bufs[i][0].at[:, 1 - col]
        return remote(src, bufs[i][1], send_y.at[i], recv_y.at[i], (d, across))

    def copy_z(i, k):
        src = bufs[i][1].at[lax.rem(line + k, 4)]
        return remote(
            src, bufs[i][2].at[k - 1], send_z.at[i, k - 1], recv_z.at[i, k - 1], (d, along(k))
        )

    def copy_x(i):
        return remote(bufs[i][3], bufs[i][4], send_x.at[i], recv_x.at[i], (1 - d, z))

    def row_push(k):
        to = lax.rem(z + k, 16)
        return remote(sums_ref.at[to], rows_ref.at[d, z], row_send.at[k], row_recv.at[k], (d, to))

    def row_pass(k):
        at = lax.rem(z + 16 - k, 16)
        return remote(
            rows_ref.at[d, at], rows_ref.at[d, at], pass_send.at[k], pass_recv.at[k], (1 - d, z)
        )

    near = remote(near_ref, near_buf, near_sem.at[0], near_sem.at[1], (1 - d, z))

    total = len(chunks)
    for i in range(total):
        copy_a(i).start()

    def push(k, carry):
        row_push(k).start()
        return carry

    lax.fori_loop(1, 16, push, 0)
    near.start()
    rows_ref[d, z] = sums_ref[z]
    row_pass(0).start()

    def stage_a(i):
        part, start, width = chunks[i]
        copy_a(i).wait_recv()

        buf = bufs[i][0]

        def add_block(b, carry):
            line_at, col_at = b // 2, lax.rem(b, 2)
            mine = parts[part][line_at, col_at, core, :, pl.ds(start, width)].astype(jnp.float32)
            got = buf[line_at, col_at].astype(jnp.float32)
            buf[line_at, col_at] = (mine + got).astype(buf.dtype)
            return carry

        lax.fori_loop(0, 8, add_block, 0)
        copy_y(i).start()

    def stage_y(i):
        copy_y(i).wait_recv()
        buf = bufs[i][1]

        def add_block(b, carry):
            mine = bufs[i][0][b, col].astype(jnp.float32)
            buf[b] = (mine + buf[b].astype(jnp.float32)).astype(buf.dtype)
            return carry

        lax.fori_loop(0, 4, add_block, 0)
        for k in range(1, 4):
            copy_z(i, k).start()

    def stage_z(i):
        for k in range(1, 4):
            copy_z(i, k).wait_recv()
        value = bufs[i][1][line].astype(jnp.float32)
        for k in range(3):
            value = value + bufs[i][2][k].astype(jnp.float32)
        bufs[i][3][...] = value.astype(bufs[i][3].dtype)
        copy_x(i).start()

    def stage_x(i):
        part, start, width = chunks[i]
        copy_x(i).wait_recv()
        totals[part][:, pl.ds(start, width)] = bufs[i][3][...].astype(jnp.float32) + bufs[i][4][
            ...
        ].astype(jnp.float32)

    def pass_on(k):
        row_push(k).wait_recv()
        row_pass(k).start()

    passed = 1
    for t in range(total + 3):
        if t < total:
            stage_a(t)
        if 0 <= t - 1 < total:
            stage_y(t - 1)
        if 0 <= t - 2 < total:
            stage_z(t - 2)
        if 0 <= t - 3 < total:
            stage_x(t - 3)
        until = min(16, 1 + (t + 1) * 15 // (total + 3))
        for k in range(passed, until):
            pass_on(k)
        passed = until
    for k in range(passed, 16):
        pass_on(k)

    near.wait()
    near_out[...] = near_ref[...].astype(jnp.float32) + near_buf[...].astype(jnp.float32)

    for i in range(total):
        copy_a(i).wait_send()
        copy_y(i).wait_send()
        for k in range(1, 4):
            copy_z(i, k).wait_send()
        copy_x(i).wait_send()

    def finish(k, carry):
        row_push(k).wait_send()
        return carry

    lax.fori_loop(1, 16, finish, 0)

    def finish_pass(k, carry):
        row_pass(k).wait_send()
        at = lax.rem(z + 16 - k, 16)
        remote(
            rows_ref.at[1 - d, at], rows_ref.at[1 - d, at], pass_send.at[k], pass_recv.at[k], (1 - d, z)
        ).wait_recv()
        return carry

    lax.fori_loop(0, 16, finish_pass, 0)


def exchange_gradients(parts, sums, near, collective_id):
    chunks = []
    for index, part in enumerate(parts):
        width = min(part.shape[4], 1024)
        for start in range(0, part.shape[4], width):
            chunks.append((index, start, width))
    half = jnp.bfloat16
    scratch = []
    for index, start, width in chunks:
        r = parts[index].shape[3]
        scratch += [
            pltpu.VMEM((4, 2, r, width), parts[index].dtype),
            pltpu.VMEM((4, r, width), parts[index].dtype),
            pltpu.VMEM((3, r, width), parts[index].dtype),
            pltpu.VMEM((r, width), parts[index].dtype),
            pltpu.VMEM((r, width), parts[index].dtype),
        ]
    scratch += [pltpu.VMEM(near.shape, half)]
    dma = pltpu.SemaphoreType.DMA
    count = len(chunks)
    scratch += [dma((count,)) for _ in range(4)] + [dma((count, 3)) for _ in range(2)]
    scratch += [dma((count,)) for _ in range(2)]
    scratch += [dma((16,)) for _ in range(4)] + [dma((2,))]
    outs = [jax.ShapeDtypeStruct(part.shape[3:], jnp.float32) for part in parts]
    outs += [jax.ShapeDtypeStruct((2,) + sums.shape, sums.dtype)]
    outs += [jax.ShapeDtypeStruct(near.shape, jnp.float32)]
    vmem = pl.BlockSpec(memory_space=pltpu.VMEM)
    return pl.pallas_call(
        functools.partial(gradient_kernel, tuple(chunks), len(parts)),
        out_shape=tuple(outs),
        in_specs=[vmem] * (len(parts) + 2),
        out_specs=tuple([vmem] * len(outs)),
        scratch_shapes=scratch,
        compiler_params=pltpu.CompilerParams(
            collective_id=collective_id, has_side_effects=True, vmem_limit_bytes=48 * 1024 * 1024
        ),
        cost_estimate=pl.CostEstimate(flops=0, bytes_accessed=200_000_000, transcendentals=0),
        name="exchange_gradients",
    )(*parts, sums, near)


SPLITS = 4
WINDOW = 3


def start_kernel(shard_rows, room, pair_rows, *refs):
    column_ref, row_ref, packet_ref, vec_ref, attn_ref, ffn_ref, word_ref = refs[:7]
    place_out, packet_out, vec_out, weight_out, rows_out = refs[7:12]
    table, rows_held, packet, slots, locals_ = refs[12:17]
    packet_sem, vec_sem, row_sem, z_sem, y_sem, x_sem, d_sem, e_sem, own_sem = refs[17:]

    d = lax.axis_index("dp")
    z = lax.axis_index("zero")
    me = d * 16 + z
    core = lax.rem(z, 2)
    col = lax.rem(z // 2, 2)
    line = z // 4
    sibling = z + 1 - 2 * core
    across = z + 2 - 4 * col
    layers = attn_ref.shape[0]
    width = attn_ref.shape[2]
    whole = 3 * width
    plane = 7 * whole // 12
    part = plane // SPLITS
    alone = whole - plane
    x_parts = -(-alone // part)
    total = layers * SPLITS

    def everyone(k):
        p = lax.rem(me + k, 32)
        return (p // 16, lax.rem(p, 16))

    barrier = pltpu.get_barrier_semaphore()

    def greet(k, carry):
        pl.semaphore_signal(barrier, inc=1, device_id=everyone(k), device_id_type=MESH)
        return carry

    lax.fori_loop(1, 32, greet, 0)
    for layer in range(layers):
        weight_out[layer, z, :, 0:width] = attn_ref[layer].astype(jnp.bfloat16)
        weight_out[layer, z, :, width:whole] = ffn_ref[layer].astype(jnp.bfloat16)
    pl.semaphore_wait(barrier, 31)

    def remote(src, dst, sems, at, to):
        return pltpu.make_async_remote_copy(
            src_ref=src,
            dst_ref=dst,
            send_sem=sems.at[(0,) + at],
            recv_sem=sems.at[(1,) + at],
            device_id=to,
            device_id_type=MESH,
        )

    def packet_copy(k, slot):
        return remote(packet, packet_out.at[slot], packet_sem, (k,), everyone(k))

    def vec_copy(k, slot):
        return remote(vec_ref, vec_out.at[slot], vec_sem, (k,), (d, lax.rem(z + k, 16)))

    def row_copy(k, slot):
        to = lax.rem(z + k, 16)
        return remote(rows_held.at[to], rows_out.at[slot], row_sem, (k,), (d, to))

    def shard(i):
        at = lax.rem(line + i % 4, 4) * 4 + lax.rem(z, 4)
        return at if i < 4 else at + 2 - 4 * col

    def stretch(at, s, ours):
        layer, p = s // SPLITS, s % SPLITS
        first = ours * (whole - part * (p + 1)) + (1 - ours) * part * p
        return weight_out.at[layer, at, :, pl.ds(pl.multiple_of(first, 128), part)]

    def handed(at, s, ours):
        layer, p = s // SPLITS, s % SPLITS
        size = min(part, alone - part * p)
        first = ours * (whole - part * p - size) + (1 - ours) * part * p
        return weight_out.at[layer, at, :, pl.ds(pl.multiple_of(first, 128), size)]

    def both(ref, sems, at, to):
        return remote(ref, ref, sems, at, to)

    def z_copy(s, k, at):
        to = lax.rem(line + k, 4) * 4 + lax.rem(z, 4)
        return both(stretch(at, s, d), z_sem, (s, k - 1), (d, to))

    def y_copy(s, j, at):
        return both(stretch(at, s, d), y_sem, (s, j), (d, across))

    def x_copy(s, i, at, ours):
        return both(handed(at, s, ours), x_sem, (s, i), (1 - d, z))

    def d_copy(s, i, at):
        return both(stretch(at, s, d), d_sem, (s, i), (d, sibling))

    def e_copy(s, i, at):
        return both(handed(at, s, 1 - d), e_sem, (s, i), (d, sibling))

    def own_copy(layer, at):
        ref = weight_out.at[layer, at]
        return both(ref, own_sem, (layer,), (d, sibling))

    def hands(s):
        return s % SPLITS < x_parts

    def spread(s, i):
        at = shard(i)
        if i < 4:
            y_copy(s, i, at).start()
        if i > 0:
            if hands(s):
                x_copy(s, i, at, d).start()
            d_copy(s, i, at).start()

    def open_piece(s):
        for k in range(1, 4):
            z_copy(s, k, z).start()
        spread(s, 0)

    for s in range(WINDOW):
        open_piece(s)

    tokens = column_ref.shape[0]
    ids_row = row_ref[...]
    lane = lax.broadcasted_iota(jnp.int32, (1, tokens), 1).astype(jnp.float32)
    block = 128

    def lead_of(b, least):
        ids = column_ref[pl.ds(pl.multiple_of(b * block, block), block), :]
        there = lax.broadcasted_iota(jnp.int32, (block, 1), 0) + b * block
        found = jnp.where(ids == ids_row, there.astype(jnp.float32), 1e9)
        return jnp.minimum(least, jnp.min(found, axis=0, keepdims=True))

    least = lax.fori_loop(0, tokens // block, lead_of, jnp.full((1, tokens), 1e9, jnp.float32))
    lead_ids = jnp.where(least == lane, ids_row, -1)

    def place_of(b, most):
        at = pl.ds(pl.multiple_of(b * block, block), block)
        ids = column_ref[at, :]
        owner = jnp.zeros_like(ids)
        for o in range(1, 16):
            owner = owner + (ids >= o * shard_rows).astype(jnp.int32)
        low_id = owner * shard_rows
        ahead = (lead_ids >= low_id) & (lead_ids < ids)
        place = jnp.sum(jnp.where(ahead, 1.0, 0.0), axis=1, keepdims=True)
        place_out[at, :] = place.astype(jnp.int32)
        inside = place < room
        slots[at, :] = jnp.where(inside, owner * 128 + place.astype(jnp.int32), -1)
        locals_[at, :] = (ids - low_id).astype(jnp.float32)
        return jnp.maximum(most, jnp.max(place, axis=0, keepdims=True))

    most = lax.fori_loop(0, tokens // block, place_of, jnp.zeros((1, 1), jnp.float32))
    packet[...] = packet_ref[...]
    lane128 = lax.broadcasted_iota(jnp.int32, (1, 128), 1)

    for o in range(16):

        def asked_of(b, best, o=o):
            at = pl.ds(pl.multiple_of(b * block, block), block)
            found = jnp.where(slots[at, :] == o * 128 + lane128, locals_[at, :], -1.0)
            return jnp.maximum(best, jnp.max(found, axis=0, keepdims=True))

        best = lax.fori_loop(0, tokens // block, asked_of, jnp.full((1, 128), -1.0, jnp.float32))
        packet[o : o + 1, :] = best.astype(jnp.int32)
    rounds = jnp.ones((1, 1), jnp.float32)
    for r in range(1, -(-tokens // room)):
        rounds = rounds + (most >= r * room).astype(jnp.float32)
    last = packet.shape[0] - 1
    packet[last : last + 1, :] = jnp.where(
        lane128 == pair_rows, rounds.astype(jnp.int32), packet_ref[last : last + 1, :]
    )

    def send_packets(k, carry):
        packet_copy(k, me).start()
        return carry

    lax.fori_loop(1, 32, send_packets, 0)

    def send_vec(k, carry):
        vec_copy(k, z).start()
        return carry

    lax.fori_loop(1, 16, send_vec, 0)
    for layer in range(layers):
        own_copy(layer, z).start()
    packet_out[me] = packet[...]
    vec_out[z] = vec_ref[...]

    body_rows = shard_rows // 16 * 16
    step = 112 if body_rows % 112 == 0 else 16

    def to_half(i, carry):
        at = pl.multiple_of(i * step, 16)
        table[pl.ds(at, step), :] = word_ref[pl.ds(at, step), :].astype(jnp.bfloat16)
        return carry

    lax.fori_loop(0, body_rows // step, to_half, 0)
    padded = table.shape[0]
    table[body_rows:padded, :] = jnp.zeros((padded - body_rows, table.shape[1]), jnp.bfloat16)
    if shard_rows > body_rows:
        table[body_rows:shard_rows, :] = word_ref[body_rows:shard_rows, :].astype(jnp.bfloat16)

    def answer_one(k, carry):
        src = lax.rem(z + k, 16)
        asked = packet_out[d * 16 + src, pl.ds(z, 1), :]
        rows_at = lax.broadcasted_iota(jnp.int32, (padded, 128), 0)
        picked = (rows_at == asked).astype(jnp.bfloat16)
        found = lax.dot_general(
            picked, table[...], (((0,), (0,)), ((), ())), preferred_element_type=jnp.float32
        )
        rows_held[src] = found[:room, :].astype(jnp.bfloat16)
        return carry

    def packet_in(k, carry):
        packet_copy(k, lax.rem(me + 32 - k, 32)).wait_recv()
        return carry

    def row_start(k, carry):
        row_copy(k, z).start()
        return carry

    def z_phase(s):
        for k in range(1, 4):
            z_copy(s, k, shard(4 - k)).wait_recv()
            spread(s, 4 - k)
        if s + WINDOW < total:
            open_piece(s + WINDOW)

    def y_phase(s):
        for j in range(4):
            y_copy(s, j, shard(4 + j)).wait_recv()
            spread(s, 4 + j)

    def x_phase(s):
        if hands(s):
            for i in range(1, 8):
                at = shard(i)
                x_copy(s, i, at, 1 - d).wait_recv()
                e_copy(s, i, at).start()

    done = 0
    for t in range(total + 2):
        if t < total:
            z_phase(t)
        if t == 1:
            lax.fori_loop(1, 32, packet_in, 0)
        if t >= 1:
            until = min(16, done + 4)
            if until > done:
                lax.fori_loop(done, until, answer_one, 0)
            done = until
        if t == total - 1:
            lax.fori_loop(1, 16, row_start, 0)
            rows_out[z] = rows_held[z]
        if 0 <= t - 1 < total:
            y_phase(t - 1)
        if 0 <= t - 2 < total:
            x_phase(t - 2)

    turn = 1 - 2 * core
    for layer in range(layers):
        own_copy(layer, z + turn).wait_recv()
        own_copy(layer, z).wait_send()
    for s in range(total):
        for i in range(1, 8):
            at = shard(i)
            d_copy(s, i, at + turn).wait_recv()
            d_copy(s, i, at).wait_send()
            if hands(s):
                e_copy(s, i, at + turn).wait_recv()
                e_copy(s, i, at).wait_send()
                x_copy(s, i, at, d).wait_send()
        for k in range(1, 4):
            z_copy(s, k, z).wait_send()
        for i in range(4):
            y_copy(s, i, shard(i)).wait_send()

    def finish(k, carry):
        back = lax.rem(z + 16 - k, 16)
        row_copy(k, back).wait_recv()
        row_copy(k, z).wait_send()
        vec_copy(k, back).wait_recv()
        vec_copy(k, z).wait_send()
        return carry

    lax.fori_loop(1, 16, finish, 0)

    def finish_packets(k, carry):
        packet_copy(k, me).wait_send()
        return carry

    lax.fori_loop(1, 32, finish_packets, 0)


def exchange_start(ids, packet, vec_rows, attn, ffn, word_table, room, pair_rows, collective_id):
    half = jnp.bfloat16
    shard_rows, features = word_table.shape
    padded = -(-shard_rows // 128) * 128
    layers, rows, width = attn.shape
    tokens = ids.shape[0]
    pieces = layers * SPLITS
    dma = pltpu.SemaphoreType.DMA
    vmem = pl.BlockSpec(memory_space=pltpu.VMEM)
    return pl.pallas_call(
        functools.partial(start_kernel, shard_rows, room, pair_rows),
        out_shape=(
            jax.ShapeDtypeStruct((tokens, 1), jnp.int32),
            jax.ShapeDtypeStruct((32,) + packet.shape, packet.dtype),
            jax.ShapeDtypeStruct((16,) + vec_rows.shape, vec_rows.dtype),
            jax.ShapeDtypeStruct((layers, 16, rows, 3 * width), half),
            jax.ShapeDtypeStruct((16, room, features), half),
        ),
        in_specs=[vmem] * 7,
        out_specs=tuple([vmem] * 5),
        scratch_shapes=[
            pltpu.VMEM((padded, features), half),
            pltpu.VMEM((16, room, features), half),
            pltpu.VMEM(packet.shape, packet.dtype),
            pltpu.VMEM((tokens, 1), jnp.int32),
            pltpu.VMEM((tokens, 1), jnp.float32),
            dma((2, 32)),
            dma((2, 16)),
            dma((2, 16)),
            dma((2, pieces, 3)),
            dma((2, pieces, 4)),
            dma((2, pieces, 8)),
            dma((2, pieces, 8)),
            dma((2, pieces, 8)),
            dma((2, layers)),
        ],
        compiler_params=pltpu.CompilerParams(
            collective_id=collective_id, has_side_effects=True, vmem_limit_bytes=48 * 1024 * 1024
        ),
        cost_estimate=pl.CostEstimate(flops=0, bytes_accessed=150_000_000, transcendentals=0),
        name="exchange_start",
    )(ids.reshape(-1, 1), ids.reshape(1, -1), packet, vec_rows, attn, ffn, word_table)


WIDTHS = (D, D * 2 // 3, D // 3, D // 6, D // 12)


def contrastive_kernel(pooled_ref, false_ref, pair_ref, loss_ref, grad_ref):
    pairs = false_ref.shape[0]
    high = lax.Precision.HIGHEST
    columns = lax.broadcasted_iota(jnp.int32, (pairs, pairs), 1)
    hit = columns == pair_ref[...]
    kept = (false_ref[...] == 0) | hit
    hits = hit.astype(jnp.float32)
    valid = (pair_ref[...] >= 0).astype(jnp.float32)
    inverse = 1.0 / jnp.maximum(jnp.sum(valid, axis=0, keepdims=True), 1.0)
    weight = valid * inverse
    named = jnp.sum(hits, axis=1, keepdims=True)
    totals = jnp.zeros((pairs, 1), jnp.float32)
    for first, width in enumerate(WIDTHS):
        span = -(-width // 128) * 128
        inside = lax.broadcasted_iota(jnp.int32, (1, span), 1) < width
        units, scales, logs = [], [], []
        for kind in range(2):
            pair_units, pair_scales = [], []
            for role in range(2):
                rows = jnp.where(inside, pooled_ref[kind, role, :, 0:span], 0.0)
                scale = lax.rsqrt(jnp.sum(rows * rows, axis=1, keepdims=True) + NORM_EPS)
                pair_units.append(rows * scale)
                pair_scales.append(scale)
            sims = lax.dot_general(
                pair_units[0],
                pair_units[1],
                (((1,), (1,)), ((), ())),
                precision=high,
                preferred_element_type=jnp.float32,
            )
            sims = jnp.where(kept, sims / SOFTMAX_TEMP, MASKED)
            shifted = sims - jnp.max(sims, axis=1, keepdims=True)
            logs.append(shifted - jnp.log(jnp.sum(jnp.exp(shifted), axis=1, keepdims=True)))
            units.append(pair_units)
            scales.append(pair_scales)
        shallow, deep = logs
        p_shallow, p_deep = jnp.exp(shallow), jnp.exp(deep)
        gap = p_deep * (deep - shallow)
        spread = jnp.sum(gap, axis=1, keepdims=True)
        totals = totals + spread - jnp.sum(jnp.where(hit, shallow + deep, 0.0), axis=1, keepdims=True)
        d_sims = (
            p_shallow * (named + 1.0) - hits - p_deep,
            gap + p_deep * (named - spread) - hits,
        )
        for kind in range(2):
            d_cos = jnp.where(kept, d_sims[kind] * weight, 0.0) / SOFTMAX_TEMP
            for role in range(2):
                unit = units[kind][role]
                d_unit = lax.dot_general(
                    d_cos,
                    units[kind][1 - role],
                    (((1 - role,), (0,)), ((), ())),
                    precision=high,
                    preferred_element_type=jnp.float32,
                )
                along = jnp.sum(d_unit * unit, axis=1, keepdims=True)
                d_rows = scales[kind][role] * (d_unit - unit * along)
                if first == 0:
                    grad_ref[kind, role] = d_rows
                else:
                    grad_ref[kind, role, :, 0:span] = grad_ref[kind, role, :, 0:span] + d_rows
    loss_ref[...] = jnp.broadcast_to(
        jnp.sum(totals * valid, axis=0, keepdims=True) * inverse, loss_ref.shape
    )


def contrastive(pooled_all, false_all, pair_all):
    vmem = pl.BlockSpec(memory_space=pltpu.VMEM)
    loss, grads = pl.pallas_call(
        contrastive_kernel,
        out_shape=(
            jax.ShapeDtypeStruct((8, 128), jnp.float32),
            jax.ShapeDtypeStruct(pooled_all.shape, jnp.float32),
        ),
        in_specs=[vmem] * 3,
        out_specs=(vmem, vmem),
        compiler_params=pltpu.CompilerParams(vmem_limit_bytes=32 * 1024 * 1024),
        cost_estimate=pl.CostEstimate(flops=10**9, bytes_accessed=3_000_000, transcendentals=10**6),
        name="contrastive",
    )(pooled_all, false_all, pair_all.reshape(-1, 1))
    return loss[0, 0], grads


def split_vectors(vec_all):
    offset = SEQ * D
    position = vec_all[:offset].reshape(SEQ, D)
    emb_gain = vec_all[offset : offset + D]
    emb_shift = vec_all[offset + D : offset + 2 * D]
    offset = offset + 2 * D
    layer_parts = []
    for layer_index in range(LAYERS):
        pieces = []
        for length_now in (D, D, D, D, D, FF, D, D, D):
            pieces.append(vec_all[offset : offset + length_now])
            offset = offset + length_now
        layer_parts.append(pieces)
    return (position, emb_gain, emb_shift, layer_parts)


def layer_norm(values, gain, shift):
    center = values - jnp.mean(values, axis=-1, keepdims=True)
    spread = jnp.mean(center * center, axis=-1, keepdims=True)
    return center * lax.rsqrt(spread + NORM_EPS) * gain + shift


def embed_tokens(rows, vec_all):
    position, emb_gain, emb_shift, layer_parts = split_vectors(vec_all)
    return layer_norm(low_back(rows) + position[None], emb_gain, emb_shift)


def encoder_layer(hidden, attn_weights, ffn_weights, vec_all, key_mask, layer_index):
    q_bias, v_bias, o_bias, gain_one, shift_one, up_bias, down_bias, gain_two, second_shift = (
        split_vectors(vec_all)[3][layer_index]
    )
    sequence_count = hidden.shape[0]
    packed = matmul(low(hidden), attn_weights[:, : 3 * D])
    packed = rounded(packed + jnp.concatenate([q_bias, jnp.zeros_like(q_bias), v_bias]))
    heads_shape = (sequence_count, SEQ, HEADS, HD)
    queries = packed[..., :D].reshape(heads_shape)
    key_rows = packed[..., D : 2 * D].reshape(heads_shape)
    value_rows = packed[..., 2 * D :].reshape(heads_shape)
    scores = low_back(einsum_plain("nqhd,nkhd->nhqk", queries, key_rows) * HD ** (-0.5))
    scores = jnp.where(key_mask[:, None, None, :], scores, MASKED)
    attention = low(jax.nn.softmax(scores, axis=-1))
    context = rounded(
        einsum_plain("nhqk,nkhd->nqhd", attention, value_rows).reshape(sequence_count, SEQ, D)
    )
    attended = low_back(matmul(context, attn_weights[:, 3 * D :]) + o_bias)
    first_out = layer_norm(hidden + attended, gain_one, shift_one)
    upward = low_back(matmul(low(first_out), ffn_weights[:, :FF]) + up_bias)
    active = rounded(jax.nn.gelu(upward, approximate=True))
    downward = low_back(einsum_plain("nsf,df->nsd", active, ffn_weights[:, FF:]) + down_bias)
    return layer_norm(first_out + downward, gain_two, second_shift)


def pool_rows(hidden, key_mask, seq_lengths):
    share = key_mask.astype(jnp.float32) / seq_lengths.astype(jnp.float32)[:, None]
    return jnp.sum(hidden * share[:, :, None], axis=1)


def normalized_rows(rows):
    return rows * lax.rsqrt(jnp.sum(rows * rows, axis=-1, keepdims=True) + NORM_EPS)


def contrastive_terms(shallow_anchor, deep_anchor, shallow_pos, deep_pos, false_neg, pair_index):
    columns = lax.broadcasted_iota(jnp.int32, false_neg.shape, 1)
    hit = columns == pair_index[:, None]
    kept_cols = (false_neg == 0) | hit
    valid_rows = (pair_index >= 0).astype(jnp.float32)
    totals = jnp.zeros(pair_index.shape, jnp.float32)
    for current_width in (D, D * 2 // 3, D // 3, D // 6, D // 12):
        log_probs = []
        for anchor_vectors, positive_rows in (
            (shallow_anchor, shallow_pos),
            (deep_anchor, deep_pos),
        ):
            similarity_scores = (
                jnp.dot(
                    normalized_rows(anchor_vectors[:, :current_width]),
                    normalized_rows(positive_rows[:, :current_width]).T,
                    precision=lax.Precision.HIGHEST,
                )
                / SOFTMAX_TEMP
            )
            similarity_scores = jnp.where(kept_cols, similarity_scores, MASKED)
            log_probs.append(jax.nn.log_softmax(similarity_scores, axis=-1))
        for log_now in log_probs:
            totals = totals - jnp.sum(jnp.where(hit, log_now, 0.0), axis=-1)
        totals = totals + jnp.sum(jnp.exp(log_probs[1]) * (log_probs[1] - log_probs[0]), axis=-1)
    return jnp.sum(totals * valid_rows)


def adam_update(master, gradient, first, second, step_rate):
    first_new = BETA_ONE * first + (1.0 - BETA_ONE) * gradient
    second_new = BETA_TWO * second + (1.0 - BETA_TWO) * gradient * gradient
    first_hat = first_new / (1.0 - BETA_ONE**ADAM_STEP)
    second_hat = second_new / (1.0 - BETA_TWO**ADAM_STEP)
    master_new = master - step_rate * (
        first_hat / (jnp.sqrt(second_hat) + ADAM_EPS) + WEIGHT_DECAY * master
    )
    return (master_new, first_new, second_new)


def pad_rows(flat, multiple):
    rows = -(-flat.shape[0] // (128 * multiple)) * multiple
    return jnp.pad(flat, (0, rows * 128 - flat.shape[0])).reshape(rows, 128)


def one_hot(index, size, dtype=jnp.bfloat16):
    return (index[:, None] == lax.broadcasted_iota(jnp.int32, (1, size), 1)).astype(dtype)


def token_plan(ids, shard_rows):
    places = lax.broadcasted_iota(jnp.int32, ids.shape, 0)
    same = ids[:, None] == ids[None, :]
    leader = jnp.min(jnp.where(same, places[None, :], ids.shape[0]), axis=1)
    leads = leader == places
    owner = ids // shard_rows
    low_id = owner * shard_rows
    ahead = leads[None, :] & (ids[None, :] >= low_id[:, None]) & (ids[None, :] < ids[:, None])
    place = jnp.sum(ahead.astype(jnp.int32), axis=1)
    return owner, place, ids - low_id


def round_slots(owner, place, local_row, round_index, room, nz):
    inside = (place >= round_index * room) & (place < (round_index + 1) * room)
    slot = jnp.where(inside, owner * room + place - round_index * room, -1)
    slots = lax.broadcasted_iota(jnp.int32, (1, nz * room), 1)
    asked = jnp.max(jnp.where(slot[:, None] == slots, local_row[:, None], -1), axis=0)
    return slot, asked


def body(
    token_ids,
    lengths,
    false_neg,
    pair_index,
    word_table,
    vectors,
    attn_w,
    ffn_w,
    word_first,
    vector_first,
    attn_first,
    ffn_first,
    word_second,
    vector_second,
    attn_second,
    ffn_second,
):
    ndp = lax.axis_size("dp")
    nz = lax.axis_size("zero")
    n = ndp * nz
    by_hand = (ndp, nz) == (2, 16)
    my_dp = lax.axis_index("dp")
    my_zero = lax.axis_index("zero")
    me = my_dp * nz + my_zero
    pair_rows = token_ids.shape[0]
    total_pairs = pair_rows * n
    flat_ids = token_ids.reshape(-1, SEQ)
    seq_rows = flat_ids.shape[0]
    tokens = seq_rows * SEQ
    seq_lengths = lengths.reshape(-1)
    key_mask = lax.broadcasted_iota(jnp.int32, flat_ids.shape, 1) < seq_lengths[:, None]
    shard_rows = word_table.shape[0]
    vec_len = vectors.shape[0]

    room = -(-(tokens * 9 // 8) // (nz * 8)) * 8
    ids = flat_ids.reshape(-1)

    def packet_of(asked, rounds_here):
        last = jnp.concatenate([pair_index, rounds_here[None].astype(jnp.int32)])
        lines = nz + false_neg.size // 128
        return jnp.concatenate(
            [
                jnp.pad(asked.reshape(nz, room), ((0, 0), (0, 128 - room)), constant_values=-1),
                false_neg.reshape(-1, 128),
                jnp.zeros((7 - lines % 8, 128), jnp.int32),
                jnp.pad(last, (0, 128 - last.shape[0]))[None],
            ]
        )

    vec_rows = pad_rows(vectors.astype(jnp.bfloat16), 16)

    def gather_layer(layer_index):
        both = jnp.concatenate(
            [attn_w[layer_index].astype(jnp.bfloat16), ffn_w[layer_index].astype(jnp.bfloat16)],
            axis=1,
        )
        return lax.all_gather(both, "zero", axis=0, tiled=True)

    if by_hand:
        packet = packet_of(jnp.zeros((nz * room,), jnp.int32), jnp.int32(0))
        place, packets, vec_parts, gathered, received = exchange_start(
            ids, packet, vec_rows, attn_w, ffn_w, word_table, room, pair_rows, 0
        )
        layer_weights = [gathered[layer].reshape(-1, 4 * D + 2 * FF) for layer in range(LAYERS)]
        owner = ids // shard_rows
        place, local_row = place.reshape(-1), ids - owner * shard_rows
        slot = jnp.where(place < room, owner * room + place, -1)
    else:
        owner, place, local_row = token_plan(ids, shard_rows)
        slot, asked = round_slots(owner, place, local_row, 0, room, nz)
        packets, vec_parts = exchange(
            [packet_of(asked, jnp.max(place) // room + 1), vec_rows],
            ["all", "zero"],
            ndp,
            nz,
            0,
            "gather_requests",
        )
        layer_weights = [gather_layer(layer_index) for layer_index in range(LAYERS)]
    asked_all = packets[:, :nz, :room]
    false_all = packets[:, nz : nz + false_neg.size // 128].reshape(total_pairs, total_pairs)
    pair_all = packets[:, -1, :pair_rows].reshape(total_pairs)
    rounds = jnp.max(packets[:, -1, pair_rows])
    vec_all = vec_parts.reshape(nz, -1)[:, :vec_len].reshape(-1).astype(jnp.float32)

    word_half = word_table.astype(jnp.bfloat16)
    asked_mine = lax.dynamic_index_in_dim(asked_all, my_zero, 1, keepdims=False)
    asked_near = lax.dynamic_slice_in_dim(asked_mine, my_dp * nz, nz, 0)

    def rows_for(wanted):
        return matmul(one_hot(wanted.reshape(-1), shard_rows), word_half).astype(jnp.bfloat16)

    def rows_from(slot_now, received):
        return matmul(one_hot(slot_now, nz * room), received.reshape(nz * room, D)).astype(
            jnp.bfloat16
        )

    if not by_hand:
        (received,) = exchange(
            [rows_for(asked_near).reshape(nz, room, D)], ["zero_p"], ndp, nz, 1, "send_rows"
        )
    rows = rows_from(slot, received)

    def more_rows(state):
        round_index, rows_now = state
        slot_now, asked_now = round_slots(owner, place, local_row, round_index, room, nz)
        wanted = lax.all_to_all(asked_now.reshape(nz, room), "zero", 0, 0, tiled=True)
        got = lax.all_to_all(rows_for(wanted).reshape(nz, room, D), "zero", 0, 0, tiled=True)
        return round_index + 1, rows_now + rows_from(slot_now, got)

    _, rows = lax.while_loop(lambda state: state[0] < rounds, more_rows, (jnp.int32(1), rows))
    rows = rows.reshape(seq_rows, SEQ, D).astype(jnp.float32)

    embedded, embed_back = jax.vjp(embed_tokens, rows, vec_all)
    hidden = embedded
    saved = []
    pooled = []
    for layer_index in range(LAYERS):
        layer_fn = functools.partial(encoder_layer, key_mask=key_mask, layer_index=layer_index)
        weights = layer_weights[layer_index]
        output, layer_back = jax.vjp(
            layer_fn,
            hidden,
            weights[:, : 4 * D].astype(jnp.float32),
            weights[:, 4 * D :].astype(jnp.float32),
            vec_all,
        )
        saved.append(layer_back)
        hidden = output
        pooled.append(pool_rows(hidden, key_mask, seq_lengths).astype(jnp.bfloat16))

    (pooled_all,) = exchange(
        [jnp.stack(pooled).reshape(-1, 128)], ["all"], ndp, nz, 2, "gather_pooled"
    )
    pooled_all = pooled_all.reshape(n, 2, pair_rows, 2, D).astype(jnp.float32)
    pooled_all = pooled_all.transpose(1, 3, 0, 2, 4).reshape(2, 2, total_pairs, D)
    if total_pairs <= 256:
        loss, pooled_grads = contrastive(pooled_all, false_all, pair_all)
    else:

        def whole_loss(pooled_now):
            summed = contrastive_terms(
                pooled_now[0, 0],
                pooled_now[1, 0],
                pooled_now[0, 1],
                pooled_now[1, 1],
                false_all,
                pair_all,
            )
            valid_total = jnp.sum((pair_all >= 0).astype(jnp.float32))
            return summed / jnp.maximum(valid_total, 1.0)

        loss, pooled_grads = jax.value_and_grad(whole_loss)(pooled_all)
    pooled_grads = lax.dynamic_slice_in_dim(pooled_grads, me * pair_rows, pair_rows, 2)
    pooled_grads = pooled_grads.transpose(0, 2, 1, 3).reshape(2, seq_rows, D)
    shallow_back, deep_back = pooled_grads[0], pooled_grads[1]
    share = key_mask.astype(jnp.float32) / seq_lengths.astype(jnp.float32)[:, None]
    grad_hidden = jnp.zeros_like(embedded)
    weight_parts = []
    vec_grad = jnp.zeros_like(vec_all)
    for layer_index in range(LAYERS - 1, -1, -1):
        if layer_index == LAYERS - 1:
            grad_hidden = grad_hidden + deep_back[:, None, :] * share[:, :, None]
        if layer_index == 0:
            grad_hidden = grad_hidden + shallow_back[:, None, :] * share[:, :, None]
        layer_back = saved[layer_index]
        grad_hidden, attn_grad, ffn_grad, vec_layer_grad = layer_back(grad_hidden)
        if by_hand and layer_index == 0:
            weight_parts.insert(0, (attn_grad.astype(jnp.bfloat16), ffn_grad.astype(jnp.bfloat16)))
        else:
            both = jnp.concatenate(
                [attn_grad.astype(jnp.bfloat16), ffn_grad.astype(jnp.bfloat16)], axis=1
            )
            both, grad_hidden = lax.optimization_barrier((both, grad_hidden))
            weight_parts.insert(0, lax.psum_scatter(both, "zero", scatter_dimension=0, tiled=True))
        vec_grad = vec_grad + vec_layer_grad
    rows_grad, vec_embed_grad = embed_back(grad_hidden)
    vec_grad = vec_grad + vec_embed_grad
    down_local = jnp.stack(
        [split_vectors(vec_grad)[3][layer_index][6] for layer_index in range(LAYERS)]
    )

    rows_grad = rows_grad.reshape(tokens, D).astype(jnp.bfloat16)

    def slot_sums(slot_now):
        picked = one_hot(slot_now, nz * room)
        return lax.dot_general(
            picked, rows_grad, (((0,), (0,)), ((), ())), preferred_element_type=jnp.float32
        ).astype(jnp.bfloat16)

    def into_rows(wanted, sums):
        return lax.dot_general(
            one_hot(wanted.reshape(-1), shard_rows),
            sums.reshape(-1, D),
            (((0,), (0,)), ((), ())),
            preferred_element_type=jnp.float32,
        )

    down_each = down_local.reshape(LAYERS, nz, -1).transpose(1, 0, 2).reshape(nz, -1)
    down_len = down_each.shape[1]
    vec_blocks = jnp.concatenate([vec_grad.reshape(nz, vec_len), down_each], axis=1)
    lines = -(-vec_blocks.shape[1] // 1024) * 8
    vec_blocks = jnp.pad(vec_blocks, ((0, 0), (0, lines * 128 - vec_blocks.shape[1])))
    sums = slot_sums(slot).reshape(nz, room, D)
    if by_hand:
        attn_part, ffn_part = weight_parts[0]
        attn_near, ffn_near, vec_near, sums_all, other_near = exchange_gradients(
            [
                attn_part.reshape(4, 2, 2, -1, 4 * D),
                ffn_part.reshape(4, 2, 2, -1, 2 * FF),
                vec_blocks.reshape(4, 2, 2, lines, 128),
            ],
            sums,
            weight_parts[1],
            3,
        )
        attn_shard = jnp.stack([attn_near, other_near[:, : 4 * D]])
        ffn_shard = jnp.stack([ffn_near, other_near[:, 4 * D :]])
        vec_sum = vec_near.reshape(-1)
    else:
        sums_all, vec_shares = exchange(
            [sums, vec_blocks.reshape(nz, lines, 128)],
            ["all_p", "all_p"],
            ndp,
            nz,
            3,
            "send_gradients",
        )
        vec_sum = jnp.sum(vec_shares.reshape(n, -1), axis=0)
        (weight_all,) = exchange([jnp.stack(weight_parts)], ["dp"], ndp, nz, 4, "sum_replicas")
        weight_sum = jnp.sum(weight_all.astype(jnp.float32), axis=0)
        attn_shard = weight_sum[:, :, : 4 * D]
        ffn_shard = weight_sum[:, :, 4 * D :]
    word_grad = into_rows(asked_mine, sums_all)

    def more_sums(state):
        round_index, grad_now = state
        slot_now, asked_now = round_slots(owner, place, local_row, round_index, room, nz)
        wanted = lax.all_to_all(asked_now.reshape(nz, room), "zero", 0, 0, tiled=True)
        got = lax.all_to_all(slot_sums(slot_now).reshape(nz, room, D), "zero", 0, 0, tiled=True)
        wanted = lax.all_gather(wanted, "dp", axis=0, tiled=True)
        got = lax.all_gather(got, "dp", axis=0, tiled=True)
        return round_index + 1, grad_now + into_rows(wanted, got)

    _, word_grad = lax.while_loop(
        lambda state: state[0] < rounds, more_sums, (jnp.int32(1), word_grad)
    )
    vec_shard = vec_sum[:vec_len]
    down_shard = vec_sum[vec_len : vec_len + down_len].reshape(LAYERS, -1)

    square_local = jnp.sum(word_grad * word_grad) + jnp.sum(vec_shard * vec_shard)
    square_local = square_local + jnp.sum(attn_shard * attn_shard) + jnp.sum(ffn_shard * ffn_shard)
    (squares,) = exchange(
        [jnp.broadcast_to(square_local, (8, 128))], ["zero"], ndp, nz, 5, "gather_squares"
    )
    square_total = jnp.sum(squares[:, 0, 0])
    grad_norm = jnp.sqrt(square_total)
    factor = jnp.minimum(1.0, CLIP_NORM / (grad_norm + 1e-06))
    word_new, word_first_new, word_second_new = adam_update(
        word_table, word_grad * factor, word_first, word_second, LEARN_RATE
    )
    vector_new, vector_first_new, vector_second_new = adam_update(
        vectors, vec_shard * factor, vector_first, vector_second, VECTOR_RATE
    )
    attn_new, attn_first_new, attn_second_new = adam_update(
        attn_w, attn_shard * factor, attn_first, attn_second, LEARN_RATE
    )
    ffn_new, ffn_first_new, ffn_second_new = adam_update(
        ffn_w, ffn_shard * factor, ffn_first, ffn_second, LEARN_RATE
    )
    return (
        loss,
        grad_norm,
        word_new,
        vector_new,
        attn_new,
        ffn_new,
        word_new.astype(jnp.bfloat16),
        vector_new.astype(jnp.bfloat16),
        attn_new.astype(jnp.bfloat16),
        ffn_new.astype(jnp.bfloat16),
        word_first_new,
        vector_first_new,
        attn_first_new,
        ffn_first_new,
        word_second_new,
        vector_second_new,
        attn_second_new,
        ffn_second_new,
        down_shard * factor,
    )


def solution(mesh):
    placed = (
        P(("dp", "zero"), None, None),
        P(("dp", "zero"), None),
        P(("dp", "zero"), None),
        P(("dp", "zero")),
        P("zero", None),
        P("zero"),
        P(None, "zero", None),
        P(None, "zero", None),
        P("zero", None),
        P("zero"),
        P(None, "zero", None),
        P(None, "zero", None),
        P("zero", None),
        P("zero"),
        P(None, "zero", None),
        P(None, "zero", None),
    )
    return jax.shard_map(
        body,
        mesh=mesh,
        in_specs=placed,
        out_specs=(
            P(),
            P(),
            P("zero", None),
            P("zero"),
            P(None, "zero", None),
            P(None, "zero", None),
            P("zero", None),
            P("zero"),
            P(None, "zero", None),
            P(None, "zero", None),
            P("zero", None),
            P("zero"),
            P(None, "zero", None),
            P(None, "zero", None),
            P("zero", None),
            P("zero"),
            P(None, "zero", None),
            P(None, "zero", None),
            P(None, "zero"),
        ),
        check_vma=False,
    )
```

```python
import functools

import jax
import jax.numpy as jnp
from jax import lax
from jax.experimental import pallas as pl
from jax.experimental.pallas import tpu as pltpu
from jax.sharding import PartitionSpec as P

D = 512
HEADS = 8
HD = 64
FF = 2048
SEQ = 128
LAYERS = 2
ADAM_STEP = 5


SOFTMAX_TEMP = 0.05
CLIP_NORM = 1.0
LEARN_RATE = 0.02
VECTOR_RATE = 0.15
BETA_ONE = 0.5
BETA_TWO = 0.5
WEIGHT_DECAY = 0.01
ADAM_EPS = 1e-08
NORM_EPS = 1e-06
MASKED = -1000000000.0

MESH = pl.DeviceIdType.MESH


def build_low():

    def rounder(value):
        return lax.optimization_barrier(value.astype(jnp.bfloat16)).astype(jnp.float32)

    def keep_fwd(value):
        return (rounder(value), None)

    def pass_bwd(kept, grad):
        return (grad,)

    wrapped = jax.custom_vjp(rounder)
    wrapped.defvjp(keep_fwd, pass_bwd)
    return wrapped


def build_low_back():

    def identity_fn(value):
        return value

    def keep_fwd(value):
        return (value, None)

    def round_bwd(kept, grad):
        return (low(grad),)

    wrapped = jax.custom_vjp(identity_fn)
    wrapped.defvjp(keep_fwd, round_bwd)
    return wrapped


def low(value):
    return build_low()(value)


def low_back(value):
    return build_low_back()(value)


def rounded(value):
    return low(low_back(value))


def matmul(left, right):
    return jnp.dot(left, right, preferred_element_type=jnp.float32)


def einsum_plain(form, left, right):
    return jnp.einsum(form, left, right, preferred_element_type=jnp.float32)


def exchange_kernel(modes, ndp, nz, *refs):
    count = len(modes)
    ins = refs[:count]
    outs = refs[count : 2 * count]
    sems = refs[2 * count :]
    d = lax.axis_index("dp")
    z = lax.axis_index("zero")
    me = d * nz + z
    n = ndp * nz

    def peer_of(group, k):
        if group == "dp":
            pd = lax.rem(d + k, ndp)
            return pd, z, pd
        if group == "zero":
            pz = lax.rem(z + k, nz)
            return d, pz, pz
        p = lax.rem(me + k, n)
        return p // nz, lax.rem(p, nz), p

    groups = {m.split("_")[0] for m in modes}
    sizes = {"all": n, "zero": nz, "dp": ndp}
    mine = {"all": me, "zero": z, "dp": d}
    barrier = pltpu.get_barrier_semaphore()
    meet = ["all"] if "all" in groups else sorted(groups)
    total = 0
    for group in meet:
        total += sizes[group] - 1

        def greet(k, carry, group=group):
            pd, pz, _ = peer_of(group, k)
            pl.semaphore_signal(barrier, inc=1, device_id=(pd, pz), device_id_type=MESH)
            return carry

        lax.fori_loop(1, sizes[group], greet, 0)
    pl.semaphore_wait(barrier, total)

    def make(a, k):
        mode = modes[a]
        group = mode.split("_")[0]
        pd, pz, _ = peer_of(group, k)
        src = ins[a].at[pz] if mode.endswith("_p") else ins[a]
        return pltpu.make_async_remote_copy(
            src_ref=src,
            dst_ref=outs[a].at[mine[group]],
            send_sem=sems[2 * a].at[k],
            recv_sem=sems[2 * a + 1].at[k],
            device_id=(pd, pz),
            device_id_type=MESH,
        )

    for a, mode in enumerate(modes):
        group = mode.split("_")[0]

        def begin(k, carry, a=a):
            make(a, k).start()
            return carry

        lax.fori_loop(1, sizes[group], begin, 0)
    for a, mode in enumerate(modes):
        group = mode.split("_")[0]
        if mode.endswith("_p"):
            outs[a][mine[group]] = ins[a][z]
        else:
            outs[a][mine[group]] = ins[a][...]
    for a, mode in enumerate(modes):
        group = mode.split("_")[0]

        def finish(k, carry, a=a):
            make(a, k).wait()
            return carry

        lax.fori_loop(1, sizes[group], finish, 0)


def exchange(arrays, modes, ndp, nz, collective_id, name):
    sizes = {"all": ndp * nz, "zero": nz, "dp": ndp}
    outs = []
    scratch = []
    moved = 0
    for array, mode in zip(arrays, modes):
        size = sizes[mode.split("_")[0]]
        block = array.shape[1:] if mode.endswith("_p") else array.shape
        outs.append(jax.ShapeDtypeStruct((size,) + block, array.dtype))
        scratch += [pltpu.SemaphoreType.DMA((size,)), pltpu.SemaphoreType.DMA((size,))]
        one = array.dtype.itemsize
        for s in block:
            one *= s
        moved += one * size
    vmem = pl.BlockSpec(memory_space=pltpu.VMEM)
    return pl.pallas_call(
        functools.partial(exchange_kernel, tuple(modes), ndp, nz),
        out_shape=tuple(outs),
        in_specs=[vmem] * len(arrays),
        out_specs=tuple([vmem] * len(arrays)),
        scratch_shapes=scratch,
        compiler_params=pltpu.CompilerParams(
            collective_id=collective_id, has_side_effects=True, vmem_limit_bytes=48 * 1024 * 1024
        ),
        cost_estimate=pl.CostEstimate(flops=0, bytes_accessed=20 * moved, transcendentals=0),
        name=name,
    )(*arrays)


def gradient_kernel(chunks, count, *refs):
    take = iter(refs)
    parts = [next(take) for _ in range(count)]
    sums_ref, near_ref = next(take), next(take)
    totals = [next(take) for _ in range(count)]
    rows_ref, near_out = next(take), next(take)
    bufs = [[next(take) for _ in range(5)] for _ in chunks]
    near_buf = next(take)
    send_a, recv_a, send_y, recv_y, send_z, recv_z, send_x, recv_x = [next(take) for _ in range(8)]
    row_send, row_recv, pass_send, pass_recv, near_sem = [next(take) for _ in range(5)]

    d = lax.axis_index("dp")
    z = lax.axis_index("zero")
    core = lax.rem(z, 2)
    col = lax.rem(z // 2, 2)
    line = z // 4
    sibling = z + 1 - 2 * core
    across = z + 2 - 4 * col

    def along(k):
        return lax.rem(line + k, 4) * 4 + lax.rem(z, 4)

    barrier = pltpu.get_barrier_semaphore()

    def greet(k, carry):
        pl.semaphore_signal(
            barrier, inc=1, device_id=(d, lax.rem(z + k, 16)), device_id_type=MESH
        )
        return carry

    lax.fori_loop(1, 16, greet, 0)
    pl.semaphore_signal(barrier, inc=1, device_id=(1 - d, z), device_id_type=MESH)
    pl.semaphore_wait(barrier, 16)

    def remote(src, dst, send, recv, to):
        return pltpu.make_async_remote_copy(
            src_ref=src,
            dst_ref=dst,
            send_sem=send,
            recv_sem=recv,
            device_id=to,
            device_id_type=MESH,
        )

    def copy_a(i):
        part, start, width = chunks[i]
        src = parts[part].at[:, :, 1 - core, :, pl.ds(start, width)]
        return remote(src, bufs[i][0], send_a.at[i], recv_a.at[i], (d, sibling))

    def copy_y(i):
        src = bufs[i][0].at[:, 1 - col]
        return remote(src, bufs[i][1], send_y.at[i], recv_y.at[i], (d, across))

    def copy_z(i, k):
        src = bufs[i][1].at[lax.rem(line + k, 4)]
        return remote(
            src, bufs[i][2].at[k - 1], send_z.at[i, k - 1], recv_z.at[i, k - 1], (d, along(k))
        )

    def copy_x(i):
        return remote(bufs[i][3], bufs[i][4], send_x.at[i], recv_x.at[i], (1 - d, z))

    def row_push(k):
        to = lax.rem(z + k, 16)
        return remote(sums_ref.at[to], rows_ref.at[d, z], row_send.at[k], row_recv.at[k], (d, to))

    def row_pass(k):
        at = lax.rem(z + 16 - k, 16)
        return remote(
            rows_ref.at[d, at], rows_ref.at[d, at], pass_send.at[k], pass_recv.at[k], (1 - d, z)
        )

    near = remote(near_ref, near_buf, near_sem.at[0], near_sem.at[1], (1 - d, z))

    total = len(chunks)
    for i in range(total):
        copy_a(i).start()

    def push(k, carry):
        row_push(k).start()
        return carry

    lax.fori_loop(1, 16, push, 0)
    near.start()
    rows_ref[d, z] = sums_ref[z]
    row_pass(0).start()

    def stage_a(i):
        part, start, width = chunks[i]
        copy_a(i).wait_recv()

        buf = bufs[i][0]

        def add_block(b, carry):
            line_at, col_at = b // 2, lax.rem(b, 2)
            mine = parts[part][line_at, col_at, core, :, pl.ds(start, width)].astype(jnp.float32)
            got = buf[line_at, col_at].astype(jnp.float32)
            buf[line_at, col_at] = (mine + got).astype(buf.dtype)
            return carry

        lax.fori_loop(0, 8, add_block, 0)
        copy_y(i).start()

    def stage_y(i):
        copy_y(i).wait_recv()
        buf = bufs[i][1]

        def add_block(b, carry):
            mine = bufs[i][0][b, col].astype(jnp.float32)
            buf[b] = (mine + buf[b].astype(jnp.float32)).astype(buf.dtype)
            return carry

        lax.fori_loop(0, 4, add_block, 0)
        for k in range(1, 4):
            copy_z(i, k).start()

    def stage_z(i):
        for k in range(1, 4):
            copy_z(i, k).wait_recv()
        value = bufs[i][1][line].astype(jnp.float32)
        for k in range(3):
            value = value + bufs[i][2][k].astype(jnp.float32)
        bufs[i][3][...] = value.astype(bufs[i][3].dtype)
        copy_x(i).start()

    def stage_x(i):
        part, start, width = chunks[i]
        copy_x(i).wait_recv()
        totals[part][:, pl.ds(start, width)] = bufs[i][3][...].astype(jnp.float32) + bufs[i][4][
            ...
        ].astype(jnp.float32)

    def pass_on(k):
        row_push(k).wait_recv()
        row_pass(k).start()

    passed = 1
    for t in range(total + 3):
        if t < total:
            stage_a(t)
        if 0 <= t - 1 < total:
            stage_y(t - 1)
        if 0 <= t - 2 < total:
            stage_z(t - 2)
        if 0 <= t - 3 < total:
            stage_x(t - 3)
        until = min(16, 1 + (t + 1) * 15 // (total + 3))
        for k in range(passed, until):
            pass_on(k)
        passed = until
    for k in range(passed, 16):
        pass_on(k)

    near.wait()
    near_out[...] = near_ref[...].astype(jnp.float32) + near_buf[...].astype(jnp.float32)

    for i in range(total):
        copy_a(i).wait_send()
        copy_y(i).wait_send()
        for k in range(1, 4):
            copy_z(i, k).wait_send()
        copy_x(i).wait_send()

    def finish(k, carry):
        row_push(k).wait_send()
        return carry

    lax.fori_loop(1, 16, finish, 0)

    def finish_pass(k, carry):
        row_pass(k).wait_send()
        at = lax.rem(z + 16 - k, 16)
        remote(
            rows_ref.at[1 - d, at], rows_ref.at[1 - d, at], pass_send.at[k], pass_recv.at[k], (1 - d, z)
        ).wait_recv()
        return carry

    lax.fori_loop(0, 16, finish_pass, 0)


def exchange_gradients(parts, sums, near, collective_id):
    chunks = []
    for index, part in enumerate(parts):
        width = part.shape[4] // -(-part.shape[4] // 1024)
        for start in range(0, part.shape[4], width):
            chunks.append((index, start, width))
    half = jnp.bfloat16
    scratch = []
    for index, start, width in chunks:
        r = parts[index].shape[3]
        scratch += [
            pltpu.VMEM((4, 2, r, width), parts[index].dtype),
            pltpu.VMEM((4, r, width), parts[index].dtype),
            pltpu.VMEM((3, r, width), parts[index].dtype),
            pltpu.VMEM((r, width), parts[index].dtype),
            pltpu.VMEM((r, width), parts[index].dtype),
        ]
    scratch += [pltpu.VMEM(near.shape, half)]
    dma = pltpu.SemaphoreType.DMA
    count = len(chunks)
    scratch += [dma((count,)) for _ in range(4)] + [dma((count, 3)) for _ in range(2)]
    scratch += [dma((count,)) for _ in range(2)]
    scratch += [dma((16,)) for _ in range(4)] + [dma((2,))]
    outs = [jax.ShapeDtypeStruct(part.shape[3:], jnp.float32) for part in parts]
    outs += [jax.ShapeDtypeStruct((2,) + sums.shape, sums.dtype)]
    outs += [jax.ShapeDtypeStruct(near.shape, jnp.float32)]
    vmem = pl.BlockSpec(memory_space=pltpu.VMEM)
    return pl.pallas_call(
        functools.partial(gradient_kernel, tuple(chunks), len(parts)),
        out_shape=tuple(outs),
        in_specs=[vmem] * (len(parts) + 2),
        out_specs=tuple([vmem] * len(outs)),
        scratch_shapes=scratch,
        compiler_params=pltpu.CompilerParams(
            collective_id=collective_id, has_side_effects=True, vmem_limit_bytes=48 * 1024 * 1024
        ),
        cost_estimate=pl.CostEstimate(flops=0, bytes_accessed=200_000_000, transcendentals=0),
        name="exchange_gradients",
    )(*parts, sums, near)


SPLITS = 4
WINDOW = 3
LAG = 3


def start_kernel(shard_rows, room, *refs):
    column_ref, row_ref, packet_ref, vec_ref, attn_ref, ffn_ref, word_ref = refs[:7]
    place_out, packet_out, asked_out, weight_out, rows_out = refs[7:12]
    table, rows_held, asked, slots, locals_ = refs[12:17]
    packet_sem, asked_sem, row_sem, z_sem, y_sem, x_sem, d_sem, e_sem, own_sem = refs[17:]

    d = lax.axis_index("dp")
    z = lax.axis_index("zero")
    me = d * 16 + z
    core = lax.rem(z, 2)
    col = lax.rem(z // 2, 2)
    line = z // 4
    sibling = z + 1 - 2 * core
    across = z + 2 - 4 * col
    layers = attn_ref.shape[0]
    width = attn_ref.shape[2]
    whole = weight_out.shape[3]
    unit = whole // 128 // SPLITS
    hand = unit * 5 // 12
    total = layers * SPLITS

    def everyone(k):
        p = lax.rem(me + k, 32)
        return (p // 16, lax.rem(p, 16))

    barrier = pltpu.get_barrier_semaphore()

    def greet(k, carry):
        pl.semaphore_signal(barrier, inc=1, device_id=everyone(k), device_id_type=MESH)
        return carry

    lax.fori_loop(1, 32, greet, 0)
    for layer in range(layers):
        weight_out[layer, z, :, 0:width] = attn_ref[layer].astype(jnp.bfloat16)
        weight_out[layer, z, :, width : 3 * width] = ffn_ref[layer].astype(jnp.bfloat16)
        weight_out[layer, z, :, 3 * width : whole] = vec_ref[layer]
    pl.semaphore_wait(barrier, 31)

    def remote(src, dst, sems, at, to):
        return pltpu.make_async_remote_copy(
            src_ref=src,
            dst_ref=dst,
            send_sem=sems.at[(0,) + at],
            recv_sem=sems.at[(1,) + at],
            device_id=to,
            device_id_type=MESH,
        )

    def packet_copy(k, slot):
        return remote(packet_ref, packet_out.at[slot], packet_sem, (k,), everyone(k))

    def asked_copy(k, slot):
        to = everyone(k)
        return remote(asked.at[to[1]], asked_out.at[slot], asked_sem, (k,), to)

    def row_copy(k, slot):
        to = lax.rem(z + k, 16)
        return remote(rows_held.at[to], rows_out.at[slot], row_sem, (k,), (d, to))

    def shard(i):
        at = lax.rem(line + i % 4, 4) * 4 + lax.rem(z, 4)
        return at if i < 4 else at + 2 - 4 * col

    def piece(s):
        layer, p = s // SPLITS, s % SPLITS
        size = unit if p < SPLITS - 1 else whole // 128 - p * unit
        return layer, p * unit, size

    def columns_of(at, s, first, size):
        layer, base, _ = piece(s)
        return weight_out.at[
            layer, at, :, pl.ds(pl.multiple_of((base + first) * 128, 128), size * 128)
        ]

    def stretch(at, s, ours):
        size = piece(s)[2]
        return columns_of(at, s, ours * hand, size - hand)

    def handed(at, s, ours):
        size = piece(s)[2]
        return columns_of(at, s, ours * (size - hand), hand)

    def both(ref, sems, at, to):
        return remote(ref, ref, sems, at, to)

    def z_copy(s, k, at):
        to = lax.rem(line + k, 4) * 4 + lax.rem(z, 4)
        return both(stretch(at, s, d), z_sem, (s, k - 1), (d, to))

    def y_copy(s, j, at):
        return both(stretch(at, s, d), y_sem, (s, j), (d, across))

    def x_copy(s, i, at, ours):
        return both(handed(at, s, ours), x_sem, (s, i), (1 - d, z))

    def d_copy(s, i, at):
        return both(stretch(at, s, d), d_sem, (s, i), (d, sibling))

    def e_copy(s, i, at):
        return both(handed(at, s, 1 - d), e_sem, (s, i), (d, sibling))

    def own_copy(layer, at):
        ref = weight_out.at[layer, at]
        return both(ref, own_sem, (layer,), (d, sibling))

    def spread(s, i):
        at = shard(i)
        if i < 4:
            y_copy(s, i, at).start()
        if i > 0:
            x_copy(s, i, at, d).start()
            d_copy(s, i, at).start()

    def open_piece(s):
        for k in range(1, 4):
            z_copy(s, k, z).start()
        spread(s, 0)

    for s in range(WINDOW):
        open_piece(s)

    tokens = column_ref.shape[0]
    ids_row = row_ref[...]
    lane = lax.broadcasted_iota(jnp.int32, (1, tokens), 1).astype(jnp.float32)
    block = 128

    def lead_of(b, least):
        ids = column_ref[pl.ds(pl.multiple_of(b * block, block), block), :]
        there = lax.broadcasted_iota(jnp.int32, (block, 1), 0) + b * block
        found = jnp.where(ids == ids_row, there.astype(jnp.float32), 1e9)
        return jnp.minimum(least, jnp.min(found, axis=0, keepdims=True))

    least = lax.fori_loop(0, tokens // block, lead_of, jnp.full((1, tokens), 1e9, jnp.float32))
    lead_ids = jnp.where(least == lane, ids_row, -1)

    def place_of(b, most):
        at = pl.ds(pl.multiple_of(b * block, block), block)
        ids = column_ref[at, :]
        owner = jnp.zeros_like(ids)
        for o in range(1, 16):
            owner = owner + (ids >= o * shard_rows).astype(jnp.int32)
        low_id = owner * shard_rows
        ahead = (lead_ids >= low_id) & (lead_ids < ids)
        place = jnp.sum(jnp.where(ahead, 1.0, 0.0), axis=1, keepdims=True)
        place_out[at, :] = place.astype(jnp.int32)
        inside = place < room
        slots[at, :] = jnp.where(inside, owner * 128 + place.astype(jnp.int32), -1)
        locals_[at, :] = (ids - low_id).astype(jnp.float32)
        return jnp.maximum(most, jnp.max(place, axis=0, keepdims=True))

    most = lax.fori_loop(0, tokens // block, place_of, jnp.zeros((1, 1), jnp.float32))
    rounds = jnp.ones((1, 1), jnp.float32)
    for r in range(1, -(-tokens // room)):
        rounds = rounds + (most >= r * room).astype(jnp.float32)
    lane128 = lax.broadcasted_iota(jnp.int32, (1, 128), 1)

    for o in range(16):

        def asked_of(b, best, o=o):
            at = pl.ds(pl.multiple_of(b * block, block), block)
            found = jnp.where(slots[at, :] == o * 128 + lane128, locals_[at, :], -1.0)
            return jnp.maximum(best, jnp.max(found, axis=0, keepdims=True))

        best = lax.fori_loop(0, tokens // block, asked_of, jnp.full((1, 128), -1.0, jnp.float32))
        asked[o] = jnp.where(lane128 == 127, rounds, best).astype(jnp.int32)

    def send_packets(k, carry):
        asked_copy(k, me).start()
        packet_copy(k, me).start()
        return carry

    lax.fori_loop(1, 32, send_packets, 0)
    for layer in range(layers):
        own_copy(layer, z).start()
    asked_out[me] = asked[z]
    packet_out[me] = packet_ref[...]

    body_rows = shard_rows // 16 * 16
    step = 112 if body_rows % 112 == 0 else 16

    def to_half(i, carry):
        at = pl.multiple_of(i * step, 16)
        table[pl.ds(at, step), :] = word_ref[pl.ds(at, step), :].astype(jnp.bfloat16)
        return carry

    lax.fori_loop(0, body_rows // step, to_half, 0)
    padded = table.shape[0]
    table[body_rows:padded, :] = jnp.zeros((padded - body_rows, table.shape[1]), jnp.bfloat16)
    if shard_rows > body_rows:
        table[body_rows:shard_rows, :] = word_ref[body_rows:shard_rows, :].astype(jnp.bfloat16)

    def answer_one(k, carry):
        src = lax.rem(z + k, 16)
        rows_at = lax.broadcasted_iota(jnp.int32, (padded, 128), 0)
        picked = (rows_at == asked_out[d * 16 + src]).astype(jnp.bfloat16)
        found = lax.dot_general(
            picked, table[...], (((0,), (0,)), ((), ())), preferred_element_type=jnp.float32
        )
        rows_held[src] = found[:room, :].astype(jnp.bfloat16)
        return carry

    def packet_in(k, carry):
        asked_copy(k, lax.rem(me + 32 - k, 32)).wait_recv()
        return carry

    def row_start(k, carry):
        row_copy(k, z).start()
        return carry

    def z_phase(s):
        for k in range(1, 4):
            z_copy(s, k, shard(4 - k)).wait_recv()
            spread(s, 4 - k)
        if s + WINDOW < total:
            open_piece(s + WINDOW)

    def y_phase(s):
        for j in range(4):
            y_copy(s, j, shard(4 + j)).wait_recv()
            spread(s, 4 + j)

    def x_phase(s):
        for i in range(1, 8):
            at = shard(i)
            x_copy(s, i, at, 1 - d).wait_recv()
            e_copy(s, i, at).start()

    done = 0
    for t in range(total + LAG):
        if t < total:
            z_phase(t)
        if t == 1:
            lax.fori_loop(1, 32, packet_in, 0)
        if t >= 1:
            until = min(16, done + 4)
            if until > done:
                lax.fori_loop(done, until, answer_one, 0)
            done = until
        if t == total - 1:
            lax.fori_loop(1, 16, row_start, 0)
            rows_out[z] = rows_held[z]
        if 0 <= t - 1 < total:
            y_phase(t - 1)
        if 0 <= t - LAG < total:
            x_phase(t - LAG)

    turn = 1 - 2 * core
    for layer in range(layers):
        own_copy(layer, z + turn).wait_recv()
        own_copy(layer, z).wait_send()
    for s in range(total):
        for i in range(1, 8):
            at = shard(i)
            d_copy(s, i, at + turn).wait_recv()
            d_copy(s, i, at).wait_send()
            e_copy(s, i, at + turn).wait_recv()
            e_copy(s, i, at).wait_send()
            x_copy(s, i, at, d).wait_send()
        for k in range(1, 4):
            z_copy(s, k, z).wait_send()
        for i in range(4):
            y_copy(s, i, shard(i)).wait_send()

    def finish(k, carry):
        back = lax.rem(z + 16 - k, 16)
        row_copy(k, back).wait_recv()
        row_copy(k, z).wait_send()
        return carry

    lax.fori_loop(1, 16, finish, 0)

    def finish_packets(k, carry):
        packet_copy(k, lax.rem(me + 32 - k, 32)).wait_recv()
        packet_copy(k, me).wait_send()
        asked_copy(k, me).wait_send()
        return carry

    lax.fori_loop(1, 32, finish_packets, 0)


def exchange_start(ids, packet, vec_rows, attn, ffn, word_table, room, collective_id):
    half = jnp.bfloat16
    shard_rows, features = word_table.shape
    padded = -(-shard_rows // 128) * 128
    layers, rows, width = attn.shape
    tokens = ids.shape[0]
    pieces = layers * SPLITS
    dma = pltpu.SemaphoreType.DMA
    vmem = pl.BlockSpec(memory_space=pltpu.VMEM)
    return pl.pallas_call(
        functools.partial(start_kernel, shard_rows, room),
        out_shape=(
            jax.ShapeDtypeStruct((tokens, 1), jnp.int32),
            jax.ShapeDtypeStruct((32,) + packet.shape, packet.dtype),
            jax.ShapeDtypeStruct((32, 1, 128), jnp.int32),
            jax.ShapeDtypeStruct((layers, 16, rows, 3 * width + vec_rows.shape[2]), half),
            jax.ShapeDtypeStruct((16, room, features), half),
        ),
        in_specs=[vmem] * 7,
        out_specs=tuple([vmem] * 5),
        scratch_shapes=[
            pltpu.VMEM((padded, features), half),
            pltpu.VMEM((16, room, features), half),
            pltpu.VMEM((16, 1, 128), jnp.int32),
            pltpu.VMEM((tokens, 1), jnp.int32),
            pltpu.VMEM((tokens, 1), jnp.float32),
            dma((2, 32)),
            dma((2, 32)),
            dma((2, 16)),
            dma((2, pieces, 3)),
            dma((2, pieces, 4)),
            dma((2, pieces, 8)),
            dma((2, pieces, 8)),
            dma((2, pieces, 8)),
            dma((2, layers)),
        ],
        compiler_params=pltpu.CompilerParams(
            collective_id=collective_id, has_side_effects=True, vmem_limit_bytes=48 * 1024 * 1024
        ),
        cost_estimate=pl.CostEstimate(flops=0, bytes_accessed=150_000_000, transcendentals=0),
        name="exchange_start",
    )(ids.reshape(-1, 1), ids.reshape(1, -1), packet, vec_rows, attn, ffn, word_table)


WIDTHS = (D, D * 2 // 3, D // 3, D // 6, D // 12)


def contrastive_kernel(pooled_ref, false_ref, pair_ref, loss_ref, grad_ref):
    pairs = false_ref.shape[0]
    high = lax.Precision.HIGHEST
    columns = lax.broadcasted_iota(jnp.int32, (pairs, pairs), 1)
    hit = columns == pair_ref[...]
    kept = (false_ref[...] == 0) | hit
    hits = hit.astype(jnp.float32)
    valid = (pair_ref[...] >= 0).astype(jnp.float32)
    inverse = 1.0 / jnp.maximum(jnp.sum(valid, axis=0, keepdims=True), 1.0)
    weight = valid * inverse
    named = jnp.sum(hits, axis=1, keepdims=True)
    totals = jnp.zeros((pairs, 1), jnp.float32)
    for first, width in enumerate(WIDTHS):
        span = -(-width // 128) * 128
        inside = lax.broadcasted_iota(jnp.int32, (1, span), 1) < width
        units, scales, logs = [], [], []
        for kind in range(2):
            pair_units, pair_scales = [], []
            for role in range(2):
                rows = jnp.where(inside, pooled_ref[kind, role, :, 0:span], 0.0)
                scale = lax.rsqrt(jnp.sum(rows * rows, axis=1, keepdims=True) + NORM_EPS)
                pair_units.append(rows * scale)
                pair_scales.append(scale)
            sims = lax.dot_general(
                pair_units[0],
                pair_units[1],
                (((1,), (1,)), ((), ())),
                precision=high,
                preferred_element_type=jnp.float32,
            )
            sims = jnp.where(kept, sims / SOFTMAX_TEMP, MASKED)
            shifted = sims - jnp.max(sims, axis=1, keepdims=True)
            logs.append(shifted - jnp.log(jnp.sum(jnp.exp(shifted), axis=1, keepdims=True)))
            units.append(pair_units)
            scales.append(pair_scales)
        shallow, deep = logs
        p_shallow, p_deep = jnp.exp(shallow), jnp.exp(deep)
        gap = p_deep * (deep - shallow)
        spread = jnp.sum(gap, axis=1, keepdims=True)
        totals = totals + spread - jnp.sum(jnp.where(hit, shallow + deep, 0.0), axis=1, keepdims=True)
        d_sims = (
            p_shallow * (named + 1.0) - hits - p_deep,
            gap + p_deep * (named - spread) - hits,
        )
        for kind in range(2):
            d_cos = jnp.where(kept, d_sims[kind] * weight, 0.0) / SOFTMAX_TEMP
            for role in range(2):
                unit = units[kind][role]
                d_unit = lax.dot_general(
                    d_cos,
                    units[kind][1 - role],
                    (((1 - role,), (0,)), ((), ())),
                    precision=high,
                    preferred_element_type=jnp.float32,
                )
                along = jnp.sum(d_unit * unit, axis=1, keepdims=True)
                d_rows = scales[kind][role] * (d_unit - unit * along)
                if first == 0:
                    grad_ref[kind, role] = d_rows
                else:
                    grad_ref[kind, role, :, 0:span] = grad_ref[kind, role, :, 0:span] + d_rows
    loss_ref[...] = jnp.broadcast_to(
        jnp.sum(totals * valid, axis=0, keepdims=True) * inverse, loss_ref.shape
    )


def contrastive(pooled_all, false_all, pair_all):
    vmem = pl.BlockSpec(memory_space=pltpu.VMEM)
    loss, grads = pl.pallas_call(
        contrastive_kernel,
        out_shape=(
            jax.ShapeDtypeStruct((8, 128), jnp.float32),
            jax.ShapeDtypeStruct(pooled_all.shape, jnp.float32),
        ),
        in_specs=[vmem] * 3,
        out_specs=(vmem, vmem),
        compiler_params=pltpu.CompilerParams(vmem_limit_bytes=32 * 1024 * 1024),
        cost_estimate=pl.CostEstimate(flops=10**9, bytes_accessed=3_000_000, transcendentals=10**6),
        name="contrastive",
    )(pooled_all, false_all, pair_all.reshape(-1, 1))
    return loss[0, 0], grads


def head_lanes():
    lane = lax.broadcasted_iota(jnp.int32, (1, 2 * HD), 1)
    return lane < HD, lane >= HD


def probabilities(queries, keys, valid):
    scores = lax.dot_general(
        queries, keys, (((1,), (1,)), ((), ())), preferred_element_type=jnp.float32
    )
    scores = jnp.where(valid, scores * HD ** (-0.5), MASKED)
    raised = jnp.exp(scores - jnp.max(scores, axis=1, keepdims=True))
    return raised / jnp.sum(raised, axis=1, keepdims=True)


def attention_kernel(mask_ref, packed_ref, context_ref):
    valid = mask_ref[0] > 0.0
    sides = head_lanes()
    for pair in range(HEADS // 2):
        at = pair * 2 * HD
        queries = packed_ref[0, :, at : at + 2 * HD]
        keys = packed_ref[0, :, D + at : D + at + 2 * HD]
        values = packed_ref[0, :, 2 * D + at : 2 * D + at + 2 * HD]
        mixed = []
        for side in sides:
            probs = probabilities(jnp.where(side, queries, 0), keys, valid).astype(jnp.bfloat16)
            mixed.append(jnp.dot(probs, values, preferred_element_type=jnp.float32))
        context_ref[0, :, at : at + 2 * HD] = jnp.where(sides[0], mixed[0], mixed[1]).astype(
            jnp.bfloat16
        )


def attention_back_kernel(mask_ref, packed_ref, grad_ref, out_ref):
    valid = mask_ref[0] > 0.0
    sides = head_lanes()
    for pair in range(HEADS // 2):
        at = pair * 2 * HD
        queries = packed_ref[0, :, at : at + 2 * HD]
        keys = packed_ref[0, :, D + at : D + at + 2 * HD]
        values = packed_ref[0, :, 2 * D + at : 2 * D + at + 2 * HD]
        grad = grad_ref[0, :, at : at + 2 * HD]
        d_queries, d_keys, d_values = [], [], []
        for side in sides:
            probs = probabilities(jnp.where(side, queries, 0), keys, valid)
            d_probs = lax.dot_general(
                jnp.where(side, grad, 0),
                values,
                (((1,), (1,)), ((), ())),
                preferred_element_type=jnp.float32,
            )
            d_values.append(
                lax.dot_general(
                    probs.astype(jnp.bfloat16),
                    grad,
                    (((0,), (0,)), ((), ())),
                    preferred_element_type=jnp.float32,
                )
            )
            shared = jnp.sum(d_probs * probs, axis=1, keepdims=True)
            d_scores = jnp.where(valid, probs * (d_probs - shared), 0.0).astype(jnp.bfloat16)
            d_queries.append(jnp.dot(d_scores, keys, preferred_element_type=jnp.float32))
            d_keys.append(
                lax.dot_general(
                    d_scores, queries, (((0,), (0,)), ((), ())), preferred_element_type=jnp.float32
                )
            )
        for third, parts in enumerate((d_queries, d_keys, d_values)):
            both = jnp.where(sides[0], parts[0], parts[1])
            if third < 2:
                both = both * HD ** (-0.5)
            out_ref[0, :, third * D + at : third * D + at + 2 * HD] = both.astype(jnp.bfloat16)


def attention_call(kernel, mask, operands, features, name):
    count = operands[0].shape[0]

    def spec(last):
        return pl.BlockSpec((1, SEQ, last), lambda i: (i, 0, 0))

    return pl.pallas_call(
        kernel,
        grid=(count,),
        out_shape=jax.ShapeDtypeStruct((count, SEQ, features), jnp.bfloat16),
        in_specs=[pl.BlockSpec((1, 1, SEQ), lambda i: (i, 0, 0))]
        + [spec(operand.shape[2]) for operand in operands],
        out_specs=spec(features),
        compiler_params=pltpu.CompilerParams(vmem_limit_bytes=32 * 1024 * 1024),
        cost_estimate=pl.CostEstimate(
            flops=10**9, bytes_accessed=count * SEQ * D * 10, transcendentals=10**6
        ),
        name=name,
    )(mask, *operands)


@jax.custom_vjp
def attend(packed, mask):
    return attend_forward(packed, mask)[0]


def attend_forward(packed, mask):
    half = packed.astype(jnp.bfloat16)
    context = attention_call(attention_kernel, mask, [half], D, "attention")
    return context.astype(jnp.float32), (half, mask)


def attend_backward(kept, grad):
    half, mask = kept
    d_packed = attention_call(
        attention_back_kernel, mask, [half, grad.astype(jnp.bfloat16)], 3 * D, "attention_back"
    )
    return d_packed.astype(jnp.float32), jnp.zeros_like(mask)


attend.defvjp(attend_forward, attend_backward)


def split_vectors(vec_all):
    offset = SEQ * D
    position = vec_all[:offset].reshape(SEQ, D)
    emb_gain = vec_all[offset : offset + D]
    emb_shift = vec_all[offset + D : offset + 2 * D]
    offset = offset + 2 * D
    layer_parts = []
    for layer_index in range(LAYERS):
        pieces = []
        for length_now in (D, D, D, D, D, FF, D, D, D):
            pieces.append(vec_all[offset : offset + length_now])
            offset = offset + length_now
        layer_parts.append(pieces)
    return (position, emb_gain, emb_shift, layer_parts)


def layer_norm(values, gain, shift):
    center = values - jnp.mean(values, axis=-1, keepdims=True)
    spread = jnp.mean(center * center, axis=-1, keepdims=True)
    return center * lax.rsqrt(spread + NORM_EPS) * gain + shift


def embed_tokens(rows, position, emb_gain, emb_shift):
    return layer_norm(low_back(rows) + position[None], emb_gain, emb_shift)


def encoder_layer(hidden, weights, vectors, mask):
    in_weights, out_weights, up_weights, down_weights = weights
    q_bias, v_bias, o_bias, gain_one, shift_one, up_bias, down_bias, gain_two, second_shift = (
        vectors
    )
    packed = matmul(low(hidden), in_weights)
    packed = packed + jnp.concatenate([q_bias, jnp.zeros_like(q_bias), v_bias])
    context = attend(packed, mask)
    attended = low_back(matmul(context, out_weights) + o_bias)
    first_out = layer_norm(hidden + attended, gain_one, shift_one)
    upward = low_back(matmul(low(first_out), up_weights) + up_bias)
    active = rounded(jax.nn.gelu(upward, approximate=True))
    downward = low_back(einsum_plain("nsf,df->nsd", active, down_weights) + down_bias)
    return layer_norm(first_out + downward, gain_two, second_shift)


def pool_rows(hidden, key_mask, seq_lengths):
    share = key_mask.astype(jnp.float32) / seq_lengths.astype(jnp.float32)[:, None]
    return jnp.sum(hidden * share[:, :, None], axis=1)


def normalized_rows(rows):
    return rows * lax.rsqrt(jnp.sum(rows * rows, axis=-1, keepdims=True) + NORM_EPS)


def contrastive_terms(shallow_anchor, deep_anchor, shallow_pos, deep_pos, false_neg, pair_index):
    columns = lax.broadcasted_iota(jnp.int32, false_neg.shape, 1)
    hit = columns == pair_index[:, None]
    kept_cols = (false_neg == 0) | hit
    valid_rows = (pair_index >= 0).astype(jnp.float32)
    totals = jnp.zeros(pair_index.shape, jnp.float32)
    for current_width in (D, D * 2 // 3, D // 3, D // 6, D // 12):
        log_probs = []
        for anchor_vectors, positive_rows in (
            (shallow_anchor, shallow_pos),
            (deep_anchor, deep_pos),
        ):
            similarity_scores = (
                jnp.dot(
                    normalized_rows(anchor_vectors[:, :current_width]),
                    normalized_rows(positive_rows[:, :current_width]).T,
                    precision=lax.Precision.HIGHEST,
                )
                / SOFTMAX_TEMP
            )
            similarity_scores = jnp.where(kept_cols, similarity_scores, MASKED)
            log_probs.append(jax.nn.log_softmax(similarity_scores, axis=-1))
        for log_now in log_probs:
            totals = totals - jnp.sum(jnp.where(hit, log_now, 0.0), axis=-1)
        totals = totals + jnp.sum(jnp.exp(log_probs[1]) * (log_probs[1] - log_probs[0]), axis=-1)
    return jnp.sum(totals * valid_rows)


def adam_update(master, gradient, first, second, step_rate):
    first_new = BETA_ONE * first + (1.0 - BETA_ONE) * gradient
    second_new = BETA_TWO * second + (1.0 - BETA_TWO) * gradient * gradient
    first_hat = first_new / (1.0 - BETA_ONE**ADAM_STEP)
    second_hat = second_new / (1.0 - BETA_TWO**ADAM_STEP)
    master_new = master - step_rate * (
        first_hat / (jnp.sqrt(second_hat) + ADAM_EPS) + WEIGHT_DECAY * master
    )
    return (master_new, first_new, second_new)


def pad_rows(flat, multiple):
    rows = -(-flat.shape[0] // (128 * multiple)) * multiple
    return jnp.pad(flat, (0, rows * 128 - flat.shape[0])).reshape(rows, 128)


def one_hot(index, size, dtype=jnp.bfloat16):
    return (index[:, None] == lax.broadcasted_iota(jnp.int32, (1, size), 1)).astype(dtype)


def token_plan(ids, shard_rows):
    places = lax.broadcasted_iota(jnp.int32, ids.shape, 0)
    same = ids[:, None] == ids[None, :]
    leader = jnp.min(jnp.where(same, places[None, :], ids.shape[0]), axis=1)
    leads = leader == places
    owner = ids // shard_rows
    low_id = owner * shard_rows
    ahead = leads[None, :] & (ids[None, :] >= low_id[:, None]) & (ids[None, :] < ids[:, None])
    place = jnp.sum(ahead.astype(jnp.int32), axis=1)
    return owner, place, ids - low_id


def round_slots(owner, place, local_row, round_index, room, nz):
    inside = (place >= round_index * room) & (place < (round_index + 1) * room)
    slot = jnp.where(inside, owner * room + place - round_index * room, -1)
    slots = lax.broadcasted_iota(jnp.int32, (1, nz * room), 1)
    asked = jnp.max(jnp.where(slot[:, None] == slots, local_row[:, None], -1), axis=0)
    return slot, asked


def body(
    token_ids,
    lengths,
    false_neg,
    pair_index,
    word_table,
    vectors,
    attn_w,
    ffn_w,
    word_first,
    vector_first,
    attn_first,
    ffn_first,
    word_second,
    vector_second,
    attn_second,
    ffn_second,
):
    ndp = lax.axis_size("dp")
    nz = lax.axis_size("zero")
    n = ndp * nz
    by_hand = (ndp, nz) == (2, 16) and token_ids.shape[0] * ndp * nz <= 256
    my_dp = lax.axis_index("dp")
    my_zero = lax.axis_index("zero")
    me = my_dp * nz + my_zero
    pair_rows = token_ids.shape[0]
    total_pairs = pair_rows * n
    flat_ids = token_ids.reshape(-1, SEQ)
    seq_rows = flat_ids.shape[0]
    tokens = seq_rows * SEQ
    seq_lengths = lengths.reshape(-1)
    key_mask = lax.broadcasted_iota(jnp.int32, flat_ids.shape, 1) < seq_lengths[:, None]
    shard_rows = word_table.shape[0]
    vec_len = vectors.shape[0]

    room = -(-(tokens * 9 // 8) // (nz * 8)) * 8
    ids = flat_ids.reshape(-1)

    def packet_of(asked, rounds_here):
        last = jnp.concatenate([pair_index, rounds_here[None].astype(jnp.int32)])
        lines = nz + false_neg.size // 128
        return jnp.concatenate(
            [
                jnp.pad(asked.reshape(nz, room), ((0, 0), (0, 128 - room)), constant_values=-1),
                false_neg.reshape(-1, 128),
                jnp.zeros((7 - lines % 8, 128), jnp.int32),
                jnp.pad(last, (0, 128 - last.shape[0]))[None],
            ]
        )

    def gather_layer(layer_index):
        both = jnp.concatenate(
            [attn_w[layer_index].astype(jnp.bfloat16), ffn_w[layer_index].astype(jnp.bfloat16)],
            axis=1,
        )
        return lax.all_gather(both, "zero", axis=0, tiled=True)

    if by_hand:
        packet = pad_rows(jnp.concatenate([false_neg.reshape(-1), pair_index]), 8)
        vec_rows = jnp.pad(vectors, (0, LAYERS * 32 * 128 - vec_len)).astype(jnp.bfloat16)
        place, packets, asked_mine, gathered, received = exchange_start(
            ids,
            packet.astype(jnp.bfloat16),
            vec_rows.reshape(LAYERS, 32, 128),
            attn_w,
            ffn_w,
            word_table,
            room,
            0,
        )
        columns = 4 * D + 2 * FF
        gathered = gathered.reshape(LAYERS, D, -1)
        layer_weights = [gathered[layer, :, :columns] for layer in range(LAYERS)]
        vec_parts = gathered[:, :, columns:].reshape(LAYERS, nz, -1).transpose(1, 0, 2)
        rounds = jnp.max(asked_mine[:, 0, 127])
        asked_mine = asked_mine[:, 0, :room]
        packets = packets.reshape(n, -1).astype(jnp.int32)
        false_all = packets[:, : false_neg.size].reshape(total_pairs, total_pairs)
        pair_all = packets[:, false_neg.size : false_neg.size + pair_rows].reshape(total_pairs)
        owner = ids // shard_rows
        place, local_row = place.reshape(-1), ids - owner * shard_rows
        slot = jnp.where(place < room, owner * room + place, -1)
    else:
        owner, place, local_row = token_plan(ids, shard_rows)
        slot, asked = round_slots(owner, place, local_row, 0, room, nz)
        packets, vec_parts = exchange(
            [
                packet_of(asked, jnp.max(place) // room + 1),
                pad_rows(vectors.astype(jnp.bfloat16), 16),
            ],
            ["all", "zero"],
            ndp,
            nz,
            0,
            "gather_requests",
        )
        layer_weights = [gather_layer(layer_index) for layer_index in range(LAYERS)]
        asked_mine = lax.dynamic_index_in_dim(packets[:, :nz, :room], my_zero, 1, keepdims=False)
        false_all = packets[:, nz : nz + false_neg.size // 128].reshape(total_pairs, total_pairs)
        pair_all = packets[:, -1, :pair_rows].reshape(total_pairs)
        rounds = jnp.max(packets[:, -1, pair_rows])
    vec_all = vec_parts.reshape(nz, -1)[:, :vec_len].reshape(-1).astype(jnp.float32)

    word_half = word_table.astype(jnp.bfloat16)
    asked_near = lax.dynamic_slice_in_dim(asked_mine, my_dp * nz, nz, 0)

    def rows_for(wanted):
        return matmul(one_hot(wanted.reshape(-1), shard_rows), word_half).astype(jnp.bfloat16)

    def rows_from(slot_now, received):
        return matmul(one_hot(slot_now, nz * room), received.reshape(nz * room, D)).astype(
            jnp.bfloat16
        )

    if not by_hand:
        (received,) = exchange(
            [rows_for(asked_near).reshape(nz, room, D)], ["zero_p"], ndp, nz, 1, "send_rows"
        )
    rows = rows_from(slot, received)

    def more_rows(state):
        round_index, rows_now = state
        slot_now, asked_now = round_slots(owner, place, local_row, round_index, room, nz)
        wanted = lax.all_to_all(asked_now.reshape(nz, room), "zero", 0, 0, tiled=True)
        got = lax.all_to_all(rows_for(wanted).reshape(nz, room, D), "zero", 0, 0, tiled=True)
        return round_index + 1, rows_now + rows_from(slot_now, got)

    _, rows = lax.while_loop(lambda state: state[0] < rounds, more_rows, (jnp.int32(1), rows))
    rows = rows.reshape(seq_rows, SEQ, D).astype(jnp.float32)

    position, emb_gain, emb_shift, layer_vectors = split_vectors(vec_all)
    embedded, embed_back = jax.vjp(embed_tokens, rows, position, emb_gain, emb_shift)
    hidden = embedded
    mask = key_mask.astype(jnp.float32)[:, None, :]
    saved = []
    pooled = []
    for layer_index in range(LAYERS):
        weights = layer_weights[layer_index]
        edges = (0, 3 * D, 4 * D, 4 * D + FF, 4 * D + 2 * FF)
        parts = [
            weights[:, first:last].astype(jnp.float32) for first, last in zip(edges, edges[1:])
        ]
        output, layer_back = jax.vjp(
            functools.partial(encoder_layer, mask=mask), hidden, parts, layer_vectors[layer_index]
        )
        saved.append(layer_back)
        hidden = output
        pooled.append(pool_rows(hidden, key_mask, seq_lengths).astype(jnp.bfloat16))

    (pooled_all,) = exchange(
        [jnp.stack(pooled).reshape(-1, 128)], ["all"], ndp, nz, 2, "gather_pooled"
    )
    pooled_all = pooled_all.reshape(n, 2, pair_rows, 2, D).astype(jnp.float32)
    pooled_all = pooled_all.transpose(1, 3, 0, 2, 4).reshape(2, 2, total_pairs, D)
    if total_pairs <= 256:
        loss, pooled_grads = contrastive(pooled_all, false_all, pair_all)
    else:

        def whole_loss(pooled_now):
            summed = contrastive_terms(
                pooled_now[0, 0],
                pooled_now[1, 0],
                pooled_now[0, 1],
                pooled_now[1, 1],
                false_all,
                pair_all,
            )
            valid_total = jnp.sum((pair_all >= 0).astype(jnp.float32))
            return summed / jnp.maximum(valid_total, 1.0)

        loss, pooled_grads = jax.value_and_grad(whole_loss)(pooled_all)
    pooled_grads = lax.dynamic_slice_in_dim(pooled_grads, me * pair_rows, pair_rows, 2)
    pooled_grads = pooled_grads.transpose(0, 2, 1, 3).reshape(2, seq_rows, D)
    shallow_back, deep_back = pooled_grads[0], pooled_grads[1]
    share = key_mask.astype(jnp.float32) / seq_lengths.astype(jnp.float32)[:, None]
    grad_hidden = jnp.zeros_like(embedded)
    weight_parts = []
    vec_grads = [None] * LAYERS
    for layer_index in range(LAYERS - 1, -1, -1):
        if layer_index == LAYERS - 1:
            grad_hidden = grad_hidden + deep_back[:, None, :] * share[:, :, None]
        if layer_index == 0:
            grad_hidden = grad_hidden + shallow_back[:, None, :] * share[:, :, None]
        layer_back = saved[layer_index]
        grad_hidden, part_grads, vec_grads[layer_index] = layer_back(grad_hidden)
        part_grads = [part.astype(jnp.bfloat16) for part in part_grads]
        if by_hand and layer_index == 0:
            weight_parts.insert(0, part_grads)
        else:
            both = jnp.concatenate(part_grads, axis=1)
            both, grad_hidden = lax.optimization_barrier((both, grad_hidden))
            weight_parts.insert(0, lax.psum_scatter(both, "zero", scatter_dimension=0, tiled=True))
    rows_grad, *embed_grads = embed_back(grad_hidden)
    vec_pieces = [part.reshape(-1) for part in embed_grads]
    for layer_index in range(LAYERS):
        vec_pieces += list(vec_grads[layer_index])
    vec_grad = jnp.concatenate(vec_pieces)
    down_local = jnp.stack([vec_grads[layer_index][6] for layer_index in range(LAYERS)])

    rows_grad = rows_grad.reshape(tokens, D).astype(jnp.bfloat16)

    def slot_sums(slot_now):
        picked = one_hot(slot_now, nz * room)
        return lax.dot_general(
            picked, rows_grad, (((0,), (0,)), ((), ())), preferred_element_type=jnp.float32
        ).astype(jnp.bfloat16)

    def into_rows(wanted, sums):
        return lax.dot_general(
            one_hot(wanted.reshape(-1), shard_rows),
            sums.reshape(-1, D),
            (((0,), (0,)), ((), ())),
            preferred_element_type=jnp.float32,
        )

    down_each = down_local.reshape(LAYERS, nz, -1).transpose(1, 0, 2).reshape(nz, -1)
    down_len = down_each.shape[1]
    vec_blocks = jnp.concatenate([vec_grad.reshape(nz, vec_len), down_each], axis=1)
    lines = -(-vec_blocks.shape[1] // 1024) * 8
    vec_blocks = jnp.pad(vec_blocks, ((0, 0), (0, lines * 128 - vec_blocks.shape[1])))
    sums = slot_sums(slot).reshape(nz, room, D)
    if by_hand:
        *near, vec_near, sums_all, other_near = exchange_gradients(
            [part.reshape(4, 2, 2, -1, part.shape[1]) for part in weight_parts[0]]
            + [vec_blocks.reshape(4, 2, 2, lines, 128)],
            sums,
            weight_parts[1],
            3,
        )
        attn_shard = jnp.stack([jnp.concatenate(near[:2], axis=1), other_near[:, : 4 * D]])
        ffn_shard = jnp.stack([jnp.concatenate(near[2:], axis=1), other_near[:, 4 * D :]])
        vec_sum = vec_near.reshape(-1)
    else:
        sums_all, vec_shares = exchange(
            [sums, vec_blocks.reshape(nz, lines, 128)],
            ["all_p", "all_p"],
            ndp,
            nz,
            3,
            "send_gradients",
        )
        vec_sum = jnp.sum(vec_shares.reshape(n, -1), axis=0)
        (weight_all,) = exchange([jnp.stack(weight_parts)], ["dp"], ndp, nz, 4, "sum_replicas")
        weight_sum = jnp.sum(weight_all.astype(jnp.float32), axis=0)
        attn_shard = weight_sum[:, :, : 4 * D]
        ffn_shard = weight_sum[:, :, 4 * D :]
    word_grad = into_rows(asked_mine, sums_all)

    def more_sums(state):
        round_index, grad_now = state
        slot_now, asked_now = round_slots(owner, place, local_row, round_index, room, nz)
        wanted = lax.all_to_all(asked_now.reshape(nz, room), "zero", 0, 0, tiled=True)
        got = lax.all_to_all(slot_sums(slot_now).reshape(nz, room, D), "zero", 0, 0, tiled=True)
        wanted = lax.all_gather(wanted, "dp", axis=0, tiled=True)
        got = lax.all_gather(got, "dp", axis=0, tiled=True)
        return round_index + 1, grad_now + into_rows(wanted, got)

    _, word_grad = lax.while_loop(
        lambda state: state[0] < rounds, more_sums, (jnp.int32(1), word_grad)
    )
    vec_shard = vec_sum[:vec_len]
    down_shard = vec_sum[vec_len : vec_len + down_len].reshape(LAYERS, -1)

    square_local = jnp.sum(word_grad * word_grad) + jnp.sum(vec_shard * vec_shard)
    square_local = square_local + jnp.sum(attn_shard * attn_shard) + jnp.sum(ffn_shard * ffn_shard)
    (squares,) = exchange(
        [jnp.broadcast_to(square_local, (8, 128))], ["zero"], ndp, nz, 5, "gather_squares"
    )
    square_total = jnp.sum(squares[:, 0, 0])
    grad_norm = jnp.sqrt(square_total)
    factor = jnp.minimum(1.0, CLIP_NORM / (grad_norm + 1e-06))
    word_new, word_first_new, word_second_new = adam_update(
        word_table, word_grad * factor, word_first, word_second, LEARN_RATE
    )
    vector_new, vector_first_new, vector_second_new = adam_update(
        vectors, vec_shard * factor, vector_first, vector_second, VECTOR_RATE
    )
    attn_new, attn_first_new, attn_second_new = adam_update(
        attn_w, attn_shard * factor, attn_first, attn_second, LEARN_RATE
    )
    ffn_new, ffn_first_new, ffn_second_new = adam_update(
        ffn_w, ffn_shard * factor, ffn_first, ffn_second, LEARN_RATE
    )
    return (
        loss,
        grad_norm,
        word_new,
        vector_new,
        attn_new,
        ffn_new,
        word_new.astype(jnp.bfloat16),
        vector_new.astype(jnp.bfloat16),
        attn_new.astype(jnp.bfloat16),
        ffn_new.astype(jnp.bfloat16),
        word_first_new,
        vector_first_new,
        attn_first_new,
        ffn_first_new,
        word_second_new,
        vector_second_new,
        attn_second_new,
        ffn_second_new,
        down_shard * factor,
    )


def solution(mesh):
    placed = (
        P(("dp", "zero"), None, None),
        P(("dp", "zero"), None),
        P(("dp", "zero"), None),
        P(("dp", "zero")),
        P("zero", None),
        P("zero"),
        P(None, "zero", None),
        P(None, "zero", None),
        P("zero", None),
        P("zero"),
        P(None, "zero", None),
        P(None, "zero", None),
        P("zero", None),
        P("zero"),
        P(None, "zero", None),
        P(None, "zero", None),
    )
    return jax.shard_map(
        body,
        mesh=mesh,
        in_specs=placed,
        out_specs=(
            P(),
            P(),
            P("zero", None),
            P("zero"),
            P(None, "zero", None),
            P(None, "zero", None),
            P("zero", None),
            P("zero"),
            P(None, "zero", None),
            P(None, "zero", None),
            P("zero", None),
            P("zero"),
            P(None, "zero", None),
            P(None, "zero", None),
            P("zero", None),
            P("zero"),
            P(None, "zero", None),
            P(None, "zero", None),
            P(None, "zero"),
        ),
        check_vma=False,
    )
```

```python
import functools

import jax
import jax.numpy as jnp
from jax import lax
from jax.experimental import pallas as pl
from jax.experimental.pallas import tpu as pltpu
from jax.sharding import PartitionSpec as P

D = 512
HEADS = 8
HD = 64
FF = 2048
SEQ = 128
LAYERS = 2
ADAM_STEP = 5


SOFTMAX_TEMP = 0.05
CLIP_NORM = 1.0
LEARN_RATE = 0.02
VECTOR_RATE = 0.15
BETA_ONE = 0.5
BETA_TWO = 0.5
WEIGHT_DECAY = 0.01
ADAM_EPS = 1e-08
NORM_EPS = 1e-06
MASKED = -1000000000.0

MESH = pl.DeviceIdType.MESH


def build_low():

    def rounder(value):
        return lax.optimization_barrier(value.astype(jnp.bfloat16)).astype(jnp.float32)

    def keep_fwd(value):
        return (rounder(value), None)

    def pass_bwd(kept, grad):
        return (grad,)

    wrapped = jax.custom_vjp(rounder)
    wrapped.defvjp(keep_fwd, pass_bwd)
    return wrapped


def build_low_back():

    def identity_fn(value):
        return value

    def keep_fwd(value):
        return (value, None)

    def round_bwd(kept, grad):
        return (low(grad),)

    wrapped = jax.custom_vjp(identity_fn)
    wrapped.defvjp(keep_fwd, round_bwd)
    return wrapped


def low(value):
    return build_low()(value)


def low_back(value):
    return build_low_back()(value)


def rounded(value):
    return low(low_back(value))


def matmul(left, right):
    return jnp.dot(left, right, preferred_element_type=jnp.float32)


def einsum_plain(form, left, right):
    return jnp.einsum(form, left, right, preferred_element_type=jnp.float32)


def exchange_kernel(modes, ndp, nz, *refs):
    count = len(modes)
    ins = refs[:count]
    outs = refs[count : 2 * count]
    sems = refs[2 * count :]
    d = lax.axis_index("dp")
    z = lax.axis_index("zero")
    me = d * nz + z
    n = ndp * nz

    def peer_of(group, k):
        if group == "dp":
            pd = lax.rem(d + k, ndp)
            return pd, z, pd
        if group == "zero":
            pz = lax.rem(z + k, nz)
            return d, pz, pz
        p = lax.rem(me + k, n)
        return p // nz, lax.rem(p, nz), p

    groups = {m.split("_")[0] for m in modes}
    sizes = {"all": n, "zero": nz, "dp": ndp}
    mine = {"all": me, "zero": z, "dp": d}
    barrier = pltpu.get_barrier_semaphore()
    meet = ["all"] if "all" in groups else sorted(groups)
    total = 0
    for group in meet:
        total += sizes[group] - 1

        def greet(k, carry, group=group):
            pd, pz, _ = peer_of(group, k)
            pl.semaphore_signal(barrier, inc=1, device_id=(pd, pz), device_id_type=MESH)
            return carry

        lax.fori_loop(1, sizes[group], greet, 0)
    pl.semaphore_wait(barrier, total)

    def make(a, k):
        mode = modes[a]
        group = mode.split("_")[0]
        pd, pz, _ = peer_of(group, k)
        src = ins[a].at[pz] if mode.endswith("_p") else ins[a]
        return pltpu.make_async_remote_copy(
            src_ref=src,
            dst_ref=outs[a].at[mine[group]],
            send_sem=sems[2 * a].at[k],
            recv_sem=sems[2 * a + 1].at[k],
            device_id=(pd, pz),
            device_id_type=MESH,
        )

    for a, mode in enumerate(modes):
        group = mode.split("_")[0]

        def begin(k, carry, a=a):
            make(a, k).start()
            return carry

        lax.fori_loop(1, sizes[group], begin, 0)
    for a, mode in enumerate(modes):
        group = mode.split("_")[0]
        if mode.endswith("_p"):
            outs[a][mine[group]] = ins[a][z]
        else:
            outs[a][mine[group]] = ins[a][...]
    for a, mode in enumerate(modes):
        group = mode.split("_")[0]

        def finish(k, carry, a=a):
            make(a, k).wait()
            return carry

        lax.fori_loop(1, sizes[group], finish, 0)


def exchange(arrays, modes, ndp, nz, collective_id, name):
    sizes = {"all": ndp * nz, "zero": nz, "dp": ndp}
    outs = []
    scratch = []
    moved = 0
    for array, mode in zip(arrays, modes):
        size = sizes[mode.split("_")[0]]
        block = array.shape[1:] if mode.endswith("_p") else array.shape
        outs.append(jax.ShapeDtypeStruct((size,) + block, array.dtype))
        scratch += [pltpu.SemaphoreType.DMA((size,)), pltpu.SemaphoreType.DMA((size,))]
        one = array.dtype.itemsize
        for s in block:
            one *= s
        moved += one * size
    vmem = pl.BlockSpec(memory_space=pltpu.VMEM)
    return pl.pallas_call(
        functools.partial(exchange_kernel, tuple(modes), ndp, nz),
        out_shape=tuple(outs),
        in_specs=[vmem] * len(arrays),
        out_specs=tuple([vmem] * len(arrays)),
        scratch_shapes=scratch,
        compiler_params=pltpu.CompilerParams(
            collective_id=collective_id, has_side_effects=True, vmem_limit_bytes=48 * 1024 * 1024
        ),
        cost_estimate=pl.CostEstimate(flops=0, bytes_accessed=20 * moved, transcendentals=0),
        name=name,
    )(*arrays)


def gradient_kernel(chunks, count, *refs):
    take = iter(refs)
    parts = [next(take) for _ in range(count)]
    sums_ref, near_ref = next(take), next(take)
    totals = [next(take) for _ in range(count)]
    rows_ref, near_out = next(take), next(take)
    bufs = [[next(take) for _ in range(5)] for _ in chunks]
    near_buf = next(take)
    send_a, recv_a, send_y, recv_y, send_z, recv_z, send_x, recv_x = [next(take) for _ in range(8)]
    row_send, row_recv, pass_send, pass_recv, near_sem = [next(take) for _ in range(5)]

    d = lax.axis_index("dp")
    z = lax.axis_index("zero")
    core = lax.rem(z, 2)
    col = lax.rem(z // 2, 2)
    line = z // 4
    sibling = z + 1 - 2 * core
    across = z + 2 - 4 * col

    def along(k):
        return lax.rem(line + k, 4) * 4 + lax.rem(z, 4)

    barrier = pltpu.get_barrier_semaphore()

    def greet(k, carry):
        pl.semaphore_signal(
            barrier, inc=1, device_id=(d, lax.rem(z + k, 16)), device_id_type=MESH
        )
        return carry

    lax.fori_loop(1, 16, greet, 0)
    pl.semaphore_signal(barrier, inc=1, device_id=(1 - d, z), device_id_type=MESH)
    pl.semaphore_wait(barrier, 16)

    def remote(src, dst, send, recv, to):
        return pltpu.make_async_remote_copy(
            src_ref=src,
            dst_ref=dst,
            send_sem=send,
            recv_sem=recv,
            device_id=to,
            device_id_type=MESH,
        )

    def copy_a(i):
        part, start, width = chunks[i]
        src = parts[part].at[:, :, 1 - core, :, pl.ds(start, width)]
        return remote(src, bufs[i][0], send_a.at[i], recv_a.at[i], (d, sibling))

    def copy_y(i):
        src = bufs[i][0].at[:, 1 - col]
        return remote(src, bufs[i][1], send_y.at[i], recv_y.at[i], (d, across))

    def copy_z(i, k):
        src = bufs[i][1].at[lax.rem(line + k, 4)]
        return remote(
            src, bufs[i][2].at[k - 1], send_z.at[i, k - 1], recv_z.at[i, k - 1], (d, along(k))
        )

    def copy_x(i):
        return remote(bufs[i][3], bufs[i][4], send_x.at[i], recv_x.at[i], (1 - d, z))

    def row_push(k):
        to = lax.rem(z + k, 16)
        return remote(sums_ref.at[to], rows_ref.at[d, z], row_send.at[k], row_recv.at[k], (d, to))

    def row_pass(k):
        at = lax.rem(z + 16 - k, 16)
        return remote(
            rows_ref.at[d, at], rows_ref.at[d, at], pass_send.at[k], pass_recv.at[k], (1 - d, z)
        )

    near = remote(near_ref, near_buf, near_sem.at[0], near_sem.at[1], (1 - d, z))

    total = len(chunks)
    for i in range(total):
        copy_a(i).start()

    def push(k, carry):
        row_push(k).start()
        return carry

    lax.fori_loop(1, 16, push, 0)
    near.start()
    rows_ref[d, z] = sums_ref[z]
    row_pass(0).start()

    def stage_a(i):
        part, start, width = chunks[i]
        copy_a(i).wait_recv()

        buf = bufs[i][0]

        def add_block(b, carry):
            line_at, col_at = b // 2, lax.rem(b, 2)
            mine = parts[part][line_at, col_at, core, :, pl.ds(start, width)].astype(jnp.float32)
            got = buf[line_at, col_at].astype(jnp.float32)
            buf[line_at, col_at] = (mine + got).astype(buf.dtype)
            return carry

        lax.fori_loop(0, 8, add_block, 0)
        copy_y(i).start()

    def stage_y(i):
        copy_y(i).wait_recv()
        buf = bufs[i][1]

        def add_block(b, carry):
            mine = bufs[i][0][b, col].astype(jnp.float32)
            buf[b] = (mine + buf[b].astype(jnp.float32)).astype(buf.dtype)
            return carry

        lax.fori_loop(0, 4, add_block, 0)
        for k in range(1, 4):
            copy_z(i, k).start()

    def stage_z(i):
        for k in range(1, 4):
            copy_z(i, k).wait_recv()
        value = bufs[i][1][line].astype(jnp.float32)
        for k in range(3):
            value = value + bufs[i][2][k].astype(jnp.float32)
        bufs[i][3][...] = value.astype(bufs[i][3].dtype)
        copy_x(i).start()

    def stage_x(i):
        part, start, width = chunks[i]
        copy_x(i).wait_recv()
        totals[part][:, pl.ds(start, width)] = bufs[i][3][...].astype(jnp.float32) + bufs[i][4][
            ...
        ].astype(jnp.float32)

    def pass_on(k):
        row_push(k).wait_recv()
        row_pass(k).start()

    passed = 1
    for t in range(total + 3):
        if t < total:
            stage_a(t)
        if 0 <= t - 1 < total:
            stage_y(t - 1)
        if 0 <= t - 2 < total:
            stage_z(t - 2)
        if 0 <= t - 3 < total:
            stage_x(t - 3)
        until = min(16, 1 + (t + 1) * 15 // (total + 3))
        for k in range(passed, until):
            pass_on(k)
        passed = until
    for k in range(passed, 16):
        pass_on(k)

    near.wait()
    near_out[...] = near_ref[...].astype(jnp.float32) + near_buf[...].astype(jnp.float32)

    for i in range(total):
        copy_a(i).wait_send()
        copy_y(i).wait_send()
        for k in range(1, 4):
            copy_z(i, k).wait_send()
        copy_x(i).wait_send()

    def finish(k, carry):
        row_push(k).wait_send()
        return carry

    lax.fori_loop(1, 16, finish, 0)

    def finish_pass(k, carry):
        row_pass(k).wait_send()
        at = lax.rem(z + 16 - k, 16)
        remote(
            rows_ref.at[1 - d, at], rows_ref.at[1 - d, at], pass_send.at[k], pass_recv.at[k], (1 - d, z)
        ).wait_recv()
        return carry

    lax.fori_loop(0, 16, finish_pass, 0)


def exchange_gradients(parts, sums, near, collective_id):
    chunks = []
    for index, part in enumerate(parts):
        width = part.shape[4] // -(-part.shape[4] // 1024)
        for start in range(0, part.shape[4], width):
            chunks.append((index, start, width))
    half = jnp.bfloat16
    scratch = []
    for index, start, width in chunks:
        r = parts[index].shape[3]
        scratch += [
            pltpu.VMEM((4, 2, r, width), parts[index].dtype),
            pltpu.VMEM((4, r, width), parts[index].dtype),
            pltpu.VMEM((3, r, width), parts[index].dtype),
            pltpu.VMEM((r, width), parts[index].dtype),
            pltpu.VMEM((r, width), parts[index].dtype),
        ]
    scratch += [pltpu.VMEM(near.shape, half)]
    dma = pltpu.SemaphoreType.DMA
    count = len(chunks)
    scratch += [dma((count,)) for _ in range(4)] + [dma((count, 3)) for _ in range(2)]
    scratch += [dma((count,)) for _ in range(2)]
    scratch += [dma((16,)) for _ in range(4)] + [dma((2,))]
    outs = [jax.ShapeDtypeStruct(part.shape[3:], jnp.float32) for part in parts]
    outs += [jax.ShapeDtypeStruct((2,) + sums.shape, sums.dtype)]
    outs += [jax.ShapeDtypeStruct(near.shape, jnp.float32)]
    vmem = pl.BlockSpec(memory_space=pltpu.VMEM)
    return pl.pallas_call(
        functools.partial(gradient_kernel, tuple(chunks), len(parts)),
        out_shape=tuple(outs),
        in_specs=[vmem] * (len(parts) + 2),
        out_specs=tuple([vmem] * len(outs)),
        scratch_shapes=scratch,
        compiler_params=pltpu.CompilerParams(
            collective_id=collective_id, has_side_effects=True, vmem_limit_bytes=48 * 1024 * 1024
        ),
        cost_estimate=pl.CostEstimate(flops=0, bytes_accessed=200_000_000, transcendentals=0),
        name="exchange_gradients",
    )(*parts, sums, near)


SPLITS = 4
WINDOW = 3
LAG = 3


def start_kernel(shard_rows, room, *refs):
    column_ref, row_ref, packet_ref, vec_ref, attn_ref, ffn_ref, word_ref = refs[:7]
    place_out, packet_out, asked_out, vec_out, rows_out, *weight_outs = refs[7:14]
    table, rows_held, asked, slots, locals_ = refs[14:19]
    packet_sem, asked_sem, vec_sem, row_sem = refs[19:23]
    z_sem, y_sem, x_sem, d_sem, e_sem, own_sem = refs[23:]

    d = lax.axis_index("dp")
    z = lax.axis_index("zero")
    me = d * 16 + z
    core = lax.rem(z, 2)
    col = lax.rem(z // 2, 2)
    line = z // 4
    sibling = z + 1 - 2 * core
    across = z + 2 - 4 * col
    layers = attn_ref.shape[0]
    width = attn_ref.shape[2]
    whole = 3 * width
    unit = whole // 128 // SPLITS
    hand = unit * 5 // 12
    total = layers * SPLITS

    def everyone(k):
        p = lax.rem(me + k, 32)
        return (p // 16, lax.rem(p, 16))

    barrier = pltpu.get_barrier_semaphore()

    def greet(k, carry):
        pl.semaphore_signal(barrier, inc=1, device_id=everyone(k), device_id_type=MESH)
        return carry

    lax.fori_loop(1, 32, greet, 0)
    for layer in range(layers):
        weight_outs[layer][z, :, 0:width] = attn_ref[layer].astype(jnp.bfloat16)
        weight_outs[layer][z, :, width:whole] = ffn_ref[layer].astype(jnp.bfloat16)
    pl.semaphore_wait(barrier, 31)

    def remote(src, dst, sems, at, to):
        return pltpu.make_async_remote_copy(
            src_ref=src,
            dst_ref=dst,
            send_sem=sems.at[(0,) + at],
            recv_sem=sems.at[(1,) + at],
            device_id=to,
            device_id_type=MESH,
        )

    def packet_copy(k, slot):
        return remote(packet_ref, packet_out.at[slot], packet_sem, (k,), everyone(k))

    def asked_copy(k, slot):
        to = everyone(k)
        return remote(asked.at[to[1]], asked_out.at[slot], asked_sem, (k,), to)

    def vec_copy(k, slot):
        return remote(vec_ref, vec_out.at[slot], vec_sem, (k,), (d, lax.rem(z + k, 16)))

    def row_copy(k, slot):
        to = lax.rem(z + k, 16)
        return remote(rows_held.at[to], rows_out.at[slot], row_sem, (k,), (d, to))

    def shard(i):
        at = lax.rem(line + i % 4, 4) * 4 + lax.rem(z, 4)
        return at if i < 4 else at + 2 - 4 * col

    def piece(s):
        layer, p = s // SPLITS, s % SPLITS
        size = unit if p < SPLITS - 1 else whole // 128 - p * unit
        return layer, p * unit, size

    def columns_of(at, s, first, size):
        layer, base, _ = piece(s)
        return weight_outs[layer].at[
            at, :, pl.ds(pl.multiple_of((base + first) * 128, 128), size * 128)
        ]

    def stretch(at, s, ours):
        size = piece(s)[2]
        return columns_of(at, s, ours * hand, size - hand)

    def handed(at, s, ours):
        size = piece(s)[2]
        return columns_of(at, s, ours * (size - hand), hand)

    def both(ref, sems, at, to):
        return remote(ref, ref, sems, at, to)

    def z_copy(s, k, at):
        to = lax.rem(line + k, 4) * 4 + lax.rem(z, 4)
        return both(stretch(at, s, d), z_sem, (s, k - 1), (d, to))

    def y_copy(s, j, at):
        return both(stretch(at, s, d), y_sem, (s, j), (d, across))

    def x_copy(s, i, at, ours):
        return both(handed(at, s, ours), x_sem, (s, i), (1 - d, z))

    def d_copy(s, i, at):
        return both(stretch(at, s, d), d_sem, (s, i), (d, sibling))

    def e_copy(s, i, at):
        return both(handed(at, s, 1 - d), e_sem, (s, i), (d, sibling))

    def own_copy(layer, at):
        ref = weight_outs[layer].at[at]
        return both(ref, own_sem, (layer,), (d, sibling))

    def spread(s, i):
        at = shard(i)
        if i < 4:
            y_copy(s, i, at).start()
        if i > 0:
            x_copy(s, i, at, d).start()
            d_copy(s, i, at).start()

    def open_piece(s):
        for k in range(1, 4):
            z_copy(s, k, z).start()
        spread(s, 0)

    for s in range(WINDOW):
        open_piece(s)

    tokens = column_ref.shape[0]
    ids_row = row_ref[...]
    lane = lax.broadcasted_iota(jnp.int32, (1, tokens), 1).astype(jnp.float32)
    block = 128

    def lead_of(b, least):
        ids = column_ref[pl.ds(pl.multiple_of(b * block, block), block), :]
        there = lax.broadcasted_iota(jnp.int32, (block, 1), 0) + b * block
        found = jnp.where(ids == ids_row, there.astype(jnp.float32), 1e9)
        return jnp.minimum(least, jnp.min(found, axis=0, keepdims=True))

    least = lax.fori_loop(0, tokens // block, lead_of, jnp.full((1, tokens), 1e9, jnp.float32))
    lead_ids = jnp.where(least == lane, ids_row, -1)

    def place_of(b, most):
        at = pl.ds(pl.multiple_of(b * block, block), block)
        ids = column_ref[at, :]
        owner = jnp.zeros_like(ids)
        for o in range(1, 16):
            owner = owner + (ids >= o * shard_rows).astype(jnp.int32)
        low_id = owner * shard_rows
        ahead = (lead_ids >= low_id) & (lead_ids < ids)
        place = jnp.sum(jnp.where(ahead, 1.0, 0.0), axis=1, keepdims=True)
        place_out[at, :] = place.astype(jnp.int32)
        inside = place < room
        slots[at, :] = jnp.where(inside, owner * 128 + place.astype(jnp.int32), -1)
        locals_[at, :] = (ids - low_id).astype(jnp.float32)
        return jnp.maximum(most, jnp.max(place, axis=0, keepdims=True))

    most = lax.fori_loop(0, tokens // block, place_of, jnp.zeros((1, 1), jnp.float32))
    rounds = jnp.ones((1, 1), jnp.float32)
    for r in range(1, -(-tokens // room)):
        rounds = rounds + (most >= r * room).astype(jnp.float32)
    lane128 = lax.broadcasted_iota(jnp.int32, (1, 128), 1)

    for o in range(16):

        def asked_of(b, best, o=o):
            at = pl.ds(pl.multiple_of(b * block, block), block)
            found = jnp.where(slots[at, :] == o * 128 + lane128, locals_[at, :], -1.0)
            return jnp.maximum(best, jnp.max(found, axis=0, keepdims=True))

        best = lax.fori_loop(0, tokens // block, asked_of, jnp.full((1, 128), -1.0, jnp.float32))
        asked[o] = jnp.where(lane128 == 127, rounds, best).astype(jnp.int32)

    def send_packets(k, carry):
        asked_copy(k, me).start()
        packet_copy(k, me).start()
        return carry

    lax.fori_loop(1, 32, send_packets, 0)

    def send_vec(k, carry):
        vec_copy(k, z).start()
        return carry

    lax.fori_loop(1, 16, send_vec, 0)
    for layer in range(layers):
        own_copy(layer, z).start()
    vec_out[z] = vec_ref[...]
    asked_out[me] = asked[z]
    packet_out[me] = packet_ref[...]

    body_rows = shard_rows // 16 * 16
    step = 112 if body_rows % 112 == 0 else 16

    def to_half(i, carry):
        at = pl.multiple_of(i * step, 16)
        table[pl.ds(at, step), :] = word_ref[pl.ds(at, step), :].astype(jnp.bfloat16)
        return carry

    lax.fori_loop(0, body_rows // step, to_half, 0)
    padded = table.shape[0]
    table[body_rows:padded, :] = jnp.zeros((padded - body_rows, table.shape[1]), jnp.bfloat16)
    if shard_rows > body_rows:
        table[body_rows:shard_rows, :] = word_ref[body_rows:shard_rows, :].astype(jnp.bfloat16)

    def answer_one(k, carry):
        src = lax.rem(z + k, 16)
        rows_at = lax.broadcasted_iota(jnp.int32, (padded, 128), 0)
        picked = (rows_at == asked_out[d * 16 + src]).astype(jnp.bfloat16)
        found = lax.dot_general(
            picked, table[...], (((0,), (0,)), ((), ())), preferred_element_type=jnp.float32
        )
        rows_held[src] = found[:room, :].astype(jnp.bfloat16)
        return carry

    def packet_in(k, carry):
        asked_copy(k, lax.rem(me + 32 - k, 32)).wait_recv()
        return carry

    def row_start(k, carry):
        row_copy(k, z).start()
        return carry

    def z_phase(s):
        for k in range(1, 4):
            z_copy(s, k, shard(4 - k)).wait_recv()
            spread(s, 4 - k)
        if s + WINDOW < total:
            open_piece(s + WINDOW)

    def y_phase(s):
        for j in range(4):
            y_copy(s, j, shard(4 + j)).wait_recv()
            spread(s, 4 + j)

    def x_phase(s):
        for i in range(1, 8):
            at = shard(i)
            x_copy(s, i, at, 1 - d).wait_recv()
            e_copy(s, i, at).start()

    done = 0
    for t in range(total + LAG):
        if t < total:
            z_phase(t)
        if t == 1:
            lax.fori_loop(1, 32, packet_in, 0)
        if t >= 1:
            until = min(16, done + 4)
            if until > done:
                lax.fori_loop(done, until, answer_one, 0)
            done = until
        if t == total - 1:
            lax.fori_loop(1, 16, row_start, 0)
            rows_out[z] = rows_held[z]
        if 0 <= t - 1 < total:
            y_phase(t - 1)
        if 0 <= t - LAG < total:
            x_phase(t - LAG)

    turn = 1 - 2 * core
    for layer in range(layers):
        own_copy(layer, z + turn).wait_recv()
        own_copy(layer, z).wait_send()
    for s in range(total):
        for i in range(1, 8):
            at = shard(i)
            d_copy(s, i, at + turn).wait_recv()
            d_copy(s, i, at).wait_send()
            e_copy(s, i, at + turn).wait_recv()
            e_copy(s, i, at).wait_send()
            x_copy(s, i, at, d).wait_send()
        for k in range(1, 4):
            z_copy(s, k, z).wait_send()
        for i in range(4):
            y_copy(s, i, shard(i)).wait_send()

    def finish(k, carry):
        back = lax.rem(z + 16 - k, 16)
        row_copy(k, back).wait_recv()
        row_copy(k, z).wait_send()
        vec_copy(k, back).wait_recv()
        vec_copy(k, z).wait_send()
        return carry

    lax.fori_loop(1, 16, finish, 0)

    def finish_packets(k, carry):
        packet_copy(k, lax.rem(me + 32 - k, 32)).wait_recv()
        packet_copy(k, me).wait_send()
        asked_copy(k, me).wait_send()
        return carry

    lax.fori_loop(1, 32, finish_packets, 0)


def exchange_start(ids, packet, vec_rows, attn, ffn, word_table, room, collective_id):
    half = jnp.bfloat16
    shard_rows, features = word_table.shape
    padded = -(-shard_rows // 128) * 128
    layers, rows, width = attn.shape
    tokens = ids.shape[0]
    pieces = layers * SPLITS
    dma = pltpu.SemaphoreType.DMA
    vmem = pl.BlockSpec(memory_space=pltpu.VMEM)
    return pl.pallas_call(
        functools.partial(start_kernel, shard_rows, room),
        out_shape=(
            jax.ShapeDtypeStruct((tokens, 1), jnp.int32),
            jax.ShapeDtypeStruct((32,) + packet.shape, packet.dtype),
            jax.ShapeDtypeStruct((32, 1, 128), jnp.int32),
            jax.ShapeDtypeStruct((16,) + vec_rows.shape, vec_rows.dtype),
            jax.ShapeDtypeStruct((16, room, features), half),
        )
        + (jax.ShapeDtypeStruct((16, rows, 3 * width), half),) * layers,
        in_specs=[vmem] * 7,
        out_specs=tuple([vmem] * (5 + layers)),
        scratch_shapes=[
            pltpu.VMEM((padded, features), half),
            pltpu.VMEM((16, room, features), half),
            pltpu.VMEM((16, 1, 128), jnp.int32),
            pltpu.VMEM((tokens, 1), jnp.int32),
            pltpu.VMEM((tokens, 1), jnp.float32),
            dma((2, 32)),
            dma((2, 32)),
            dma((2, 16)),
            dma((2, 16)),
            dma((2, pieces, 3)),
            dma((2, pieces, 4)),
            dma((2, pieces, 8)),
            dma((2, pieces, 8)),
            dma((2, pieces, 8)),
            dma((2, layers)),
        ],
        compiler_params=pltpu.CompilerParams(
            collective_id=collective_id, has_side_effects=True, vmem_limit_bytes=48 * 1024 * 1024
        ),
        cost_estimate=pl.CostEstimate(flops=0, bytes_accessed=150_000_000, transcendentals=0),
        name="exchange_start",
    )(ids.reshape(-1, 1), ids.reshape(1, -1), packet, vec_rows, attn, ffn, word_table)


WIDTHS = (D, D * 2 // 3, D // 3, D // 6, D // 12)


def gather_rows(block_ref, all_ref, z_sem, near_sem):
    d = lax.axis_index("dp")
    z = lax.axis_index("zero")
    line, spot = z // 4, lax.rem(z, 4)

    def at_line(k):
        return lax.rem(line + k, 4) * 4 + spot

    def near_by(j):
        across = j // 4
        return lax.rem(d + across, 2), line * 4 + lax.rem(spot + j % 4, 4)

    barrier = pltpu.get_barrier_semaphore()
    for k in range(1, 4):
        pl.semaphore_signal(barrier, inc=1, device_id=(d, at_line(k)), device_id_type=MESH)
    for j in range(1, 8):
        pl.semaphore_signal(barrier, inc=1, device_id=near_by(j), device_id_type=MESH)
    pl.semaphore_wait(barrier, 10)

    def z_copy(k):
        return pltpu.make_async_remote_copy(
            src_ref=block_ref,
            dst_ref=all_ref.at[d * 16 + z],
            send_sem=z_sem.at[0, k],
            recv_sem=z_sem.at[1, k],
            device_id=(d, at_line(k)),
            device_id_type=MESH,
        )

    def z_arrival(k):
        ref = all_ref.at[d * 16 + at_line(4 - k)]
        return pltpu.make_async_remote_copy(
            src_ref=ref,
            dst_ref=ref,
            send_sem=z_sem.at[0, k],
            recv_sem=z_sem.at[1, k],
            device_id=(d, at_line(k)),
            device_id_type=MESH,
        )

    def near_copy(i, j, from_d, from_z):
        ref = all_ref.at[from_d * 16 + from_z]
        return pltpu.make_async_remote_copy(
            src_ref=ref,
            dst_ref=ref,
            send_sem=near_sem.at[0, i, j],
            recv_sem=near_sem.at[1, i, j],
            device_id=near_by(j),
            device_id_type=MESH,
        )

    for k in range(1, 4):
        z_copy(k).start()
    all_ref[d * 16 + z] = block_ref[...]
    for j in range(1, 8):
        near_copy(0, j, d, z).start()
    for k in range(1, 4):
        z_arrival(k).wait_recv()
        for j in range(1, 8):
            near_copy(4 - k, j, d, at_line(4 - k)).start()
    for i in range(4):
        for j in range(1, 8):
            back = lax.rem(line + i, 4) * 4 + lax.rem(spot + 4 - j % 4, 4)
            near_copy(i, j, lax.rem(d + j // 4, 2), back).wait_recv()
            near_copy(i, j, d, at_line(i)).wait_send()
    for k in range(1, 4):
        z_copy(k).wait_send()


def contrastive_kernel(
    block_ref, false_ref, pair_ref, loss_ref, own_ref, all_ref, pooled_ref, grad_ref, z_sem, near_sem
):
    me = lax.axis_index("dp") * 16 + lax.axis_index("zero")
    gather_rows(block_ref, all_ref, z_sem, near_sem)
    upper = lax.broadcasted_iota(jnp.int32, (8, 1), 0) < 4
    for kind in range(2):
        for two in range(all_ref.shape[0] // 2):
            even = all_ref[2 * two, kind].astype(jnp.float32)
            odd = all_ref[2 * two + 1, kind].astype(jnp.float32)
            at = slice(8 * two, 8 * two + 8)
            pooled_ref[kind, 0, at, :] = jnp.where(upper, even, pltpu.roll(odd, 4, 0))
            pooled_ref[kind, 1, at, :] = jnp.where(upper, pltpu.roll(even, 4, 0), odd)
    contrastive_math(pooled_ref, false_ref, pair_ref, loss_ref, grad_ref)
    first = pl.multiple_of(me // 2 * 8, 8)
    swap = lax.rem(me, 2) == 1
    for kind in range(2):
        for role in range(2):
            rows = grad_ref[kind, role, pl.ds(first, 8), :]
            own_ref[kind, role] = jnp.where(swap, pltpu.roll(rows, 4, 0), rows)


def contrastive_math(pooled_ref, false_ref, pair_ref, loss_ref, grad_ref):
    pairs = false_ref.shape[0]
    high = lax.Precision.HIGHEST
    columns = lax.broadcasted_iota(jnp.int32, (pairs, pairs), 1)
    hit = columns == pair_ref[...]
    kept = (false_ref[...] == 0) | hit
    hits = hit.astype(jnp.float32)
    valid = (pair_ref[...] >= 0).astype(jnp.float32)
    inverse = 1.0 / jnp.maximum(jnp.sum(valid, axis=0, keepdims=True), 1.0)
    weight = valid * inverse
    named = jnp.sum(hits, axis=1, keepdims=True)
    totals = jnp.zeros((pairs, 1), jnp.float32)
    for first, width in enumerate(WIDTHS):
        span = -(-width // 128) * 128
        inside = lax.broadcasted_iota(jnp.int32, (1, span), 1) < width
        units, scales, logs = [], [], []
        for kind in range(2):
            pair_units, pair_scales = [], []
            for role in range(2):
                rows = jnp.where(inside, pooled_ref[kind, role, :, 0:span], 0.0)
                scale = lax.rsqrt(jnp.sum(rows * rows, axis=1, keepdims=True) + NORM_EPS)
                pair_units.append(rows * scale)
                pair_scales.append(scale)
            sims = lax.dot_general(
                pair_units[0],
                pair_units[1],
                (((1,), (1,)), ((), ())),
                precision=high,
                preferred_element_type=jnp.float32,
            )
            sims = jnp.where(kept, sims / SOFTMAX_TEMP, MASKED)
            shifted = sims - jnp.max(sims, axis=1, keepdims=True)
            logs.append(shifted - jnp.log(jnp.sum(jnp.exp(shifted), axis=1, keepdims=True)))
            units.append(pair_units)
            scales.append(pair_scales)
        shallow, deep = logs
        p_shallow, p_deep = jnp.exp(shallow), jnp.exp(deep)
        gap = p_deep * (deep - shallow)
        spread = jnp.sum(gap, axis=1, keepdims=True)
        totals = totals + spread - jnp.sum(jnp.where(hit, shallow + deep, 0.0), axis=1, keepdims=True)
        d_sims = (
            p_shallow * (named + 1.0) - hits - p_deep,
            gap + p_deep * (named - spread) - hits,
        )
        for kind in range(2):
            d_cos = jnp.where(kept, d_sims[kind] * weight, 0.0) / SOFTMAX_TEMP
            for role in range(2):
                unit = units[kind][role]
                d_unit = lax.dot_general(
                    d_cos,
                    units[kind][1 - role],
                    (((1 - role,), (0,)), ((), ())),
                    precision=high,
                    preferred_element_type=jnp.float32,
                )
                along = jnp.sum(d_unit * unit, axis=1, keepdims=True)
                d_rows = scales[kind][role] * (d_unit - unit * along)
                if first == 0:
                    grad_ref[kind, role] = d_rows
                else:
                    grad_ref[kind, role, :, 0:span] = grad_ref[kind, role, :, 0:span] + d_rows
    loss_ref[...] = jnp.broadcast_to(
        jnp.sum(totals * valid, axis=0, keepdims=True) * inverse, loss_ref.shape
    )


def contrastive(block, false_all, pair_all, collective_id):
    vmem = pl.BlockSpec(memory_space=pltpu.VMEM)
    pairs = false_all.shape[0]
    dma = pltpu.SemaphoreType.DMA
    whole = pltpu.VMEM((2, 2, pairs, D), jnp.float32)
    loss, grads = pl.pallas_call(
        contrastive_kernel,
        out_shape=(
            jax.ShapeDtypeStruct((8, 128), jnp.float32),
            jax.ShapeDtypeStruct((2, 2, 8, D), jnp.float32),
        ),
        in_specs=[vmem] * 3,
        out_specs=(vmem, vmem),
        scratch_shapes=[
            pltpu.VMEM((32,) + block.shape, block.dtype),
            whole,
            whole,
            dma((2, 4)),
            dma((2, 4, 8)),
        ],
        compiler_params=pltpu.CompilerParams(
            collective_id=collective_id, has_side_effects=True, vmem_limit_bytes=32 * 1024 * 1024
        ),
        cost_estimate=pl.CostEstimate(flops=10**9, bytes_accessed=3_000_000, transcendentals=10**6),
        name="contrastive",
    )(block, false_all, pair_all.reshape(-1, 1))
    return loss[0, 0], grads


PAIRS_OF_HEADS = HEADS // 2


def by_side(rows):
    lane = lax.broadcasted_iota(jnp.int32, (1, 2 * HD), 1)
    zero = jnp.zeros_like(rows)
    return jnp.concatenate([jnp.where(lane < HD, rows, zero), jnp.where(lane < HD, zero, rows)])


def join_sides(stacked):
    lane = lax.broadcasted_iota(jnp.int32, (1, 2 * HD), 1)
    return jnp.where(lane < HD, stacked[:SEQ], stacked[SEQ:])


def contract(left, right, left_dim, right_dim):
    return lax.dot_general(
        left, right, (((left_dim,), (right_dim,)), ((), ())), preferred_element_type=jnp.float32
    )


def thirds(packed_ref):
    for pair in range(PAIRS_OF_HEADS):
        at = pair * 2 * HD
        yield [packed_ref[0, :, t * D + at : t * D + at + 2 * HD] for t in range(3)]


def probabilities(scores, valid):
    scores = jnp.where(valid, scores * HD ** (-0.5), MASKED)
    raised = jnp.exp(scores - jnp.max(scores, axis=1, keepdims=True))
    return raised * (1.0 / jnp.sum(raised, axis=1, keepdims=True))


def attention_kernel(mask_ref, packed_ref, context_ref):
    valid = mask_ref[0] > 0.0
    parts = list(thirds(packed_ref))
    scores = [contract(by_side(queries), keys, 1, 1) for queries, keys, _ in parts]
    probs = [probabilities(now, valid).astype(jnp.bfloat16) for now in scores]
    for pair in range(PAIRS_OF_HEADS):
        mixed = contract(probs[pair], parts[pair][2], 1, 0)
        at = pair * 2 * HD
        context_ref[0, :, at : at + 2 * HD] = join_sides(mixed).astype(jnp.bfloat16)


def attention_back_kernel(mask_ref, packed_ref, grad_ref, out_ref):
    valid = mask_ref[0] > 0.0
    parts = list(thirds(packed_ref))
    queries = [by_side(part[0]) for part in parts]
    grads = [
        by_side(grad_ref[0, :, pair * 2 * HD : (pair + 1) * 2 * HD])
        for pair in range(PAIRS_OF_HEADS)
    ]
    scores = [contract(now, part[1], 1, 1) for now, part in zip(queries, parts)]
    d_probs = [contract(now, part[2], 1, 1) for now, part in zip(grads, parts)]
    probs = [probabilities(now, valid) for now in scores]
    d_scores = []
    for now, d_now in zip(probs, d_probs):
        shared = jnp.sum(d_now * now, axis=1, keepdims=True)
        d_scores.append(jnp.where(valid, now * (d_now - shared), 0.0).astype(jnp.bfloat16))
    for pair in range(PAIRS_OF_HEADS):
        d_queries = join_sides(contract(d_scores[pair], parts[pair][1], 1, 0)) * HD ** (-0.5)
        d_keys = contract(d_scores[pair], queries[pair], 0, 0) * HD ** (-0.5)
        d_values = contract(probs[pair].astype(jnp.bfloat16), grads[pair], 0, 0)
        for third, now in enumerate((d_queries, d_keys, d_values)):
            at = third * D + pair * 2 * HD
            out_ref[0, :, at : at + 2 * HD] = now.astype(jnp.bfloat16)


def attention_call(kernel, mask, operands, features, name):
    count = operands[0].shape[0]

    def spec(last):
        return pl.BlockSpec((1, SEQ, last), lambda i: (i, 0, 0))

    return pl.pallas_call(
        kernel,
        grid=(count,),
        out_shape=jax.ShapeDtypeStruct((count, SEQ, features), jnp.bfloat16),
        in_specs=[pl.BlockSpec((1, 1, SEQ), lambda i: (i, 0, 0))]
        + [spec(operand.shape[2]) for operand in operands],
        out_specs=spec(features),
        compiler_params=pltpu.CompilerParams(vmem_limit_bytes=32 * 1024 * 1024),
        cost_estimate=pl.CostEstimate(
            flops=10**9, bytes_accessed=count * SEQ * D * 10, transcendentals=10**6
        ),
        name=name,
    )(mask, *operands)


@jax.custom_vjp
def attend(packed, mask):
    return attend_forward(packed, mask)[0]


def attend_forward(packed, mask):
    half = packed.astype(jnp.bfloat16)
    context = attention_call(attention_kernel, mask, [half], D, "attention")
    return context.astype(jnp.float32), (half, mask)


def attend_backward(kept, grad):
    half, mask = kept
    d_packed = attention_call(
        attention_back_kernel, mask, [half, grad.astype(jnp.bfloat16)], 3 * D, "attention_back"
    )
    return d_packed.astype(jnp.float32), jnp.zeros_like(mask)


attend.defvjp(attend_forward, attend_backward)


LAYER_ROWS = 8 + FF // D


def layer_vectors(rows):
    up = 5 + FF // D
    return [rows[i] for i in range(5)] + [rows[5:up].reshape(FF)] + [rows[up + i] for i in range(3)]


def layer_norm(values, gain, shift):
    center = values - jnp.mean(values, axis=-1, keepdims=True)
    spread = jnp.mean(center * center, axis=-1, keepdims=True)
    return center * lax.rsqrt(spread + NORM_EPS) * gain + shift


def embed_tokens(rows, vectors):
    return layer_norm(low_back(rows) + vectors[None, :SEQ], vectors[SEQ], vectors[SEQ + 1])


def encoder_layer(hidden, weights, vectors, mask):
    in_weights, out_weights, up_weights, down_weights = weights
    q_bias, v_bias, o_bias, gain_one, shift_one, up_bias, down_bias, gain_two, second_shift = (
        layer_vectors(vectors)
    )
    packed = matmul(low(hidden), in_weights)
    packed = packed + jnp.concatenate([q_bias, jnp.zeros_like(q_bias), v_bias])
    context = attend(packed, mask)
    attended = low_back(matmul(context, out_weights) + o_bias)
    first_out = layer_norm(hidden + attended, gain_one, shift_one)
    upward = low_back(matmul(low(first_out), up_weights) + up_bias)
    active = rounded(jax.nn.gelu(upward, approximate=True))
    downward = low_back(einsum_plain("nsf,df->nsd", active, down_weights) + down_bias)
    return layer_norm(first_out + downward, gain_two, second_shift)


def pool_rows(hidden, key_mask, seq_lengths):
    share = key_mask.astype(jnp.float32) / seq_lengths.astype(jnp.float32)[:, None]
    return jnp.sum(hidden * share[:, :, None], axis=1)


def normalized_rows(rows):
    return rows * lax.rsqrt(jnp.sum(rows * rows, axis=-1, keepdims=True) + NORM_EPS)


def contrastive_terms(shallow_anchor, deep_anchor, shallow_pos, deep_pos, false_neg, pair_index):
    columns = lax.broadcasted_iota(jnp.int32, false_neg.shape, 1)
    hit = columns == pair_index[:, None]
    kept_cols = (false_neg == 0) | hit
    valid_rows = (pair_index >= 0).astype(jnp.float32)
    totals = jnp.zeros(pair_index.shape, jnp.float32)
    for current_width in (D, D * 2 // 3, D // 3, D // 6, D // 12):
        log_probs = []
        for anchor_vectors, positive_rows in (
            (shallow_anchor, shallow_pos),
            (deep_anchor, deep_pos),
        ):
            similarity_scores = (
                jnp.dot(
                    normalized_rows(anchor_vectors[:, :current_width]),
                    normalized_rows(positive_rows[:, :current_width]).T,
                    precision=lax.Precision.HIGHEST,
                )
                / SOFTMAX_TEMP
            )
            similarity_scores = jnp.where(kept_cols, similarity_scores, MASKED)
            log_probs.append(jax.nn.log_softmax(similarity_scores, axis=-1))
        for log_now in log_probs:
            totals = totals - jnp.sum(jnp.where(hit, log_now, 0.0), axis=-1)
        totals = totals + jnp.sum(jnp.exp(log_probs[1]) * (log_probs[1] - log_probs[0]), axis=-1)
    return jnp.sum(totals * valid_rows)


def adam_update(master, gradient, first, second, step_rate):
    first_new = BETA_ONE * first + (1.0 - BETA_ONE) * gradient
    second_new = BETA_TWO * second + (1.0 - BETA_TWO) * gradient * gradient
    first_hat = first_new / (1.0 - BETA_ONE**ADAM_STEP)
    second_hat = second_new / (1.0 - BETA_TWO**ADAM_STEP)
    master_new = master - step_rate * (
        first_hat / (jnp.sqrt(second_hat) + ADAM_EPS) + WEIGHT_DECAY * master
    )
    return (master_new, first_new, second_new)


def pad_rows(flat, multiple):
    rows = -(-flat.shape[0] // (128 * multiple)) * multiple
    return jnp.pad(flat, (0, rows * 128 - flat.shape[0])).reshape(rows, 128)


def one_hot(index, size, dtype=jnp.bfloat16):
    return (index[:, None] == lax.broadcasted_iota(jnp.int32, (1, size), 1)).astype(dtype)


def token_plan(ids, shard_rows):
    places = lax.broadcasted_iota(jnp.int32, ids.shape, 0)
    same = ids[:, None] == ids[None, :]
    leader = jnp.min(jnp.where(same, places[None, :], ids.shape[0]), axis=1)
    leads = leader == places
    owner = ids // shard_rows
    low_id = owner * shard_rows
    ahead = leads[None, :] & (ids[None, :] >= low_id[:, None]) & (ids[None, :] < ids[:, None])
    place = jnp.sum(ahead.astype(jnp.int32), axis=1)
    return owner, place, ids - low_id


def round_slots(owner, place, local_row, round_index, room, nz):
    inside = (place >= round_index * room) & (place < (round_index + 1) * room)
    slot = jnp.where(inside, owner * room + place - round_index * room, -1)
    slots = lax.broadcasted_iota(jnp.int32, (1, nz * room), 1)
    asked = jnp.max(jnp.where(slot[:, None] == slots, local_row[:, None], -1), axis=0)
    return slot, asked


def body(
    token_ids,
    lengths,
    false_neg,
    pair_index,
    word_table,
    vectors,
    attn_w,
    ffn_w,
    word_first,
    vector_first,
    attn_first,
    ffn_first,
    word_second,
    vector_second,
    attn_second,
    ffn_second,
):
    ndp = lax.axis_size("dp")
    nz = lax.axis_size("zero")
    n = ndp * nz
    by_hand = (ndp, nz) == (2, 16) and token_ids.shape[0] * ndp * nz <= 256
    my_dp = lax.axis_index("dp")
    my_zero = lax.axis_index("zero")
    me = my_dp * nz + my_zero
    pair_rows = token_ids.shape[0]
    total_pairs = pair_rows * n
    flat_ids = token_ids.reshape(-1, SEQ)
    seq_rows = flat_ids.shape[0]
    tokens = seq_rows * SEQ
    seq_lengths = lengths.reshape(-1)
    key_mask = lax.broadcasted_iota(jnp.int32, flat_ids.shape, 1) < seq_lengths[:, None]
    shard_rows = word_table.shape[0]
    vec_len = vectors.shape[0]

    room = -(-(tokens * 9 // 8) // (nz * 8)) * 8
    ids = flat_ids.reshape(-1)

    def packet_of(asked, rounds_here):
        last = jnp.concatenate([pair_index, rounds_here[None].astype(jnp.int32)])
        lines = nz + false_neg.size // 128
        return jnp.concatenate(
            [
                jnp.pad(asked.reshape(nz, room), ((0, 0), (0, 128 - room)), constant_values=-1),
                false_neg.reshape(-1, 128),
                jnp.zeros((7 - lines % 8, 128), jnp.int32),
                jnp.pad(last, (0, 128 - last.shape[0]))[None],
            ]
        )

    def gather_layer(layer_index):
        both = jnp.concatenate(
            [attn_w[layer_index].astype(jnp.bfloat16), ffn_w[layer_index].astype(jnp.bfloat16)],
            axis=1,
        )
        return lax.all_gather(both, "zero", axis=0, tiled=True)

    if by_hand:
        packet = pad_rows(jnp.concatenate([false_neg.reshape(-1), pair_index]), 8)
        place, packets, asked_mine, vec_parts, received, *gathered = exchange_start(
            ids,
            packet.astype(jnp.bfloat16),
            pad_rows(vectors.astype(jnp.bfloat16), 16),
            attn_w,
            ffn_w,
            word_table,
            room,
            0,
        )
        layer_weights = [part.reshape(D, -1) for part in gathered]
        rounds = jnp.max(asked_mine[:, 0, 127])
        asked_mine = asked_mine[:, 0, :room]
        packets = packets.reshape(n, -1).astype(jnp.int32)
        false_all = packets[:, : false_neg.size].reshape(total_pairs, total_pairs)
        pair_all = packets[:, false_neg.size : false_neg.size + pair_rows].reshape(total_pairs)
        owner = ids // shard_rows
        place, local_row = place.reshape(-1), ids - owner * shard_rows
        slot = jnp.where(place < room, owner * room + place, -1)
    else:
        owner, place, local_row = token_plan(ids, shard_rows)
        slot, asked = round_slots(owner, place, local_row, 0, room, nz)
        packets, vec_parts = exchange(
            [
                packet_of(asked, jnp.max(place) // room + 1),
                pad_rows(vectors.astype(jnp.bfloat16), 16),
            ],
            ["all", "zero"],
            ndp,
            nz,
            0,
            "gather_requests",
        )
        layer_weights = [gather_layer(layer_index) for layer_index in range(LAYERS)]
        asked_mine = lax.dynamic_index_in_dim(packets[:, :nz, :room], my_zero, 1, keepdims=False)
        false_all = packets[:, nz : nz + false_neg.size // 128].reshape(total_pairs, total_pairs)
        pair_all = packets[:, -1, :pair_rows].reshape(total_pairs)
        rounds = jnp.max(packets[:, -1, pair_rows])
    vec_all = vec_parts.reshape(nz, -1)[:, :vec_len].reshape(-1).astype(jnp.float32)

    asked_near = lax.dynamic_slice_in_dim(asked_mine, my_dp * nz, nz, 0)

    def rows_for(wanted):
        table, wanted = lax.optimization_barrier((word_table, wanted))
        picked = one_hot(wanted.reshape(-1), shard_rows)
        return matmul(picked, table.astype(jnp.bfloat16)).astype(jnp.bfloat16)

    def rows_from(slot_now, received):
        return matmul(one_hot(slot_now, nz * room), received.reshape(nz * room, D)).astype(
            jnp.bfloat16
        )

    if not by_hand:
        (received,) = exchange(
            [rows_for(asked_near).reshape(nz, room, D)], ["zero_p"], ndp, nz, 1, "send_rows"
        )
    rows = rows_from(slot, received)

    def more_rows(state):
        round_index, rows_now = state
        slot_now, asked_now = round_slots(owner, place, local_row, round_index, room, nz)
        wanted = lax.all_to_all(asked_now.reshape(nz, room), "zero", 0, 0, tiled=True)
        got = lax.all_to_all(rows_for(wanted).reshape(nz, room, D), "zero", 0, 0, tiled=True)
        return round_index + 1, rows_now + rows_from(slot_now, got)

    _, rows = lax.while_loop(lambda state: state[0] < rounds, more_rows, (jnp.int32(1), rows))
    rows = rows.reshape(seq_rows, SEQ, D).astype(jnp.float32)

    vec_rows = vec_all.reshape(-1, D)
    edges = [0] + [SEQ + 2 + i * LAYER_ROWS for i in range(LAYERS + 1)]
    vec_parts = [vec_rows[first:last] for first, last in zip(edges, edges[1:])]
    embedded, embed_back = jax.vjp(embed_tokens, rows, vec_parts[0])
    hidden = embedded
    mask = key_mask.astype(jnp.float32)[:, None, :]
    saved = []
    pooled = []
    for layer_index in range(LAYERS):
        weights = layer_weights[layer_index]
        edges = (0, 3 * D, 4 * D, 4 * D + FF, 4 * D + 2 * FF)
        parts = [
            weights[:, first:last].astype(jnp.float32) for first, last in zip(edges, edges[1:])
        ]
        output, layer_back = jax.vjp(
            functools.partial(encoder_layer, mask=mask), hidden, parts, vec_parts[1 + layer_index]
        )
        saved.append(layer_back)
        hidden = output
        pooled.append(pool_rows(hidden, key_mask, seq_lengths).astype(jnp.bfloat16))

    if by_hand and pair_rows == 4:
        block = jnp.stack(pooled).reshape(2, pair_rows, 2, D).transpose(0, 2, 1, 3)
        loss, pooled_grads = contrastive(block.reshape(2, 2 * pair_rows, D), false_all, pair_all, 2)
        pooled_grads = pooled_grads[:, :, :pair_rows]
    else:
        (pooled_all,) = exchange(
            [jnp.stack(pooled).reshape(-1, 128)], ["all"], ndp, nz, 2, "gather_pooled"
        )
        pooled_all = pooled_all.reshape(n, 2, pair_rows, 2, D).astype(jnp.float32)
        pooled_all = pooled_all.transpose(1, 3, 0, 2, 4).reshape(2, 2, total_pairs, D)

        def whole_loss(pooled_now):
            summed = contrastive_terms(
                pooled_now[0, 0],
                pooled_now[1, 0],
                pooled_now[0, 1],
                pooled_now[1, 1],
                false_all,
                pair_all,
            )
            valid_total = jnp.sum((pair_all >= 0).astype(jnp.float32))
            return summed / jnp.maximum(valid_total, 1.0)

        loss, pooled_grads = jax.value_and_grad(whole_loss)(pooled_all)
        pooled_grads = lax.dynamic_slice_in_dim(pooled_grads, me * pair_rows, pair_rows, 2)
    pooled_grads = pooled_grads.transpose(0, 2, 1, 3).reshape(2, seq_rows, D)
    shallow_back, deep_back = pooled_grads[0], pooled_grads[1]
    share = key_mask.astype(jnp.float32) / seq_lengths.astype(jnp.float32)[:, None]
    grad_hidden = jnp.zeros_like(embedded)
    weight_parts = []
    vec_grads = [None] * LAYERS
    for layer_index in range(LAYERS - 1, -1, -1):
        if layer_index == LAYERS - 1:
            grad_hidden = grad_hidden + deep_back[:, None, :] * share[:, :, None]
        if layer_index == 0:
            grad_hidden = grad_hidden + shallow_back[:, None, :] * share[:, :, None]
        layer_back = saved[layer_index]
        grad_hidden, part_grads, vec_grads[layer_index] = layer_back(grad_hidden)
        part_grads = [part.astype(jnp.bfloat16) for part in part_grads]
        if by_hand and layer_index == 0:
            weight_parts.insert(0, part_grads)
        else:
            both = jnp.concatenate(part_grads, axis=1)
            both, grad_hidden = lax.optimization_barrier((both, grad_hidden))
            weight_parts.insert(0, lax.psum_scatter(both, "zero", scatter_dimension=0, tiled=True))
    rows_grad, embed_grads = embed_back(grad_hidden)
    vec_grad = jnp.concatenate([embed_grads] + vec_grads, axis=0)
    down_local = jnp.stack([part[5 + FF // D] for part in vec_grads])

    rows_grad = rows_grad.reshape(tokens, D).astype(jnp.bfloat16)

    def slot_sums(slot_now):
        picked = one_hot(slot_now, nz * room)
        return lax.dot_general(
            picked, rows_grad, (((0,), (0,)), ((), ())), preferred_element_type=jnp.float32
        ).astype(jnp.bfloat16)

    def into_rows(wanted, sums):
        return lax.dot_general(
            one_hot(wanted.reshape(-1), shard_rows),
            sums.reshape(-1, D),
            (((0,), (0,)), ((), ())),
            preferred_element_type=jnp.float32,
        )

    down_each = down_local.reshape(LAYERS, nz, -1).transpose(1, 0, 2).reshape(nz, -1)
    down_len = down_each.shape[1]
    vec_blocks = jnp.concatenate([vec_grad.reshape(nz, vec_len), down_each], axis=1)
    lines = -(-vec_blocks.shape[1] // 1024) * 8
    vec_blocks = jnp.pad(vec_blocks, ((0, 0), (0, lines * 128 - vec_blocks.shape[1])))
    sums = slot_sums(slot).reshape(nz, room, D)
    if by_hand:
        *near, vec_near, sums_all, other_near = exchange_gradients(
            [part.reshape(4, 2, 2, -1, part.shape[1]) for part in weight_parts[0]]
            + [vec_blocks.reshape(4, 2, 2, lines, 128)],
            sums,
            weight_parts[1],
            3,
        )
        attn_shard = jnp.stack([jnp.concatenate(near[:2], axis=1), other_near[:, : 4 * D]])
        ffn_shard = jnp.stack([jnp.concatenate(near[2:], axis=1), other_near[:, 4 * D :]])
        vec_sum = vec_near.reshape(-1)
    else:
        sums_all, vec_shares = exchange(
            [sums, vec_blocks.reshape(nz, lines, 128)],
            ["all_p", "all_p"],
            ndp,
            nz,
            3,
            "send_gradients",
        )
        vec_sum = jnp.sum(vec_shares.reshape(n, -1), axis=0)
        (weight_all,) = exchange([jnp.stack(weight_parts)], ["dp"], ndp, nz, 4, "sum_replicas")
        weight_sum = jnp.sum(weight_all.astype(jnp.float32), axis=0)
        attn_shard = weight_sum[:, :, : 4 * D]
        ffn_shard = weight_sum[:, :, 4 * D :]
    word_grad = into_rows(asked_mine, sums_all)

    def more_sums(state):
        round_index, grad_now = state
        slot_now, asked_now = round_slots(owner, place, local_row, round_index, room, nz)
        wanted = lax.all_to_all(asked_now.reshape(nz, room), "zero", 0, 0, tiled=True)
        got = lax.all_to_all(slot_sums(slot_now).reshape(nz, room, D), "zero", 0, 0, tiled=True)
        wanted = lax.all_gather(wanted, "dp", axis=0, tiled=True)
        got = lax.all_gather(got, "dp", axis=0, tiled=True)
        return round_index + 1, grad_now + into_rows(wanted, got)

    _, word_grad = lax.while_loop(
        lambda state: state[0] < rounds, more_sums, (jnp.int32(1), word_grad)
    )
    vec_shard = vec_sum[:vec_len]
    down_shard = vec_sum[vec_len : vec_len + down_len].reshape(LAYERS, -1)

    square_local = jnp.sum(word_grad * word_grad) + jnp.sum(vec_shard * vec_shard)
    square_local = square_local + jnp.sum(attn_shard * attn_shard) + jnp.sum(ffn_shard * ffn_shard)
    (squares,) = exchange(
        [jnp.broadcast_to(square_local, (8, 128))], ["zero"], ndp, nz, 5, "gather_squares"
    )
    square_total = jnp.sum(squares[:, 0, 0])
    grad_norm = jnp.sqrt(square_total)
    factor = jnp.minimum(1.0, CLIP_NORM / (grad_norm + 1e-06))
    word_new, word_first_new, word_second_new = adam_update(
        word_table, word_grad * factor, word_first, word_second, LEARN_RATE
    )
    vector_new, vector_first_new, vector_second_new = adam_update(
        vectors, vec_shard * factor, vector_first, vector_second, VECTOR_RATE
    )
    attn_new, attn_first_new, attn_second_new = adam_update(
        attn_w, attn_shard * factor, attn_first, attn_second, LEARN_RATE
    )
    ffn_new, ffn_first_new, ffn_second_new = adam_update(
        ffn_w, ffn_shard * factor, ffn_first, ffn_second, LEARN_RATE
    )
    return (
        loss,
        grad_norm,
        word_new,
        vector_new,
        attn_new,
        ffn_new,
        word_new.astype(jnp.bfloat16),
        vector_new.astype(jnp.bfloat16),
        attn_new.astype(jnp.bfloat16),
        ffn_new.astype(jnp.bfloat16),
        word_first_new,
        vector_first_new,
        attn_first_new,
        ffn_first_new,
        word_second_new,
        vector_second_new,
        attn_second_new,
        ffn_second_new,
        down_shard * factor,
    )


def solution(mesh):
    placed = (
        P(("dp", "zero"), None, None),
        P(("dp", "zero"), None),
        P(("dp", "zero"), None),
        P(("dp", "zero")),
        P("zero", None),
        P("zero"),
        P(None, "zero", None),
        P(None, "zero", None),
        P("zero", None),
        P("zero"),
        P(None, "zero", None),
        P(None, "zero", None),
        P("zero", None),
        P("zero"),
        P(None, "zero", None),
        P(None, "zero", None),
    )
    return jax.shard_map(
        body,
        mesh=mesh,
        in_specs=placed,
        out_specs=(
            P(),
            P(),
            P("zero", None),
            P("zero"),
            P(None, "zero", None),
            P(None, "zero", None),
            P("zero", None),
            P("zero"),
            P(None, "zero", None),
            P(None, "zero", None),
            P("zero", None),
            P("zero"),
            P(None, "zero", None),
            P(None, "zero", None),
            P("zero", None),
            P("zero"),
            P(None, "zero", None),
            P(None, "zero", None),
            P(None, "zero"),
        ),
        check_vma=False,
    )
```

```python
import functools

import jax
import jax.numpy as jnp
from jax import lax
from jax.experimental import pallas as pl
from jax.experimental.pallas import tpu as pltpu
from jax.sharding import PartitionSpec as P

D = 512
HEADS = 8
HD = 64
FF = 2048
SEQ = 128
LAYERS = 2
ADAM_STEP = 5


SOFTMAX_TEMP = 0.05
CLIP_NORM = 1.0
LEARN_RATE = 0.02
VECTOR_RATE = 0.15
BETA_ONE = 0.5
BETA_TWO = 0.5
WEIGHT_DECAY = 0.01
ADAM_EPS = 1e-08
NORM_EPS = 1e-06
MASKED = -1000000000.0

MESH = pl.DeviceIdType.MESH


def build_low():

    def rounder(value):
        return lax.optimization_barrier(value.astype(jnp.bfloat16)).astype(jnp.float32)

    def keep_fwd(value):
        return (rounder(value), None)

    def pass_bwd(kept, grad):
        return (grad,)

    wrapped = jax.custom_vjp(rounder)
    wrapped.defvjp(keep_fwd, pass_bwd)
    return wrapped


def build_low_back():

    def identity_fn(value):
        return value

    def keep_fwd(value):
        return (value, None)

    def round_bwd(kept, grad):
        return (low(grad),)

    wrapped = jax.custom_vjp(identity_fn)
    wrapped.defvjp(keep_fwd, round_bwd)
    return wrapped


def low(value):
    return build_low()(value)


def low_back(value):
    return build_low_back()(value)


def rounded(value):
    return low(low_back(value))


def matmul(left, right):
    return jnp.dot(left, right, preferred_element_type=jnp.float32)


def einsum_plain(form, left, right):
    return jnp.einsum(form, left, right, preferred_element_type=jnp.float32)


def exchange_kernel(modes, ndp, nz, *refs):
    count = len(modes)
    ins = refs[:count]
    outs = refs[count : 2 * count]
    sems = refs[2 * count :]
    d = lax.axis_index("dp")
    z = lax.axis_index("zero")
    me = d * nz + z
    n = ndp * nz

    def peer_of(group, k):
        if group == "dp":
            pd = lax.rem(d + k, ndp)
            return pd, z, pd
        if group == "zero":
            pz = lax.rem(z + k, nz)
            return d, pz, pz
        p = lax.rem(me + k, n)
        return p // nz, lax.rem(p, nz), p

    groups = {m.split("_")[0] for m in modes}
    sizes = {"all": n, "zero": nz, "dp": ndp}
    mine = {"all": me, "zero": z, "dp": d}
    barrier = pltpu.get_barrier_semaphore()
    meet = ["all"] if "all" in groups else sorted(groups)
    total = 0
    for group in meet:
        total += sizes[group] - 1

        def greet(k, carry, group=group):
            pd, pz, _ = peer_of(group, k)
            pl.semaphore_signal(barrier, inc=1, device_id=(pd, pz), device_id_type=MESH)
            return carry

        lax.fori_loop(1, sizes[group], greet, 0)
    pl.semaphore_wait(barrier, total)

    def make(a, k):
        mode = modes[a]
        group = mode.split("_")[0]
        pd, pz, _ = peer_of(group, k)
        src = ins[a].at[pz] if mode.endswith("_p") else ins[a]
        return pltpu.make_async_remote_copy(
            src_ref=src,
            dst_ref=outs[a].at[mine[group]],
            send_sem=sems[2 * a].at[k],
            recv_sem=sems[2 * a + 1].at[k],
            device_id=(pd, pz),
            device_id_type=MESH,
        )

    for a, mode in enumerate(modes):
        group = mode.split("_")[0]

        def begin(k, carry, a=a):
            make(a, k).start()
            return carry

        lax.fori_loop(1, sizes[group], begin, 0)
    for a, mode in enumerate(modes):
        group = mode.split("_")[0]
        if mode.endswith("_p"):
            outs[a][mine[group]] = ins[a][z]
        else:
            outs[a][mine[group]] = ins[a][...]
    for a, mode in enumerate(modes):
        group = mode.split("_")[0]

        def finish(k, carry, a=a):
            make(a, k).wait()
            return carry

        lax.fori_loop(1, sizes[group], finish, 0)


def exchange(arrays, modes, ndp, nz, collective_id, name):
    sizes = {"all": ndp * nz, "zero": nz, "dp": ndp}
    outs = []
    scratch = []
    moved = 0
    for array, mode in zip(arrays, modes):
        size = sizes[mode.split("_")[0]]
        block = array.shape[1:] if mode.endswith("_p") else array.shape
        outs.append(jax.ShapeDtypeStruct((size,) + block, array.dtype))
        scratch += [pltpu.SemaphoreType.DMA((size,)), pltpu.SemaphoreType.DMA((size,))]
        one = array.dtype.itemsize
        for s in block:
            one *= s
        moved += one * size
    vmem = pl.BlockSpec(memory_space=pltpu.VMEM)
    return pl.pallas_call(
        functools.partial(exchange_kernel, tuple(modes), ndp, nz),
        out_shape=tuple(outs),
        in_specs=[vmem] * len(arrays),
        out_specs=tuple([vmem] * len(arrays)),
        scratch_shapes=scratch,
        compiler_params=pltpu.CompilerParams(
            collective_id=collective_id, has_side_effects=True, vmem_limit_bytes=48 * 1024 * 1024
        ),
        cost_estimate=pl.CostEstimate(flops=0, bytes_accessed=20 * moved, transcendentals=0),
        name=name,
    )(*arrays)


def gradient_kernel(chunks, matrices, vec_len, *refs):
    take = iter(refs)
    pairs = [(next(take), next(take)) for _ in range(matrices)]
    vec_ref, sums_ref, near_ref, asked_ref, extra_ref = [next(take) for _ in range(5)]
    attn_out, ffn_out, word_out, vec_out, stats_out = [next(take) for _ in range(5)]
    held = [None if m is None else next(take) for m, _, _ in chunks]
    bufs = [[next(take) for _ in range(5)] for _ in chunks]
    near_buf, rows_ref, added, square_ref, squares_ref = [next(take) for _ in range(5)]
    send_a, recv_a, send_y, recv_y, send_z, recv_z, send_x, recv_x = [next(take) for _ in range(8)]
    row_send, row_recv, pass_send, pass_recv, near_sem, extra_sem, square_sem = [
        next(take) for _ in range(7)
    ]

    d = lax.axis_index("dp")
    z = lax.axis_index("zero")
    core = lax.rem(z, 2)
    col = lax.rem(z // 2, 2)
    line = z // 4
    sibling = z + 1 - 2 * core
    across = z + 2 - 4 * col
    attn_width = attn_out.shape[2]

    def along(k):
        return lax.rem(line + k, 4) * 4 + lax.rem(z, 4)

    barrier = pltpu.get_barrier_semaphore()

    def greet(k, carry):
        pl.semaphore_signal(
            barrier, inc=1, device_id=(d, lax.rem(z + k, 16)), device_id_type=MESH
        )
        return carry

    lax.fori_loop(1, 16, greet, 0)
    pl.semaphore_signal(barrier, inc=1, device_id=(1 - d, z), device_id_type=MESH)
    pl.semaphore_wait(barrier, 16)

    def remote(src, dst, send, recv, to):
        return pltpu.make_async_remote_copy(
            src_ref=src,
            dst_ref=dst,
            send_sem=send,
            recv_sem=recv,
            device_id=to,
            device_id_type=MESH,
        )

    def part_of(i):
        return vec_ref if held[i] is None else held[i]

    def copy_a(i):
        src = part_of(i).at[:, :, 1 - core]
        return remote(src, bufs[i][0], send_a.at[i], recv_a.at[i], (d, sibling))

    def copy_y(i):
        src = bufs[i][0].at[:, 1 - col]
        return remote(src, bufs[i][1], send_y.at[i], recv_y.at[i], (d, across))

    def copy_z(i, k):
        src = bufs[i][1].at[lax.rem(line + k, 4)]
        return remote(
            src, bufs[i][2].at[k - 1], send_z.at[i, k - 1], recv_z.at[i, k - 1], (d, along(k))
        )

    def copy_x(i):
        return remote(bufs[i][3], bufs[i][4], send_x.at[i], recv_x.at[i], (1 - d, z))

    def row_push(k):
        to = lax.rem(z + k, 16)
        return remote(sums_ref.at[to], rows_ref.at[d, z], row_send.at[k], row_recv.at[k], (d, to))

    def row_pass(k):
        at = lax.rem(z + 16 - k, 16)
        return remote(
            rows_ref.at[d, at], rows_ref.at[d, at], pass_send.at[k], pass_recv.at[k], (1 - d, z)
        )

    near = remote(near_ref, near_buf, near_sem.at[0], near_sem.at[1], (1 - d, z))
    extra = pltpu.make_async_copy(extra_ref, word_out, extra_sem)
    extra.start()

    total = len(chunks)

    def push(k, carry):
        row_push(k).start()
        return carry

    lax.fori_loop(1, 16, push, 0)
    near.start()
    rows_ref[d, z] = sums_ref[z]
    row_pass(0).start()

    def compute(i):
        matrix, start, width = chunks[i]
        if matrix is not None:
            left, right = pairs[matrix]

            def rows_of(j, carry):
                at = pl.ds(pl.multiple_of(j * 128, 128), 128)
                found = lax.dot_general(
                    left[:, at],
                    right[:, start : start + width],
                    (((0,), (0,)), ((), ())),
                    preferred_element_type=jnp.float32,
                )
                held[i][j] = found.astype(jnp.bfloat16).reshape(2, 2, 32, width)
                return carry

            lax.fori_loop(0, 4, rows_of, 0)
        copy_a(i).start()

    def stage_a(i):
        copy_a(i).wait_recv()
        buf = bufs[i][0]

        def add_block(b, carry):
            line_at, col_at = b // 2, lax.rem(b, 2)
            mine = part_of(i)[line_at, col_at, core].astype(jnp.float32)
            got = buf[line_at, col_at].astype(jnp.float32)
            buf[line_at, col_at] = (mine + got).astype(buf.dtype)
            return carry

        lax.fori_loop(0, 8, add_block, 0)
        copy_y(i).start()

    def stage_y(i):
        copy_y(i).wait_recv()
        buf = bufs[i][1]

        def add_block(b, carry):
            mine = bufs[i][0][b, col].astype(jnp.float32)
            buf[b] = (mine + buf[b].astype(jnp.float32)).astype(buf.dtype)
            return carry

        lax.fori_loop(0, 4, add_block, 0)
        for k in range(1, 4):
            copy_z(i, k).start()

    def stage_z(i):
        for k in range(1, 4):
            copy_z(i, k).wait_recv()
        value = bufs[i][1][line].astype(jnp.float32)
        for k in range(3):
            value = value + bufs[i][2][k].astype(jnp.float32)
        bufs[i][3][...] = value.astype(bufs[i][3].dtype)
        copy_x(i).start()

    def stage_x(i):
        matrix, start, width = chunks[i]
        copy_x(i).wait_recv()
        value = bufs[i][3][...].astype(jnp.float32) + bufs[i][4][...].astype(jnp.float32)
        if matrix is None:
            vec_out[...] = value
        else:
            first = start + sum(pairs[m][1].shape[1] for m in range(matrix))
            if first < attn_width:
                attn_out[0, :, first : first + width] = value
            else:
                ffn_out[0, :, first - attn_width : first - attn_width + width] = value

    def pass_on(k):
        row_push(k).wait_recv()
        row_pass(k).start()

    tiles = added.shape[0] // 128
    spots = rows_ref.shape[1] * rows_ref.shape[2]

    def into_rows(plane, tile):
        lane = lax.broadcasted_iota(jnp.int32, (1, 128), 1) + tile * 128
        picked = (asked_ref[plane] == lane).astype(jnp.bfloat16)
        return lax.dot_general(
            picked,
            rows_ref[plane].reshape(spots, rows_ref.shape[3]),
            (((0,), (0,)), ((), ())),
            preferred_element_type=jnp.float32,
        )

    def own_plane(tile, carry):
        added[pl.ds(pl.multiple_of(tile * 128, 128), 128), :] = into_rows(d, tile)
        return carry

    compute(0)
    passed = 1
    for t in range(total + 3):
        if t + 1 < total:
            compute(t + 1)
        if t < total:
            stage_a(t)
        if 0 <= t - 1 < total:
            stage_y(t - 1)
        if 0 <= t - 2 < total:
            stage_z(t - 2)
        if 0 <= t - 3 < total:
            stage_x(t - 3)
        until = min(16, 1 + (t + 1) * 15 // (total - 1))
        for k in range(passed, until):
            pass_on(k)
        passed = until
        if t == total - 1:
            lax.fori_loop(0, tiles, own_plane, 0)

    near.wait()
    attn_out[1] = near_ref[:, :attn_width].astype(jnp.float32) + near_buf[:, :attn_width].astype(
        jnp.float32
    )
    ffn_out[1] = near_ref[:, attn_width:].astype(jnp.float32) + near_buf[:, attn_width:].astype(
        jnp.float32
    )

    def arrived(k, carry):
        at = lax.rem(z + 16 - k, 16)
        ref = rows_ref.at[1 - d, at]
        remote(ref, ref, pass_send.at[k], pass_recv.at[k], (1 - d, z)).wait_recv()
        return carry

    lax.fori_loop(0, 16, arrived, 0)
    extra.wait()
    features = word_out.shape[1]

    def add_rows(tile, count, first):
        at = pl.ds(first, count)
        value = (added[at, :] + into_rows(1 - d, tile)[:count]) + word_out[at, :]
        word_out[at, :] = value
        return jnp.sum(value * value, axis=0, keepdims=True)

    full = word_out.shape[0] // 128

    def other_plane(tile, carry):
        return carry + add_rows(tile, 128, pl.multiple_of(tile * 128, 128))

    squares = lax.fori_loop(0, full, other_plane, jnp.zeros((1, features), jnp.float32))
    if word_out.shape[0] % 128:
        squares = squares + add_rows(full, word_out.shape[0] % 128, full * 128)
    square = jnp.sum(squares, axis=1, keepdims=True)
    for out in (attn_out, ffn_out):

        def of_rows(r, carry, out=out):
            at = pl.ds(pl.multiple_of(r * 8, 8), 8)
            for layer in range(out.shape[0]):
                value = out[layer, at, :]
                carry = carry + jnp.sum(value * value, axis=0, keepdims=True)
            return carry

        found = lax.fori_loop(
            0, out.shape[1] // 8, of_rows, jnp.zeros((1, out.shape[2]), jnp.float32)
        )
        square = square + jnp.sum(found, axis=1, keepdims=True)
    place = lax.broadcasted_iota(jnp.int32, vec_out.shape, 0) * 128 + lax.broadcasted_iota(
        jnp.int32, vec_out.shape, 1
    )
    value = jnp.where(place < vec_len, vec_out[...], 0.0)
    found = jnp.sum(value * value, axis=0, keepdims=True)
    square = square + jnp.sum(found, axis=1, keepdims=True)
    square_ref[...] = jnp.broadcast_to(square, square_ref.shape)

    def square_copy(k, slot):
        return remote(
            square_ref,
            squares_ref.at[slot],
            square_sem.at[0, k],
            square_sem.at[1, k],
            (d, lax.rem(z + k, 16)),
        )

    def send_square(k, carry):
        square_copy(k, z).start()
        return carry

    lax.fori_loop(1, 16, send_square, 0)
    squares_ref[z] = square_ref[...]

    for i in range(total):
        copy_a(i).wait_send()
        copy_y(i).wait_send()
        for k in range(1, 4):
            copy_z(i, k).wait_send()
        copy_x(i).wait_send()

    def finish(k, carry):
        row_push(k).wait_send()
        square_copy(k, lax.rem(z + 16 - k, 16)).wait_recv()
        square_copy(k, z).wait_send()
        return carry

    lax.fori_loop(1, 16, finish, 0)

    def finish_pass(k, carry):
        row_pass(k).wait_send()
        return carry

    lax.fori_loop(0, 16, finish_pass, 0)
    norm = squares_ref[0]
    for slot in range(1, 16):
        norm = norm + squares_ref[slot]
    norm = jnp.sqrt(norm)
    stats_out[0:1, :] = norm
    stats_out[1:2, :] = jnp.minimum(1.0, CLIP_NORM / (norm + 1e-06))


def exchange_gradients(pairs, vec_parts, sums, near, asked, extra, vec_len, collective_id):
    chunks = [(None, 0, 128)]
    for index in (3, 2, 0, 1):
        columns = pairs[index][1].shape[1]
        width = columns // -(-columns // 1024)
        for start in range(0, columns, width):
            chunks.append((index, start, width))
    half = jnp.bfloat16
    held, bufs = [], []
    for index, start, width in chunks:
        kind = vec_parts.dtype if index is None else half
        r = vec_parts.shape[3] if index is None else 32
        if index is not None:
            held.append(pltpu.VMEM((4, 2, 2, r, width), kind))
        bufs += [
            pltpu.VMEM((4, 2, r, width), kind),
            pltpu.VMEM((4, r, width), kind),
            pltpu.VMEM((3, r, width), kind),
            pltpu.VMEM((r, width), kind),
            pltpu.VMEM((r, width), kind),
        ]
    shard_rows, features = extra.shape
    dma = pltpu.SemaphoreType.DMA
    count = len(chunks)
    scratch = held + bufs
    scratch += [
        pltpu.VMEM(near.shape, half),
        pltpu.VMEM((2,) + sums.shape, half),
        pltpu.VMEM((-(-shard_rows // 128) * 128, features), jnp.float32),
        pltpu.VMEM((1, 128), jnp.float32),
        pltpu.VMEM((16, 1, 128), jnp.float32),
    ]
    scratch += [dma((count,)) for _ in range(4)] + [dma((count, 3)) for _ in range(2)]
    scratch += [dma((count,)) for _ in range(2)]
    scratch += [dma((16,)) for _ in range(4)] + [dma((2,)), dma, dma((2, 16))]
    rows = near.shape[0]
    outs = [
        jax.ShapeDtypeStruct((2, rows, 4 * D), jnp.float32),
        jax.ShapeDtypeStruct((2, rows, 2 * FF), jnp.float32),
        jax.ShapeDtypeStruct(extra.shape, jnp.float32),
        jax.ShapeDtypeStruct(vec_parts.shape[3:], jnp.float32),
        jax.ShapeDtypeStruct((8, 128), jnp.float32),
    ]
    vmem = pl.BlockSpec(memory_space=pltpu.VMEM)
    return pl.pallas_call(
        functools.partial(gradient_kernel, tuple(chunks), len(pairs), vec_len),
        out_shape=tuple(outs),
        in_specs=[vmem] * (2 * len(pairs) + 4) + [pl.BlockSpec(memory_space=pl.ANY)],
        out_specs=tuple([vmem] * len(outs)),
        scratch_shapes=scratch,
        compiler_params=pltpu.CompilerParams(
            collective_id=collective_id, has_side_effects=True, vmem_limit_bytes=58 * 1024 * 1024
        ),
        cost_estimate=pl.CostEstimate(flops=0, bytes_accessed=200_000_000, transcendentals=0),
        name="exchange_gradients",
    )(*[array for pair in pairs for array in pair], vec_parts, sums, near, asked, extra)


SPLITS = 4
WINDOW = 3
LAG = 3


def start_kernel(shard_rows, room, *refs):
    column_ref, row_ref, packet_ref, vec_ref, attn_ref, ffn_ref, word_ref = refs[:7]
    place_out, slot_out, packet_out, asked_out, vec_out, rows_out, *weight_outs = refs[7:15]
    table, rows_held, asked, slots, locals_ = refs[15:20]
    packet_sem, asked_sem, vec_sem, row_sem = refs[20:24]
    z_sem, y_sem, x_sem, d_sem, e_sem, own_sem = refs[24:]

    d = lax.axis_index("dp")
    z = lax.axis_index("zero")
    me = d * 16 + z
    core = lax.rem(z, 2)
    col = lax.rem(z // 2, 2)
    line = z // 4
    sibling = z + 1 - 2 * core
    across = z + 2 - 4 * col
    layers = attn_ref.shape[0]
    width = attn_ref.shape[2]
    whole = 3 * width
    unit = whole // 128 // SPLITS
    hand = unit * 5 // 12
    total = layers * SPLITS

    def everyone(k):
        p = lax.rem(me + k, 32)
        return (p // 16, lax.rem(p, 16))

    barrier = pltpu.get_barrier_semaphore()

    def greet(k, carry):
        pl.semaphore_signal(barrier, inc=1, device_id=everyone(k), device_id_type=MESH)
        return carry

    lax.fori_loop(1, 32, greet, 0)
    for layer in range(layers):
        weight_outs[layer][z, :, 0:width] = attn_ref[layer].astype(jnp.bfloat16)
        weight_outs[layer][z, :, width:whole] = ffn_ref[layer].astype(jnp.bfloat16)
    pl.semaphore_wait(barrier, 31)

    def remote(src, dst, sems, at, to):
        return pltpu.make_async_remote_copy(
            src_ref=src,
            dst_ref=dst,
            send_sem=sems.at[(0,) + at],
            recv_sem=sems.at[(1,) + at],
            device_id=to,
            device_id_type=MESH,
        )

    def packet_copy(k, slot):
        return remote(packet_ref, packet_out.at[slot], packet_sem, (k,), everyone(k))

    def asked_copy(k, slot):
        to = everyone(k)
        return remote(asked.at[to[1]], asked_out.at[slot], asked_sem, (k,), to)

    def vec_copy(k, slot):
        return remote(vec_ref, vec_out.at[slot], vec_sem, (k,), (d, lax.rem(z + k, 16)))

    def row_copy(k, slot):
        to = lax.rem(z + k, 16)
        return remote(rows_held.at[to], rows_out.at[slot], row_sem, (k,), (d, to))

    def shard(i):
        at = lax.rem(line + i % 4, 4) * 4 + lax.rem(z, 4)
        return at if i < 4 else at + 2 - 4 * col

    def piece(s):
        layer, p = s // SPLITS, s % SPLITS
        size = unit if p < SPLITS - 1 else whole // 128 - p * unit
        return layer, p * unit, size

    def columns_of(at, s, first, size):
        layer, base, _ = piece(s)
        return weight_outs[layer].at[
            at, :, pl.ds(pl.multiple_of((base + first) * 128, 128), size * 128)
        ]

    def stretch(at, s, ours):
        size = piece(s)[2]
        return columns_of(at, s, ours * hand, size - hand)

    def handed(at, s, ours):
        size = piece(s)[2]
        return columns_of(at, s, ours * (size - hand), hand)

    def both(ref, sems, at, to):
        return remote(ref, ref, sems, at, to)

    def z_copy(s, k, at):
        to = lax.rem(line + k, 4) * 4 + lax.rem(z, 4)
        return both(stretch(at, s, d), z_sem, (s, k - 1), (d, to))

    def y_copy(s, j, at):
        return both(stretch(at, s, d), y_sem, (s, j), (d, across))

    def x_copy(s, i, at, ours):
        return both(handed(at, s, ours), x_sem, (s, i), (1 - d, z))

    def d_copy(s, i, at):
        return both(stretch(at, s, d), d_sem, (s, i), (d, sibling))

    def e_copy(s, i, at):
        return both(handed(at, s, 1 - d), e_sem, (s, i), (d, sibling))

    def own_copy(layer, at):
        ref = weight_outs[layer].at[at]
        return both(ref, own_sem, (layer,), (d, sibling))

    def spread(s, i):
        at = shard(i)
        if i < 4:
            y_copy(s, i, at).start()
        if i > 0:
            x_copy(s, i, at, d).start()
            d_copy(s, i, at).start()

    def open_piece(s):
        for k in range(1, 4):
            z_copy(s, k, z).start()
        spread(s, 0)

    for s in range(WINDOW):
        open_piece(s)

    tokens = column_ref.shape[0]
    ids_row = row_ref[...]
    lane = lax.broadcasted_iota(jnp.int32, (1, tokens), 1).astype(jnp.float32)
    block = 128

    def lead_of(b, least):
        ids = column_ref[pl.ds(pl.multiple_of(b * block, block), block), :]
        there = lax.broadcasted_iota(jnp.int32, (block, 1), 0) + b * block
        found = jnp.where(ids == ids_row, there.astype(jnp.float32), 1e9)
        return jnp.minimum(least, jnp.min(found, axis=0, keepdims=True))

    least = lax.fori_loop(0, tokens // block, lead_of, jnp.full((1, tokens), 1e9, jnp.float32))
    lead_ids = jnp.where(least == lane, ids_row, -1)

    def place_of(b, most):
        at = pl.ds(pl.multiple_of(b * block, block), block)
        ids = column_ref[at, :]
        owner = jnp.zeros_like(ids)
        for o in range(1, 16):
            owner = owner + (ids >= o * shard_rows).astype(jnp.int32)
        low_id = owner * shard_rows
        ahead = (lead_ids >= low_id) & (lead_ids < ids)
        place = jnp.sum(jnp.where(ahead, 1.0, 0.0), axis=1, keepdims=True)
        place_out[at, :] = place.astype(jnp.int32)
        inside = place < room
        slots[at, :] = jnp.where(inside, owner * 128 + place.astype(jnp.int32), -1)
        slot_out[at, :] = jnp.where(inside, owner * room + place.astype(jnp.int32), -1)
        locals_[at, :] = (ids - low_id).astype(jnp.float32)
        return jnp.maximum(most, jnp.max(place, axis=0, keepdims=True))

    most = lax.fori_loop(0, tokens // block, place_of, jnp.zeros((1, 1), jnp.float32))
    rounds = jnp.ones((1, 1), jnp.float32)
    for r in range(1, -(-tokens // room)):
        rounds = rounds + (most >= r * room).astype(jnp.float32)
    lane128 = lax.broadcasted_iota(jnp.int32, (1, 128), 1)

    for o in range(16):

        def asked_of(b, best, o=o):
            at = pl.ds(pl.multiple_of(b * block, block), block)
            found = jnp.where(slots[at, :] == o * 128 + lane128, locals_[at, :], -1.0)
            return jnp.maximum(best, jnp.max(found, axis=0, keepdims=True))

        best = lax.fori_loop(0, tokens // block, asked_of, jnp.full((1, 128), -1.0, jnp.float32))
        asked[o] = jnp.where(lane128 == 127, rounds, best).astype(jnp.int32)

    def send_packets(k, carry):
        asked_copy(k, me).start()
        packet_copy(k, me).start()
        return carry

    lax.fori_loop(1, 32, send_packets, 0)

    def send_vec(k, carry):
        vec_copy(k, z).start()
        return carry

    lax.fori_loop(1, 16, send_vec, 0)
    for layer in range(layers):
        own_copy(layer, z).start()
    vec_out[z] = vec_ref[...]
    asked_out[me] = asked[z]
    packet_out[me] = packet_ref[...]

    body_rows = shard_rows // 16 * 16
    step = 112 if body_rows % 112 == 0 else 16

    def to_half(i, carry):
        at = pl.multiple_of(i * step, 16)
        table[pl.ds(at, step), :] = word_ref[pl.ds(at, step), :].astype(jnp.bfloat16)
        return carry

    lax.fori_loop(0, body_rows // step, to_half, 0)
    padded = table.shape[0]
    table[body_rows:padded, :] = jnp.zeros((padded - body_rows, table.shape[1]), jnp.bfloat16)
    if shard_rows > body_rows:
        table[body_rows:shard_rows, :] = word_ref[body_rows:shard_rows, :].astype(jnp.bfloat16)

    def answer_one(k, carry):
        src = lax.rem(z + k, 16)
        rows_at = lax.broadcasted_iota(jnp.int32, (padded, 128), 0)
        picked = (rows_at == asked_out[d * 16 + src]).astype(jnp.bfloat16)
        found = lax.dot_general(
            picked, table[...], (((0,), (0,)), ((), ())), preferred_element_type=jnp.float32
        )
        rows_held[src] = found[:room, :].astype(jnp.bfloat16)
        return carry

    def packet_in(k, carry):
        asked_copy(k, lax.rem(me + 32 - k, 32)).wait_recv()
        return carry

    def row_start(k, carry):
        row_copy(k, z).start()
        return carry

    def z_phase(s):
        for k in range(1, 4):
            z_copy(s, k, shard(4 - k)).wait_recv()
            spread(s, 4 - k)
        if s + WINDOW < total:
            open_piece(s + WINDOW)

    def y_phase(s):
        for j in range(4):
            y_copy(s, j, shard(4 + j)).wait_recv()
            spread(s, 4 + j)

    def x_phase(s):
        for i in range(1, 8):
            at = shard(i)
            x_copy(s, i, at, 1 - d).wait_recv()
            e_copy(s, i, at).start()

    done = 0
    for t in range(total + LAG):
        if t < total:
            z_phase(t)
        if t == 1:
            lax.fori_loop(1, 32, packet_in, 0)
        if t >= 1:
            until = min(16, done + 4)
            if until > done:
                lax.fori_loop(done, until, answer_one, 0)
            done = until
        if t == total - 1:
            lax.fori_loop(1, 16, row_start, 0)
            rows_out[z] = rows_held[z]
        if 0 <= t - 1 < total:
            y_phase(t - 1)
        if 0 <= t - LAG < total:
            x_phase(t - LAG)

    turn = 1 - 2 * core
    for layer in range(layers):
        own_copy(layer, z + turn).wait_recv()
        own_copy(layer, z).wait_send()
    for s in range(total):
        for i in range(1, 8):
            at = shard(i)
            d_copy(s, i, at + turn).wait_recv()
            d_copy(s, i, at).wait_send()
            e_copy(s, i, at + turn).wait_recv()
            e_copy(s, i, at).wait_send()
            x_copy(s, i, at, d).wait_send()
        for k in range(1, 4):
            z_copy(s, k, z).wait_send()
        for i in range(4):
            y_copy(s, i, shard(i)).wait_send()

    def finish(k, carry):
        back = lax.rem(z + 16 - k, 16)
        row_copy(k, back).wait_recv()
        row_copy(k, z).wait_send()
        vec_copy(k, back).wait_recv()
        vec_copy(k, z).wait_send()
        return carry

    lax.fori_loop(1, 16, finish, 0)

    def finish_packets(k, carry):
        packet_copy(k, lax.rem(me + 32 - k, 32)).wait_recv()
        packet_copy(k, me).wait_send()
        asked_copy(k, me).wait_send()
        return carry

    lax.fori_loop(1, 32, finish_packets, 0)


def exchange_start(ids, packet, vec_rows, attn, ffn, word_table, room, collective_id):
    half = jnp.bfloat16
    shard_rows, features = word_table.shape
    padded = -(-shard_rows // 128) * 128
    layers, rows, width = attn.shape
    tokens = ids.shape[0]
    pieces = layers * SPLITS
    dma = pltpu.SemaphoreType.DMA
    vmem = pl.BlockSpec(memory_space=pltpu.VMEM)
    return pl.pallas_call(
        functools.partial(start_kernel, shard_rows, room),
        out_shape=(
            jax.ShapeDtypeStruct((tokens, 1), jnp.int32),
            jax.ShapeDtypeStruct((tokens, 1), jnp.int32),
            jax.ShapeDtypeStruct((32,) + packet.shape, packet.dtype),
            jax.ShapeDtypeStruct((32, 1, 128), jnp.int32),
            jax.ShapeDtypeStruct((16,) + vec_rows.shape, vec_rows.dtype),
            jax.ShapeDtypeStruct((16, room, features), half),
        )
        + (jax.ShapeDtypeStruct((16, rows, 3 * width), half),) * layers,
        in_specs=[vmem] * 7,
        out_specs=tuple([vmem] * (6 + layers)),
        scratch_shapes=[
            pltpu.VMEM((padded, features), half),
            pltpu.VMEM((16, room, features), half),
            pltpu.VMEM((16, 1, 128), jnp.int32),
            pltpu.VMEM((tokens, 1), jnp.int32),
            pltpu.VMEM((tokens, 1), jnp.float32),
            dma((2, 32)),
            dma((2, 32)),
            dma((2, 16)),
            dma((2, 16)),
            dma((2, pieces, 3)),
            dma((2, pieces, 4)),
            dma((2, pieces, 8)),
            dma((2, pieces, 8)),
            dma((2, pieces, 8)),
            dma((2, layers)),
        ],
        compiler_params=pltpu.CompilerParams(
            collective_id=collective_id, has_side_effects=True, vmem_limit_bytes=48 * 1024 * 1024
        ),
        cost_estimate=pl.CostEstimate(flops=0, bytes_accessed=150_000_000, transcendentals=0),
        name="exchange_start",
    )(ids.reshape(-1, 1), ids.reshape(1, -1), packet, vec_rows, attn, ffn, word_table)


WIDTHS = (D, D * 2 // 3, D // 3, D // 6, D // 12)


def gather_rows(block_ref, all_ref, z_sem, near_sem):
    d = lax.axis_index("dp")
    z = lax.axis_index("zero")
    line, spot = z // 4, lax.rem(z, 4)

    def at_line(k):
        return lax.rem(line + k, 4) * 4 + spot

    def near_by(j):
        across = j // 4
        return lax.rem(d + across, 2), line * 4 + lax.rem(spot + j % 4, 4)

    barrier = pltpu.get_barrier_semaphore()
    for k in range(1, 4):
        pl.semaphore_signal(barrier, inc=1, device_id=(d, at_line(k)), device_id_type=MESH)
    for j in range(1, 8):
        pl.semaphore_signal(barrier, inc=1, device_id=near_by(j), device_id_type=MESH)
    pl.semaphore_wait(barrier, 10)

    def z_copy(k):
        return pltpu.make_async_remote_copy(
            src_ref=block_ref,
            dst_ref=all_ref.at[d * 16 + z],
            send_sem=z_sem.at[0, k],
            recv_sem=z_sem.at[1, k],
            device_id=(d, at_line(k)),
            device_id_type=MESH,
        )

    def z_arrival(k):
        ref = all_ref.at[d * 16 + at_line(4 - k)]
        return pltpu.make_async_remote_copy(
            src_ref=ref,
            dst_ref=ref,
            send_sem=z_sem.at[0, k],
            recv_sem=z_sem.at[1, k],
            device_id=(d, at_line(k)),
            device_id_type=MESH,
        )

    def near_copy(i, j, from_d, from_z):
        ref = all_ref.at[from_d * 16 + from_z]
        return pltpu.make_async_remote_copy(
            src_ref=ref,
            dst_ref=ref,
            send_sem=near_sem.at[0, i, j],
            recv_sem=near_sem.at[1, i, j],
            device_id=near_by(j),
            device_id_type=MESH,
        )

    for k in range(1, 4):
        z_copy(k).start()
    all_ref[d * 16 + z] = block_ref[...]
    for j in range(1, 8):
        near_copy(0, j, d, z).start()
    for k in range(1, 4):
        z_arrival(k).wait_recv()
        for j in range(1, 8):
            near_copy(4 - k, j, d, at_line(4 - k)).start()
    for i in range(4):
        for j in range(1, 8):
            back = lax.rem(line + i, 4) * 4 + lax.rem(spot + 4 - j % 4, 4)
            near_copy(i, j, lax.rem(d + j // 4, 2), back).wait_recv()
            near_copy(i, j, d, at_line(i)).wait_send()
    for k in range(1, 4):
        z_copy(k).wait_send()


def contrastive_kernel(
    block_ref, false_ref, pair_ref, loss_ref, own_ref, all_ref, pooled_ref, grad_ref, z_sem, near_sem
):
    me = lax.axis_index("dp") * 16 + lax.axis_index("zero")
    gather_rows(block_ref, all_ref, z_sem, near_sem)
    upper = lax.broadcasted_iota(jnp.int32, (8, 1), 0) < 4
    for kind in range(2):
        for two in range(all_ref.shape[0] // 2):
            even = all_ref[2 * two, kind].astype(jnp.float32)
            odd = all_ref[2 * two + 1, kind].astype(jnp.float32)
            at = slice(8 * two, 8 * two + 8)
            pooled_ref[kind, 0, at, :] = jnp.where(upper, even, pltpu.roll(odd, 4, 0))
            pooled_ref[kind, 1, at, :] = jnp.where(upper, pltpu.roll(even, 4, 0), odd)
    contrastive_math(pooled_ref, false_ref, pair_ref, loss_ref, grad_ref)
    first = pl.multiple_of(me // 2 * 8, 8)
    swap = lax.rem(me, 2) == 1
    for kind in range(2):
        for role in range(2):
            rows = grad_ref[kind, role, pl.ds(first, 8), :]
            own_ref[kind, role] = jnp.where(swap, pltpu.roll(rows, 4, 0), rows)


def contrastive_math(pooled_ref, false_ref, pair_ref, loss_ref, grad_ref):
    pairs = false_ref.shape[0]
    high = lax.Precision.HIGHEST
    columns = lax.broadcasted_iota(jnp.int32, (pairs, pairs), 1)
    hit = columns == pair_ref[...]
    kept = (false_ref[...] == 0) | hit
    hits = hit.astype(jnp.float32)
    valid = (pair_ref[...] >= 0).astype(jnp.float32)
    inverse = 1.0 / jnp.maximum(jnp.sum(valid, axis=0, keepdims=True), 1.0)
    weight = valid * inverse
    named = jnp.sum(hits, axis=1, keepdims=True)
    totals = jnp.zeros((pairs, 1), jnp.float32)
    for first, width in enumerate(WIDTHS):
        span = -(-width // 128) * 128
        inside = lax.broadcasted_iota(jnp.int32, (1, span), 1) < width
        units, scales, logs = [], [], []
        for kind in range(2):
            pair_units, pair_scales = [], []
            for role in range(2):
                rows = jnp.where(inside, pooled_ref[kind, role, :, 0:span], 0.0)
                scale = lax.rsqrt(jnp.sum(rows * rows, axis=1, keepdims=True) + NORM_EPS)
                pair_units.append(rows * scale)
                pair_scales.append(scale)
            sims = lax.dot_general(
                pair_units[0],
                pair_units[1],
                (((1,), (1,)), ((), ())),
                precision=high,
                preferred_element_type=jnp.float32,
            )
            sims = jnp.where(kept, sims / SOFTMAX_TEMP, MASKED)
            shifted = sims - jnp.max(sims, axis=1, keepdims=True)
            logs.append(shifted - jnp.log(jnp.sum(jnp.exp(shifted), axis=1, keepdims=True)))
            units.append(pair_units)
            scales.append(pair_scales)
        shallow, deep = logs
        p_shallow, p_deep = jnp.exp(shallow), jnp.exp(deep)
        gap = p_deep * (deep - shallow)
        spread = jnp.sum(gap, axis=1, keepdims=True)
        totals = totals + spread - jnp.sum(jnp.where(hit, shallow + deep, 0.0), axis=1, keepdims=True)
        d_sims = (
            p_shallow * (named + 1.0) - hits - p_deep,
            gap + p_deep * (named - spread) - hits,
        )
        for kind in range(2):
            d_cos = jnp.where(kept, d_sims[kind] * weight, 0.0) / SOFTMAX_TEMP
            for role in range(2):
                unit = units[kind][role]
                d_unit = lax.dot_general(
                    d_cos,
                    units[kind][1 - role],
                    (((1 - role,), (0,)), ((), ())),
                    precision=high,
                    preferred_element_type=jnp.float32,
                )
                along = jnp.sum(d_unit * unit, axis=1, keepdims=True)
                d_rows = scales[kind][role] * (d_unit - unit * along)
                if first == 0:
                    grad_ref[kind, role] = d_rows
                else:
                    grad_ref[kind, role, :, 0:span] = grad_ref[kind, role, :, 0:span] + d_rows
    loss_ref[...] = jnp.broadcast_to(
        jnp.sum(totals * valid, axis=0, keepdims=True) * inverse, loss_ref.shape
    )


def contrastive(block, false_all, pair_all, collective_id):
    vmem = pl.BlockSpec(memory_space=pltpu.VMEM)
    pairs = false_all.shape[0]
    dma = pltpu.SemaphoreType.DMA
    whole = pltpu.VMEM((2, 2, pairs, D), jnp.float32)
    loss, grads = pl.pallas_call(
        contrastive_kernel,
        out_shape=(
            jax.ShapeDtypeStruct((8, 128), jnp.float32),
            jax.ShapeDtypeStruct((2, 2, 8, D), jnp.float32),
        ),
        in_specs=[vmem] * 3,
        out_specs=(vmem, vmem),
        scratch_shapes=[
            pltpu.VMEM((32,) + block.shape, block.dtype),
            whole,
            whole,
            dma((2, 4)),
            dma((2, 4, 8)),
        ],
        compiler_params=pltpu.CompilerParams(
            collective_id=collective_id, has_side_effects=True, vmem_limit_bytes=32 * 1024 * 1024
        ),
        cost_estimate=pl.CostEstimate(flops=10**9, bytes_accessed=3_000_000, transcendentals=10**6),
        name="contrastive",
    )(block, false_all, pair_all.reshape(-1, 1))
    return loss[0, 0], grads


PAIRS_OF_HEADS = HEADS // 2


def by_side(rows):
    lane = lax.broadcasted_iota(jnp.int32, (1, 2 * HD), 1)
    zero = jnp.zeros_like(rows)
    return jnp.concatenate([jnp.where(lane < HD, rows, zero), jnp.where(lane < HD, zero, rows)])


def join_sides(stacked):
    lane = lax.broadcasted_iota(jnp.int32, (1, 2 * HD), 1)
    return jnp.where(lane < HD, stacked[:SEQ], stacked[SEQ:])


def contract(left, right, left_dim, right_dim):
    return lax.dot_general(
        left, right, (((left_dim,), (right_dim,)), ((), ())), preferred_element_type=jnp.float32
    )


def thirds(packed_ref):
    for pair in range(PAIRS_OF_HEADS):
        at = pair * 2 * HD
        yield [packed_ref[0, :, t * D + at : t * D + at + 2 * HD] for t in range(3)]


def probabilities(scores, valid):
    scores = jnp.where(valid, scores * HD ** (-0.5), MASKED)
    raised = jnp.exp(scores - jnp.max(scores, axis=1, keepdims=True))
    return raised * (1.0 / jnp.sum(raised, axis=1, keepdims=True))


def attention_kernel(mask_ref, packed_ref, context_ref):
    valid = mask_ref[0] > 0.0
    parts = list(thirds(packed_ref))
    scores = [contract(by_side(queries), keys, 1, 1) for queries, keys, _ in parts]
    probs = [probabilities(now, valid).astype(jnp.bfloat16) for now in scores]
    for pair in range(PAIRS_OF_HEADS):
        mixed = contract(probs[pair], parts[pair][2], 1, 0)
        at = pair * 2 * HD
        context_ref[0, :, at : at + 2 * HD] = join_sides(mixed).astype(jnp.bfloat16)


def attention_back_kernel(mask_ref, packed_ref, grad_ref, out_ref):
    valid = mask_ref[0] > 0.0
    parts = list(thirds(packed_ref))
    queries = [by_side(part[0]) for part in parts]
    grads = [
        by_side(grad_ref[0, :, pair * 2 * HD : (pair + 1) * 2 * HD])
        for pair in range(PAIRS_OF_HEADS)
    ]
    scores = [contract(now, part[1], 1, 1) for now, part in zip(queries, parts)]
    d_probs = [contract(now, part[2], 1, 1) for now, part in zip(grads, parts)]
    probs = [probabilities(now, valid) for now in scores]
    d_scores = []
    for now, d_now in zip(probs, d_probs):
        shared = jnp.sum(d_now * now, axis=1, keepdims=True)
        d_scores.append(jnp.where(valid, now * (d_now - shared), 0.0).astype(jnp.bfloat16))
    for pair in range(PAIRS_OF_HEADS):
        d_queries = join_sides(contract(d_scores[pair], parts[pair][1], 1, 0)) * HD ** (-0.5)
        d_keys = contract(d_scores[pair], queries[pair], 0, 0) * HD ** (-0.5)
        d_values = contract(probs[pair].astype(jnp.bfloat16), grads[pair], 0, 0)
        for third, now in enumerate((d_queries, d_keys, d_values)):
            at = third * D + pair * 2 * HD
            out_ref[0, :, at : at + 2 * HD] = now.astype(jnp.bfloat16)


def attention_call(kernel, mask, operands, features, name):
    count = operands[0].shape[0]

    def spec(last):
        return pl.BlockSpec((1, SEQ, last), lambda i: (i, 0, 0))

    return pl.pallas_call(
        kernel,
        grid=(count,),
        out_shape=jax.ShapeDtypeStruct((count, SEQ, features), jnp.bfloat16),
        in_specs=[pl.BlockSpec((1, 1, SEQ), lambda i: (i, 0, 0))]
        + [spec(operand.shape[2]) for operand in operands],
        out_specs=spec(features),
        compiler_params=pltpu.CompilerParams(vmem_limit_bytes=32 * 1024 * 1024),
        cost_estimate=pl.CostEstimate(
            flops=10**9, bytes_accessed=count * SEQ * D * 10, transcendentals=10**6
        ),
        name=name,
    )(mask, *operands)


LAYER_ROWS = 8 + FF // D


def layer_vectors(rows):
    up = 5 + FF // D
    return [rows[i] for i in range(5)] + [rows[5:up].reshape(FF)] + [rows[up + i] for i in range(3)]


def layer_norm(values, gain, shift):
    center = values - jnp.mean(values, axis=-1, keepdims=True)
    spread = jnp.mean(center * center, axis=-1, keepdims=True)
    return center * lax.rsqrt(spread + NORM_EPS) * gain + shift


def embed_tokens(rows, vectors):
    return layer_norm(low_back(rows) + vectors[None, :SEQ], vectors[SEQ], vectors[SEQ + 1])


def norm_forward(values, gain, shift):
    center = values - jnp.mean(values, axis=-1, keepdims=True)
    inverse = lax.rsqrt(jnp.mean(center * center, axis=-1, keepdims=True) + NORM_EPS)
    normal = center * inverse
    return normal * gain + shift, normal, inverse


def norm_back(grad, normal, inverse, gain):
    scaled = grad * gain
    mean = jnp.mean(scaled, axis=-1, keepdims=True)
    along = jnp.mean(scaled * normal, axis=-1, keepdims=True)
    return (
        (scaled - mean - normal * along) * inverse,
        jnp.sum(grad * normal, axis=(0, 1)),
        jnp.sum(grad, axis=(0, 1)),
    )


GELU_SCALE = 0.7978845608028654


def gelu(value):
    bent = jnp.tanh(GELU_SCALE * (value + 0.044715 * value * value * value))
    return 0.5 * value * (1.0 + bent)


def gelu_slope(value):
    square = value * value
    bent = jnp.tanh(GELU_SCALE * (value + 0.044715 * square * value))
    inner = GELU_SCALE * (1.0 + 3.0 * 0.044715 * square)
    return 0.5 * (1.0 + bent) + 0.5 * value * (1.0 - bent * bent) * inner


def layer_forward(hidden, weights, vectors, mask):
    in_weights, out_weights, up_weights, down_weights = weights
    q_bias, v_bias, o_bias, gain_one, shift_one, up_bias, down_bias, gain_two, second_shift = (
        layer_vectors(vectors)
    )
    half = jnp.bfloat16
    entry = hidden.astype(half)
    bias = jnp.concatenate([q_bias, jnp.zeros_like(q_bias), v_bias])
    packed = (matmul(entry, in_weights) + bias).astype(half)
    context = attention_call(attention_kernel, mask, [packed], D, "attention")
    attended = matmul(context, out_weights) + o_bias
    first, normal_one, inverse_one = norm_forward(hidden + attended, gain_one, shift_one)
    middle = first.astype(half)
    upward = matmul(middle, up_weights) + up_bias
    active = gelu(upward).astype(half)
    downward = einsum_plain("nsf,df->nsd", active, down_weights) + down_bias
    output, normal_two, inverse_two = norm_forward(first + downward, gain_two, second_shift)
    kept = (
        entry, packed, context, middle, upward, active,
        normal_one, inverse_one, normal_two, inverse_two,
    )
    return output, kept


def layer_backward(kept, weights, vectors, mask, grad):
    in_weights, out_weights, up_weights, down_weights = weights
    entry, packed, context, middle, upward, active = kept[:6]
    normal_one, inverse_one, normal_two, inverse_two = kept[6:]
    gain_one, gain_two = layer_vectors(vectors)[3], layer_vectors(vectors)[7]
    half = jnp.bfloat16

    def total(value):
        return jnp.sum(value.astype(jnp.float32), axis=(0, 1))

    d_second, d_gain_two, d_shift_two = norm_back(grad, normal_two, inverse_two, gain_two)
    d_down = d_second.astype(half)
    d_active = jnp.einsum("nsd,df->nsf", d_down, down_weights, preferred_element_type=jnp.float32)
    d_active = d_active.astype(half).astype(jnp.float32)
    d_up = (d_active * gelu_slope(upward)).astype(half)
    d_first = d_second + jnp.einsum(
        "nsf,df->nsd", d_up, up_weights, preferred_element_type=jnp.float32
    )
    d_middle, d_gain_one, d_shift_one = norm_back(d_first, normal_one, inverse_one, gain_one)
    d_attended = d_middle.astype(half)
    d_context = jnp.einsum(
        "nsd,ed->nse", d_attended, out_weights, preferred_element_type=jnp.float32
    ).astype(half)
    d_packed = attention_call(
        attention_back_kernel, mask, [packed, d_context], 3 * D, "attention_back"
    )
    d_hidden = d_middle + jnp.einsum(
        "nsp,dp->nsd", d_packed, in_weights, preferred_element_type=jnp.float32
    )
    packed_total = total(d_packed)
    pieces = [
        packed_total[:D], packed_total[2 * D :], total(d_attended), d_gain_one, d_shift_one,
        total(d_up), total(d_down), d_gain_two, d_shift_two,
    ]
    d_vectors, at = jnp.zeros((LAYER_ROWS, D), jnp.float32), 0
    for piece in pieces:
        rows = piece.reshape(-1, D)
        d_vectors = d_vectors + jnp.pad(rows, ((at, LAYER_ROWS - at - rows.shape[0]), (0, 0)))
        at = at + rows.shape[0]
    flat = [
        (left.reshape(-1, left.shape[2]), right.reshape(-1, right.shape[2]))
        for left, right in (
            (entry, d_packed), (context, d_attended), (middle, d_up), (d_down, active)
        )
    ]
    return d_hidden, flat, d_vectors


def weight_gradient(left, right):
    return lax.dot_general(
        left, right, (((0,), (0,)), ((), ())), preferred_element_type=jnp.float32
    ).astype(jnp.bfloat16)


def pool_rows(hidden, key_mask, seq_lengths):
    share = key_mask.astype(jnp.float32) / seq_lengths.astype(jnp.float32)[:, None]
    return jnp.sum(hidden * share[:, :, None], axis=1)


def normalized_rows(rows):
    return rows * lax.rsqrt(jnp.sum(rows * rows, axis=-1, keepdims=True) + NORM_EPS)


def contrastive_terms(shallow_anchor, deep_anchor, shallow_pos, deep_pos, false_neg, pair_index):
    columns = lax.broadcasted_iota(jnp.int32, false_neg.shape, 1)
    hit = columns == pair_index[:, None]
    kept_cols = (false_neg == 0) | hit
    valid_rows = (pair_index >= 0).astype(jnp.float32)
    totals = jnp.zeros(pair_index.shape, jnp.float32)
    for current_width in (D, D * 2 // 3, D // 3, D // 6, D // 12):
        log_probs = []
        for anchor_vectors, positive_rows in (
            (shallow_anchor, shallow_pos),
            (deep_anchor, deep_pos),
        ):
            similarity_scores = (
                jnp.dot(
                    normalized_rows(anchor_vectors[:, :current_width]),
                    normalized_rows(positive_rows[:, :current_width]).T,
                    precision=lax.Precision.HIGHEST,
                )
                / SOFTMAX_TEMP
            )
            similarity_scores = jnp.where(kept_cols, similarity_scores, MASKED)
            log_probs.append(jax.nn.log_softmax(similarity_scores, axis=-1))
        for log_now in log_probs:
            totals = totals - jnp.sum(jnp.where(hit, log_now, 0.0), axis=-1)
        totals = totals + jnp.sum(jnp.exp(log_probs[1]) * (log_probs[1] - log_probs[0]), axis=-1)
    return jnp.sum(totals * valid_rows)


def adam_update(master, gradient, first, second, step_rate):
    first_new = BETA_ONE * first + (1.0 - BETA_ONE) * gradient
    second_new = BETA_TWO * second + (1.0 - BETA_TWO) * gradient * gradient
    first_hat = first_new / (1.0 - BETA_ONE**ADAM_STEP)
    second_hat = second_new / (1.0 - BETA_TWO**ADAM_STEP)
    master_new = master - step_rate * (
        first_hat / (jnp.sqrt(second_hat) + ADAM_EPS) + WEIGHT_DECAY * master
    )
    return (master_new, first_new, second_new)


def pad_rows(flat, multiple):
    rows = -(-flat.shape[0] // (128 * multiple)) * multiple
    return jnp.pad(flat, (0, rows * 128 - flat.shape[0])).reshape(rows, 128)


def one_hot(index, size, dtype=jnp.bfloat16):
    return (index[:, None] == lax.broadcasted_iota(jnp.int32, (1, size), 1)).astype(dtype)


def token_plan(ids, shard_rows):
    places = lax.broadcasted_iota(jnp.int32, ids.shape, 0)
    same = ids[:, None] == ids[None, :]
    leader = jnp.min(jnp.where(same, places[None, :], ids.shape[0]), axis=1)
    leads = leader == places
    owner = ids // shard_rows
    low_id = owner * shard_rows
    ahead = leads[None, :] & (ids[None, :] >= low_id[:, None]) & (ids[None, :] < ids[:, None])
    place = jnp.sum(ahead.astype(jnp.int32), axis=1)
    return owner, place, ids - low_id


def round_slots(owner, place, local_row, round_index, room, nz):
    inside = (place >= round_index * room) & (place < (round_index + 1) * room)
    slot = jnp.where(inside, owner * room + place - round_index * room, -1)
    slots = lax.broadcasted_iota(jnp.int32, (1, nz * room), 1)
    asked = jnp.max(jnp.where(slot[:, None] == slots, local_row[:, None], -1), axis=0)
    return slot, asked


def body(
    token_ids,
    lengths,
    false_neg,
    pair_index,
    word_table,
    vectors,
    attn_w,
    ffn_w,
    word_first,
    vector_first,
    attn_first,
    ffn_first,
    word_second,
    vector_second,
    attn_second,
    ffn_second,
):
    ndp = lax.axis_size("dp")
    nz = lax.axis_size("zero")
    n = ndp * nz
    by_hand = (ndp, nz) == (2, 16) and token_ids.shape[0] * ndp * nz <= 256
    my_dp = lax.axis_index("dp")
    my_zero = lax.axis_index("zero")
    me = my_dp * nz + my_zero
    pair_rows = token_ids.shape[0]
    total_pairs = pair_rows * n
    flat_ids = token_ids.reshape(-1, SEQ)
    seq_rows = flat_ids.shape[0]
    tokens = seq_rows * SEQ
    seq_lengths = lengths.reshape(-1)
    key_mask = lax.broadcasted_iota(jnp.int32, flat_ids.shape, 1) < seq_lengths[:, None]
    shard_rows = word_table.shape[0]
    vec_len = vectors.shape[0]

    room = -(-(tokens * 9 // 8) // (nz * 8)) * 8
    ids = flat_ids.reshape(-1)

    def packet_of(asked, rounds_here):
        last = jnp.concatenate([pair_index, rounds_here[None].astype(jnp.int32)])
        lines = nz + false_neg.size // 128
        return jnp.concatenate(
            [
                jnp.pad(asked.reshape(nz, room), ((0, 0), (0, 128 - room)), constant_values=-1),
                false_neg.reshape(-1, 128),
                jnp.zeros((7 - lines % 8, 128), jnp.int32),
                jnp.pad(last, (0, 128 - last.shape[0]))[None],
            ]
        )

    def gather_layer(layer_index):
        both = jnp.concatenate(
            [attn_w[layer_index].astype(jnp.bfloat16), ffn_w[layer_index].astype(jnp.bfloat16)],
            axis=1,
        )
        return lax.all_gather(both, "zero", axis=0, tiled=True)

    if by_hand:
        packet = pad_rows(jnp.concatenate([false_neg.reshape(-1), pair_index]), 8)
        place, slot, packets, asked_mine, vec_parts, received, *gathered = exchange_start(
            ids,
            packet.astype(jnp.bfloat16),
            pad_rows(vectors.astype(jnp.bfloat16), 16),
            attn_w,
            ffn_w,
            word_table,
            room,
            0,
        )
        layer_weights = [part.reshape(D, -1) for part in gathered]
        rounds = jnp.max(asked_mine[:, 0, 127])
        asked_mine = asked_mine[:, 0, :room]
        packets = packets.reshape(n, -1).astype(jnp.int32)
        false_all = packets[:, : false_neg.size].reshape(total_pairs, total_pairs)
        pair_all = packets[:, false_neg.size : false_neg.size + pair_rows].reshape(total_pairs)
        place, slot = place.reshape(-1), slot.reshape(-1)
    else:
        owner, place, local_row = token_plan(ids, shard_rows)
        slot, asked = round_slots(owner, place, local_row, 0, room, nz)
        packets, vec_parts = exchange(
            [
                packet_of(asked, jnp.max(place) // room + 1),
                pad_rows(vectors.astype(jnp.bfloat16), 16),
            ],
            ["all", "zero"],
            ndp,
            nz,
            0,
            "gather_requests",
        )
        layer_weights = [gather_layer(layer_index) for layer_index in range(LAYERS)]
        asked_mine = lax.dynamic_index_in_dim(packets[:, :nz, :room], my_zero, 1, keepdims=False)
        false_all = packets[:, nz : nz + false_neg.size // 128].reshape(total_pairs, total_pairs)
        pair_all = packets[:, -1, :pair_rows].reshape(total_pairs)
        rounds = jnp.max(packets[:, -1, pair_rows])
    vec_all = vec_parts.reshape(nz, -1)[:, :vec_len].reshape(-1).astype(jnp.float32)

    asked_near = lax.dynamic_slice_in_dim(asked_mine, my_dp * nz, nz, 0)

    def rows_for(wanted):
        picked = one_hot(wanted.reshape(-1), shard_rows)
        return matmul(picked, word_table.astype(jnp.bfloat16)).astype(jnp.bfloat16)

    def rows_from(slot_now, received):
        return matmul(one_hot(slot_now, nz * room), received.reshape(nz * room, D)).astype(
            jnp.bfloat16
        )

    if not by_hand:
        (received,) = exchange(
            [rows_for(asked_near).reshape(nz, room, D)], ["zero_p"], ndp, nz, 1, "send_rows"
        )
    rows = rows_from(slot, received)

    def round_of(round_index):
        owner = ids // shard_rows
        local_row = ids - owner * shard_rows
        return round_slots(owner, place, local_row, round_index, room, nz)

    def more_rows(state):
        round_index, rows_now = state
        slot_now, asked_now = round_of(round_index)
        wanted = lax.all_to_all(asked_now.reshape(nz, room), "zero", 0, 0, tiled=True)
        got = lax.all_to_all(rows_for(wanted).reshape(nz, room, D), "zero", 0, 0, tiled=True)
        return round_index + 1, rows_now + rows_from(slot_now, got)

    def further(step, value):
        return lax.cond(
            rounds > 1,
            lambda now: lax.while_loop(
                lambda state: state[0] < rounds, step, (jnp.int32(1), now)
            )[1],
            lambda now: now,
            value,
        )

    rows = further(more_rows, rows)
    rows = rows.reshape(seq_rows, SEQ, D).astype(jnp.float32)

    vec_rows = vec_all.reshape(-1, D)
    edges = [0] + [SEQ + 2 + i * LAYER_ROWS for i in range(LAYERS + 1)]
    vec_parts = [vec_rows[first:last] for first, last in zip(edges, edges[1:])]
    embedded, embed_back = jax.vjp(embed_tokens, rows, vec_parts[0])
    hidden = embedded
    mask = key_mask.astype(jnp.float32)[:, None, :]
    saved = []
    layer_parts = []
    pooled = []
    for layer_index in range(LAYERS):
        weights = layer_weights[layer_index]
        edges = (0, 3 * D, 4 * D, 4 * D + FF, 4 * D + 2 * FF)
        parts = [weights[:, first:last] for first, last in zip(edges, edges[1:])]
        layer_parts.append(parts)
        hidden, kept = layer_forward(hidden, parts, vec_parts[1 + layer_index], mask)
        saved.append(kept)
        pooled.append(pool_rows(hidden, key_mask, seq_lengths).astype(jnp.bfloat16))

    if by_hand and pair_rows == 4:
        block = jnp.stack(pooled).reshape(2, pair_rows, 2, D).transpose(0, 2, 1, 3)
        loss, pooled_grads = contrastive(block.reshape(2, 2 * pair_rows, D), false_all, pair_all, 2)
        pooled_grads = pooled_grads[:, :, :pair_rows]
    else:
        (pooled_all,) = exchange(
            [jnp.stack(pooled).reshape(-1, 128)], ["all"], ndp, nz, 2, "gather_pooled"
        )
        pooled_all = pooled_all.reshape(n, 2, pair_rows, 2, D).astype(jnp.float32)
        pooled_all = pooled_all.transpose(1, 3, 0, 2, 4).reshape(2, 2, total_pairs, D)

        def whole_loss(pooled_now):
            summed = contrastive_terms(
                pooled_now[0, 0],
                pooled_now[1, 0],
                pooled_now[0, 1],
                pooled_now[1, 1],
                false_all,
                pair_all,
            )
            valid_total = jnp.sum((pair_all >= 0).astype(jnp.float32))
            return summed / jnp.maximum(valid_total, 1.0)

        loss, pooled_grads = jax.value_and_grad(whole_loss)(pooled_all)
        pooled_grads = lax.dynamic_slice_in_dim(pooled_grads, me * pair_rows, pair_rows, 2)
    pooled_grads = pooled_grads.transpose(0, 2, 1, 3).reshape(2, seq_rows, D)
    shallow_back, deep_back = pooled_grads[0], pooled_grads[1]
    share = key_mask.astype(jnp.float32) / seq_lengths.astype(jnp.float32)[:, None]
    grad_hidden = jnp.zeros_like(embedded)
    weight_parts = []
    vec_grads = [None] * LAYERS
    for layer_index in range(LAYERS - 1, -1, -1):
        if layer_index == LAYERS - 1:
            grad_hidden = grad_hidden + deep_back[:, None, :] * share[:, :, None]
        if layer_index == 0:
            grad_hidden = grad_hidden + shallow_back[:, None, :] * share[:, :, None]
        grad_hidden, pairs, vec_grads[layer_index] = layer_backward(
            saved[layer_index],
            layer_parts[layer_index],
            vec_parts[1 + layer_index],
            mask,
            grad_hidden,
        )
        if by_hand and layer_index == 0:
            weight_parts.insert(0, pairs)
        else:
            both = jnp.concatenate([weight_gradient(*pair) for pair in pairs], axis=1)
            both, grad_hidden = lax.optimization_barrier((both, grad_hidden))
            weight_parts.insert(0, lax.psum_scatter(both, "zero", scatter_dimension=0, tiled=True))
    rows_grad, embed_grads = embed_back(grad_hidden)
    vec_grad = jnp.concatenate([embed_grads] + vec_grads, axis=0)
    down_local = jnp.stack([part[5 + FF // D] for part in vec_grads])

    rows_grad = rows_grad.reshape(tokens, D).astype(jnp.bfloat16)

    def slot_sums(slot_now):
        picked = one_hot(slot_now, nz * room)
        return lax.dot_general(
            picked, rows_grad, (((0,), (0,)), ((), ())), preferred_element_type=jnp.float32
        ).astype(jnp.bfloat16)

    def into_rows(wanted, sums):
        return lax.dot_general(
            one_hot(wanted.reshape(-1), shard_rows),
            sums.reshape(-1, D),
            (((0,), (0,)), ((), ())),
            preferred_element_type=jnp.float32,
        )

    down_each = down_local.reshape(LAYERS, nz, -1).transpose(1, 0, 2).reshape(nz, -1)
    down_len = down_each.shape[1]
    vec_blocks = jnp.concatenate([vec_grad.reshape(nz, vec_len), down_each], axis=1)
    lines = -(-vec_blocks.shape[1] // 1024) * 8
    vec_blocks = jnp.pad(vec_blocks, ((0, 0), (0, lines * 128 - vec_blocks.shape[1])))
    sums = slot_sums(slot).reshape(nz, room, D)

    def more_sums(state):
        round_index, grad_now = state
        slot_now, asked_now = round_of(round_index)
        wanted = lax.all_to_all(asked_now.reshape(nz, room), "zero", 0, 0, tiled=True)
        got = lax.all_to_all(slot_sums(slot_now).reshape(nz, room, D), "zero", 0, 0, tiled=True)
        wanted = lax.all_gather(wanted, "dp", axis=0, tiled=True)
        got = lax.all_gather(got, "dp", axis=0, tiled=True)
        return round_index + 1, grad_now + into_rows(wanted, got)

    if by_hand:
        extra = further(more_sums, jnp.zeros((shard_rows, D), jnp.float32))
        attn_shard, ffn_shard, word_grad, vec_sum, stats = exchange_gradients(
            weight_parts[0],
            vec_blocks.reshape(4, 2, 2, lines, 128),
            sums,
            weight_parts[1],
            asked_mine.reshape(ndp, nz * room, 1),
            extra,
            vec_len,
            3,
        )
        vec_sum = vec_sum.reshape(-1)
        grad_norm, factor = stats[0, 0], stats[1, 0]
    else:
        sums_all, vec_shares = exchange(
            [sums, vec_blocks.reshape(nz, lines, 128)],
            ["all_p", "all_p"],
            ndp,
            nz,
            3,
            "send_gradients",
        )
        vec_sum = jnp.sum(vec_shares.reshape(n, -1), axis=0)
        (weight_all,) = exchange([jnp.stack(weight_parts)], ["dp"], ndp, nz, 4, "sum_replicas")
        weight_sum = jnp.sum(weight_all.astype(jnp.float32), axis=0)
        attn_shard = weight_sum[:, :, : 4 * D]
        ffn_shard = weight_sum[:, :, 4 * D :]
        word_grad = further(more_sums, into_rows(asked_mine, sums_all))
    vec_shard = vec_sum[:vec_len]
    down_shard = vec_sum[vec_len : vec_len + down_len].reshape(LAYERS, -1)

    if not by_hand:
        square_local = jnp.sum(word_grad * word_grad) + jnp.sum(vec_shard * vec_shard)
        square_local = square_local + jnp.sum(attn_shard * attn_shard)
        square_local = square_local + jnp.sum(ffn_shard * ffn_shard)
        (squares,) = exchange(
            [jnp.broadcast_to(square_local, (8, 128))], ["zero"], ndp, nz, 5, "gather_squares"
        )
        grad_norm = jnp.sqrt(jnp.sum(squares[:, 0, 0]))
        factor = jnp.minimum(1.0, CLIP_NORM / (grad_norm + 1e-06))
    word_new, word_first_new, word_second_new = adam_update(
        word_table, word_grad * factor, word_first, word_second, LEARN_RATE
    )
    vector_new, vector_first_new, vector_second_new = adam_update(
        vectors, vec_shard * factor, vector_first, vector_second, VECTOR_RATE
    )
    attn_new, attn_first_new, attn_second_new = adam_update(
        attn_w, attn_shard * factor, attn_first, attn_second, LEARN_RATE
    )
    ffn_new, ffn_first_new, ffn_second_new = adam_update(
        ffn_w, ffn_shard * factor, ffn_first, ffn_second, LEARN_RATE
    )
    return (
        loss,
        grad_norm,
        word_new,
        vector_new,
        attn_new,
        ffn_new,
        word_new.astype(jnp.bfloat16),
        vector_new.astype(jnp.bfloat16),
        attn_new.astype(jnp.bfloat16),
        ffn_new.astype(jnp.bfloat16),
        word_first_new,
        vector_first_new,
        attn_first_new,
        ffn_first_new,
        word_second_new,
        vector_second_new,
        attn_second_new,
        ffn_second_new,
        down_shard * factor,
    )


def solution(mesh):
    placed = (
        P(("dp", "zero"), None, None),
        P(("dp", "zero"), None),
        P(("dp", "zero"), None),
        P(("dp", "zero")),
        P("zero", None),
        P("zero"),
        P(None, "zero", None),
        P(None, "zero", None),
        P("zero", None),
        P("zero"),
        P(None, "zero", None),
        P(None, "zero", None),
        P("zero", None),
        P("zero"),
        P(None, "zero", None),
        P(None, "zero", None),
    )
    return jax.shard_map(
        body,
        mesh=mesh,
        in_specs=placed,
        out_specs=(
            P(),
            P(),
            P("zero", None),
            P("zero"),
            P(None, "zero", None),
            P(None, "zero", None),
            P("zero", None),
            P("zero"),
            P(None, "zero", None),
            P(None, "zero", None),
            P("zero", None),
            P("zero"),
            P(None, "zero", None),
            P(None, "zero", None),
            P("zero", None),
            P("zero"),
            P(None, "zero", None),
            P(None, "zero", None),
            P(None, "zero"),
        ),
        check_vma=False,
    )
```

```python
import functools

import jax
import jax.numpy as jnp
from jax import lax
from jax.experimental import pallas as pl
from jax.experimental.pallas import tpu as pltpu
from jax.sharding import PartitionSpec as P

D = 512
HEADS = 8
HD = 64
FF = 2048
SEQ = 128
LAYERS = 2
ADAM_STEP = 5


SOFTMAX_TEMP = 0.05
CLIP_NORM = 1.0
LEARN_RATE = 0.02
VECTOR_RATE = 0.15
BETA_ONE = 0.5
BETA_TWO = 0.5
WEIGHT_DECAY = 0.01
ADAM_EPS = 1e-08
NORM_EPS = 1e-06
MASKED = -1000000000.0

MESH = pl.DeviceIdType.MESH


def build_low():

    def rounder(value):
        return lax.optimization_barrier(value.astype(jnp.bfloat16)).astype(jnp.float32)

    def keep_fwd(value):
        return (rounder(value), None)

    def pass_bwd(kept, grad):
        return (grad,)

    wrapped = jax.custom_vjp(rounder)
    wrapped.defvjp(keep_fwd, pass_bwd)
    return wrapped


def build_low_back():

    def identity_fn(value):
        return value

    def keep_fwd(value):
        return (value, None)

    def round_bwd(kept, grad):
        return (low(grad),)

    wrapped = jax.custom_vjp(identity_fn)
    wrapped.defvjp(keep_fwd, round_bwd)
    return wrapped


def low(value):
    return build_low()(value)


def low_back(value):
    return build_low_back()(value)


def rounded(value):
    return low(low_back(value))


def matmul(left, right):
    return jnp.dot(left, right, preferred_element_type=jnp.float32)


def einsum_plain(form, left, right):
    return jnp.einsum(form, left, right, preferred_element_type=jnp.float32)


def exchange_kernel(modes, ndp, nz, *refs):
    count = len(modes)
    ins = refs[:count]
    outs = refs[count : 2 * count]
    sems = refs[2 * count :]
    d = lax.axis_index("dp")
    z = lax.axis_index("zero")
    me = d * nz + z
    n = ndp * nz

    def peer_of(group, k):
        if group == "dp":
            pd = lax.rem(d + k, ndp)
            return pd, z, pd
        if group == "zero":
            pz = lax.rem(z + k, nz)
            return d, pz, pz
        p = lax.rem(me + k, n)
        return p // nz, lax.rem(p, nz), p

    groups = {m.split("_")[0] for m in modes}
    sizes = {"all": n, "zero": nz, "dp": ndp}
    mine = {"all": me, "zero": z, "dp": d}
    barrier = pltpu.get_barrier_semaphore()
    meet = ["all"] if "all" in groups else sorted(groups)
    total = 0
    for group in meet:
        total += sizes[group] - 1

        def greet(k, carry, group=group):
            pd, pz, _ = peer_of(group, k)
            pl.semaphore_signal(barrier, inc=1, device_id=(pd, pz), device_id_type=MESH)
            return carry

        lax.fori_loop(1, sizes[group], greet, 0)
    pl.semaphore_wait(barrier, total)

    def make(a, k):
        mode = modes[a]
        group = mode.split("_")[0]
        pd, pz, _ = peer_of(group, k)
        src = ins[a].at[pz] if mode.endswith("_p") else ins[a]
        return pltpu.make_async_remote_copy(
            src_ref=src,
            dst_ref=outs[a].at[mine[group]],
            send_sem=sems[2 * a].at[k],
            recv_sem=sems[2 * a + 1].at[k],
            device_id=(pd, pz),
            device_id_type=MESH,
        )

    for a, mode in enumerate(modes):
        group = mode.split("_")[0]

        def begin(k, carry, a=a):
            make(a, k).start()
            return carry

        lax.fori_loop(1, sizes[group], begin, 0)
    for a, mode in enumerate(modes):
        group = mode.split("_")[0]
        if mode.endswith("_p"):
            outs[a][mine[group]] = ins[a][z]
        else:
            outs[a][mine[group]] = ins[a][...]
    for a, mode in enumerate(modes):
        group = mode.split("_")[0]

        def finish(k, carry, a=a):
            make(a, k).wait()
            return carry

        lax.fori_loop(1, sizes[group], finish, 0)


def exchange(arrays, modes, ndp, nz, collective_id, name):
    sizes = {"all": ndp * nz, "zero": nz, "dp": ndp}
    outs = []
    scratch = []
    moved = 0
    for array, mode in zip(arrays, modes):
        size = sizes[mode.split("_")[0]]
        block = array.shape[1:] if mode.endswith("_p") else array.shape
        outs.append(jax.ShapeDtypeStruct((size,) + block, array.dtype))
        scratch += [pltpu.SemaphoreType.DMA((size,)), pltpu.SemaphoreType.DMA((size,))]
        one = array.dtype.itemsize
        for s in block:
            one *= s
        moved += one * size
    vmem = pl.BlockSpec(memory_space=pltpu.VMEM)
    return pl.pallas_call(
        functools.partial(exchange_kernel, tuple(modes), ndp, nz),
        out_shape=tuple(outs),
        in_specs=[vmem] * len(arrays),
        out_specs=tuple([vmem] * len(arrays)),
        scratch_shapes=scratch,
        compiler_params=pltpu.CompilerParams(
            collective_id=collective_id, has_side_effects=True, vmem_limit_bytes=48 * 1024 * 1024
        ),
        cost_estimate=pl.CostEstimate(flops=0, bytes_accessed=20 * moved, transcendentals=0),
        name=name,
    )(*arrays)


CHUNK = 1024
LAG_Z = 3
REST_EACH = 4


def gradient_kernel(chunks, matrices, vec_len, *refs):
    take = iter(refs)
    pairs = [(next(take), next(take)) for _ in range(matrices)]
    vec_ref, sums_ref, near_ref, asked_ref = [next(take) for _ in range(4)]
    attn_out, ffn_out, word_out, vec_out, stats_out = [next(take) for _ in range(5)]
    held = [None if m is None else next(take) for m, _, _ in chunks]
    bufs = [[next(take) for _ in range(5)] for _ in chunks]
    near_buf, rows_ref, sum_ref, square_ref, squares_ref = [next(take) for _ in range(5)]
    send_a, recv_a, send_y, recv_y, send_z, recv_z, send_x, recv_x = [next(take) for _ in range(8)]
    row_send, row_recv, pass_send, pass_recv, near_sem, square_sem = [
        next(take) for _ in range(6)
    ]

    d = lax.axis_index("dp")
    z = lax.axis_index("zero")
    core = lax.rem(z, 2)
    col = lax.rem(z // 2, 2)
    line = z // 4
    sibling = z + 1 - 2 * core
    across = z + 2 - 4 * col
    attn_width = attn_out.shape[2]

    def along(k):
        return lax.rem(line + k, 4) * 4 + lax.rem(z, 4)

    barrier = pltpu.get_barrier_semaphore()

    def greet(k, carry):
        pl.semaphore_signal(
            barrier, inc=1, device_id=(d, lax.rem(z + k, 16)), device_id_type=MESH
        )
        return carry

    lax.fori_loop(1, 16, greet, 0)
    pl.semaphore_signal(barrier, inc=1, device_id=(1 - d, z), device_id_type=MESH)
    pl.semaphore_wait(barrier, 16)

    def remote(src, dst, send, recv, to):
        return pltpu.make_async_remote_copy(
            src_ref=src,
            dst_ref=dst,
            send_sem=send,
            recv_sem=recv,
            device_id=to,
            device_id_type=MESH,
        )

    def part_of(i):
        return vec_ref if held[i] is None else held[i]

    def copy_a(i):
        src = part_of(i).at[:, :, 1 - core]
        return remote(src, bufs[i][0], send_a.at[i], recv_a.at[i], (d, sibling))

    def copy_y(i):
        src = bufs[i][0].at[:, 1 - col]
        return remote(src, bufs[i][1], send_y.at[i], recv_y.at[i], (d, across))

    def copy_z(i, k):
        src = bufs[i][1].at[lax.rem(line + k, 4)]
        return remote(
            src, bufs[i][2].at[k - 1], send_z.at[i, k - 1], recv_z.at[i, k - 1], (d, along(k))
        )

    def copy_x(i):
        return remote(bufs[i][3], bufs[i][4], send_x.at[i], recv_x.at[i], (1 - d, z))

    def row_push(k):
        to = lax.rem(z + k, 16)
        return remote(sums_ref.at[to], rows_ref.at[d, z], row_send.at[k], row_recv.at[k], (d, to))

    def row_pass(k):
        at = lax.rem(z + 16 - k, 16)
        return remote(
            rows_ref.at[d, at], rows_ref.at[d, at], pass_send.at[k], pass_recv.at[k], (1 - d, z)
        )

    near = remote(near_ref, near_buf, near_sem.at[0], near_sem.at[1], (1 - d, z))

    total = len(chunks)

    def push(k, carry):
        row_push(k).start()
        return carry

    lax.fori_loop(1, 16, push, 0)
    near.start()
    rows_ref[d, z] = sums_ref[z]
    row_pass(0).start()

    def compute(i):
        matrix, start, width = chunks[i]
        if matrix is not None:
            left, right = pairs[matrix]

            def rows_of(j, carry):
                at = pl.ds(pl.multiple_of(j * 128, 128), 128)
                found = lax.dot_general(
                    left[:, at],
                    right[:, start : start + width],
                    (((0,), (0,)), ((), ())),
                    preferred_element_type=jnp.float32,
                )
                held[i][j] = found.astype(jnp.bfloat16).reshape(2, 2, 32, width)
                return carry

            lax.fori_loop(0, 4, rows_of, 0)
        copy_a(i).start()

    def stage_a(i):
        copy_a(i).wait_recv()
        buf = bufs[i][0]

        def add_block(b, carry):
            line_at, col_at = b // 2, lax.rem(b, 2)
            mine = part_of(i)[line_at, col_at, core].astype(jnp.float32)
            got = buf[line_at, col_at].astype(jnp.float32)
            buf[line_at, col_at] = (mine + got).astype(buf.dtype)
            return carry

        lax.fori_loop(0, 8, add_block, 0)
        copy_y(i).start()

    def stage_y(i):
        copy_y(i).wait_recv()
        buf = bufs[i][1]

        def add_block(b, carry):
            mine = bufs[i][0][b, col].astype(jnp.float32)
            buf[b] = (mine + buf[b].astype(jnp.float32)).astype(buf.dtype)
            return carry

        lax.fori_loop(0, 4, add_block, 0)
        for k in range(1, 4):
            copy_z(i, k).start()

    def stage_z(i):
        for k in range(1, 4):
            copy_z(i, k).wait_recv()
        value = bufs[i][1][line].astype(jnp.float32)
        for k in range(3):
            value = value + bufs[i][2][k].astype(jnp.float32)
        bufs[i][3][...] = value.astype(bufs[i][3].dtype)
        copy_x(i).start()

    def stage_x(i):
        matrix, start, width = chunks[i]
        copy_x(i).wait_recv()
        value = bufs[i][3][...].astype(jnp.float32) + bufs[i][4][...].astype(jnp.float32)
        if matrix is None:
            vec_out[...] = value
        else:
            first = start + sum(pairs[m][1].shape[1] for m in range(matrix))
            if first < attn_width:
                attn_out[0, :, first : first + width] = value
            else:
                ffn_out[0, :, first - attn_width : first - attn_width + width] = value

    def pass_on(k):
        row_push(k).wait_recv()
        row_pass(k).start()

    shard_rows, features = word_out.shape
    tiles = -(-shard_rows // 128)
    spots = rows_ref.shape[1] * rows_ref.shape[2]
    sum_ref[...] = jnp.zeros_like(sum_ref)

    def into_rows(plane, first, count):
        row = lax.broadcasted_iota(jnp.int32, (128, 1), 0) + first
        picked = (asked_ref[plane] == row).astype(jnp.bfloat16)
        return jnp.dot(
            picked, rows_ref[plane].reshape(spots, features), preferred_element_type=jnp.float32
        )[:count]

    def own_rows(tile):
        first, count = tile * 128, min(128, shard_rows - tile * 128)
        word_out[first : first + count, :] = into_rows(d, first, count)

    def all_arrived():
        def arrived(k, carry):
            ref = rows_ref.at[1 - d, lax.rem(z + 16 - k, 16)]
            remote(ref, ref, pass_send.at[k], pass_recv.at[k], (1 - d, z)).wait_recv()
            return carry

        lax.fori_loop(0, 16, arrived, 0)

    def other_rows(tile):
        first, count = tile * 128, min(128, shard_rows - tile * 128)
        value = word_out[first : first + count, :] + into_rows(1 - d, first, count)
        word_out[first : first + count, :] = value
        sum_ref[...] = sum_ref[...] + jnp.sum(value * value, axis=0, keepdims=True)

    rest = [functools.partial(own_rows, tile) for tile in range(tiles)]
    rest += [all_arrived] + [functools.partial(other_rows, tile) for tile in range(tiles)]

    compute(0)
    passed = 1
    for t in range(total + LAG_Z + 2):
        if t + 1 < total:
            compute(t + 1)
        if t < total:
            stage_a(t)
        if 0 <= t - 1 < total:
            stage_y(t - 1)
        if 0 <= t - 1 - LAG_Z < total:
            stage_z(t - 1 - LAG_Z)
        if 0 <= t - 2 - LAG_Z < total:
            stage_x(t - 2 - LAG_Z)
        until = min(16, 1 + (t + 1) * 15 // (total - 2))
        for k in range(passed, until):
            pass_on(k)
        passed = until
        if t >= total - 2:
            for _ in range(min(len(rest), REST_EACH)):
                rest.pop(0)()
    while rest:
        rest.pop(0)()

    near.wait()
    attn_out[1] = near_ref[:, :attn_width].astype(jnp.float32) + near_buf[:, :attn_width].astype(
        jnp.float32
    )
    ffn_out[1] = near_ref[:, attn_width:].astype(jnp.float32) + near_buf[:, attn_width:].astype(
        jnp.float32
    )
    squares = sum_ref[...]
    square = jnp.sum(squares, axis=1, keepdims=True)
    for out in (attn_out, ffn_out):

        def of_rows(r, carry, out=out):
            at = pl.ds(pl.multiple_of(r * 8, 8), 8)
            for layer in range(out.shape[0]):
                value = out[layer, at, :]
                carry = carry + jnp.sum(value * value, axis=0, keepdims=True)
            return carry

        found = lax.fori_loop(
            0, out.shape[1] // 8, of_rows, jnp.zeros((1, out.shape[2]), jnp.float32)
        )
        square = square + jnp.sum(found, axis=1, keepdims=True)
    place = lax.broadcasted_iota(jnp.int32, vec_out.shape, 0) * 128 + lax.broadcasted_iota(
        jnp.int32, vec_out.shape, 1
    )
    value = jnp.where(place < vec_len, vec_out[...], 0.0)
    found = jnp.sum(value * value, axis=0, keepdims=True)
    square = square + jnp.sum(found, axis=1, keepdims=True)
    square_ref[...] = jnp.broadcast_to(square, square_ref.shape)

    def square_copy(k, slot):
        return remote(
            square_ref,
            squares_ref.at[slot],
            square_sem.at[0, k],
            square_sem.at[1, k],
            (d, lax.rem(z + k, 16)),
        )

    def send_square(k, carry):
        square_copy(k, z).start()
        return carry

    lax.fori_loop(1, 16, send_square, 0)
    squares_ref[z] = square_ref[...]

    for i in range(total):
        copy_a(i).wait_send()
        copy_y(i).wait_send()
        for k in range(1, 4):
            copy_z(i, k).wait_send()
        copy_x(i).wait_send()

    def finish(k, carry):
        row_push(k).wait_send()
        square_copy(k, lax.rem(z + 16 - k, 16)).wait_recv()
        square_copy(k, z).wait_send()
        return carry

    lax.fori_loop(1, 16, finish, 0)

    def finish_pass(k, carry):
        row_pass(k).wait_send()
        return carry

    lax.fori_loop(0, 16, finish_pass, 0)
    norm = squares_ref[0]
    for slot in range(1, 16):
        norm = norm + squares_ref[slot]
    stats_out[...] = jnp.broadcast_to(norm, stats_out.shape)


def exchange_gradients(pairs, vec_parts, sums, near, asked, shard_rows, vec_len, collective_id):
    chunks = [(None, 0, 128)]
    for index in (3, 2, 0, 1):
        columns = pairs[index][1].shape[1]
        width = columns // -(-columns // CHUNK)
        for start in range(0, columns, width):
            chunks.append((index, start, width))
    half = jnp.bfloat16
    held, bufs = [], []
    for index, start, width in chunks:
        kind = vec_parts.dtype if index is None else half
        r = vec_parts.shape[3] if index is None else 32
        if index is not None:
            held.append(pltpu.VMEM((4, 2, 2, r, width), kind))
        bufs += [
            pltpu.VMEM((4, 2, r, width), kind),
            pltpu.VMEM((4, r, width), kind),
            pltpu.VMEM((3, r, width), kind),
            pltpu.VMEM((r, width), kind),
            pltpu.VMEM((r, width), kind),
        ]
    features = sums.shape[2]
    dma = pltpu.SemaphoreType.DMA
    count = len(chunks)
    scratch = held + bufs
    scratch += [
        pltpu.VMEM(near.shape, half),
        pltpu.VMEM((2,) + sums.shape, half),
        pltpu.VMEM((1, features), jnp.float32),
        pltpu.VMEM((1, 128), jnp.float32),
        pltpu.VMEM((16, 1, 128), jnp.float32),
    ]
    scratch += [dma((count,)) for _ in range(4)] + [dma((count, 3)) for _ in range(2)]
    scratch += [dma((count,)) for _ in range(2)]
    scratch += [dma((16,)) for _ in range(4)] + [dma((2,)), dma((2, 16))]
    rows = near.shape[0]
    outs = [
        jax.ShapeDtypeStruct((2, rows, 4 * D), jnp.float32),
        jax.ShapeDtypeStruct((2, rows, 2 * FF), jnp.float32),
        jax.ShapeDtypeStruct((shard_rows, features), jnp.float32),
        jax.ShapeDtypeStruct(vec_parts.shape[3:], jnp.float32),
        jax.ShapeDtypeStruct((8, 128), jnp.float32),
    ]
    vmem = pl.BlockSpec(memory_space=pltpu.VMEM)
    return pl.pallas_call(
        functools.partial(gradient_kernel, tuple(chunks), len(pairs), vec_len),
        out_shape=tuple(outs),
        in_specs=[vmem] * (2 * len(pairs) + 4),
        out_specs=tuple([vmem] * len(outs)),
        scratch_shapes=scratch,
        compiler_params=pltpu.CompilerParams(
            collective_id=collective_id, has_side_effects=True, vmem_limit_bytes=58 * 1024 * 1024
        ),
        cost_estimate=pl.CostEstimate(flops=0, bytes_accessed=200_000_000, transcendentals=0),
        name="exchange_gradients",
    )(*[array for pair in pairs for array in pair], vec_parts, sums, near, asked)


SPLITS = 4
WINDOW = 3
LAG = 3


def start_kernel(shard_rows, room, *refs):
    column_ref, row_ref, packet_ref, vec_ref, attn_ref, ffn_ref, word_ref = refs[:7]
    place_out, slot_out, packet_out, asked_out, vec_out, rows_out, *weight_outs = refs[7:15]
    table, rows_held, asked, slots, locals_ = refs[15:20]
    packet_sem, asked_sem, vec_sem, row_sem = refs[20:24]
    z_sem, y_sem, x_sem, d_sem, e_sem, own_sem = refs[24:]

    d = lax.axis_index("dp")
    z = lax.axis_index("zero")
    me = d * 16 + z
    core = lax.rem(z, 2)
    col = lax.rem(z // 2, 2)
    line = z // 4
    sibling = z + 1 - 2 * core
    across = z + 2 - 4 * col
    layers = attn_ref.shape[0]
    width = attn_ref.shape[2]
    whole = 3 * width
    unit = whole // 128 // SPLITS
    hand = unit * 5 // 12
    total = layers * SPLITS

    def everyone(k):
        p = lax.rem(me + k, 32)
        return (p // 16, lax.rem(p, 16))

    barrier = pltpu.get_barrier_semaphore()

    def greet(k, carry):
        pl.semaphore_signal(barrier, inc=1, device_id=everyone(k), device_id_type=MESH)
        return carry

    lax.fori_loop(1, 32, greet, 0)
    for layer in range(layers):
        weight_outs[layer][z, :, 0:width] = attn_ref[layer].astype(jnp.bfloat16)
        weight_outs[layer][z, :, width:whole] = ffn_ref[layer].astype(jnp.bfloat16)
    pl.semaphore_wait(barrier, 31)

    def remote(src, dst, sems, at, to):
        return pltpu.make_async_remote_copy(
            src_ref=src,
            dst_ref=dst,
            send_sem=sems.at[(0,) + at],
            recv_sem=sems.at[(1,) + at],
            device_id=to,
            device_id_type=MESH,
        )

    def packet_copy(k, slot):
        return remote(packet_ref, packet_out.at[slot], packet_sem, (k,), everyone(k))

    def asked_copy(k, slot):
        to = everyone(k)
        return remote(asked.at[to[1]], asked_out.at[slot], asked_sem, (k,), to)

    def vec_copy(k, slot):
        return remote(vec_ref, vec_out.at[slot], vec_sem, (k,), (d, lax.rem(z + k, 16)))

    def row_copy(k, slot):
        to = lax.rem(z + k, 16)
        return remote(rows_held.at[to], rows_out.at[slot], row_sem, (k,), (d, to))

    def shard(i):
        at = lax.rem(line + i % 4, 4) * 4 + lax.rem(z, 4)
        return at if i < 4 else at + 2 - 4 * col

    def piece(s):
        layer, p = s // SPLITS, s % SPLITS
        size = unit if p < SPLITS - 1 else whole // 128 - p * unit
        return layer, p * unit, size

    def columns_of(at, s, first, size):
        layer, base, _ = piece(s)
        return weight_outs[layer].at[
            at, :, pl.ds(pl.multiple_of((base + first) * 128, 128), size * 128)
        ]

    def stretch(at, s, ours):
        size = piece(s)[2]
        return columns_of(at, s, ours * hand, size - hand)

    def handed(at, s, ours):
        size = piece(s)[2]
        return columns_of(at, s, ours * (size - hand), hand)

    def both(ref, sems, at, to):
        return remote(ref, ref, sems, at, to)

    def z_copy(s, k, at):
        to = lax.rem(line + k, 4) * 4 + lax.rem(z, 4)
        return both(stretch(at, s, d), z_sem, (s, k - 1), (d, to))

    def y_copy(s, j, at):
        return both(stretch(at, s, d), y_sem, (s, j), (d, across))

    def x_copy(s, i, at, ours):
        return both(handed(at, s, ours), x_sem, (s, i), (1 - d, z))

    def d_copy(s, i, at):
        return both(stretch(at, s, d), d_sem, (s, i), (d, sibling))

    def e_copy(s, i, at):
        return both(handed(at, s, 1 - d), e_sem, (s, i), (d, sibling))

    def own_copy(layer, at):
        ref = weight_outs[layer].at[at]
        return both(ref, own_sem, (layer,), (d, sibling))

    def spread(s, i):
        at = shard(i)
        if i < 4:
            y_copy(s, i, at).start()
        if i > 0:
            x_copy(s, i, at, d).start()
            d_copy(s, i, at).start()

    def open_piece(s):
        for k in range(1, 4):
            z_copy(s, k, z).start()
        spread(s, 0)

    for s in range(WINDOW):
        open_piece(s)

    tokens = column_ref.shape[0]
    ids_row = row_ref[...]
    lane = lax.broadcasted_iota(jnp.int32, (1, tokens), 1).astype(jnp.float32)
    block = 128

    def lead_of(b, least):
        ids = column_ref[pl.ds(pl.multiple_of(b * block, block), block), :]
        there = lax.broadcasted_iota(jnp.int32, (block, 1), 0) + b * block
        found = jnp.where(ids == ids_row, there.astype(jnp.float32), 1e9)
        return jnp.minimum(least, jnp.min(found, axis=0, keepdims=True))

    least = lax.fori_loop(0, tokens // block, lead_of, jnp.full((1, tokens), 1e9, jnp.float32))
    lead_ids = jnp.where(least == lane, ids_row, -1)

    def place_of(b, most):
        at = pl.ds(pl.multiple_of(b * block, block), block)
        ids = column_ref[at, :]
        owner = jnp.zeros_like(ids)
        for o in range(1, 16):
            owner = owner + (ids >= o * shard_rows).astype(jnp.int32)
        low_id = owner * shard_rows
        ahead = (lead_ids >= low_id) & (lead_ids < ids)
        place = jnp.sum(jnp.where(ahead, 1.0, 0.0), axis=1, keepdims=True)
        place_out[at, :] = place.astype(jnp.int32)
        inside = place < room
        slots[at, :] = jnp.where(inside, owner * 128 + place.astype(jnp.int32), -1)
        slot_out[at, :] = jnp.where(inside, owner * room + place.astype(jnp.int32), -1)
        locals_[at, :] = (ids - low_id).astype(jnp.float32)
        return jnp.maximum(most, jnp.max(place, axis=0, keepdims=True))

    most = lax.fori_loop(0, tokens // block, place_of, jnp.zeros((1, 1), jnp.float32))
    rounds = jnp.ones((1, 1), jnp.float32)
    for r in range(1, -(-tokens // room)):
        rounds = rounds + (most >= r * room).astype(jnp.float32)
    lane128 = lax.broadcasted_iota(jnp.int32, (1, 128), 1)

    for o in range(16):

        def asked_of(b, best, o=o):
            at = pl.ds(pl.multiple_of(b * block, block), block)
            found = jnp.where(slots[at, :] == o * 128 + lane128, locals_[at, :], -1.0)
            return jnp.maximum(best, jnp.max(found, axis=0, keepdims=True))

        best = lax.fori_loop(0, tokens // block, asked_of, jnp.full((1, 128), -1.0, jnp.float32))
        asked[o] = jnp.where(lane128 == 127, rounds, best).astype(jnp.int32)

    def send_packets(k, carry):
        asked_copy(k, me).start()
        packet_copy(k, me).start()
        return carry

    lax.fori_loop(1, 32, send_packets, 0)

    def send_vec(k, carry):
        vec_copy(k, z).start()
        return carry

    lax.fori_loop(1, 16, send_vec, 0)
    for layer in range(layers):
        own_copy(layer, z).start()
    vec_out[z] = vec_ref[...]
    asked_out[me] = asked[z]
    packet_out[me] = packet_ref[...]

    body_rows = shard_rows // 16 * 16
    step = 112 if body_rows % 112 == 0 else 16

    def to_half(i, carry):
        at = pl.multiple_of(i * step, 16)
        table[pl.ds(at, step), :] = word_ref[pl.ds(at, step), :].astype(jnp.bfloat16)
        return carry

    lax.fori_loop(0, body_rows // step, to_half, 0)
    padded = table.shape[0]
    table[body_rows:padded, :] = jnp.zeros((padded - body_rows, table.shape[1]), jnp.bfloat16)
    if shard_rows > body_rows:
        table[body_rows:shard_rows, :] = word_ref[body_rows:shard_rows, :].astype(jnp.bfloat16)

    def answer_one(k, carry):
        src = lax.rem(z + k, 16)
        rows_at = lax.broadcasted_iota(jnp.int32, (padded, 128), 0)
        picked = (rows_at == asked_out[d * 16 + src]).astype(jnp.bfloat16)
        found = lax.dot_general(
            picked, table[...], (((0,), (0,)), ((), ())), preferred_element_type=jnp.float32
        )
        rows_held[src] = found[:room, :].astype(jnp.bfloat16)
        return carry

    def packet_in(k, carry):
        asked_copy(k, lax.rem(me + 32 - k, 32)).wait_recv()
        return carry

    def row_start(k, carry):
        row_copy(k, z).start()
        return carry

    def z_phase(s):
        for k in range(1, 4):
            z_copy(s, k, shard(4 - k)).wait_recv()
            spread(s, 4 - k)
        if s + WINDOW < total:
            open_piece(s + WINDOW)

    def y_phase(s):
        for j in range(4):
            y_copy(s, j, shard(4 + j)).wait_recv()
            spread(s, 4 + j)

    def x_phase(s):
        for i in range(1, 8):
            at = shard(i)
            x_copy(s, i, at, 1 - d).wait_recv()
            e_copy(s, i, at).start()

    done = 0
    for t in range(total + LAG):
        if t < total:
            z_phase(t)
        if t == 1:
            lax.fori_loop(1, 32, packet_in, 0)
        if t >= 1:
            until = min(16, done + 4)
            if until > done:
                lax.fori_loop(done, until, answer_one, 0)
            done = until
        if t == total - 1:
            lax.fori_loop(1, 16, row_start, 0)
            rows_out[z] = rows_held[z]
        if 0 <= t - 1 < total:
            y_phase(t - 1)
        if 0 <= t - LAG < total:
            x_phase(t - LAG)

    turn = 1 - 2 * core
    for layer in range(layers):
        own_copy(layer, z + turn).wait_recv()
        own_copy(layer, z).wait_send()
    for s in range(total):
        for i in range(1, 8):
            at = shard(i)
            d_copy(s, i, at + turn).wait_recv()
            d_copy(s, i, at).wait_send()
            e_copy(s, i, at + turn).wait_recv()
            e_copy(s, i, at).wait_send()
            x_copy(s, i, at, d).wait_send()
        for k in range(1, 4):
            z_copy(s, k, z).wait_send()
        for i in range(4):
            y_copy(s, i, shard(i)).wait_send()

    def finish(k, carry):
        back = lax.rem(z + 16 - k, 16)
        row_copy(k, back).wait_recv()
        row_copy(k, z).wait_send()
        vec_copy(k, back).wait_recv()
        vec_copy(k, z).wait_send()
        return carry

    lax.fori_loop(1, 16, finish, 0)

    def finish_packets(k, carry):
        packet_copy(k, lax.rem(me + 32 - k, 32)).wait_recv()
        packet_copy(k, me).wait_send()
        asked_copy(k, me).wait_send()
        return carry

    lax.fori_loop(1, 32, finish_packets, 0)


def exchange_start(ids, packet, vec_rows, attn, ffn, word_table, room, collective_id):
    half = jnp.bfloat16
    shard_rows, features = word_table.shape
    padded = -(-shard_rows // 128) * 128
    layers, rows, width = attn.shape
    tokens = ids.shape[0]
    pieces = layers * SPLITS
    dma = pltpu.SemaphoreType.DMA
    vmem = pl.BlockSpec(memory_space=pltpu.VMEM)
    return pl.pallas_call(
        functools.partial(start_kernel, shard_rows, room),
        out_shape=(
            jax.ShapeDtypeStruct((tokens, 1), jnp.int32),
            jax.ShapeDtypeStruct((tokens, 1), jnp.int32),
            jax.ShapeDtypeStruct((32,) + packet.shape, packet.dtype),
            jax.ShapeDtypeStruct((32, 1, 128), jnp.int32),
            jax.ShapeDtypeStruct((16,) + vec_rows.shape, vec_rows.dtype),
            jax.ShapeDtypeStruct((16, room, features), half),
        )
        + (jax.ShapeDtypeStruct((16, rows, 3 * width), half),) * layers,
        in_specs=[vmem] * 7,
        out_specs=tuple([vmem] * (6 + layers)),
        scratch_shapes=[
            pltpu.VMEM((padded, features), half),
            pltpu.VMEM((16, room, features), half),
            pltpu.VMEM((16, 1, 128), jnp.int32),
            pltpu.VMEM((tokens, 1), jnp.int32),
            pltpu.VMEM((tokens, 1), jnp.float32),
            dma((2, 32)),
            dma((2, 32)),
            dma((2, 16)),
            dma((2, 16)),
            dma((2, pieces, 3)),
            dma((2, pieces, 4)),
            dma((2, pieces, 8)),
            dma((2, pieces, 8)),
            dma((2, pieces, 8)),
            dma((2, layers)),
        ],
        compiler_params=pltpu.CompilerParams(
            collective_id=collective_id, has_side_effects=True, vmem_limit_bytes=48 * 1024 * 1024
        ),
        cost_estimate=pl.CostEstimate(flops=0, bytes_accessed=150_000_000, transcendentals=0),
        name="exchange_start",
    )(ids.reshape(-1, 1), ids.reshape(1, -1), packet, vec_rows, attn, ffn, word_table)


WIDTHS = (D, D * 2 // 3, D // 3, D // 6, D // 12)


def gather_rows(block_ref, all_ref, z_sem, near_sem):
    d = lax.axis_index("dp")
    z = lax.axis_index("zero")
    line, spot = z // 4, lax.rem(z, 4)

    def at_line(k):
        return lax.rem(line + k, 4) * 4 + spot

    def near_by(j):
        across = j // 4
        return lax.rem(d + across, 2), line * 4 + lax.rem(spot + j % 4, 4)

    barrier = pltpu.get_barrier_semaphore()
    for k in range(1, 4):
        pl.semaphore_signal(barrier, inc=1, device_id=(d, at_line(k)), device_id_type=MESH)
    for j in range(1, 8):
        pl.semaphore_signal(barrier, inc=1, device_id=near_by(j), device_id_type=MESH)
    pl.semaphore_wait(barrier, 10)

    def z_copy(k):
        return pltpu.make_async_remote_copy(
            src_ref=block_ref,
            dst_ref=all_ref.at[d * 16 + z],
            send_sem=z_sem.at[0, k],
            recv_sem=z_sem.at[1, k],
            device_id=(d, at_line(k)),
            device_id_type=MESH,
        )

    def z_arrival(k):
        ref = all_ref.at[d * 16 + at_line(4 - k)]
        return pltpu.make_async_remote_copy(
            src_ref=ref,
            dst_ref=ref,
            send_sem=z_sem.at[0, k],
            recv_sem=z_sem.at[1, k],
            device_id=(d, at_line(k)),
            device_id_type=MESH,
        )

    def near_copy(i, j, from_d, from_z):
        ref = all_ref.at[from_d * 16 + from_z]
        return pltpu.make_async_remote_copy(
            src_ref=ref,
            dst_ref=ref,
            send_sem=near_sem.at[0, i, j],
            recv_sem=near_sem.at[1, i, j],
            device_id=near_by(j),
            device_id_type=MESH,
        )

    for k in range(1, 4):
        z_copy(k).start()
    all_ref[d * 16 + z] = block_ref[...]
    for j in range(1, 8):
        near_copy(0, j, d, z).start()
    for k in range(1, 4):
        z_arrival(k).wait_recv()
        for j in range(1, 8):
            near_copy(4 - k, j, d, at_line(4 - k)).start()
    for i in range(4):
        for j in range(1, 8):
            back = lax.rem(line + i, 4) * 4 + lax.rem(spot + 4 - j % 4, 4)
            near_copy(i, j, lax.rem(d + j // 4, 2), back).wait_recv()
            near_copy(i, j, d, at_line(i)).wait_send()
    for k in range(1, 4):
        z_copy(k).wait_send()


def contrastive_kernel(
    block_ref, false_ref, pair_ref, loss_ref, own_ref, all_ref, pooled_ref, grad_ref, z_sem, near_sem
):
    me = lax.axis_index("dp") * 16 + lax.axis_index("zero")
    gather_rows(block_ref, all_ref, z_sem, near_sem)
    upper = lax.broadcasted_iota(jnp.int32, (8, 1), 0) < 4
    for kind in range(2):
        for two in range(all_ref.shape[0] // 2):
            even = all_ref[2 * two, kind].astype(jnp.float32)
            odd = all_ref[2 * two + 1, kind].astype(jnp.float32)
            at = slice(8 * two, 8 * two + 8)
            pooled_ref[kind, 0, at, :] = jnp.where(upper, even, pltpu.roll(odd, 4, 0))
            pooled_ref[kind, 1, at, :] = jnp.where(upper, pltpu.roll(even, 4, 0), odd)
    contrastive_math(pooled_ref, false_ref, pair_ref, loss_ref, grad_ref)
    first = pl.multiple_of(me // 2 * 8, 8)
    swap = lax.rem(me, 2) == 1
    for kind in range(2):
        for role in range(2):
            rows = grad_ref[kind, role, pl.ds(first, 8), :]
            own_ref[kind, role] = jnp.where(swap, pltpu.roll(rows, 4, 0), rows)


def contrastive_math(pooled_ref, false_ref, pair_ref, loss_ref, grad_ref):
    pairs = false_ref.shape[0]
    high = lax.Precision.HIGHEST
    columns = lax.broadcasted_iota(jnp.int32, (pairs, pairs), 1)
    hit = columns == pair_ref[...]
    kept = (false_ref[...] == 0) | hit
    hits = hit.astype(jnp.float32)
    valid = (pair_ref[...] >= 0).astype(jnp.float32)
    inverse = 1.0 / jnp.maximum(jnp.sum(valid, axis=0, keepdims=True), 1.0)
    weight = valid * inverse
    named = jnp.sum(hits, axis=1, keepdims=True)
    totals = jnp.zeros((pairs, 1), jnp.float32)
    for first, width in enumerate(WIDTHS):
        span = -(-width // 128) * 128
        inside = lax.broadcasted_iota(jnp.int32, (1, span), 1) < width
        units, scales, logs = [], [], []
        for kind in range(2):
            pair_units, pair_scales = [], []
            for role in range(2):
                rows = jnp.where(inside, pooled_ref[kind, role, :, 0:span], 0.0)
                scale = lax.rsqrt(jnp.sum(rows * rows, axis=1, keepdims=True) + NORM_EPS)
                pair_units.append(rows * scale)
                pair_scales.append(scale)
            sims = lax.dot_general(
                pair_units[0],
                pair_units[1],
                (((1,), (1,)), ((), ())),
                precision=high,
                preferred_element_type=jnp.float32,
            )
            sims = jnp.where(kept, sims / SOFTMAX_TEMP, MASKED)
            shifted = sims - jnp.max(sims, axis=1, keepdims=True)
            logs.append(shifted - jnp.log(jnp.sum(jnp.exp(shifted), axis=1, keepdims=True)))
            units.append(pair_units)
            scales.append(pair_scales)
        shallow, deep = logs
        p_shallow, p_deep = jnp.exp(shallow), jnp.exp(deep)
        gap = p_deep * (deep - shallow)
        spread = jnp.sum(gap, axis=1, keepdims=True)
        totals = totals + spread - jnp.sum(jnp.where(hit, shallow + deep, 0.0), axis=1, keepdims=True)
        d_sims = (
            p_shallow * (named + 1.0) - hits - p_deep,
            gap + p_deep * (named - spread) - hits,
        )
        for kind in range(2):
            d_cos = jnp.where(kept, d_sims[kind] * weight, 0.0) / SOFTMAX_TEMP
            for role in range(2):
                unit = units[kind][role]
                d_unit = lax.dot_general(
                    d_cos,
                    units[kind][1 - role],
                    (((1 - role,), (0,)), ((), ())),
                    precision=high,
                    preferred_element_type=jnp.float32,
                )
                along = jnp.sum(d_unit * unit, axis=1, keepdims=True)
                d_rows = scales[kind][role] * (d_unit - unit * along)
                if first == 0:
                    grad_ref[kind, role] = d_rows
                else:
                    grad_ref[kind, role, :, 0:span] = grad_ref[kind, role, :, 0:span] + d_rows
    loss_ref[...] = jnp.broadcast_to(
        jnp.sum(totals * valid, axis=0, keepdims=True) * inverse, loss_ref.shape
    )


def contrastive(block, false_all, pair_all, collective_id):
    vmem = pl.BlockSpec(memory_space=pltpu.VMEM)
    pairs = false_all.shape[0]
    dma = pltpu.SemaphoreType.DMA
    whole = pltpu.VMEM((2, 2, pairs, D), jnp.float32)
    loss, grads = pl.pallas_call(
        contrastive_kernel,
        out_shape=(
            jax.ShapeDtypeStruct((8, 128), jnp.float32),
            jax.ShapeDtypeStruct((2, 2, 8, D), jnp.float32),
        ),
        in_specs=[vmem] * 3,
        out_specs=(vmem, vmem),
        scratch_shapes=[
            pltpu.VMEM((32,) + block.shape, block.dtype),
            whole,
            whole,
            dma((2, 4)),
            dma((2, 4, 8)),
        ],
        compiler_params=pltpu.CompilerParams(
            collective_id=collective_id, has_side_effects=True, vmem_limit_bytes=32 * 1024 * 1024
        ),
        cost_estimate=pl.CostEstimate(flops=10**9, bytes_accessed=3_000_000, transcendentals=10**6),
        name="contrastive",
    )(block, false_all, pair_all.reshape(-1, 1))
    return loss[0, 0], grads


PAIRS_OF_HEADS = HEADS // 2


def by_side(rows):
    lane = lax.broadcasted_iota(jnp.int32, (1, 2 * HD), 1)
    zero = jnp.zeros_like(rows)
    return jnp.concatenate([jnp.where(lane < HD, rows, zero), jnp.where(lane < HD, zero, rows)])


def join_sides(stacked):
    lane = lax.broadcasted_iota(jnp.int32, (1, 2 * HD), 1)
    return jnp.where(lane < HD, stacked[:SEQ], stacked[SEQ:])


def contract(left, right, left_dim, right_dim):
    return lax.dot_general(
        left, right, (((left_dim,), (right_dim,)), ((), ())), preferred_element_type=jnp.float32
    )


def thirds(packed_ref):
    for pair in range(PAIRS_OF_HEADS):
        at = pair * 2 * HD
        yield [packed_ref[0, :, t * D + at : t * D + at + 2 * HD] for t in range(3)]


def probabilities(scores, valid):
    scores = jnp.where(valid, scores * HD ** (-0.5), MASKED)
    raised = jnp.exp(scores - jnp.max(scores, axis=1, keepdims=True))
    return raised * (1.0 / jnp.sum(raised, axis=1, keepdims=True))


def attention_kernel(mask_ref, packed_ref, context_ref):
    valid = mask_ref[0] > 0.0
    parts = list(thirds(packed_ref))
    scores = [contract(by_side(queries), keys, 1, 1) for queries, keys, _ in parts]
    probs = [probabilities(now, valid).astype(jnp.bfloat16) for now in scores]
    for pair in range(PAIRS_OF_HEADS):
        mixed = contract(probs[pair], parts[pair][2], 1, 0)
        at = pair * 2 * HD
        context_ref[0, :, at : at + 2 * HD] = join_sides(mixed).astype(jnp.bfloat16)


def attention_back_kernel(mask_ref, packed_ref, grad_ref, out_ref):
    valid = mask_ref[0] > 0.0
    parts = list(thirds(packed_ref))
    queries = [by_side(part[0]) for part in parts]
    grads = [
        by_side(grad_ref[0, :, pair * 2 * HD : (pair + 1) * 2 * HD])
        for pair in range(PAIRS_OF_HEADS)
    ]
    scores = [contract(now, part[1], 1, 1) for now, part in zip(queries, parts)]
    d_probs = [contract(now, part[2], 1, 1) for now, part in zip(grads, parts)]
    probs = [probabilities(now, valid) for now in scores]
    d_scores = []
    for now, d_now in zip(probs, d_probs):
        shared = jnp.sum(d_now * now, axis=1, keepdims=True)
        d_scores.append(jnp.where(valid, now * (d_now - shared), 0.0).astype(jnp.bfloat16))
    for pair in range(PAIRS_OF_HEADS):
        d_queries = join_sides(contract(d_scores[pair], parts[pair][1], 1, 0)) * HD ** (-0.5)
        d_keys = contract(d_scores[pair], queries[pair], 0, 0) * HD ** (-0.5)
        d_values = contract(probs[pair].astype(jnp.bfloat16), grads[pair], 0, 0)
        for third, now in enumerate((d_queries, d_keys, d_values)):
            at = third * D + pair * 2 * HD
            out_ref[0, :, at : at + 2 * HD] = now.astype(jnp.bfloat16)


def attention_call(kernel, mask, operands, features, name):
    count = operands[0].shape[0]

    def spec(last):
        return pl.BlockSpec((1, SEQ, last), lambda i: (i, 0, 0))

    return pl.pallas_call(
        kernel,
        grid=(count,),
        out_shape=jax.ShapeDtypeStruct((count, SEQ, features), jnp.bfloat16),
        in_specs=[pl.BlockSpec((1, 1, SEQ), lambda i: (i, 0, 0))]
        + [spec(operand.shape[2]) for operand in operands],
        out_specs=spec(features),
        compiler_params=pltpu.CompilerParams(vmem_limit_bytes=32 * 1024 * 1024),
        cost_estimate=pl.CostEstimate(
            flops=10**9, bytes_accessed=count * SEQ * D * 10, transcendentals=10**6
        ),
        name=name,
    )(mask, *operands)


LAYER_ROWS = 8 + FF // D


def layer_vectors(rows):
    up = 5 + FF // D
    return [rows[i] for i in range(5)] + [rows[5:up].reshape(FF)] + [rows[up + i] for i in range(3)]


def layer_norm(values, gain, shift):
    center = values - jnp.mean(values, axis=-1, keepdims=True)
    spread = jnp.mean(center * center, axis=-1, keepdims=True)
    return center * lax.rsqrt(spread + NORM_EPS) * gain + shift


def embed_tokens(rows, vectors):
    return layer_norm(low_back(rows) + vectors[None, :SEQ], vectors[SEQ], vectors[SEQ + 1])


def norm_forward(values, gain, shift):
    center = values - jnp.mean(values, axis=-1, keepdims=True)
    inverse = lax.rsqrt(jnp.mean(center * center, axis=-1, keepdims=True) + NORM_EPS)
    normal = center * inverse
    return normal * gain + shift, normal, inverse


def norm_back(grad, normal, inverse, gain):
    scaled = grad * gain
    mean = jnp.mean(scaled, axis=-1, keepdims=True)
    along = jnp.mean(scaled * normal, axis=-1, keepdims=True)
    return (
        (scaled - mean - normal * along) * inverse,
        jnp.sum(grad * normal, axis=(0, 1)),
        jnp.sum(grad, axis=(0, 1)),
    )


GELU_SCALE = 0.7978845608028654


def gelu(value):
    bent = jnp.tanh(GELU_SCALE * (value + 0.044715 * value * value * value))
    return 0.5 * value * (1.0 + bent)


def gelu_slope(value):
    square = value * value
    bent = jnp.tanh(GELU_SCALE * (value + 0.044715 * square * value))
    inner = GELU_SCALE * (1.0 + 3.0 * 0.044715 * square)
    return 0.5 * (1.0 + bent) + 0.5 * value * (1.0 - bent * bent) * inner


def layer_forward(hidden, weights, vectors, mask):
    in_weights, out_weights, up_weights, down_weights = weights
    q_bias, v_bias, o_bias, gain_one, shift_one, up_bias, down_bias, gain_two, second_shift = (
        layer_vectors(vectors)
    )
    half = jnp.bfloat16
    entry = lax.optimization_barrier(hidden.astype(half))
    bias = jnp.concatenate([q_bias, jnp.zeros_like(q_bias), v_bias])
    packed = (matmul(entry, in_weights) + bias).astype(half)
    context = attention_call(attention_kernel, mask, [packed], D, "attention")
    attended = matmul(context, out_weights) + o_bias
    first, normal_one, inverse_one = norm_forward(hidden + attended, gain_one, shift_one)
    middle = lax.optimization_barrier(first.astype(half))
    upward = matmul(middle, up_weights) + up_bias
    active = lax.optimization_barrier(gelu(upward).astype(half))
    downward = einsum_plain("nsf,df->nsd", active, down_weights) + down_bias
    output, normal_two, inverse_two = norm_forward(first + downward, gain_two, second_shift)
    kept = (
        entry, packed, context, middle, upward, active,
        normal_one, inverse_one, normal_two, inverse_two,
    )
    return output, kept


def layer_backward(kept, weights, vectors, mask, grad):
    in_weights, out_weights, up_weights, down_weights = weights
    entry, packed, context, middle, upward, active = kept[:6]
    normal_one, inverse_one, normal_two, inverse_two = kept[6:]
    gain_one, gain_two = layer_vectors(vectors)[3], layer_vectors(vectors)[7]
    half = jnp.bfloat16

    def total(value):
        return jnp.sum(value.astype(jnp.float32), axis=(0, 1))

    d_second, d_gain_two, d_shift_two = norm_back(grad, normal_two, inverse_two, gain_two)
    d_down = lax.optimization_barrier(d_second.astype(half))
    d_active = jnp.einsum("nsd,df->nsf", d_down, down_weights, preferred_element_type=jnp.float32)
    d_active = lax.optimization_barrier(d_active.astype(half)).astype(jnp.float32)
    d_up = lax.optimization_barrier((d_active * gelu_slope(upward)).astype(half))
    d_first = d_second + jnp.einsum(
        "nsf,df->nsd", d_up, up_weights, preferred_element_type=jnp.float32
    )
    d_middle, d_gain_one, d_shift_one = norm_back(d_first, normal_one, inverse_one, gain_one)
    d_attended = lax.optimization_barrier(d_middle.astype(half))
    d_context = jnp.einsum(
        "nsd,ed->nse", d_attended, out_weights, preferred_element_type=jnp.float32
    ).astype(half)
    d_packed = attention_call(
        attention_back_kernel, mask, [packed, d_context], 3 * D, "attention_back"
    )
    d_hidden = d_middle + jnp.einsum(
        "nsp,dp->nsd", d_packed, in_weights, preferred_element_type=jnp.float32
    )
    packed_total = total(d_packed)
    pieces = [
        packed_total[:D], packed_total[2 * D :], total(d_attended), d_gain_one, d_shift_one,
        total(d_up), total(d_down), d_gain_two, d_shift_two,
    ]
    d_vectors, at = jnp.zeros((LAYER_ROWS, D), jnp.float32), 0
    for piece in pieces:
        rows = piece.reshape(-1, D)
        d_vectors = d_vectors + jnp.pad(rows, ((at, LAYER_ROWS - at - rows.shape[0]), (0, 0)))
        at = at + rows.shape[0]
    flat = [
        (left.reshape(-1, left.shape[2]), right.reshape(-1, right.shape[2]))
        for left, right in (
            (entry, d_packed), (context, d_attended), (middle, d_up), (d_down, active)
        )
    ]
    return d_hidden, flat, d_vectors


def weight_gradient(left, right):
    return lax.dot_general(
        left, right, (((0,), (0,)), ((), ())), preferred_element_type=jnp.float32
    ).astype(jnp.bfloat16)


def pool_rows(hidden, key_mask, seq_lengths):
    share = key_mask.astype(jnp.float32) / seq_lengths.astype(jnp.float32)[:, None]
    return jnp.sum(hidden * share[:, :, None], axis=1)


def normalized_rows(rows):
    return rows * lax.rsqrt(jnp.sum(rows * rows, axis=-1, keepdims=True) + NORM_EPS)


def contrastive_terms(shallow_anchor, deep_anchor, shallow_pos, deep_pos, false_neg, pair_index):
    columns = lax.broadcasted_iota(jnp.int32, false_neg.shape, 1)
    hit = columns == pair_index[:, None]
    kept_cols = (false_neg == 0) | hit
    valid_rows = (pair_index >= 0).astype(jnp.float32)
    totals = jnp.zeros(pair_index.shape, jnp.float32)
    for current_width in (D, D * 2 // 3, D // 3, D // 6, D // 12):
        log_probs = []
        for anchor_vectors, positive_rows in (
            (shallow_anchor, shallow_pos),
            (deep_anchor, deep_pos),
        ):
            similarity_scores = (
                jnp.dot(
                    normalized_rows(anchor_vectors[:, :current_width]),
                    normalized_rows(positive_rows[:, :current_width]).T,
                    precision=lax.Precision.HIGHEST,
                )
                / SOFTMAX_TEMP
            )
            similarity_scores = jnp.where(kept_cols, similarity_scores, MASKED)
            log_probs.append(jax.nn.log_softmax(similarity_scores, axis=-1))
        for log_now in log_probs:
            totals = totals - jnp.sum(jnp.where(hit, log_now, 0.0), axis=-1)
        totals = totals + jnp.sum(jnp.exp(log_probs[1]) * (log_probs[1] - log_probs[0]), axis=-1)
    return jnp.sum(totals * valid_rows)


def adam_update(master, gradient, first, second, step_rate):
    first_new = BETA_ONE * first + (1.0 - BETA_ONE) * gradient
    second_new = BETA_TWO * second + (1.0 - BETA_TWO) * gradient * gradient
    first_hat = first_new / (1.0 - BETA_ONE**ADAM_STEP)
    second_hat = second_new / (1.0 - BETA_TWO**ADAM_STEP)
    master_new = master - step_rate * (
        first_hat / (jnp.sqrt(second_hat) + ADAM_EPS) + WEIGHT_DECAY * master
    )
    return (master_new, first_new, second_new)


def pad_rows(flat, multiple):
    rows = -(-flat.shape[0] // (128 * multiple)) * multiple
    return jnp.pad(flat, (0, rows * 128 - flat.shape[0])).reshape(rows, 128)


def one_hot(index, size, dtype=jnp.bfloat16):
    return (index[:, None] == lax.broadcasted_iota(jnp.int32, (1, size), 1)).astype(dtype)


def token_plan(ids, shard_rows):
    places = lax.broadcasted_iota(jnp.int32, ids.shape, 0)
    same = ids[:, None] == ids[None, :]
    leader = jnp.min(jnp.where(same, places[None, :], ids.shape[0]), axis=1)
    leads = leader == places
    owner = ids // shard_rows
    low_id = owner * shard_rows
    ahead = leads[None, :] & (ids[None, :] >= low_id[:, None]) & (ids[None, :] < ids[:, None])
    place = jnp.sum(ahead.astype(jnp.int32), axis=1)
    return owner, place, ids - low_id


def round_slots(owner, place, local_row, round_index, room, nz):
    inside = (place >= round_index * room) & (place < (round_index + 1) * room)
    slot = jnp.where(inside, owner * room + place - round_index * room, -1)
    slots = lax.broadcasted_iota(jnp.int32, (1, nz * room), 1)
    asked = jnp.max(jnp.where(slot[:, None] == slots, local_row[:, None], -1), axis=0)
    return slot, asked


def body(
    token_ids,
    lengths,
    false_neg,
    pair_index,
    word_table,
    vectors,
    attn_w,
    ffn_w,
    word_first,
    vector_first,
    attn_first,
    ffn_first,
    word_second,
    vector_second,
    attn_second,
    ffn_second,
):
    ndp = lax.axis_size("dp")
    nz = lax.axis_size("zero")
    n = ndp * nz
    by_hand = (ndp, nz) == (2, 16) and token_ids.shape[0] * ndp * nz <= 256
    my_dp = lax.axis_index("dp")
    my_zero = lax.axis_index("zero")
    me = my_dp * nz + my_zero
    pair_rows = token_ids.shape[0]
    total_pairs = pair_rows * n
    flat_ids = token_ids.reshape(-1, SEQ)
    seq_rows = flat_ids.shape[0]
    tokens = seq_rows * SEQ
    seq_lengths = lengths.reshape(-1)
    key_mask = lax.broadcasted_iota(jnp.int32, flat_ids.shape, 1) < seq_lengths[:, None]
    shard_rows = word_table.shape[0]
    vec_len = vectors.shape[0]

    room = -(-(tokens * 9 // 8) // (nz * 8)) * 8
    ids = flat_ids.reshape(-1)

    def packet_of(asked, rounds_here):
        last = jnp.concatenate([pair_index, rounds_here[None].astype(jnp.int32)])
        lines = nz + false_neg.size // 128
        return jnp.concatenate(
            [
                jnp.pad(asked.reshape(nz, room), ((0, 0), (0, 128 - room)), constant_values=-1),
                false_neg.reshape(-1, 128),
                jnp.zeros((7 - lines % 8, 128), jnp.int32),
                jnp.pad(last, (0, 128 - last.shape[0]))[None],
            ]
        )

    def gather_layer(layer_index):
        both = jnp.concatenate(
            [attn_w[layer_index].astype(jnp.bfloat16), ffn_w[layer_index].astype(jnp.bfloat16)],
            axis=1,
        )
        return lax.all_gather(both, "zero", axis=0, tiled=True)

    if by_hand:
        packet = pad_rows(jnp.concatenate([false_neg.reshape(-1), pair_index]), 8)
        place, slot, packets, asked_mine, vec_parts, received, *gathered = exchange_start(
            ids,
            packet.astype(jnp.bfloat16),
            pad_rows(vectors.astype(jnp.bfloat16), 16),
            attn_w,
            ffn_w,
            word_table,
            room,
            0,
        )
        layer_weights = [part.reshape(D, -1) for part in gathered]
        rounds = jnp.max(asked_mine[:, 0, 127])
        asked_mine = asked_mine[:, 0, :room]
        packets = packets.reshape(n, -1).astype(jnp.int32)
        false_all = packets[:, : false_neg.size].reshape(total_pairs, total_pairs)
        pair_all = packets[:, false_neg.size : false_neg.size + pair_rows].reshape(total_pairs)
        place, slot = place.reshape(-1), slot.reshape(-1)
    else:
        owner, place, local_row = token_plan(ids, shard_rows)
        slot, asked = round_slots(owner, place, local_row, 0, room, nz)
        packets, vec_parts = exchange(
            [
                packet_of(asked, jnp.max(place) // room + 1),
                pad_rows(vectors.astype(jnp.bfloat16), 16),
            ],
            ["all", "zero"],
            ndp,
            nz,
            0,
            "gather_requests",
        )
        layer_weights = [gather_layer(layer_index) for layer_index in range(LAYERS)]
        asked_mine = lax.dynamic_index_in_dim(packets[:, :nz, :room], my_zero, 1, keepdims=False)
        false_all = packets[:, nz : nz + false_neg.size // 128].reshape(total_pairs, total_pairs)
        pair_all = packets[:, -1, :pair_rows].reshape(total_pairs)
        rounds = jnp.max(packets[:, -1, pair_rows])
    vec_all = vec_parts.reshape(nz, -1)[:, :vec_len].reshape(-1).astype(jnp.float32)

    asked_near = lax.dynamic_slice_in_dim(asked_mine, my_dp * nz, nz, 0)

    def rows_for(wanted):
        picked = one_hot(wanted.reshape(-1), shard_rows, jnp.float32)
        return jnp.dot(picked, word_table, precision=lax.Precision.HIGHEST).astype(jnp.bfloat16)

    def rows_from(slot_now, received):
        return matmul(one_hot(slot_now, nz * room), received.reshape(nz * room, D)).astype(
            jnp.bfloat16
        )

    if not by_hand:
        (received,) = exchange(
            [rows_for(asked_near).reshape(nz, room, D)], ["zero_p"], ndp, nz, 1, "send_rows"
        )
    rows = rows_from(slot, received)

    def round_of(round_index):
        owner = ids // shard_rows
        local_row = ids - owner * shard_rows
        return round_slots(owner, place, local_row, round_index, room, nz)

    def more_rows(state):
        round_index, rows_now = state
        slot_now, asked_now = round_of(round_index)
        wanted = lax.all_to_all(asked_now.reshape(nz, room), "zero", 0, 0, tiled=True)
        got = lax.all_to_all(rows_for(wanted).reshape(nz, room, D), "zero", 0, 0, tiled=True)
        return round_index + 1, rows_now + rows_from(slot_now, got)

    def further(step, *value):
        return lax.while_loop(lambda state: state[0] < rounds, step, (jnp.int32(1), *value))[1:]

    (rows,) = further(more_rows, rows)
    rows = rows.reshape(seq_rows, SEQ, D).astype(jnp.float32)

    vec_rows = vec_all.reshape(-1, D)
    edges = [0] + [SEQ + 2 + i * LAYER_ROWS for i in range(LAYERS + 1)]
    vec_parts = [vec_rows[first:last] for first, last in zip(edges, edges[1:])]
    embedded, embed_back = jax.vjp(embed_tokens, rows, vec_parts[0])
    hidden = embedded
    mask = key_mask.astype(jnp.float32)[:, None, :]
    saved = []
    layer_parts = []
    pooled = []
    for layer_index in range(LAYERS):
        weights = layer_weights[layer_index]
        edges = (0, 3 * D, 4 * D, 4 * D + FF, 4 * D + 2 * FF)
        parts = [weights[:, first:last] for first, last in zip(edges, edges[1:])]
        layer_parts.append(parts)
        hidden, kept = layer_forward(hidden, parts, vec_parts[1 + layer_index], mask)
        saved.append(kept)
        pooled.append(pool_rows(hidden, key_mask, seq_lengths).astype(jnp.bfloat16))

    if by_hand and pair_rows == 4:
        block = jnp.stack(pooled).reshape(2, pair_rows, 2, D).transpose(0, 2, 1, 3)
        loss, pooled_grads = contrastive(block.reshape(2, 2 * pair_rows, D), false_all, pair_all, 2)
        pooled_grads = pooled_grads[:, :, :pair_rows]
    else:
        (pooled_all,) = exchange(
            [jnp.stack(pooled).reshape(-1, 128)], ["all"], ndp, nz, 2, "gather_pooled"
        )
        pooled_all = pooled_all.reshape(n, 2, pair_rows, 2, D).astype(jnp.float32)
        pooled_all = pooled_all.transpose(1, 3, 0, 2, 4).reshape(2, 2, total_pairs, D)

        def whole_loss(pooled_now):
            summed = contrastive_terms(
                pooled_now[0, 0],
                pooled_now[1, 0],
                pooled_now[0, 1],
                pooled_now[1, 1],
                false_all,
                pair_all,
            )
            valid_total = jnp.sum((pair_all >= 0).astype(jnp.float32))
            return summed / jnp.maximum(valid_total, 1.0)

        loss, pooled_grads = jax.value_and_grad(whole_loss)(pooled_all)
        pooled_grads = lax.dynamic_slice_in_dim(pooled_grads, me * pair_rows, pair_rows, 2)
    pooled_grads = pooled_grads.transpose(0, 2, 1, 3).reshape(2, seq_rows, D)
    shallow_back, deep_back = pooled_grads[0], pooled_grads[1]
    share = key_mask.astype(jnp.float32) / seq_lengths.astype(jnp.float32)[:, None]
    grad_hidden = jnp.zeros_like(embedded)
    weight_parts = []
    vec_grads = [None] * LAYERS
    for layer_index in range(LAYERS - 1, -1, -1):
        if layer_index == LAYERS - 1:
            grad_hidden = grad_hidden + deep_back[:, None, :] * share[:, :, None]
        if layer_index == 0:
            grad_hidden = grad_hidden + shallow_back[:, None, :] * share[:, :, None]
        grad_hidden, pairs, vec_grads[layer_index] = layer_backward(
            saved[layer_index],
            layer_parts[layer_index],
            vec_parts[1 + layer_index],
            mask,
            grad_hidden,
        )
        if by_hand and layer_index == 0:
            weight_parts.insert(0, pairs)
        else:
            both = jnp.concatenate([weight_gradient(*pair) for pair in pairs], axis=1)
            both, grad_hidden = lax.optimization_barrier((both, grad_hidden))
            weight_parts.insert(0, lax.psum_scatter(both, "zero", scatter_dimension=0, tiled=True))
    rows_grad, embed_grads = embed_back(grad_hidden)
    vec_grad = jnp.concatenate([embed_grads] + vec_grads, axis=0)
    down_local = jnp.stack([part[5 + FF // D] for part in vec_grads])

    rows_grad = rows_grad.reshape(tokens, D).astype(jnp.bfloat16)

    def slot_sums(slot_now):
        picked = one_hot(slot_now, nz * room)
        return lax.dot_general(
            picked, rows_grad, (((0,), (0,)), ((), ())), preferred_element_type=jnp.float32
        ).astype(jnp.bfloat16)

    def into_rows(wanted, sums):
        return lax.dot_general(
            one_hot(wanted.reshape(-1), shard_rows),
            sums.reshape(-1, D),
            (((0,), (0,)), ((), ())),
            preferred_element_type=jnp.float32,
        )

    down_each = down_local.reshape(LAYERS, nz, -1).transpose(1, 0, 2).reshape(nz, -1)
    down_len = down_each.shape[1]
    vec_blocks = jnp.concatenate([vec_grad.reshape(nz, vec_len), down_each], axis=1)
    lines = -(-vec_blocks.shape[1] // 1024) * 8
    vec_blocks = jnp.pad(vec_blocks, ((0, 0), (0, lines * 128 - vec_blocks.shape[1])))
    sums = slot_sums(slot).reshape(nz, room, D)

    def more_sums(state):
        round_index, grad_now, square_now = state
        slot_now, asked_now = round_of(round_index)
        wanted = lax.all_to_all(asked_now.reshape(nz, room), "zero", 0, 0, tiled=True)
        got = lax.all_to_all(slot_sums(slot_now).reshape(nz, room, D), "zero", 0, 0, tiled=True)
        wanted = lax.all_gather(wanted, "dp", axis=0, tiled=True)
        got = lax.all_gather(got, "dp", axis=0, tiled=True)
        grad_next = grad_now + into_rows(wanted, got)
        grown = jnp.sum(grad_next * grad_next) - jnp.sum(grad_now * grad_now)
        return round_index + 1, grad_next, square_now + lax.psum(grown, "zero")

    if by_hand:
        attn_shard, ffn_shard, word_grad, vec_sum, squares = exchange_gradients(
            weight_parts[0],
            vec_blocks.reshape(4, 2, 2, lines, 128),
            sums,
            weight_parts[1],
            asked_mine.reshape(ndp, 1, nz * room),
            shard_rows,
            vec_len,
            3,
        )
        vec_sum = vec_sum.reshape(-1)
        square_total = squares[0, 0]
    else:
        sums_all, vec_shares = exchange(
            [sums, vec_blocks.reshape(nz, lines, 128)],
            ["all_p", "all_p"],
            ndp,
            nz,
            3,
            "send_gradients",
        )
        vec_sum = jnp.sum(vec_shares.reshape(n, -1), axis=0)
        (weight_all,) = exchange([jnp.stack(weight_parts)], ["dp"], ndp, nz, 4, "sum_replicas")
        weight_sum = jnp.sum(weight_all.astype(jnp.float32), axis=0)
        attn_shard = weight_sum[:, :, : 4 * D]
        ffn_shard = weight_sum[:, :, 4 * D :]
        word_grad = into_rows(asked_mine, sums_all)
    vec_shard = vec_sum[:vec_len]
    down_shard = vec_sum[vec_len : vec_len + down_len].reshape(LAYERS, -1)

    if not by_hand:
        square_local = jnp.sum(word_grad * word_grad) + jnp.sum(vec_shard * vec_shard)
        square_local = square_local + jnp.sum(attn_shard * attn_shard)
        square_local = square_local + jnp.sum(ffn_shard * ffn_shard)
        (squares,) = exchange(
            [jnp.broadcast_to(square_local, (8, 128))], ["zero"], ndp, nz, 5, "gather_squares"
        )
        square_total = jnp.sum(squares[:, 0, 0])
    word_grad, square_total = further(more_sums, word_grad, square_total)
    grad_norm = jnp.sqrt(square_total)
    factor = jnp.minimum(1.0, CLIP_NORM / (grad_norm + 1e-06))
    word_new, word_first_new, word_second_new = adam_update(
        word_table, word_grad * factor, word_first, word_second, LEARN_RATE
    )
    vector_new, vector_first_new, vector_second_new = adam_update(
        vectors, vec_shard * factor, vector_first, vector_second, VECTOR_RATE
    )
    attn_new, attn_first_new, attn_second_new = adam_update(
        attn_w, attn_shard * factor, attn_first, attn_second, LEARN_RATE
    )
    ffn_new, ffn_first_new, ffn_second_new = adam_update(
        ffn_w, ffn_shard * factor, ffn_first, ffn_second, LEARN_RATE
    )
    return (
        loss,
        grad_norm,
        word_new,
        vector_new,
        attn_new,
        ffn_new,
        word_new.astype(jnp.bfloat16),
        vector_new.astype(jnp.bfloat16),
        attn_new.astype(jnp.bfloat16),
        ffn_new.astype(jnp.bfloat16),
        word_first_new,
        vector_first_new,
        attn_first_new,
        ffn_first_new,
        word_second_new,
        vector_second_new,
        attn_second_new,
        ffn_second_new,
        down_shard * factor,
    )


def solution(mesh):
    placed = (
        P(("dp", "zero"), None, None),
        P(("dp", "zero"), None),
        P(("dp", "zero"), None),
        P(("dp", "zero")),
        P("zero", None),
        P("zero"),
        P(None, "zero", None),
        P(None, "zero", None),
        P("zero", None),
        P("zero"),
        P(None, "zero", None),
        P(None, "zero", None),
        P("zero", None),
        P("zero"),
        P(None, "zero", None),
        P(None, "zero", None),
    )
    return jax.shard_map(
        body,
        mesh=mesh,
        in_specs=placed,
        out_specs=(
            P(),
            P(),
            P("zero", None),
            P("zero"),
            P(None, "zero", None),
            P(None, "zero", None),
            P("zero", None),
            P("zero"),
            P(None, "zero", None),
            P(None, "zero", None),
            P("zero", None),
            P("zero"),
            P(None, "zero", None),
            P(None, "zero", None),
            P("zero", None),
            P("zero"),
            P(None, "zero", None),
            P(None, "zero", None),
            P(None, "zero"),
        ),
        check_vma=False,
    )
```

```python
import functools

import jax
import jax.numpy as jnp
from jax import lax
from jax.experimental import pallas as pl
from jax.experimental.pallas import tpu as pltpu
from jax.sharding import PartitionSpec as P

D = 512
HEADS = 8
HD = 64
FF = 2048
SEQ = 128
LAYERS = 2
ADAM_STEP = 5


SOFTMAX_TEMP = 0.05
CLIP_NORM = 1.0
LEARN_RATE = 0.02
VECTOR_RATE = 0.15
BETA_ONE = 0.5
BETA_TWO = 0.5
WEIGHT_DECAY = 0.01
ADAM_EPS = 1e-08
NORM_EPS = 1e-06
MASKED = -1000000000.0

MESH = pl.DeviceIdType.MESH


def build_low():

    def rounder(value):
        return lax.optimization_barrier(value.astype(jnp.bfloat16)).astype(jnp.float32)

    def keep_fwd(value):
        return (rounder(value), None)

    def pass_bwd(kept, grad):
        return (grad,)

    wrapped = jax.custom_vjp(rounder)
    wrapped.defvjp(keep_fwd, pass_bwd)
    return wrapped


def build_low_back():

    def identity_fn(value):
        return value

    def keep_fwd(value):
        return (value, None)

    def round_bwd(kept, grad):
        return (low(grad),)

    wrapped = jax.custom_vjp(identity_fn)
    wrapped.defvjp(keep_fwd, round_bwd)
    return wrapped


def low(value):
    return build_low()(value)


def low_back(value):
    return build_low_back()(value)


def rounded(value):
    return low(low_back(value))


def matmul(left, right):
    return jnp.dot(left, right, preferred_element_type=jnp.float32)


def einsum_plain(form, left, right):
    return jnp.einsum(form, left, right, preferred_element_type=jnp.float32)


def exchange_kernel(modes, ndp, nz, *refs):
    count = len(modes)
    ins = refs[:count]
    outs = refs[count : 2 * count]
    sems = refs[2 * count :]
    d = lax.axis_index("dp")
    z = lax.axis_index("zero")
    me = d * nz + z
    n = ndp * nz

    def peer_of(group, k):
        if group == "dp":
            pd = lax.rem(d + k, ndp)
            return pd, z, pd
        if group == "zero":
            pz = lax.rem(z + k, nz)
            return d, pz, pz
        p = lax.rem(me + k, n)
        return p // nz, lax.rem(p, nz), p

    groups = {m.split("_")[0] for m in modes}
    sizes = {"all": n, "zero": nz, "dp": ndp}
    mine = {"all": me, "zero": z, "dp": d}
    barrier = pltpu.get_barrier_semaphore()
    meet = ["all"] if "all" in groups else sorted(groups)
    total = 0
    for group in meet:
        total += sizes[group] - 1

        def greet(k, carry, group=group):
            pd, pz, _ = peer_of(group, k)
            pl.semaphore_signal(barrier, inc=1, device_id=(pd, pz), device_id_type=MESH)
            return carry

        lax.fori_loop(1, sizes[group], greet, 0)
    pl.semaphore_wait(barrier, total)

    def make(a, k):
        mode = modes[a]
        group = mode.split("_")[0]
        pd, pz, _ = peer_of(group, k)
        src = ins[a].at[pz] if mode.endswith("_p") else ins[a]
        return pltpu.make_async_remote_copy(
            src_ref=src,
            dst_ref=outs[a].at[mine[group]],
            send_sem=sems[2 * a].at[k],
            recv_sem=sems[2 * a + 1].at[k],
            device_id=(pd, pz),
            device_id_type=MESH,
        )

    for a, mode in enumerate(modes):
        group = mode.split("_")[0]

        def begin(k, carry, a=a):
            make(a, k).start()
            return carry

        lax.fori_loop(1, sizes[group], begin, 0)
    for a, mode in enumerate(modes):
        group = mode.split("_")[0]
        if mode.endswith("_p"):
            outs[a][mine[group]] = ins[a][z]
        else:
            outs[a][mine[group]] = ins[a][...]
    for a, mode in enumerate(modes):
        group = mode.split("_")[0]

        def finish(k, carry, a=a):
            make(a, k).wait()
            return carry

        lax.fori_loop(1, sizes[group], finish, 0)


def exchange(arrays, modes, ndp, nz, collective_id, name):
    sizes = {"all": ndp * nz, "zero": nz, "dp": ndp}
    outs = []
    scratch = []
    moved = 0
    for array, mode in zip(arrays, modes):
        size = sizes[mode.split("_")[0]]
        block = array.shape[1:] if mode.endswith("_p") else array.shape
        outs.append(jax.ShapeDtypeStruct((size,) + block, array.dtype))
        scratch += [pltpu.SemaphoreType.DMA((size,)), pltpu.SemaphoreType.DMA((size,))]
        one = array.dtype.itemsize
        for s in block:
            one *= s
        moved += one * size
    vmem = pl.BlockSpec(memory_space=pltpu.VMEM)
    return pl.pallas_call(
        functools.partial(exchange_kernel, tuple(modes), ndp, nz),
        out_shape=tuple(outs),
        in_specs=[vmem] * len(arrays),
        out_specs=tuple([vmem] * len(arrays)),
        scratch_shapes=scratch,
        compiler_params=pltpu.CompilerParams(
            collective_id=collective_id, has_side_effects=True, vmem_limit_bytes=48 * 1024 * 1024
        ),
        cost_estimate=pl.CostEstimate(flops=0, bytes_accessed=20 * moved, transcendentals=0),
        name=name,
    )(*arrays)


CHUNK = 1024
LAG_Z = 3
REST_EACH = 4
HALVED = (2,)


def gradient_kernel(chunks, matrices, vec_len, *refs):
    take = iter(refs)
    pairs = [(next(take), next(take)) for _ in range(matrices)]
    vec_ref, sums_ref, near_ref, asked_ref = [next(take) for _ in range(4)]
    attn_out, ffn_out, word_out, vec_out, stats_out = [next(take) for _ in range(5)]
    held = [None if chunk[1] is None else next(take) for chunk in chunks]
    bufs = [[next(take) for _ in range(6 if chunk[4] else 5)] for chunk in chunks]
    near_buf, rows_ref, sum_ref, square_ref, squares_ref = [next(take) for _ in range(5)]
    send_a, recv_a, send_y, recv_y, send_z, recv_z, send_x, recv_x = [next(take) for _ in range(8)]
    send_h, recv_h = next(take), next(take)
    row_send, row_recv, pass_send, pass_recv, near_sem, square_sem = [
        next(take) for _ in range(6)
    ]

    d = lax.axis_index("dp")
    z = lax.axis_index("zero")
    core = lax.rem(z, 2)
    col = lax.rem(z // 2, 2)
    line = z // 4
    sibling = z + 1 - 2 * core
    across = z + 2 - 4 * col
    attn_width = attn_out.shape[2]

    def along(k):
        return lax.rem(line + k, 4) * 4 + lax.rem(z, 4)

    barrier = pltpu.get_barrier_semaphore()

    def greet(k, carry):
        pl.semaphore_signal(
            barrier, inc=1, device_id=(d, lax.rem(z + k, 16)), device_id_type=MESH
        )
        return carry

    lax.fori_loop(1, 16, greet, 0)
    pl.semaphore_signal(barrier, inc=1, device_id=(1 - d, z), device_id_type=MESH)
    pl.semaphore_wait(barrier, 16)

    def remote(src, dst, send, recv, to):
        return pltpu.make_async_remote_copy(
            src_ref=src,
            dst_ref=dst,
            send_sem=send,
            recv_sem=recv,
            device_id=to,
            device_id_type=MESH,
        )

    def part_of(i):
        return vec_ref if held[i] is None else held[i]

    def halves(i):
        return chunks[i][4]

    def after_y(i):
        return bufs[i][1 + halves(i)]

    def half_rows(i, which):
        rows = bufs[i][0].shape[2] // 2
        return pl.ds(pl.multiple_of(which * rows, 16), rows)

    def copy_a(i):
        src = part_of(i).at[:, :, 1 - core]
        return remote(src, bufs[i][0], send_a.at[i], recv_a.at[i], (d, sibling))

    def copy_h(i):
        src = bufs[i][0].at[:, :, half_rows(i, 1 - d)]
        return remote(src, bufs[i][1], send_h.at[i], recv_h.at[i], (1 - d, z))

    def copy_y(i):
        src = bufs[i][halves(i)].at[:, 1 - col]
        return remote(src, after_y(i), send_y.at[i], recv_y.at[i], (d, across))

    def copy_z(i, k):
        src = after_y(i).at[lax.rem(line + k, 4)]
        into = bufs[i][-3].at[k - 1]
        return remote(src, into, send_z.at[i, k - 1], recv_z.at[i, k - 1], (d, along(k)))

    def copy_x(i):
        return remote(bufs[i][-2], bufs[i][-1], send_x.at[i], recv_x.at[i], (1 - d, z))

    def row_push(k):
        to = lax.rem(z + k, 16)
        return remote(sums_ref.at[to], rows_ref.at[d, z], row_send.at[k], row_recv.at[k], (d, to))

    def row_pass(k):
        at = lax.rem(z + 16 - k, 16)
        return remote(
            rows_ref.at[d, at], rows_ref.at[d, at], pass_send.at[k], pass_recv.at[k], (1 - d, z)
        )

    near = remote(near_ref, near_buf, near_sem.at[0], near_sem.at[1], (1 - d, z))

    total = len(chunks)

    def push(k, carry):
        row_push(k).start()
        return carry

    lax.fori_loop(1, 16, push, 0)
    near.start()
    rows_ref[d, z] = sums_ref[z]
    row_pass(0).start()

    def compute(i):
        _, matrix, start, width, _ = chunks[i]
        if matrix is not None:
            left, right = pairs[matrix]

            def rows_of(j, carry):
                at = pl.ds(pl.multiple_of(j * 128, 128), 128)
                found = lax.dot_general(
                    left[:, at],
                    right[:, start : start + width],
                    (((0,), (0,)), ((), ())),
                    preferred_element_type=jnp.float32,
                )
                held[i][j] = found.astype(jnp.bfloat16).reshape(2, 2, 32, width)
                return carry

            lax.fori_loop(0, 4, rows_of, 0)
        copy_a(i).start()

    def add_into(buf, count, place, mine):
        def add_block(b, carry):
            at = place(b)
            value = mine(b).astype(jnp.float32) + buf[at].astype(jnp.float32)
            buf[at] = value.astype(buf.dtype)
            return carry

        lax.fori_loop(0, count, add_block, 0)

    def stage_a(i):
        copy_a(i).wait_recv()
        add_into(
            bufs[i][0],
            8,
            lambda b: (b // 2, lax.rem(b, 2)),
            lambda b: part_of(i)[b // 2, lax.rem(b, 2), core],
        )
        (copy_h if halves(i) else copy_y)(i).start()

    def stage_h(i):
        copy_h(i).wait_recv()
        add_into(
            bufs[i][1],
            8,
            lambda b: (b // 2, lax.rem(b, 2)),
            lambda b: bufs[i][0][b // 2, lax.rem(b, 2), half_rows(i, d), :],
        )
        copy_y(i).start()

    def stage_y(i):
        copy_y(i).wait_recv()
        add_into(after_y(i), 4, lambda b: b, lambda b: bufs[i][halves(i)][b, col])
        for k in range(1, 4):
            copy_z(i, k).start()

    def stage_z(i):
        for k in range(1, 4):
            copy_z(i, k).wait_recv()
        value = after_y(i)[line].astype(jnp.float32)
        for k in range(3):
            value = value + bufs[i][-3][k].astype(jnp.float32)
        bufs[i][-2][...] = value.astype(bufs[i][-2].dtype)
        copy_x(i).start()

    def stage_x(i):
        target, _, start, width, _ = chunks[i]
        copy_x(i).wait_recv()
        mine, other = bufs[i][-2][...].astype(jnp.float32), bufs[i][-1][...].astype(jnp.float32)
        if target is None:
            vec_out[...] = mine + other
            return
        layer, first = target[0], target[1] + start
        out, first = (attn_out, first) if first < attn_width else (ffn_out, first - attn_width)
        if halves(i):
            out[layer, half_rows(i, d), first : first + width] = mine
            out[layer, half_rows(i, 1 - d), first : first + width] = other
        else:
            out[layer, :, first : first + width] = mine + other

    def steps_of(i):
        if halves(i):
            order = ((stage_a, 0), (stage_h, 1), (stage_y, 2), (stage_z, 2 + LAG_Z), (stage_x, 3 + LAG_Z))
        else:
            order = ((stage_a, 0), (stage_y, 1), (stage_z, 1 + LAG_Z), (stage_x, 2 + LAG_Z))
        return [(i + later, now) for now, later in order]

    def pass_on(k):
        row_push(k).wait_recv()
        row_pass(k).start()

    shard_rows, features = word_out.shape
    tiles = -(-shard_rows // 128)
    spots = rows_ref.shape[1] * rows_ref.shape[2]
    sum_ref[...] = jnp.zeros_like(sum_ref)

    def into_rows(plane, first, count):
        row = lax.broadcasted_iota(jnp.int32, (128, 1), 0) + first
        picked = (asked_ref[plane] == row).astype(jnp.bfloat16)
        return jnp.dot(
            picked, rows_ref[plane].reshape(spots, features), preferred_element_type=jnp.float32
        )[:count]

    def own_rows(tile):
        first, count = tile * 128, min(128, shard_rows - tile * 128)
        word_out[first : first + count, :] = into_rows(d, first, count)

    def all_arrived():
        def arrived(k, carry):
            ref = rows_ref.at[1 - d, lax.rem(z + 16 - k, 16)]
            remote(ref, ref, pass_send.at[k], pass_recv.at[k], (1 - d, z)).wait_recv()
            return carry

        lax.fori_loop(0, 16, arrived, 0)

    def other_rows(tile):
        first, count = tile * 128, min(128, shard_rows - tile * 128)
        value = word_out[first : first + count, :] + into_rows(1 - d, first, count)
        word_out[first : first + count, :] = value
        sum_ref[...] = sum_ref[...] + jnp.sum(value * value, axis=0, keepdims=True)

    rest = [functools.partial(own_rows, tile) for tile in range(tiles)]
    rest += [all_arrived] + [functools.partial(other_rows, tile) for tile in range(tiles)]

    compute(0)
    passed = 1
    for t in range(total + LAG_Z + 3):
        if t + 1 < total:
            compute(t + 1)
        for i in range(total - 1, -1, -1):
            for at, now in steps_of(i):
                if at == t:
                    now(i)
        until = min(16, 1 + (t + 1) * 15 // (total - 2))
        for k in range(passed, until):
            pass_on(k)
        passed = until
        if t >= total - 2:
            for _ in range(min(len(rest), REST_EACH)):
                rest.pop(0)()
    while rest:
        rest.pop(0)()

    near.wait()
    ffn_out[1] = near_ref[...].astype(jnp.float32) + near_buf[...].astype(jnp.float32)
    squares = sum_ref[...]
    square = jnp.sum(squares, axis=1, keepdims=True)
    for out in (attn_out, ffn_out):

        def of_rows(r, carry, out=out):
            at = pl.ds(pl.multiple_of(r * 8, 8), 8)
            for layer in range(out.shape[0]):
                value = out[layer, at, :]
                carry = carry + jnp.sum(value * value, axis=0, keepdims=True)
            return carry

        found = lax.fori_loop(
            0, out.shape[1] // 8, of_rows, jnp.zeros((1, out.shape[2]), jnp.float32)
        )
        square = square + jnp.sum(found, axis=1, keepdims=True)
    place = lax.broadcasted_iota(jnp.int32, vec_out.shape, 0) * 128 + lax.broadcasted_iota(
        jnp.int32, vec_out.shape, 1
    )
    value = jnp.where(place < vec_len, vec_out[...], 0.0)
    found = jnp.sum(value * value, axis=0, keepdims=True)
    square = square + jnp.sum(found, axis=1, keepdims=True)
    square_ref[...] = jnp.broadcast_to(square, square_ref.shape)

    def square_copy(k, slot):
        return remote(
            square_ref,
            squares_ref.at[slot],
            square_sem.at[0, k],
            square_sem.at[1, k],
            (d, lax.rem(z + k, 16)),
        )

    def send_square(k, carry):
        square_copy(k, z).start()
        return carry

    lax.fori_loop(1, 16, send_square, 0)
    squares_ref[z] = square_ref[...]

    for i in range(total):
        copy_a(i).wait_send()
        if halves(i):
            copy_h(i).wait_send()
        copy_y(i).wait_send()
        for k in range(1, 4):
            copy_z(i, k).wait_send()
        copy_x(i).wait_send()

    def finish(k, carry):
        row_push(k).wait_send()
        square_copy(k, lax.rem(z + 16 - k, 16)).wait_recv()
        square_copy(k, z).wait_send()
        return carry

    lax.fori_loop(1, 16, finish, 0)

    def finish_pass(k, carry):
        row_pass(k).wait_send()
        return carry

    lax.fori_loop(0, 16, finish_pass, 0)
    norm = squares_ref[0]
    for slot in range(1, 16):
        norm = norm + squares_ref[slot]
    stats_out[...] = jnp.broadcast_to(norm, stats_out.shape)


def exchange_gradients(pairs, vec_parts, sums, near, asked, shard_rows, vec_len, collective_id):
    spans = []
    for index, (_, right) in enumerate(pairs):
        layer, matrix = index // 4, index % 4
        columns = right.shape[1]
        width = columns // -(-columns // CHUNK)
        offset = sum(pairs[m][1].shape[1] for m in range(matrix))
        for start in range(0, columns, width):
            spans.append(((layer, offset), index, start, width, index in HALVED))
    plain = [chunk for chunk in spans if not chunk[4]]
    halved = [chunk for chunk in spans if chunk[4]]
    chunks = [(None, None, 0, 128, False)]
    while plain or halved:
        chunks += halved[:1] + plain[:1]
        halved, plain = halved[1:], plain[1:]
    half = jnp.bfloat16
    held, bufs = [], []
    for _, index, _, width, halves in chunks:
        kind = vec_parts.dtype if index is None else half
        r = vec_parts.shape[3] if index is None else 32
        if index is not None:
            held.append(pltpu.VMEM((4, 2, 2, r, width), kind))
        bufs.append(pltpu.VMEM((4, 2, r, width), kind))
        if halves:
            r = r // 2
            bufs.append(pltpu.VMEM((4, 2, r, width), kind))
        bufs += [
            pltpu.VMEM((4, r, width), kind),
            pltpu.VMEM((3, r, width), kind),
            pltpu.VMEM((r, width), kind),
            pltpu.VMEM((r, width), kind),
        ]
    features = sums.shape[2]
    dma = pltpu.SemaphoreType.DMA
    count = len(chunks)
    scratch = held + bufs
    scratch += [
        pltpu.VMEM(near.shape, half),
        pltpu.VMEM((2,) + sums.shape, half),
        pltpu.VMEM((1, features), jnp.float32),
        pltpu.VMEM((1, 128), jnp.float32),
        pltpu.VMEM((16, 1, 128), jnp.float32),
    ]
    scratch += [dma((count,)) for _ in range(4)] + [dma((count, 3)) for _ in range(2)]
    scratch += [dma((count,)) for _ in range(4)]
    scratch += [dma((16,)) for _ in range(4)] + [dma((2,)), dma((2, 16))]
    rows = near.shape[0]
    outs = [
        jax.ShapeDtypeStruct((2, rows, 4 * D), jnp.float32),
        jax.ShapeDtypeStruct((2, rows, 2 * FF), jnp.float32),
        jax.ShapeDtypeStruct((shard_rows, features), jnp.float32),
        jax.ShapeDtypeStruct(vec_parts.shape[3:], jnp.float32),
        jax.ShapeDtypeStruct((8, 128), jnp.float32),
    ]
    vmem = pl.BlockSpec(memory_space=pltpu.VMEM)
    return pl.pallas_call(
        functools.partial(gradient_kernel, tuple(chunks), len(pairs), vec_len),
        out_shape=tuple(outs),
        in_specs=[vmem] * (2 * len(pairs) + 4),
        out_specs=tuple([vmem] * len(outs)),
        scratch_shapes=scratch,
        compiler_params=pltpu.CompilerParams(
            collective_id=collective_id, has_side_effects=True, vmem_limit_bytes=58 * 1024 * 1024
        ),
        cost_estimate=pl.CostEstimate(flops=0, bytes_accessed=200_000_000, transcendentals=0),
        name="exchange_gradients",
    )(*[array for pair in pairs for array in pair], vec_parts, sums, near, asked)


SPLITS = 4
WINDOW = 3
LAG = 3


def start_kernel(shard_rows, room, *refs):
    column_ref, row_ref, packet_ref, vec_ref, attn_ref, ffn_ref, word_ref = refs[:7]
    place_out, slot_out, packet_out, asked_out, vec_out, rows_out, *weight_outs = refs[7:15]
    table, rows_held, asked, slots, locals_ = refs[15:20]
    packet_sem, asked_sem, vec_sem, row_sem = refs[20:24]
    z_sem, y_sem, x_sem, d_sem, e_sem, own_sem = refs[24:]

    d = lax.axis_index("dp")
    z = lax.axis_index("zero")
    me = d * 16 + z
    core = lax.rem(z, 2)
    col = lax.rem(z // 2, 2)
    line = z // 4
    sibling = z + 1 - 2 * core
    across = z + 2 - 4 * col
    layers = attn_ref.shape[0]
    width = attn_ref.shape[2]
    whole = 3 * width
    unit = whole // 128 // SPLITS
    hand = unit * 5 // 12
    total = layers * SPLITS

    def everyone(k):
        p = lax.rem(me + k, 32)
        return (p // 16, lax.rem(p, 16))

    barrier = pltpu.get_barrier_semaphore()

    def greet(k, carry):
        pl.semaphore_signal(barrier, inc=1, device_id=everyone(k), device_id_type=MESH)
        return carry

    lax.fori_loop(1, 32, greet, 0)
    for layer in range(layers):
        weight_outs[layer][z, :, 0:width] = attn_ref[layer].astype(jnp.bfloat16)
        weight_outs[layer][z, :, width:whole] = ffn_ref[layer].astype(jnp.bfloat16)
    pl.semaphore_wait(barrier, 31)

    def remote(src, dst, sems, at, to):
        return pltpu.make_async_remote_copy(
            src_ref=src,
            dst_ref=dst,
            send_sem=sems.at[(0,) + at],
            recv_sem=sems.at[(1,) + at],
            device_id=to,
            device_id_type=MESH,
        )

    def packet_copy(k, slot):
        return remote(packet_ref, packet_out.at[slot], packet_sem, (k,), everyone(k))

    def asked_copy(k, slot):
        to = everyone(k)
        return remote(asked.at[to[1]], asked_out.at[slot], asked_sem, (k,), to)

    def vec_copy(k, slot):
        return remote(vec_ref, vec_out.at[slot], vec_sem, (k,), (d, lax.rem(z + k, 16)))

    def row_copy(k, slot):
        to = lax.rem(z + k, 16)
        return remote(rows_held.at[to], rows_out.at[slot], row_sem, (k,), (d, to))

    def shard(i):
        at = lax.rem(line + i % 4, 4) * 4 + lax.rem(z, 4)
        return at if i < 4 else at + 2 - 4 * col

    def piece(s):
        layer, p = s // SPLITS, s % SPLITS
        size = unit if p < SPLITS - 1 else whole // 128 - p * unit
        return layer, p * unit, size

    def columns_of(at, s, first, size):
        layer, base, _ = piece(s)
        return weight_outs[layer].at[
            at, :, pl.ds(pl.multiple_of((base + first) * 128, 128), size * 128)
        ]

    def stretch(at, s, ours):
        size = piece(s)[2]
        return columns_of(at, s, ours * hand, size - hand)

    def handed(at, s, ours):
        size = piece(s)[2]
        return columns_of(at, s, ours * (size - hand), hand)

    def both(ref, sems, at, to):
        return remote(ref, ref, sems, at, to)

    def z_copy(s, k, at):
        to = lax.rem(line + k, 4) * 4 + lax.rem(z, 4)
        return both(stretch(at, s, d), z_sem, (s, k - 1), (d, to))

    def y_copy(s, j, at):
        return both(stretch(at, s, d), y_sem, (s, j), (d, across))

    def x_copy(s, i, at, ours):
        return both(handed(at, s, ours), x_sem, (s, i), (1 - d, z))

    def d_copy(s, i, at):
        return both(stretch(at, s, d), d_sem, (s, i), (d, sibling))

    def e_copy(s, i, at):
        return both(handed(at, s, 1 - d), e_sem, (s, i), (d, sibling))

    def own_copy(layer, at):
        ref = weight_outs[layer].at[at]
        return both(ref, own_sem, (layer,), (d, sibling))

    def spread(s, i):
        at = shard(i)
        if i < 4:
            y_copy(s, i, at).start()
        if i > 0:
            x_copy(s, i, at, d).start()
            d_copy(s, i, at).start()

    def open_piece(s):
        for k in range(1, 4):
            z_copy(s, k, z).start()
        spread(s, 0)

    for s in range(WINDOW):
        open_piece(s)

    tokens = column_ref.shape[0]
    ids_row = row_ref[...]
    lane = lax.broadcasted_iota(jnp.int32, (1, tokens), 1).astype(jnp.float32)
    block = 128

    def lead_of(b, least):
        ids = column_ref[pl.ds(pl.multiple_of(b * block, block), block), :]
        there = lax.broadcasted_iota(jnp.int32, (block, 1), 0) + b * block
        found = jnp.where(ids == ids_row, there.astype(jnp.float32), 1e9)
        return jnp.minimum(least, jnp.min(found, axis=0, keepdims=True))

    least = lax.fori_loop(0, tokens // block, lead_of, jnp.full((1, tokens), 1e9, jnp.float32))
    lead_ids = jnp.where(least == lane, ids_row, -1)

    def place_of(b, most):
        at = pl.ds(pl.multiple_of(b * block, block), block)
        ids = column_ref[at, :]
        owner = jnp.zeros_like(ids)
        for o in range(1, 16):
            owner = owner + (ids >= o * shard_rows).astype(jnp.int32)
        low_id = owner * shard_rows
        ahead = (lead_ids >= low_id) & (lead_ids < ids)
        place = jnp.sum(jnp.where(ahead, 1.0, 0.0), axis=1, keepdims=True)
        place_out[at, :] = place.astype(jnp.int32)
        inside = place < room
        slots[at, :] = jnp.where(inside, owner * 128 + place.astype(jnp.int32), -1)
        slot_out[at, :] = jnp.where(inside, owner * room + place.astype(jnp.int32), -1)
        locals_[at, :] = (ids - low_id).astype(jnp.float32)
        return jnp.maximum(most, jnp.max(place, axis=0, keepdims=True))

    most = lax.fori_loop(0, tokens // block, place_of, jnp.zeros((1, 1), jnp.float32))
    rounds = jnp.ones((1, 1), jnp.float32)
    for r in range(1, -(-tokens // room)):
        rounds = rounds + (most >= r * room).astype(jnp.float32)
    lane128 = lax.broadcasted_iota(jnp.int32, (1, 128), 1)

    for o in range(16):

        def asked_of(b, best, o=o):
            at = pl.ds(pl.multiple_of(b * block, block), block)
            found = jnp.where(slots[at, :] == o * 128 + lane128, locals_[at, :], -1.0)
            return jnp.maximum(best, jnp.max(found, axis=0, keepdims=True))

        best = lax.fori_loop(0, tokens // block, asked_of, jnp.full((1, 128), -1.0, jnp.float32))
        asked[o] = jnp.where(lane128 == 127, rounds, best).astype(jnp.int32)

    def send_packets(k, carry):
        asked_copy(k, me).start()
        packet_copy(k, me).start()
        return carry

    lax.fori_loop(1, 32, send_packets, 0)

    def send_vec(k, carry):
        vec_copy(k, z).start()
        return carry

    lax.fori_loop(1, 16, send_vec, 0)
    for layer in range(layers):
        own_copy(layer, z).start()
    vec_out[z] = vec_ref[...]
    asked_out[me] = asked[z]
    packet_out[me] = packet_ref[...]

    body_rows = shard_rows // 16 * 16
    step = 112 if body_rows % 112 == 0 else 16

    def to_half(i, carry):
        at = pl.multiple_of(i * step, 16)
        table[pl.ds(at, step), :] = word_ref[pl.ds(at, step), :].astype(jnp.bfloat16)
        return carry

    lax.fori_loop(0, body_rows // step, to_half, 0)
    padded = table.shape[0]
    table[body_rows:padded, :] = jnp.zeros((padded - body_rows, table.shape[1]), jnp.bfloat16)
    if shard_rows > body_rows:
        table[body_rows:shard_rows, :] = word_ref[body_rows:shard_rows, :].astype(jnp.bfloat16)

    def answer_one(k, carry):
        src = lax.rem(z + k, 16)
        rows_at = lax.broadcasted_iota(jnp.int32, (padded, 128), 0)
        picked = (rows_at == asked_out[d * 16 + src]).astype(jnp.bfloat16)
        found = lax.dot_general(
            picked, table[...], (((0,), (0,)), ((), ())), preferred_element_type=jnp.float32
        )
        rows_held[src] = found[:room, :].astype(jnp.bfloat16)
        return carry

    def packet_in(k, carry):
        asked_copy(k, lax.rem(me + 32 - k, 32)).wait_recv()
        return carry

    def row_start(k, carry):
        row_copy(k, z).start()
        return carry

    def z_phase(s):
        for k in range(1, 4):
            z_copy(s, k, shard(4 - k)).wait_recv()
            spread(s, 4 - k)
        if s + WINDOW < total:
            open_piece(s + WINDOW)

    def y_phase(s):
        for j in range(4):
            y_copy(s, j, shard(4 + j)).wait_recv()
            spread(s, 4 + j)

    def x_phase(s):
        for i in range(1, 8):
            at = shard(i)
            x_copy(s, i, at, 1 - d).wait_recv()
            e_copy(s, i, at).start()

    done = 0
    for t in range(total + LAG):
        if t < total:
            z_phase(t)
        if t == 1:
            lax.fori_loop(1, 32, packet_in, 0)
        if t >= 1:
            until = min(16, done + 4)
            if until > done:
                lax.fori_loop(done, until, answer_one, 0)
            done = until
        if t == total - 1:
            lax.fori_loop(1, 16, row_start, 0)
            rows_out[z] = rows_held[z]
        if 0 <= t - 1 < total:
            y_phase(t - 1)
        if 0 <= t - LAG < total:
            x_phase(t - LAG)

    turn = 1 - 2 * core
    for layer in range(layers):
        own_copy(layer, z + turn).wait_recv()
        own_copy(layer, z).wait_send()
    for s in range(total):
        for i in range(1, 8):
            at = shard(i)
            d_copy(s, i, at + turn).wait_recv()
            d_copy(s, i, at).wait_send()
            e_copy(s, i, at + turn).wait_recv()
            e_copy(s, i, at).wait_send()
            x_copy(s, i, at, d).wait_send()
        for k in range(1, 4):
            z_copy(s, k, z).wait_send()
        for i in range(4):
            y_copy(s, i, shard(i)).wait_send()

    def finish(k, carry):
        back = lax.rem(z + 16 - k, 16)
        row_copy(k, back).wait_recv()
        row_copy(k, z).wait_send()
        vec_copy(k, back).wait_recv()
        vec_copy(k, z).wait_send()
        return carry

    lax.fori_loop(1, 16, finish, 0)

    def finish_packets(k, carry):
        packet_copy(k, lax.rem(me + 32 - k, 32)).wait_recv()
        packet_copy(k, me).wait_send()
        asked_copy(k, me).wait_send()
        return carry

    lax.fori_loop(1, 32, finish_packets, 0)


def exchange_start(ids, packet, vec_rows, attn, ffn, word_table, room, collective_id):
    half = jnp.bfloat16
    shard_rows, features = word_table.shape
    padded = -(-shard_rows // 128) * 128
    layers, rows, width = attn.shape
    tokens = ids.shape[0]
    pieces = layers * SPLITS
    dma = pltpu.SemaphoreType.DMA
    vmem = pl.BlockSpec(memory_space=pltpu.VMEM)
    return pl.pallas_call(
        functools.partial(start_kernel, shard_rows, room),
        out_shape=(
            jax.ShapeDtypeStruct((tokens, 1), jnp.int32),
            jax.ShapeDtypeStruct((tokens, 1), jnp.int32),
            jax.ShapeDtypeStruct((32,) + packet.shape, packet.dtype),
            jax.ShapeDtypeStruct((32, 1, 128), jnp.int32),
            jax.ShapeDtypeStruct((16,) + vec_rows.shape, vec_rows.dtype),
            jax.ShapeDtypeStruct((16, room, features), half),
        )
        + (jax.ShapeDtypeStruct((16, rows, 3 * width), half),) * layers,
        in_specs=[vmem] * 7,
        out_specs=tuple([vmem] * (6 + layers)),
        scratch_shapes=[
            pltpu.VMEM((padded, features), half),
            pltpu.VMEM((16, room, features), half),
            pltpu.VMEM((16, 1, 128), jnp.int32),
            pltpu.VMEM((tokens, 1), jnp.int32),
            pltpu.VMEM((tokens, 1), jnp.float32),
            dma((2, 32)),
            dma((2, 32)),
            dma((2, 16)),
            dma((2, 16)),
            dma((2, pieces, 3)),
            dma((2, pieces, 4)),
            dma((2, pieces, 8)),
            dma((2, pieces, 8)),
            dma((2, pieces, 8)),
            dma((2, layers)),
        ],
        compiler_params=pltpu.CompilerParams(
            collective_id=collective_id, has_side_effects=True, vmem_limit_bytes=48 * 1024 * 1024
        ),
        cost_estimate=pl.CostEstimate(flops=0, bytes_accessed=150_000_000, transcendentals=0),
        name="exchange_start",
    )(ids.reshape(-1, 1), ids.reshape(1, -1), packet, vec_rows, attn, ffn, word_table)


WIDTHS = (D, D * 2 // 3, D // 3, D // 6, D // 12)


def gather_rows(block_ref, all_ref, z_sem, near_sem):
    d = lax.axis_index("dp")
    z = lax.axis_index("zero")
    line, spot = z // 4, lax.rem(z, 4)

    def at_line(k):
        return lax.rem(line + k, 4) * 4 + spot

    def near_by(j):
        across = j // 4
        return lax.rem(d + across, 2), line * 4 + lax.rem(spot + j % 4, 4)

    barrier = pltpu.get_barrier_semaphore()
    for k in range(1, 4):
        pl.semaphore_signal(barrier, inc=1, device_id=(d, at_line(k)), device_id_type=MESH)
    for j in range(1, 8):
        pl.semaphore_signal(barrier, inc=1, device_id=near_by(j), device_id_type=MESH)
    pl.semaphore_wait(barrier, 10)

    def z_copy(k):
        return pltpu.make_async_remote_copy(
            src_ref=block_ref,
            dst_ref=all_ref.at[d * 16 + z],
            send_sem=z_sem.at[0, k],
            recv_sem=z_sem.at[1, k],
            device_id=(d, at_line(k)),
            device_id_type=MESH,
        )

    def z_arrival(k):
        ref = all_ref.at[d * 16 + at_line(4 - k)]
        return pltpu.make_async_remote_copy(
            src_ref=ref,
            dst_ref=ref,
            send_sem=z_sem.at[0, k],
            recv_sem=z_sem.at[1, k],
            device_id=(d, at_line(k)),
            device_id_type=MESH,
        )

    def near_copy(i, j, from_d, from_z):
        ref = all_ref.at[from_d * 16 + from_z]
        return pltpu.make_async_remote_copy(
            src_ref=ref,
            dst_ref=ref,
            send_sem=near_sem.at[0, i, j],
            recv_sem=near_sem.at[1, i, j],
            device_id=near_by(j),
            device_id_type=MESH,
        )

    for k in range(1, 4):
        z_copy(k).start()
    all_ref[d * 16 + z] = block_ref[...]
    for j in range(1, 8):
        near_copy(0, j, d, z).start()
    for k in range(1, 4):
        z_arrival(k).wait_recv()
        for j in range(1, 8):
            near_copy(4 - k, j, d, at_line(4 - k)).start()
    for i in range(4):
        for j in range(1, 8):
            back = lax.rem(line + i, 4) * 4 + lax.rem(spot + 4 - j % 4, 4)
            near_copy(i, j, lax.rem(d + j // 4, 2), back).wait_recv()
            near_copy(i, j, d, at_line(i)).wait_send()
    for k in range(1, 4):
        z_copy(k).wait_send()


def contrastive_kernel(
    block_ref, false_ref, pair_ref, loss_ref, own_ref, all_ref, pooled_ref, grad_ref, z_sem, near_sem
):
    me = lax.axis_index("dp") * 16 + lax.axis_index("zero")
    gather_rows(block_ref, all_ref, z_sem, near_sem)
    upper = lax.broadcasted_iota(jnp.int32, (8, 1), 0) < 4
    for kind in range(2):
        for two in range(all_ref.shape[0] // 2):
            even = all_ref[2 * two, kind].astype(jnp.float32)
            odd = all_ref[2 * two + 1, kind].astype(jnp.float32)
            at = slice(8 * two, 8 * two + 8)
            pooled_ref[kind, 0, at, :] = jnp.where(upper, even, pltpu.roll(odd, 4, 0))
            pooled_ref[kind, 1, at, :] = jnp.where(upper, pltpu.roll(even, 4, 0), odd)
    contrastive_math(pooled_ref, false_ref, pair_ref, loss_ref, grad_ref)
    first = pl.multiple_of(me // 2 * 8, 8)
    swap = lax.rem(me, 2) == 1
    for kind in range(2):
        for role in range(2):
            rows = grad_ref[kind, role, pl.ds(first, 8), :]
            own_ref[kind, role] = jnp.where(swap, pltpu.roll(rows, 4, 0), rows)


def contrastive_math(pooled_ref, false_ref, pair_ref, loss_ref, grad_ref):
    pairs = false_ref.shape[0]
    high = lax.Precision.HIGHEST
    columns = lax.broadcasted_iota(jnp.int32, (pairs, pairs), 1)
    hit = columns == pair_ref[...]
    kept = (false_ref[...] == 0) | hit
    hits = hit.astype(jnp.float32)
    valid = (pair_ref[...] >= 0).astype(jnp.float32)
    inverse = 1.0 / jnp.maximum(jnp.sum(valid, axis=0, keepdims=True), 1.0)
    weight = valid * inverse
    named = jnp.sum(hits, axis=1, keepdims=True)
    totals = jnp.zeros((pairs, 1), jnp.float32)
    for first, width in enumerate(WIDTHS):
        span = -(-width // 128) * 128
        inside = lax.broadcasted_iota(jnp.int32, (1, span), 1) < width
        units, scales, logs = [], [], []
        for kind in range(2):
            pair_units, pair_scales = [], []
            for role in range(2):
                rows = jnp.where(inside, pooled_ref[kind, role, :, 0:span], 0.0)
                scale = lax.rsqrt(jnp.sum(rows * rows, axis=1, keepdims=True) + NORM_EPS)
                pair_units.append(rows * scale)
                pair_scales.append(scale)
            sims = lax.dot_general(
                pair_units[0],
                pair_units[1],
                (((1,), (1,)), ((), ())),
                precision=high,
                preferred_element_type=jnp.float32,
            )
            sims = jnp.where(kept, sims / SOFTMAX_TEMP, MASKED)
            shifted = sims - jnp.max(sims, axis=1, keepdims=True)
            logs.append(shifted - jnp.log(jnp.sum(jnp.exp(shifted), axis=1, keepdims=True)))
            units.append(pair_units)
            scales.append(pair_scales)
        shallow, deep = logs
        p_shallow, p_deep = jnp.exp(shallow), jnp.exp(deep)
        gap = p_deep * (deep - shallow)
        spread = jnp.sum(gap, axis=1, keepdims=True)
        totals = totals + spread - jnp.sum(jnp.where(hit, shallow + deep, 0.0), axis=1, keepdims=True)
        d_sims = (
            p_shallow * (named + 1.0) - hits - p_deep,
            gap + p_deep * (named - spread) - hits,
        )
        for kind in range(2):
            d_cos = jnp.where(kept, d_sims[kind] * weight, 0.0) / SOFTMAX_TEMP
            for role in range(2):
                unit = units[kind][role]
                d_unit = lax.dot_general(
                    d_cos,
                    units[kind][1 - role],
                    (((1 - role,), (0,)), ((), ())),
                    precision=high,
                    preferred_element_type=jnp.float32,
                )
                along = jnp.sum(d_unit * unit, axis=1, keepdims=True)
                d_rows = scales[kind][role] * (d_unit - unit * along)
                if first == 0:
                    grad_ref[kind, role] = d_rows
                else:
                    grad_ref[kind, role, :, 0:span] = grad_ref[kind, role, :, 0:span] + d_rows
    loss_ref[...] = jnp.broadcast_to(
        jnp.sum(totals * valid, axis=0, keepdims=True) * inverse, loss_ref.shape
    )


def contrastive(block, false_all, pair_all, collective_id):
    vmem = pl.BlockSpec(memory_space=pltpu.VMEM)
    pairs = false_all.shape[0]
    dma = pltpu.SemaphoreType.DMA
    whole = pltpu.VMEM((2, 2, pairs, D), jnp.float32)
    loss, grads = pl.pallas_call(
        contrastive_kernel,
        out_shape=(
            jax.ShapeDtypeStruct((8, 128), jnp.float32),
            jax.ShapeDtypeStruct((2, 2, 8, D), jnp.float32),
        ),
        in_specs=[vmem] * 3,
        out_specs=(vmem, vmem),
        scratch_shapes=[
            pltpu.VMEM((32,) + block.shape, block.dtype),
            whole,
            whole,
            dma((2, 4)),
            dma((2, 4, 8)),
        ],
        compiler_params=pltpu.CompilerParams(
            collective_id=collective_id, has_side_effects=True, vmem_limit_bytes=32 * 1024 * 1024
        ),
        cost_estimate=pl.CostEstimate(flops=10**9, bytes_accessed=3_000_000, transcendentals=10**6),
        name="contrastive",
    )(block, false_all, pair_all.reshape(-1, 1))
    return loss[0, 0], grads


PAIRS_OF_HEADS = HEADS // 2


def by_side(rows):
    lane = lax.broadcasted_iota(jnp.int32, (1, 2 * HD), 1)
    zero = jnp.zeros_like(rows)
    return jnp.concatenate([jnp.where(lane < HD, rows, zero), jnp.where(lane < HD, zero, rows)])


def join_sides(stacked):
    lane = lax.broadcasted_iota(jnp.int32, (1, 2 * HD), 1)
    return jnp.where(lane < HD, stacked[:SEQ], stacked[SEQ:])


def contract(left, right, left_dim, right_dim):
    return lax.dot_general(
        left, right, (((left_dim,), (right_dim,)), ((), ())), preferred_element_type=jnp.float32
    )


def thirds(packed_ref):
    for pair in range(PAIRS_OF_HEADS):
        at = pair * 2 * HD
        yield [packed_ref[0, :, t * D + at : t * D + at + 2 * HD] for t in range(3)]


def probabilities(scores, valid):
    scores = jnp.where(valid, scores * HD ** (-0.5), MASKED)
    raised = jnp.exp(scores - jnp.max(scores, axis=1, keepdims=True))
    return raised * (1.0 / jnp.sum(raised, axis=1, keepdims=True))


def attention_kernel(mask_ref, packed_ref, context_ref):
    valid = mask_ref[0] > 0.0
    parts = list(thirds(packed_ref))
    scores = [contract(by_side(queries), keys, 1, 1) for queries, keys, _ in parts]
    probs = [probabilities(now, valid).astype(jnp.bfloat16) for now in scores]
    for pair in range(PAIRS_OF_HEADS):
        mixed = contract(probs[pair], parts[pair][2], 1, 0)
        at = pair * 2 * HD
        context_ref[0, :, at : at + 2 * HD] = join_sides(mixed).astype(jnp.bfloat16)


def attention_back_kernel(mask_ref, packed_ref, grad_ref, out_ref):
    valid = mask_ref[0] > 0.0
    parts = list(thirds(packed_ref))
    queries = [by_side(part[0]) for part in parts]
    grads = [
        by_side(grad_ref[0, :, pair * 2 * HD : (pair + 1) * 2 * HD])
        for pair in range(PAIRS_OF_HEADS)
    ]
    scores = [contract(now, part[1], 1, 1) for now, part in zip(queries, parts)]
    d_probs = [contract(now, part[2], 1, 1) for now, part in zip(grads, parts)]
    probs = [probabilities(now, valid) for now in scores]
    d_scores = []
    for now, d_now in zip(probs, d_probs):
        shared = jnp.sum(d_now * now, axis=1, keepdims=True)
        d_scores.append(jnp.where(valid, now * (d_now - shared), 0.0).astype(jnp.bfloat16))
    for pair in range(PAIRS_OF_HEADS):
        d_queries = join_sides(contract(d_scores[pair], parts[pair][1], 1, 0)) * HD ** (-0.5)
        d_keys = contract(d_scores[pair], queries[pair], 0, 0) * HD ** (-0.5)
        d_values = contract(probs[pair].astype(jnp.bfloat16), grads[pair], 0, 0)
        for third, now in enumerate((d_queries, d_keys, d_values)):
            at = third * D + pair * 2 * HD
            out_ref[0, :, at : at + 2 * HD] = now.astype(jnp.bfloat16)


def attention_call(kernel, mask, operands, features, name):
    count = operands[0].shape[0]

    def spec(last):
        return pl.BlockSpec((1, SEQ, last), lambda i: (i, 0, 0))

    return pl.pallas_call(
        kernel,
        grid=(count,),
        out_shape=jax.ShapeDtypeStruct((count, SEQ, features), jnp.bfloat16),
        in_specs=[pl.BlockSpec((1, 1, SEQ), lambda i: (i, 0, 0))]
        + [spec(operand.shape[2]) for operand in operands],
        out_specs=spec(features),
        compiler_params=pltpu.CompilerParams(vmem_limit_bytes=32 * 1024 * 1024),
        cost_estimate=pl.CostEstimate(
            flops=10**9, bytes_accessed=count * SEQ * D * 10, transcendentals=10**6
        ),
        name=name,
    )(mask, *operands)


GELU_SCALE = 0.7978845608028654


def feed_back_kernel(middle_ref, down_ref, up_weights, down_weights, bias_ref, *outs):
    active_ref, d_up_ref, d_first_ref, total_ref = outs
    middle, d_down = middle_ref[...], down_ref[...]
    tile = FF // 4
    d_first = jnp.zeros(d_first_ref.shape, jnp.float32)
    for start in range(0, FF, tile):
        at = slice(start, start + tile)
        upward = contract(middle, up_weights[:, at], 1, 0) + bias_ref[:, at]
        d_active = contract(d_down, down_weights[:, at], 1, 0).astype(jnp.bfloat16)
        square = upward * upward
        bent = jnp.tanh(GELU_SCALE * (upward + 0.044715 * (square * upward)))
        share = 0.5 * (1.0 + bent)
        inner = GELU_SCALE * (1.0 + 3.0 * 0.044715 * square)
        slope = share + 0.5 * upward * (1.0 - bent * bent) * inner
        active_ref[:, at] = (upward * share).astype(jnp.bfloat16)
        d_up = (d_active.astype(jnp.float32) * slope).astype(jnp.bfloat16)
        d_up_ref[:, at] = d_up
        d_first = d_first + contract(d_up, up_weights[:, at], 1, 1)
        found = jnp.sum(d_up.astype(jnp.float32), axis=0, keepdims=True)
        before = jnp.where(pl.program_id(0) == 0, 0.0, total_ref[:, at])
        total_ref[:, at] = before + found
    d_first_ref[...] = d_first


def feed_back(middle, d_down, weights, up_bias):
    tokens = middle.shape[0]
    rows = 256
    half = jnp.bfloat16

    def by_rows(columns):
        return pl.BlockSpec((rows, columns), lambda i: (i, 0))

    def matrix(which):
        return pl.BlockSpec((D, FF), lambda i: (0, which))

    whole = pl.BlockSpec((1, FF), lambda i: (0, 0))
    return pl.pallas_call(
        feed_back_kernel,
        grid=(tokens // rows,),
        out_shape=(
            jax.ShapeDtypeStruct((tokens, FF), half),
            jax.ShapeDtypeStruct((tokens, FF), half),
            jax.ShapeDtypeStruct((tokens, D), jnp.float32),
            jax.ShapeDtypeStruct((1, FF), jnp.float32),
        ),
        in_specs=[by_rows(D), by_rows(D), matrix(1), matrix(2), whole],
        out_specs=(by_rows(FF), by_rows(FF), by_rows(D), whole),
        compiler_params=pltpu.CompilerParams(vmem_limit_bytes=40 * 1024 * 1024),
        cost_estimate=pl.CostEstimate(
            flops=6 * tokens * D * FF, bytes_accessed=24 * tokens * D, transcendentals=tokens * FF
        ),
        name="feed_back",
    )(middle, d_down, weights, weights, up_bias.reshape(1, FF))


LAYER_ROWS = 8 + FF // D


def layer_vectors(rows):
    up = 5 + FF // D
    return [rows[i] for i in range(5)] + [rows[5:up].reshape(FF)] + [rows[up + i] for i in range(3)]


def layer_norm(values, gain, shift):
    center = values - jnp.mean(values, axis=-1, keepdims=True)
    spread = jnp.mean(center * center, axis=-1, keepdims=True)
    return center * lax.rsqrt(spread + NORM_EPS) * gain + shift


def embed_tokens(rows, vectors):
    return layer_norm(low_back(rows) + vectors[None, :SEQ], vectors[SEQ], vectors[SEQ + 1])


def norm_forward(values, gain, shift):
    center = values - jnp.mean(values, axis=-1, keepdims=True)
    inverse = lax.rsqrt(jnp.mean(center * center, axis=-1, keepdims=True) + NORM_EPS)
    normal = center * inverse
    return normal * gain + shift, normal, inverse


def norm_back(grad, normal, inverse, gain):
    scaled = grad * gain
    mean = jnp.mean(scaled, axis=-1, keepdims=True)
    along = jnp.mean(scaled * normal, axis=-1, keepdims=True)
    return (
        (scaled - mean - normal * along) * inverse,
        jnp.sum(grad * normal, axis=(0, 1)),
        jnp.sum(grad, axis=(0, 1)),
    )


def gelu(value):
    bent = jnp.tanh(GELU_SCALE * (value + 0.044715 * value * value * value))
    return 0.5 * value * (1.0 + bent)


EDGES = (0, 3 * D, 4 * D, 4 * D + FF, 4 * D + 2 * FF)


def four_matrices(weights):
    return [weights[:, first:last] for first, last in zip(EDGES, EDGES[1:])]


def layer_forward(hidden, weights, vectors, mask):
    in_weights, out_weights, up_weights, down_weights = four_matrices(weights)
    q_bias, v_bias, o_bias, gain_one, shift_one, up_bias, down_bias, gain_two, second_shift = (
        layer_vectors(vectors)
    )
    half = jnp.bfloat16
    entry = lax.optimization_barrier(hidden.astype(half))
    bias = jnp.concatenate([q_bias, jnp.zeros_like(q_bias), v_bias])
    packed = (matmul(entry, in_weights) + bias).astype(half)
    context = attention_call(attention_kernel, mask, [packed], D, "attention")
    attended = matmul(context, out_weights) + o_bias
    first, normal_one, inverse_one = norm_forward(hidden + attended, gain_one, shift_one)
    middle = lax.optimization_barrier(first.astype(half))
    upward = matmul(middle, up_weights) + up_bias
    active = lax.optimization_barrier(gelu(upward).astype(half))
    downward = einsum_plain("nsf,df->nsd", active, down_weights) + down_bias
    output, normal_two, inverse_two = norm_forward(first + downward, gain_two, second_shift)
    kept = (
        entry, packed, context, middle,
        normal_one, inverse_one, normal_two, inverse_two,
    )
    return output, kept


def layer_backward(kept, weights, vectors, mask, grad, midway):
    in_weights, out_weights, _, _ = four_matrices(weights)
    entry, packed, context, middle = kept[:4]
    normal_one, inverse_one, normal_two, inverse_two = kept[4:]
    gain_one, gain_two = layer_vectors(vectors)[3], layer_vectors(vectors)[7]
    half = jnp.bfloat16

    def total(value):
        return jnp.sum(value.astype(jnp.float32), axis=(0, 1))

    d_second, d_gain_two, d_shift_two = norm_back(grad, normal_two, inverse_two, gain_two)
    d_down = lax.optimization_barrier(d_second.astype(half))
    flat_middle, flat_down = middle.reshape(-1, D), d_down.reshape(-1, D)
    active, d_up, d_first, d_up_bias = feed_back(
        flat_middle, flat_down, weights, layer_vectors(vectors)[5]
    )
    feed_pairs = [(flat_middle, d_up), (flat_down, active)]
    d_first = midway(feed_pairs, d_second + d_first.reshape(d_second.shape))
    d_middle, d_gain_one, d_shift_one = norm_back(d_first, normal_one, inverse_one, gain_one)
    d_attended = lax.optimization_barrier(d_middle.astype(half))
    d_context = jnp.einsum(
        "nsd,ed->nse", d_attended, out_weights, preferred_element_type=jnp.float32
    ).astype(half)
    d_packed = attention_call(
        attention_back_kernel, mask, [packed, d_context], 3 * D, "attention_back"
    )
    d_hidden = d_middle + jnp.einsum(
        "nsp,dp->nsd", d_packed, in_weights, preferred_element_type=jnp.float32
    )
    packed_total = total(d_packed)
    pieces = [
        packed_total[:D], packed_total[2 * D :], total(d_attended), d_gain_one, d_shift_one,
        d_up_bias, total(d_down), d_gain_two, d_shift_two,
    ]
    d_vectors, at = jnp.zeros((LAYER_ROWS, D), jnp.float32), 0
    for piece in pieces:
        rows = piece.reshape(-1, D)
        d_vectors = d_vectors + jnp.pad(rows, ((at, LAYER_ROWS - at - rows.shape[0]), (0, 0)))
        at = at + rows.shape[0]
    flat = [
        (left.reshape(-1, left.shape[2]), right.reshape(-1, right.shape[2]))
        for left, right in ((entry, d_packed), (context, d_attended))
    ]
    return d_hidden, flat + feed_pairs, d_vectors


def weight_gradient(left, right):
    return lax.dot_general(
        left, right, (((0,), (0,)), ((), ())), preferred_element_type=jnp.float32
    ).astype(jnp.bfloat16)


def pool_rows(hidden, key_mask, seq_lengths):
    share = key_mask.astype(jnp.float32) / seq_lengths.astype(jnp.float32)[:, None]
    return jnp.sum(hidden * share[:, :, None], axis=1)


def normalized_rows(rows):
    return rows * lax.rsqrt(jnp.sum(rows * rows, axis=-1, keepdims=True) + NORM_EPS)


def contrastive_terms(shallow_anchor, deep_anchor, shallow_pos, deep_pos, false_neg, pair_index):
    columns = lax.broadcasted_iota(jnp.int32, false_neg.shape, 1)
    hit = columns == pair_index[:, None]
    kept_cols = (false_neg == 0) | hit
    valid_rows = (pair_index >= 0).astype(jnp.float32)
    totals = jnp.zeros(pair_index.shape, jnp.float32)
    for current_width in (D, D * 2 // 3, D // 3, D // 6, D // 12):
        log_probs = []
        for anchor_vectors, positive_rows in (
            (shallow_anchor, shallow_pos),
            (deep_anchor, deep_pos),
        ):
            similarity_scores = (
                jnp.dot(
                    normalized_rows(anchor_vectors[:, :current_width]),
                    normalized_rows(positive_rows[:, :current_width]).T,
                    precision=lax.Precision.HIGHEST,
                )
                / SOFTMAX_TEMP
            )
            similarity_scores = jnp.where(kept_cols, similarity_scores, MASKED)
            log_probs.append(jax.nn.log_softmax(similarity_scores, axis=-1))
        for log_now in log_probs:
            totals = totals - jnp.sum(jnp.where(hit, log_now, 0.0), axis=-1)
        totals = totals + jnp.sum(jnp.exp(log_probs[1]) * (log_probs[1] - log_probs[0]), axis=-1)
    return jnp.sum(totals * valid_rows)


def adam_update(master, gradient, first, second, step_rate):
    first_new = BETA_ONE * first + (1.0 - BETA_ONE) * gradient
    second_new = BETA_TWO * second + (1.0 - BETA_TWO) * gradient * gradient
    first_hat = first_new / (1.0 - BETA_ONE**ADAM_STEP)
    second_hat = second_new / (1.0 - BETA_TWO**ADAM_STEP)
    master_new = master - step_rate * (
        first_hat / (jnp.sqrt(second_hat) + ADAM_EPS) + WEIGHT_DECAY * master
    )
    return (master_new, first_new, second_new)


def pad_rows(flat, multiple):
    rows = -(-flat.shape[0] // (128 * multiple)) * multiple
    return jnp.pad(flat, (0, rows * 128 - flat.shape[0])).reshape(rows, 128)


def one_hot(index, size, dtype=jnp.bfloat16):
    return (index[:, None] == lax.broadcasted_iota(jnp.int32, (1, size), 1)).astype(dtype)


def token_plan(ids, shard_rows):
    places = lax.broadcasted_iota(jnp.int32, ids.shape, 0)
    same = ids[:, None] == ids[None, :]
    leader = jnp.min(jnp.where(same, places[None, :], ids.shape[0]), axis=1)
    leads = leader == places
    owner = ids // shard_rows
    low_id = owner * shard_rows
    ahead = leads[None, :] & (ids[None, :] >= low_id[:, None]) & (ids[None, :] < ids[:, None])
    place = jnp.sum(ahead.astype(jnp.int32), axis=1)
    return owner, place, ids - low_id


def round_slots(owner, place, local_row, round_index, room, nz):
    inside = (place >= round_index * room) & (place < (round_index + 1) * room)
    slot = jnp.where(inside, owner * room + place - round_index * room, -1)
    slots = lax.broadcasted_iota(jnp.int32, (1, nz * room), 1)
    asked = jnp.max(jnp.where(slot[:, None] == slots, local_row[:, None], -1), axis=0)
    return slot, asked


def body(
    token_ids,
    lengths,
    false_neg,
    pair_index,
    word_table,
    vectors,
    attn_w,
    ffn_w,
    word_first,
    vector_first,
    attn_first,
    ffn_first,
    word_second,
    vector_second,
    attn_second,
    ffn_second,
):
    ndp = lax.axis_size("dp")
    nz = lax.axis_size("zero")
    n = ndp * nz
    by_hand = (ndp, nz) == (2, 16) and token_ids.shape[0] * ndp * nz <= 256
    my_dp = lax.axis_index("dp")
    my_zero = lax.axis_index("zero")
    me = my_dp * nz + my_zero
    pair_rows = token_ids.shape[0]
    total_pairs = pair_rows * n
    flat_ids = token_ids.reshape(-1, SEQ)
    seq_rows = flat_ids.shape[0]
    tokens = seq_rows * SEQ
    seq_lengths = lengths.reshape(-1)
    key_mask = lax.broadcasted_iota(jnp.int32, flat_ids.shape, 1) < seq_lengths[:, None]
    shard_rows = word_table.shape[0]
    vec_len = vectors.shape[0]

    room = -(-(tokens * 9 // 8) // (nz * 8)) * 8
    ids = flat_ids.reshape(-1)

    def packet_of(asked, rounds_here):
        last = jnp.concatenate([pair_index, rounds_here[None].astype(jnp.int32)])
        lines = nz + false_neg.size // 128
        return jnp.concatenate(
            [
                jnp.pad(asked.reshape(nz, room), ((0, 0), (0, 128 - room)), constant_values=-1),
                false_neg.reshape(-1, 128),
                jnp.zeros((7 - lines % 8, 128), jnp.int32),
                jnp.pad(last, (0, 128 - last.shape[0]))[None],
            ]
        )

    def gather_layer(layer_index):
        both = jnp.concatenate(
            [attn_w[layer_index].astype(jnp.bfloat16), ffn_w[layer_index].astype(jnp.bfloat16)],
            axis=1,
        )
        return lax.all_gather(both, "zero", axis=0, tiled=True)

    if by_hand:
        packet = pad_rows(jnp.concatenate([false_neg.reshape(-1), pair_index]), 8)
        place, slot, packets, asked_mine, vec_parts, received, *gathered = exchange_start(
            ids,
            packet.astype(jnp.bfloat16),
            pad_rows(vectors.astype(jnp.bfloat16), 16),
            attn_w,
            ffn_w,
            word_table,
            room,
            0,
        )
        layer_weights = [part.reshape(D, -1) for part in gathered]
        rounds = jnp.max(asked_mine[:, 0, 127])
        asked_mine = asked_mine[:, 0, :room]
        packets = packets.reshape(n, -1).astype(jnp.int32)
        false_all = packets[:, : false_neg.size].reshape(total_pairs, total_pairs)
        pair_all = packets[:, false_neg.size : false_neg.size + pair_rows].reshape(total_pairs)
        place, slot = place.reshape(-1), slot.reshape(-1)
    else:
        owner, place, local_row = token_plan(ids, shard_rows)
        slot, asked = round_slots(owner, place, local_row, 0, room, nz)
        packets, vec_parts = exchange(
            [
                packet_of(asked, jnp.max(place) // room + 1),
                pad_rows(vectors.astype(jnp.bfloat16), 16),
            ],
            ["all", "zero"],
            ndp,
            nz,
            0,
            "gather_requests",
        )
        layer_weights = [gather_layer(layer_index) for layer_index in range(LAYERS)]
        asked_mine = lax.dynamic_index_in_dim(packets[:, :nz, :room], my_zero, 1, keepdims=False)
        false_all = packets[:, nz : nz + false_neg.size // 128].reshape(total_pairs, total_pairs)
        pair_all = packets[:, -1, :pair_rows].reshape(total_pairs)
        rounds = jnp.max(packets[:, -1, pair_rows])
    vec_all = vec_parts.reshape(nz, -1)[:, :vec_len].reshape(-1).astype(jnp.float32)

    asked_near = lax.dynamic_slice_in_dim(asked_mine, my_dp * nz, nz, 0)

    def rows_for(wanted):
        picked = one_hot(wanted.reshape(-1), shard_rows, jnp.float32)
        return jnp.dot(picked, word_table, precision=lax.Precision.HIGHEST).astype(jnp.bfloat16)

    def rows_from(slot_now, received):
        return matmul(one_hot(slot_now, nz * room), received.reshape(nz * room, D)).astype(
            jnp.bfloat16
        )

    if not by_hand:
        (received,) = exchange(
            [rows_for(asked_near).reshape(nz, room, D)], ["zero_p"], ndp, nz, 1, "send_rows"
        )
    rows = rows_from(slot, received)

    def round_of(round_index):
        owner = ids // shard_rows
        local_row = ids - owner * shard_rows
        return round_slots(owner, place, local_row, round_index, room, nz)

    def more_rows(state):
        round_index, rows_now = state
        slot_now, asked_now = round_of(round_index)
        wanted = lax.all_to_all(asked_now.reshape(nz, room), "zero", 0, 0, tiled=True)
        got = lax.all_to_all(rows_for(wanted).reshape(nz, room, D), "zero", 0, 0, tiled=True)
        return round_index + 1, rows_now + rows_from(slot_now, got)

    def further(step, *value):
        return lax.while_loop(lambda state: state[0] < rounds, step, (jnp.int32(1), *value))[1:]

    (rows,) = further(more_rows, rows)
    rows = rows.reshape(seq_rows, SEQ, D).astype(jnp.float32)

    vec_rows = vec_all.reshape(-1, D)
    edges = [0] + [SEQ + 2 + i * LAYER_ROWS for i in range(LAYERS + 1)]
    vec_parts = [vec_rows[first:last] for first, last in zip(edges, edges[1:])]
    embedded, embed_back = jax.vjp(embed_tokens, rows, vec_parts[0])
    hidden = embedded
    mask = key_mask.astype(jnp.float32)[:, None, :]
    saved = []
    pooled = []
    for layer_index in range(LAYERS):
        weights = layer_weights[layer_index]
        hidden, kept = layer_forward(hidden, weights, vec_parts[1 + layer_index], mask)
        saved.append(kept)
        pooled.append(pool_rows(hidden, key_mask, seq_lengths).astype(jnp.bfloat16))

    if by_hand and pair_rows == 4:
        block = jnp.stack(pooled).reshape(2, pair_rows, 2, D).transpose(0, 2, 1, 3)
        loss, pooled_grads = contrastive(block.reshape(2, 2 * pair_rows, D), false_all, pair_all, 2)
        pooled_grads = pooled_grads[:, :, :pair_rows]
    else:
        (pooled_all,) = exchange(
            [jnp.stack(pooled).reshape(-1, 128)], ["all"], ndp, nz, 2, "gather_pooled"
        )
        pooled_all = pooled_all.reshape(n, 2, pair_rows, 2, D).astype(jnp.float32)
        pooled_all = pooled_all.transpose(1, 3, 0, 2, 4).reshape(2, 2, total_pairs, D)

        def whole_loss(pooled_now):
            summed = contrastive_terms(
                pooled_now[0, 0],
                pooled_now[1, 0],
                pooled_now[0, 1],
                pooled_now[1, 1],
                false_all,
                pair_all,
            )
            valid_total = jnp.sum((pair_all >= 0).astype(jnp.float32))
            return summed / jnp.maximum(valid_total, 1.0)

        loss, pooled_grads = jax.value_and_grad(whole_loss)(pooled_all)
        pooled_grads = lax.dynamic_slice_in_dim(pooled_grads, me * pair_rows, pair_rows, 2)
    pooled_grads = pooled_grads.transpose(0, 2, 1, 3).reshape(2, seq_rows, D)
    shallow_back, deep_back = pooled_grads[0], pooled_grads[1]
    share = key_mask.astype(jnp.float32) / seq_lengths.astype(jnp.float32)[:, None]
    grad_hidden = jnp.zeros_like(embedded)
    weight_parts, layer_pairs = [], []
    vec_grads = [None] * LAYERS
    for layer_index in range(LAYERS - 1, -1, -1):
        if layer_index == LAYERS - 1:
            grad_hidden = grad_hidden + deep_back[:, None, :] * share[:, :, None]
        if layer_index == 0:
            grad_hidden = grad_hidden + shallow_back[:, None, :] * share[:, :, None]
        by_scatter = []

        def scatter(pairs, after):
            both = jnp.concatenate([weight_gradient(*pair) for pair in pairs], axis=1)
            both, after = lax.optimization_barrier((both, after))
            by_scatter.append(lax.psum_scatter(both, "zero", scatter_dimension=0, tiled=True))
            return after

        early = by_hand and layer_index == LAYERS - 1
        grad_hidden, pairs, vec_grads[layer_index] = layer_backward(
            saved[layer_index],
            layer_weights[layer_index],
            vec_parts[1 + layer_index],
            mask,
            grad_hidden,
            scatter if early else lambda pairs, after: after,
        )
        if not by_hand:
            grad_hidden = scatter(pairs, grad_hidden)
        layer_pairs.insert(0, pairs)
        weight_parts = by_scatter + weight_parts
    rows_grad, embed_grads = embed_back(grad_hidden)
    vec_grad = jnp.concatenate([embed_grads] + vec_grads, axis=0)
    down_local = jnp.stack([part[5 + FF // D] for part in vec_grads])

    rows_grad = rows_grad.reshape(tokens, D).astype(jnp.bfloat16)

    def slot_sums(slot_now):
        picked = one_hot(slot_now, nz * room)
        return lax.dot_general(
            picked, rows_grad, (((0,), (0,)), ((), ())), preferred_element_type=jnp.float32
        ).astype(jnp.bfloat16)

    def into_rows(wanted, sums):
        return lax.dot_general(
            one_hot(wanted.reshape(-1), shard_rows),
            sums.reshape(-1, D),
            (((0,), (0,)), ((), ())),
            preferred_element_type=jnp.float32,
        )

    down_each = down_local.reshape(LAYERS, nz, -1).transpose(1, 0, 2).reshape(nz, -1)
    down_len = down_each.shape[1]
    vec_blocks = jnp.concatenate([vec_grad.reshape(nz, vec_len), down_each], axis=1)
    lines = -(-vec_blocks.shape[1] // 1024) * 8
    vec_blocks = jnp.pad(vec_blocks, ((0, 0), (0, lines * 128 - vec_blocks.shape[1])))
    sums = slot_sums(slot).reshape(nz, room, D)

    def more_sums(state):
        round_index, grad_now, square_now = state
        slot_now, asked_now = round_of(round_index)
        wanted = lax.all_to_all(asked_now.reshape(nz, room), "zero", 0, 0, tiled=True)
        got = lax.all_to_all(slot_sums(slot_now).reshape(nz, room, D), "zero", 0, 0, tiled=True)
        wanted = lax.all_gather(wanted, "dp", axis=0, tiled=True)
        got = lax.all_gather(got, "dp", axis=0, tiled=True)
        grad_next = grad_now + into_rows(wanted, got)
        grown = jnp.sum(grad_next * grad_next) - jnp.sum(grad_now * grad_now)
        return round_index + 1, grad_next, square_now + lax.psum(grown, "zero")

    if by_hand:
        attn_shard, ffn_shard, word_grad, vec_sum, squares = exchange_gradients(
            layer_pairs[0] + layer_pairs[1][:2],
            vec_blocks.reshape(4, 2, 2, lines, 128),
            sums,
            weight_parts[0],
            asked_mine.reshape(ndp, 1, nz * room),
            shard_rows,
            vec_len,
            3,
        )
        vec_sum = vec_sum.reshape(-1)
        square_total = squares[0, 0]
    else:
        sums_all, vec_shares = exchange(
            [sums, vec_blocks.reshape(nz, lines, 128)],
            ["all_p", "all_p"],
            ndp,
            nz,
            3,
            "send_gradients",
        )
        vec_sum = jnp.sum(vec_shares.reshape(n, -1), axis=0)
        (weight_all,) = exchange([jnp.stack(weight_parts)], ["dp"], ndp, nz, 4, "sum_replicas")
        weight_sum = jnp.sum(weight_all.astype(jnp.float32), axis=0)
        attn_shard = weight_sum[:, :, : 4 * D]
        ffn_shard = weight_sum[:, :, 4 * D :]
        word_grad = into_rows(asked_mine, sums_all)
    vec_shard = vec_sum[:vec_len]
    down_shard = vec_sum[vec_len : vec_len + down_len].reshape(LAYERS, -1)

    if not by_hand:
        square_local = jnp.sum(word_grad * word_grad) + jnp.sum(vec_shard * vec_shard)
        square_local = square_local + jnp.sum(attn_shard * attn_shard)
        square_local = square_local + jnp.sum(ffn_shard * ffn_shard)
        (squares,) = exchange(
            [jnp.broadcast_to(square_local, (8, 128))], ["zero"], ndp, nz, 5, "gather_squares"
        )
        square_total = jnp.sum(squares[:, 0, 0])
    word_grad, square_total = further(more_sums, word_grad, square_total)
    grad_norm = jnp.sqrt(square_total)
    factor = jnp.minimum(1.0, CLIP_NORM / (grad_norm + 1e-06))
    word_new, word_first_new, word_second_new = adam_update(
        word_table, word_grad * factor, word_first, word_second, LEARN_RATE
    )
    vector_new, vector_first_new, vector_second_new = adam_update(
        vectors, vec_shard * factor, vector_first, vector_second, VECTOR_RATE
    )
    attn_new, attn_first_new, attn_second_new = adam_update(
        attn_w, attn_shard * factor, attn_first, attn_second, LEARN_RATE
    )
    ffn_new, ffn_first_new, ffn_second_new = adam_update(
        ffn_w, ffn_shard * factor, ffn_first, ffn_second, LEARN_RATE
    )
    return (
        loss,
        grad_norm,
        word_new,
        vector_new,
        attn_new,
        ffn_new,
        word_new.astype(jnp.bfloat16),
        vector_new.astype(jnp.bfloat16),
        attn_new.astype(jnp.bfloat16),
        ffn_new.astype(jnp.bfloat16),
        word_first_new,
        vector_first_new,
        attn_first_new,
        ffn_first_new,
        word_second_new,
        vector_second_new,
        attn_second_new,
        ffn_second_new,
        down_shard * factor,
    )


def solution(mesh):
    placed = (
        P(("dp", "zero"), None, None),
        P(("dp", "zero"), None),
        P(("dp", "zero"), None),
        P(("dp", "zero")),
        P("zero", None),
        P("zero"),
        P(None, "zero", None),
        P(None, "zero", None),
        P("zero", None),
        P("zero"),
        P(None, "zero", None),
        P(None, "zero", None),
        P("zero", None),
        P("zero"),
        P(None, "zero", None),
        P(None, "zero", None),
    )
    return jax.shard_map(
        body,
        mesh=mesh,
        in_specs=placed,
        out_specs=(
            P(),
            P(),
            P("zero", None),
            P("zero"),
            P(None, "zero", None),
            P(None, "zero", None),
            P("zero", None),
            P("zero"),
            P(None, "zero", None),
            P(None, "zero", None),
            P("zero", None),
            P("zero"),
            P(None, "zero", None),
            P(None, "zero", None),
            P("zero", None),
            P("zero"),
            P(None, "zero", None),
            P(None, "zero", None),
            P(None, "zero"),
        ),
        check_vma=False,
    )
```

```python
import functools

import jax
import jax.numpy as jnp
from jax import lax
from jax.experimental import pallas as pl
from jax.experimental.pallas import tpu as pltpu
from jax.sharding import PartitionSpec as P

D = 512
HEADS = 8
HD = 64
FF = 2048
SEQ = 128
LAYERS = 2
ADAM_STEP = 5


SOFTMAX_TEMP = 0.05
CLIP_NORM = 1.0
LEARN_RATE = 0.02
VECTOR_RATE = 0.15
BETA_ONE = 0.5
BETA_TWO = 0.5
WEIGHT_DECAY = 0.01
ADAM_EPS = 1e-08
NORM_EPS = 1e-06
MASKED = -1000000000.0

MESH = pl.DeviceIdType.MESH


def build_low():

    def rounder(value):
        return lax.optimization_barrier(value.astype(jnp.bfloat16)).astype(jnp.float32)

    def keep_fwd(value):
        return (rounder(value), None)

    def pass_bwd(kept, grad):
        return (grad,)

    wrapped = jax.custom_vjp(rounder)
    wrapped.defvjp(keep_fwd, pass_bwd)
    return wrapped


def build_low_back():

    def identity_fn(value):
        return value

    def keep_fwd(value):
        return (value, None)

    def round_bwd(kept, grad):
        return (low(grad),)

    wrapped = jax.custom_vjp(identity_fn)
    wrapped.defvjp(keep_fwd, round_bwd)
    return wrapped


def low(value):
    return build_low()(value)


def low_back(value):
    return build_low_back()(value)


def rounded(value):
    return low(low_back(value))


def matmul(left, right):
    return jnp.dot(left, right, preferred_element_type=jnp.float32)


def einsum_plain(form, left, right):
    return jnp.einsum(form, left, right, preferred_element_type=jnp.float32)


def exchange_kernel(modes, ndp, nz, *refs):
    count = len(modes)
    ins = refs[:count]
    outs = refs[count : 2 * count]
    sems = refs[2 * count :]
    d = lax.axis_index("dp")
    z = lax.axis_index("zero")
    me = d * nz + z
    n = ndp * nz

    def peer_of(group, k):
        if group == "dp":
            pd = lax.rem(d + k, ndp)
            return pd, z, pd
        if group == "zero":
            pz = lax.rem(z + k, nz)
            return d, pz, pz
        p = lax.rem(me + k, n)
        return p // nz, lax.rem(p, nz), p

    groups = {m.split("_")[0] for m in modes}
    sizes = {"all": n, "zero": nz, "dp": ndp}
    mine = {"all": me, "zero": z, "dp": d}
    barrier = pltpu.get_barrier_semaphore()
    meet = ["all"] if "all" in groups else sorted(groups)
    total = 0
    for group in meet:
        total += sizes[group] - 1

        def greet(k, carry, group=group):
            pd, pz, _ = peer_of(group, k)
            pl.semaphore_signal(barrier, inc=1, device_id=(pd, pz), device_id_type=MESH)
            return carry

        lax.fori_loop(1, sizes[group], greet, 0)
    pl.semaphore_wait(barrier, total)

    def make(a, k):
        mode = modes[a]
        group = mode.split("_")[0]
        pd, pz, _ = peer_of(group, k)
        src = ins[a].at[pz] if mode.endswith("_p") else ins[a]
        return pltpu.make_async_remote_copy(
            src_ref=src,
            dst_ref=outs[a].at[mine[group]],
            send_sem=sems[2 * a].at[k],
            recv_sem=sems[2 * a + 1].at[k],
            device_id=(pd, pz),
            device_id_type=MESH,
        )

    for a, mode in enumerate(modes):
        group = mode.split("_")[0]

        def begin(k, carry, a=a):
            make(a, k).start()
            return carry

        lax.fori_loop(1, sizes[group], begin, 0)
    for a, mode in enumerate(modes):
        group = mode.split("_")[0]
        if mode.endswith("_p"):
            outs[a][mine[group]] = ins[a][z]
        else:
            outs[a][mine[group]] = ins[a][...]
    for a, mode in enumerate(modes):
        group = mode.split("_")[0]

        def finish(k, carry, a=a):
            make(a, k).wait()
            return carry

        lax.fori_loop(1, sizes[group], finish, 0)


def exchange(arrays, modes, ndp, nz, collective_id, name):
    sizes = {"all": ndp * nz, "zero": nz, "dp": ndp}
    outs = []
    scratch = []
    moved = 0
    for array, mode in zip(arrays, modes):
        size = sizes[mode.split("_")[0]]
        block = array.shape[1:] if mode.endswith("_p") else array.shape
        outs.append(jax.ShapeDtypeStruct((size,) + block, array.dtype))
        scratch += [pltpu.SemaphoreType.DMA((size,)), pltpu.SemaphoreType.DMA((size,))]
        one = array.dtype.itemsize
        for s in block:
            one *= s
        moved += one * size
    vmem = pl.BlockSpec(memory_space=pltpu.VMEM)
    return pl.pallas_call(
        functools.partial(exchange_kernel, tuple(modes), ndp, nz),
        out_shape=tuple(outs),
        in_specs=[vmem] * len(arrays),
        out_specs=tuple([vmem] * len(arrays)),
        scratch_shapes=scratch,
        compiler_params=pltpu.CompilerParams(
            collective_id=collective_id, has_side_effects=True, vmem_limit_bytes=48 * 1024 * 1024
        ),
        cost_estimate=pl.CostEstimate(flops=0, bytes_accessed=20 * moved, transcendentals=0),
        name=name,
    )(*arrays)


CHUNK = 1024
LAG_Z = 3
REST_EACH = 4
HALVED = (2,)


def gradient_kernel(chunks, matrices, vec_len, *refs):
    take = iter(refs)
    pairs = [(next(take), next(take)) for _ in range(matrices)]
    vec_ref, sums_ref, near_ref, asked_ref = [next(take) for _ in range(4)]
    attn_out, ffn_out, word_out, vec_out, stats_out = [next(take) for _ in range(5)]
    held = [None if chunk[1] is None else next(take) for chunk in chunks]
    bufs = [[next(take) for _ in range(6 if chunk[4] else 5)] for chunk in chunks]
    near_buf, rows_ref, sum_ref, square_ref, squares_ref = [next(take) for _ in range(5)]
    left_buf, right_buf, fetch_sem = [next(take) for _ in range(3)]
    send_a, recv_a, send_y, recv_y, send_z, recv_z, send_x, recv_x = [next(take) for _ in range(8)]
    send_h, recv_h = next(take), next(take)
    row_send, row_recv, pass_send, pass_recv, near_sem, square_sem = [
        next(take) for _ in range(6)
    ]

    d = lax.axis_index("dp")
    z = lax.axis_index("zero")
    core = lax.rem(z, 2)
    col = lax.rem(z // 2, 2)
    line = z // 4
    sibling = z + 1 - 2 * core
    across = z + 2 - 4 * col
    attn_width = attn_out.shape[2]

    def along(k):
        return lax.rem(line + k, 4) * 4 + lax.rem(z, 4)

    barrier = pltpu.get_barrier_semaphore()

    def greet(k, carry):
        pl.semaphore_signal(
            barrier, inc=1, device_id=(d, lax.rem(z + k, 16)), device_id_type=MESH
        )
        return carry

    lax.fori_loop(1, 16, greet, 0)
    pl.semaphore_signal(barrier, inc=1, device_id=(1 - d, z), device_id_type=MESH)
    pl.semaphore_wait(barrier, 16)

    def remote(src, dst, send, recv, to):
        return pltpu.make_async_remote_copy(
            src_ref=src,
            dst_ref=dst,
            send_sem=send,
            recv_sem=recv,
            device_id=to,
            device_id_type=MESH,
        )

    def part_of(i):
        return vec_ref if held[i] is None else held[i]

    def halves(i):
        return chunks[i][4]

    def after_y(i):
        return bufs[i][1 + halves(i)]

    def half_rows(i, which):
        rows = bufs[i][0].shape[2] // 2
        return pl.ds(pl.multiple_of(which * rows, 16), rows)

    def copy_a(i):
        src = part_of(i).at[:, :, 1 - core]
        return remote(src, bufs[i][0], send_a.at[i], recv_a.at[i], (d, sibling))

    def copy_h(i):
        src = bufs[i][0].at[:, :, half_rows(i, 1 - d)]
        return remote(src, bufs[i][1], send_h.at[i], recv_h.at[i], (1 - d, z))

    def copy_y(i):
        src = bufs[i][halves(i)].at[:, 1 - col]
        return remote(src, after_y(i), send_y.at[i], recv_y.at[i], (d, across))

    def copy_z(i, k):
        src = after_y(i).at[lax.rem(line + k, 4)]
        into = bufs[i][-3].at[k - 1]
        return remote(src, into, send_z.at[i, k - 1], recv_z.at[i, k - 1], (d, along(k)))

    def copy_x(i):
        return remote(bufs[i][-2], bufs[i][-1], send_x.at[i], recv_x.at[i], (1 - d, z))

    def row_push(k):
        to = lax.rem(z + k, 16)
        return remote(sums_ref.at[to], rows_ref.at[d, z], row_send.at[k], row_recv.at[k], (d, to))

    def row_pass(k):
        at = lax.rem(z + 16 - k, 16)
        return remote(
            rows_ref.at[d, at], rows_ref.at[d, at], pass_send.at[k], pass_recv.at[k], (1 - d, z)
        )

    near = remote(near_ref, near_buf, near_sem.at[0], near_sem.at[1], (1 - d, z))

    total = len(chunks)

    def push(k, carry):
        row_push(k).start()
        return carry

    lax.fori_loop(1, 16, push, 0)
    near.start()
    rows_ref[d, z] = sums_ref[z]
    row_pass(0).start()

    made = [i for i in range(total) if held[i] is not None]

    def fetches(i):
        _, matrix, start, width, _ = chunks[i]
        slot = made.index(i) % 2
        left, right = pairs[matrix]
        return (
            pltpu.make_async_copy(left, left_buf.at[slot], fetch_sem.at[0, slot]),
            pltpu.make_async_copy(
                right.at[:, pl.ds(start, width)],
                right_buf.at[slot, :, pl.ds(0, width)],
                fetch_sem.at[1, slot],
            ),
        )

    for copy in fetches(made[0]):
        copy.start()

    def compute(i):
        _, matrix, start, width, _ = chunks[i]
        if matrix is not None:
            place = made.index(i)
            slot = place % 2
            if place + 1 < len(made):
                for copy in fetches(made[place + 1]):
                    copy.start()
            for copy in fetches(i):
                copy.wait()

            def rows_of(j, carry):
                at = pl.ds(pl.multiple_of(j * 128, 128), 128)
                found = lax.dot_general(
                    left_buf[slot, :, at],
                    right_buf[slot, :, 0:width],
                    (((0,), (0,)), ((), ())),
                    preferred_element_type=jnp.float32,
                )
                held[i][j] = found.astype(jnp.bfloat16).reshape(2, 2, 32, width)
                return carry

            lax.fori_loop(0, 4, rows_of, 0)
        copy_a(i).start()

    def add_into(buf, count, place, mine):
        def add_block(b, carry):
            at = place(b)
            value = mine(b).astype(jnp.float32) + buf[at].astype(jnp.float32)
            buf[at] = value.astype(buf.dtype)
            return carry

        lax.fori_loop(0, count, add_block, 0)

    def stage_a(i):
        copy_a(i).wait_recv()
        add_into(
            bufs[i][0],
            8,
            lambda b: (b // 2, lax.rem(b, 2)),
            lambda b: part_of(i)[b // 2, lax.rem(b, 2), core],
        )
        (copy_h if halves(i) else copy_y)(i).start()

    def stage_h(i):
        copy_h(i).wait_recv()
        add_into(
            bufs[i][1],
            8,
            lambda b: (b // 2, lax.rem(b, 2)),
            lambda b: bufs[i][0][b // 2, lax.rem(b, 2), half_rows(i, d), :],
        )
        copy_y(i).start()

    def stage_y(i):
        copy_y(i).wait_recv()
        add_into(after_y(i), 4, lambda b: b, lambda b: bufs[i][halves(i)][b, col])
        for k in range(1, 4):
            copy_z(i, k).start()

    def stage_z(i):
        for k in range(1, 4):
            copy_z(i, k).wait_recv()
        value = after_y(i)[line].astype(jnp.float32)
        for k in range(3):
            value = value + bufs[i][-3][k].astype(jnp.float32)
        bufs[i][-2][...] = value.astype(bufs[i][-2].dtype)
        copy_x(i).start()

    def stage_x(i):
        target, _, start, width, _ = chunks[i]
        copy_x(i).wait_recv()
        mine, other = bufs[i][-2][...].astype(jnp.float32), bufs[i][-1][...].astype(jnp.float32)
        if target is None:
            vec_out[...] = mine + other
            return
        layer, first = target[0], target[1] + start
        out, first = (attn_out, first) if first < attn_width else (ffn_out, first - attn_width)
        if halves(i):
            out[layer, half_rows(i, d), first : first + width] = mine
            out[layer, half_rows(i, 1 - d), first : first + width] = other
        else:
            out[layer, :, first : first + width] = mine + other

    def steps_of(i):
        if halves(i):
            order = ((stage_a, 0), (stage_h, 1), (stage_y, 2), (stage_z, 2 + LAG_Z), (stage_x, 3 + LAG_Z))
        else:
            order = ((stage_a, 0), (stage_y, 1), (stage_z, 1 + LAG_Z), (stage_x, 2 + LAG_Z))
        return [(i + later, now) for now, later in order]

    def pass_on(k):
        row_push(k).wait_recv()
        row_pass(k).start()

    shard_rows, features = word_out.shape
    tiles = -(-shard_rows // 128)
    spots = rows_ref.shape[1] * rows_ref.shape[2]
    sum_ref[...] = jnp.zeros_like(sum_ref)

    def into_rows(plane, first, count):
        row = lax.broadcasted_iota(jnp.int32, (128, 1), 0) + first
        picked = (asked_ref[plane] == row).astype(jnp.bfloat16)
        return jnp.dot(
            picked, rows_ref[plane].reshape(spots, features), preferred_element_type=jnp.float32
        )[:count]

    def own_rows(tile):
        first, count = tile * 128, min(128, shard_rows - tile * 128)
        word_out[first : first + count, :] = into_rows(d, first, count)

    def all_arrived():
        def arrived(k, carry):
            ref = rows_ref.at[1 - d, lax.rem(z + 16 - k, 16)]
            remote(ref, ref, pass_send.at[k], pass_recv.at[k], (1 - d, z)).wait_recv()
            return carry

        lax.fori_loop(0, 16, arrived, 0)

    def other_rows(tile):
        first, count = tile * 128, min(128, shard_rows - tile * 128)
        value = word_out[first : first + count, :] + into_rows(1 - d, first, count)
        word_out[first : first + count, :] = value
        sum_ref[...] = sum_ref[...] + jnp.sum(value * value, axis=0, keepdims=True)

    rest = [functools.partial(own_rows, tile) for tile in range(tiles)]
    rest += [all_arrived] + [functools.partial(other_rows, tile) for tile in range(tiles)]

    compute(0)
    passed = 1
    for t in range(total + LAG_Z + 3):
        if t + 1 < total:
            compute(t + 1)
        for i in range(total - 1, -1, -1):
            for at, now in steps_of(i):
                if at == t:
                    now(i)
        until = min(16, 1 + (t + 1) * 15 // (total - 2))
        for k in range(passed, until):
            pass_on(k)
        passed = until
        if t >= total - 2:
            for _ in range(min(len(rest), REST_EACH)):
                rest.pop(0)()
    while rest:
        rest.pop(0)()

    near.wait()
    ffn_out[1] = near_ref[...].astype(jnp.float32) + near_buf[...].astype(jnp.float32)
    squares = sum_ref[...]
    square = jnp.sum(squares, axis=1, keepdims=True)
    for out in (attn_out, ffn_out):

        def of_rows(r, carry, out=out):
            at = pl.ds(pl.multiple_of(r * 8, 8), 8)
            for layer in range(out.shape[0]):
                value = out[layer, at, :]
                carry = carry + jnp.sum(value * value, axis=0, keepdims=True)
            return carry

        found = lax.fori_loop(
            0, out.shape[1] // 8, of_rows, jnp.zeros((1, out.shape[2]), jnp.float32)
        )
        square = square + jnp.sum(found, axis=1, keepdims=True)
    place = lax.broadcasted_iota(jnp.int32, vec_out.shape, 0) * 128 + lax.broadcasted_iota(
        jnp.int32, vec_out.shape, 1
    )
    value = jnp.where(place < vec_len, vec_out[...], 0.0)
    found = jnp.sum(value * value, axis=0, keepdims=True)
    square = square + jnp.sum(found, axis=1, keepdims=True)
    square_ref[...] = jnp.broadcast_to(square, square_ref.shape)

    def square_copy(k, slot):
        return remote(
            square_ref,
            squares_ref.at[slot],
            square_sem.at[0, k],
            square_sem.at[1, k],
            (d, lax.rem(z + k, 16)),
        )

    def send_square(k, carry):
        square_copy(k, z).start()
        return carry

    lax.fori_loop(1, 16, send_square, 0)
    squares_ref[z] = square_ref[...]

    for i in range(total):
        copy_a(i).wait_send()
        if halves(i):
            copy_h(i).wait_send()
        copy_y(i).wait_send()
        for k in range(1, 4):
            copy_z(i, k).wait_send()
        copy_x(i).wait_send()

    def finish(k, carry):
        row_push(k).wait_send()
        square_copy(k, lax.rem(z + 16 - k, 16)).wait_recv()
        square_copy(k, z).wait_send()
        return carry

    lax.fori_loop(1, 16, finish, 0)

    def finish_pass(k, carry):
        row_pass(k).wait_send()
        return carry

    lax.fori_loop(0, 16, finish_pass, 0)
    norm = squares_ref[0]
    for slot in range(1, 16):
        norm = norm + squares_ref[slot]
    stats_out[...] = jnp.broadcast_to(norm, stats_out.shape)


def exchange_gradients(pairs, vec_parts, sums, near, asked, shard_rows, vec_len, collective_id):
    spans = []
    for index, (_, right) in enumerate(pairs):
        layer, matrix = index // 4, index % 4
        columns = right.shape[1]
        width = columns // -(-columns // CHUNK)
        offset = sum(pairs[m][1].shape[1] for m in range(matrix))
        for start in range(0, columns, width):
            spans.append(((layer, offset), index, start, width, index in HALVED))
    plain = [chunk for chunk in spans if not chunk[4]]
    halved = [chunk for chunk in spans if chunk[4]]
    chunks = [(None, None, 0, 128, False)]
    while plain or halved:
        chunks += halved[:1] + plain[:1]
        halved, plain = halved[1:], plain[1:]
    half = jnp.bfloat16
    held, bufs = [], []
    for _, index, _, width, halves in chunks:
        kind = vec_parts.dtype if index is None else half
        r = vec_parts.shape[3] if index is None else 32
        if index is not None:
            held.append(pltpu.VMEM((4, 2, 2, r, width), kind))
        bufs.append(pltpu.VMEM((4, 2, r, width), kind))
        if halves:
            r = r // 2
            bufs.append(pltpu.VMEM((4, 2, r, width), kind))
        bufs += [
            pltpu.VMEM((4, r, width), kind),
            pltpu.VMEM((3, r, width), kind),
            pltpu.VMEM((r, width), kind),
            pltpu.VMEM((r, width), kind),
        ]
    features = sums.shape[2]
    dma = pltpu.SemaphoreType.DMA
    count = len(chunks)
    scratch = held + bufs
    scratch += [
        pltpu.VMEM(near.shape, half),
        pltpu.VMEM((2,) + sums.shape, half),
        pltpu.VMEM((1, features), jnp.float32),
        pltpu.VMEM((1, 128), jnp.float32),
        pltpu.VMEM((16, 1, 128), jnp.float32),
        pltpu.VMEM((2,) + pairs[0][0].shape, half),
        pltpu.VMEM((2, pairs[0][0].shape[0], max(chunk[3] for chunk in chunks)), half),
        dma((2, 2)),
    ]
    scratch += [dma((count,)) for _ in range(4)] + [dma((count, 3)) for _ in range(2)]
    scratch += [dma((count,)) for _ in range(4)]
    scratch += [dma((16,)) for _ in range(4)] + [dma((2,)), dma((2, 16))]
    rows = near.shape[0]
    outs = [
        jax.ShapeDtypeStruct((2, rows, 4 * D), jnp.float32),
        jax.ShapeDtypeStruct((2, rows, 2 * FF), jnp.float32),
        jax.ShapeDtypeStruct((shard_rows, features), jnp.float32),
        jax.ShapeDtypeStruct(vec_parts.shape[3:], jnp.float32),
        jax.ShapeDtypeStruct((8, 128), jnp.float32),
    ]
    vmem = pl.BlockSpec(memory_space=pltpu.VMEM)
    return pl.pallas_call(
        functools.partial(gradient_kernel, tuple(chunks), len(pairs), vec_len),
        out_shape=tuple(outs),
        in_specs=[pl.BlockSpec(memory_space=pl.ANY)] * (2 * len(pairs)) + [vmem] * 4,
        out_specs=tuple([vmem] * len(outs)),
        scratch_shapes=scratch,
        compiler_params=pltpu.CompilerParams(
            collective_id=collective_id, has_side_effects=True, vmem_limit_bytes=40 * 1024 * 1024
        ),
        cost_estimate=pl.CostEstimate(flops=0, bytes_accessed=200_000_000, transcendentals=0),
        name="exchange_gradients",
    )(*[array for pair in pairs for array in pair], vec_parts, sums, near, asked)


SPLITS = 4
WINDOW = 2
LAG = 3


def start_kernel(shard_rows, room, *refs):
    column_ref, row_ref, packet_ref, vec_ref, attn_ref, ffn_ref, word_ref = refs[:7]
    place_out, slot_out, packet_out, asked_out, vec_out, rows_out, *weight_outs = refs[7:15]
    table, rows_held, asked, words, own = refs[15:20]
    packet_sem, near_sem, far_sem, vec_sem, row_sem = refs[20:25]
    z_sem, y_sem, x_sem, d_sem, e_sem, own_sem, word_sem, self_sem = refs[25:]

    d = lax.axis_index("dp")
    z = lax.axis_index("zero")
    me = d * 16 + z
    core = lax.rem(z, 2)
    col = lax.rem(z // 2, 2)
    line = z // 4
    sibling = z + 1 - 2 * core
    across = z + 2 - 4 * col
    layers = attn_ref.shape[0]
    width = attn_ref.shape[2]
    whole = 3 * width
    unit = whole // 128 // SPLITS
    hand = unit * 5 // 12
    total = layers * SPLITS

    def everyone(k):
        p = lax.rem(me + k, 32)
        return (p // 16, lax.rem(p, 16))

    barrier = pltpu.get_barrier_semaphore()

    def greet(k, carry):
        pl.semaphore_signal(barrier, inc=1, device_id=everyone(k), device_id_type=MESH)
        return carry

    lax.fori_loop(1, 32, greet, 0)
    word_copy = pltpu.make_async_copy(word_ref, words, word_sem)
    word_copy.start()

    def self_copy(layer):
        return pltpu.make_async_copy(own.at[layer], weight_outs[layer].at[z], self_sem.at[layer])

    for layer in range(layers):
        own[layer, :, 0:width] = attn_ref[layer].astype(jnp.bfloat16)
        own[layer, :, width:whole] = ffn_ref[layer].astype(jnp.bfloat16)
        self_copy(layer).start()
    for layer in range(layers):
        self_copy(layer).wait()
    pl.semaphore_wait(barrier, 31)

    def remote(src, dst, sems, at, to):
        return pltpu.make_async_remote_copy(
            src_ref=src,
            dst_ref=dst,
            send_sem=sems.at[(0,) + at],
            recv_sem=sems.at[(1,) + at],
            device_id=to,
            device_id_type=MESH,
        )

    def packet_copy(k, slot):
        return remote(packet_ref, packet_out.at[slot], packet_sem, (k,), everyone(k))

    def near_copy(k, slot):
        to = lax.rem(z + k, 16)
        return remote(asked.at[to], asked_out.at[slot], near_sem, (k,), (d, to))

    def far_copy(k, slot):
        to = lax.rem(z + k, 16)
        return remote(asked.at[to], asked_out.at[slot], far_sem, (k,), (1 - d, to))

    def vec_copy(k, slot):
        return remote(vec_ref, vec_out.at[slot], vec_sem, (k,), (d, lax.rem(z + k, 16)))

    def row_copy(k, slot):
        to = lax.rem(z + k, 16)
        return remote(rows_held.at[to], rows_out.at[slot], row_sem, (k,), (d, to))

    def shard(i):
        at = lax.rem(line + i % 4, 4) * 4 + lax.rem(z, 4)
        return at if i < 4 else at + 2 - 4 * col

    def piece(s):
        layer, p = s // SPLITS, s % SPLITS
        size = unit if p < SPLITS - 1 else whole // 128 - p * unit
        return layer, p * unit, size

    def columns_of(at, s, first, size):
        layer, base, _ = piece(s)
        return weight_outs[layer].at[
            at, :, pl.ds(pl.multiple_of((base + first) * 128, 128), size * 128)
        ]

    def stretch(at, s, ours):
        size = piece(s)[2]
        return columns_of(at, s, ours * hand, size - hand)

    def handed(at, s, ours):
        size = piece(s)[2]
        return columns_of(at, s, ours * (size - hand), hand)

    def both(ref, sems, at, to):
        return remote(ref, ref, sems, at, to)

    def z_copy(s, k, at):
        to = lax.rem(line + k, 4) * 4 + lax.rem(z, 4)
        return both(stretch(at, s, d), z_sem, (s, k - 1), (d, to))

    def y_copy(s, j, at):
        return both(stretch(at, s, d), y_sem, (s, j), (d, across))

    def x_copy(s, i, at, ours):
        return both(handed(at, s, ours), x_sem, (s, i), (1 - d, z))

    def d_copy(s, i, at):
        return both(stretch(at, s, d), d_sem, (s, i), (d, sibling))

    def e_copy(s, i, at):
        return both(handed(at, s, 1 - d), e_sem, (s, i), (d, sibling))

    def own_copy(layer, at):
        ref = weight_outs[layer].at[at]
        return both(ref, own_sem, (layer,), (d, sibling))

    def spread(s, i):
        at = shard(i)
        if i < 4:
            y_copy(s, i, at).start()
        if i > 0:
            x_copy(s, i, at, d).start()
            d_copy(s, i, at).start()

    def open_piece(s):
        for k in range(1, 4):
            z_copy(s, k, z).start()
        spread(s, 0)

    for s in range(WINDOW):
        open_piece(s)

    tokens = column_ref.shape[0]
    ids_row = row_ref[...]
    lane = lax.broadcasted_iota(jnp.int32, (1, tokens), 1).astype(jnp.float32)
    block = 128

    def lead_of(b, least):
        ids = column_ref[pl.ds(pl.multiple_of(b * block, block), block), :]
        there = lax.broadcasted_iota(jnp.int32, (block, 1), 0) + b * block
        found = jnp.where(ids == ids_row, there.astype(jnp.float32), 1e9)
        return jnp.minimum(least, jnp.min(found, axis=0, keepdims=True))

    least = lax.fori_loop(0, tokens // block, lead_of, jnp.full((1, tokens), 1e9, jnp.float32))
    lead_ids = jnp.where(least == lane, ids_row, -1)

    lane128 = lax.broadcasted_iota(jnp.int32, (1, 128), 1).astype(jnp.float32)

    def place_of(b, carry):
        most, best = carry
        at = pl.ds(pl.multiple_of(b * block, block), block)
        ids = column_ref[at, :]
        owner = jnp.floor((ids.astype(jnp.float32) + 0.5) * (1.0 / shard_rows))
        low_id = owner.astype(jnp.int32) * shard_rows
        ahead = (lead_ids >= low_id) & (lead_ids < ids)
        place = jnp.sum(jnp.where(ahead, 1.0, 0.0), axis=1, keepdims=True)
        place_out[at, :] = place.astype(jnp.int32)
        inside = place < room
        slot_out[at, :] = jnp.where(inside, owner * room + place, -1.0).astype(jnp.int32)
        slot = jnp.broadcast_to(jnp.where(inside, owner * 128.0 + place, -1.0), (block, 128))
        local = jnp.broadcast_to((ids - low_id).astype(jnp.float32), (block, 128))
        grown = []
        for o in range(16):
            found = jnp.where(slot == o * 128.0 + lane128, local, -1.0)
            found = jnp.max(found.reshape(block // 8, 8, 128), axis=0)
            grown.append(jnp.maximum(best[o], found))
        return jnp.maximum(most, jnp.max(place, axis=0, keepdims=True)), tuple(grown)

    most, best = lax.fori_loop(
        0,
        tokens // block,
        place_of,
        (jnp.zeros((1, 1), jnp.float32), (jnp.full((8, 128), -1.0, jnp.float32),) * 16),
    )
    rounds = jnp.ones((1, 1), jnp.float32)
    for r in range(1, -(-tokens // room)):
        rounds = rounds + (most >= r * room).astype(jnp.float32)
    for o in range(16):
        found = jnp.max(best[o], axis=0, keepdims=True)
        asked[o] = jnp.where(lane128 == 127.0, rounds, found).astype(jnp.int32)

    def send_near(k, carry):
        near_copy(k, me).start()
        return carry

    lax.fori_loop(1, 16, send_near, 0)

    def send_far(k, carry):
        far_copy(k, me).start()
        return carry

    lax.fori_loop(0, 16, send_far, 0)

    def send_packets(k, carry):
        packet_copy(k, me).start()
        return carry

    lax.fori_loop(1, 32, send_packets, 0)

    def send_vec(k, carry):
        vec_copy(k, z).start()
        return carry

    lax.fori_loop(1, 16, send_vec, 0)
    for layer in range(layers):
        own_copy(layer, z).start()
    vec_out[z] = vec_ref[...]
    asked_out[me] = asked[z]
    packet_out[me] = packet_ref[...]

    body_rows = shard_rows // 16 * 16
    step = 112 if body_rows % 112 == 0 else 16

    def to_half(i, carry):
        at = pl.multiple_of(i * step, 16)
        table[pl.ds(at, step), :] = words[pl.ds(at, step), :].astype(jnp.bfloat16)
        return carry

    word_copy.wait()
    lax.fori_loop(0, body_rows // step, to_half, 0)
    padded = table.shape[0]
    table[body_rows:padded, :] = jnp.zeros((padded - body_rows, table.shape[1]), jnp.bfloat16)
    if shard_rows > body_rows:
        table[body_rows:shard_rows, :] = words[body_rows:shard_rows, :].astype(jnp.bfloat16)

    def answer_one(k, carry):
        src = lax.rem(z + k, 16)
        rows_at = lax.broadcasted_iota(jnp.int32, (padded, 128), 0)
        picked = (rows_at == asked_out[d * 16 + src]).astype(jnp.bfloat16)
        found = lax.dot_general(
            picked, table[...], (((0,), (0,)), ((), ())), preferred_element_type=jnp.float32
        )
        rows_held[src] = found[:room, :].astype(jnp.bfloat16)
        return carry

    def packet_in(k, carry):
        near_copy(k, d * 16 + lax.rem(z + 16 - k, 16)).wait_recv()
        return carry

    def row_start(k, carry):
        row_copy(k, z).start()
        return carry

    def z_phase(s):
        for k in range(1, 4):
            z_copy(s, k, shard(4 - k)).wait_recv()
            spread(s, 4 - k)
        if s + WINDOW < total:
            open_piece(s + WINDOW)

    def y_phase(s):
        for j in range(4):
            y_copy(s, j, shard(4 + j)).wait_recv()
            spread(s, 4 + j)

    def x_phase(s):
        for i in range(1, 8):
            at = shard(i)
            x_copy(s, i, at, 1 - d).wait_recv()
            e_copy(s, i, at).start()

    done = 0
    for t in range(total + LAG):
        if t < total:
            z_phase(t)
        if t == 1:
            lax.fori_loop(1, 16, packet_in, 0)
        if t >= 1:
            until = min(16, done + 4)
            if until > done:
                lax.fori_loop(done, until, answer_one, 0)
            done = until
        if t == total - 1:
            lax.fori_loop(1, 16, row_start, 0)
            rows_out[z] = rows_held[z]
        if 0 <= t - 1 < total:
            y_phase(t - 1)
        if 0 <= t - LAG < total:
            x_phase(t - LAG)

    turn = 1 - 2 * core
    for layer in range(layers):
        own_copy(layer, z + turn).wait_recv()
        own_copy(layer, z).wait_send()
    for s in range(total):
        for i in range(1, 8):
            at = shard(i)
            d_copy(s, i, at + turn).wait_recv()
            d_copy(s, i, at).wait_send()
            e_copy(s, i, at + turn).wait_recv()
            e_copy(s, i, at).wait_send()
            x_copy(s, i, at, d).wait_send()
        for k in range(1, 4):
            z_copy(s, k, z).wait_send()
        for i in range(4):
            y_copy(s, i, shard(i)).wait_send()

    def finish(k, carry):
        back = lax.rem(z + 16 - k, 16)
        row_copy(k, back).wait_recv()
        row_copy(k, z).wait_send()
        vec_copy(k, back).wait_recv()
        vec_copy(k, z).wait_send()
        near_copy(k, me).wait_send()
        return carry

    lax.fori_loop(1, 16, finish, 0)

    def finish_packets(k, carry):
        packet_copy(k, lax.rem(me + 32 - k, 32)).wait_recv()
        packet_copy(k, me).wait_send()
        return carry

    lax.fori_loop(1, 32, finish_packets, 0)

    def finish_far(k, carry):
        far_copy(k, (1 - d) * 16 + lax.rem(z + 16 - k, 16)).wait_recv()
        far_copy(k, me).wait_send()
        return carry

    lax.fori_loop(0, 16, finish_far, 0)


def exchange_start(ids, packet, vec_rows, attn, ffn, word_table, room, collective_id):
    half = jnp.bfloat16
    shard_rows, features = word_table.shape
    padded = -(-shard_rows // 128) * 128
    layers, rows, width = attn.shape
    tokens = ids.shape[0]
    pieces = layers * SPLITS
    dma = pltpu.SemaphoreType.DMA
    vmem = pl.BlockSpec(memory_space=pltpu.VMEM)
    anywhere = pl.BlockSpec(memory_space=pl.ANY)
    return pl.pallas_call(
        functools.partial(start_kernel, shard_rows, room),
        out_shape=(
            jax.ShapeDtypeStruct((tokens, 1), jnp.int32),
            jax.ShapeDtypeStruct((tokens, 1), jnp.int32),
            jax.ShapeDtypeStruct((32,) + packet.shape, packet.dtype),
            jax.ShapeDtypeStruct((32, 1, 128), jnp.int32),
            jax.ShapeDtypeStruct((16,) + vec_rows.shape, vec_rows.dtype),
            jax.ShapeDtypeStruct((16, room, features), half),
        )
        + (jax.ShapeDtypeStruct((16, rows, 3 * width), half),) * layers,
        in_specs=[vmem] * 6 + [anywhere],
        out_specs=tuple([vmem] * 6 + [anywhere] * layers),
        scratch_shapes=[
            pltpu.VMEM((padded, features), half),
            pltpu.VMEM((16, room, features), half),
            pltpu.VMEM((16, 1, 128), jnp.int32),
            pltpu.VMEM(word_table.shape, word_table.dtype),
            pltpu.VMEM((layers, rows, 3 * width), half),
            dma((2, 32)),
            dma((2, 16)),
            dma((2, 16)),
            dma((2, 16)),
            dma((2, 16)),
            dma((2, pieces, 3)),
            dma((2, pieces, 4)),
            dma((2, pieces, 8)),
            dma((2, pieces, 8)),
            dma((2, pieces, 8)),
            dma((2, layers)),
            dma,
            dma((layers,)),
        ],
        compiler_params=pltpu.CompilerParams(
            collective_id=collective_id, has_side_effects=True, vmem_limit_bytes=48 * 1024 * 1024
        ),
        cost_estimate=pl.CostEstimate(flops=0, bytes_accessed=150_000_000, transcendentals=0),
        name="exchange_start",
    )(ids.reshape(-1, 1), ids.reshape(1, -1), packet, vec_rows, attn, ffn, word_table)


WIDTHS = (D, D * 2 // 3, D // 3, D // 6, D // 12)


def gather_rows(block_ref, all_ref, z_sem, near_sem):
    d = lax.axis_index("dp")
    z = lax.axis_index("zero")
    line, spot = z // 4, lax.rem(z, 4)

    def at_line(k):
        return lax.rem(line + k, 4) * 4 + spot

    def near_by(j):
        across = j // 4
        return lax.rem(d + across, 2), line * 4 + lax.rem(spot + j % 4, 4)

    barrier = pltpu.get_barrier_semaphore()
    for k in range(1, 4):
        pl.semaphore_signal(barrier, inc=1, device_id=(d, at_line(k)), device_id_type=MESH)
    for j in range(1, 8):
        pl.semaphore_signal(barrier, inc=1, device_id=near_by(j), device_id_type=MESH)
    pl.semaphore_wait(barrier, 10)

    def z_copy(k):
        return pltpu.make_async_remote_copy(
            src_ref=block_ref,
            dst_ref=all_ref.at[d * 16 + z],
            send_sem=z_sem.at[0, k],
            recv_sem=z_sem.at[1, k],
            device_id=(d, at_line(k)),
            device_id_type=MESH,
        )

    def z_arrival(k):
        ref = all_ref.at[d * 16 + at_line(4 - k)]
        return pltpu.make_async_remote_copy(
            src_ref=ref,
            dst_ref=ref,
            send_sem=z_sem.at[0, k],
            recv_sem=z_sem.at[1, k],
            device_id=(d, at_line(k)),
            device_id_type=MESH,
        )

    def near_copy(i, j, from_d, from_z):
        ref = all_ref.at[from_d * 16 + from_z]
        return pltpu.make_async_remote_copy(
            src_ref=ref,
            dst_ref=ref,
            send_sem=near_sem.at[0, i, j],
            recv_sem=near_sem.at[1, i, j],
            device_id=near_by(j),
            device_id_type=MESH,
        )

    for k in range(1, 4):
        z_copy(k).start()
    all_ref[d * 16 + z] = block_ref[...]
    for j in range(1, 8):
        near_copy(0, j, d, z).start()
    for k in range(1, 4):
        z_arrival(k).wait_recv()
        for j in range(1, 8):
            near_copy(4 - k, j, d, at_line(4 - k)).start()
    for i in range(4):
        for j in range(1, 8):
            back = lax.rem(line + i, 4) * 4 + lax.rem(spot + 4 - j % 4, 4)
            near_copy(i, j, lax.rem(d + j // 4, 2), back).wait_recv()
            near_copy(i, j, d, at_line(i)).wait_send()
    for k in range(1, 4):
        z_copy(k).wait_send()


def contrastive_kernel(
    block_ref, false_ref, pair_ref, loss_ref, own_ref, all_ref, pooled_ref, grad_ref, z_sem, near_sem
):
    me = lax.axis_index("dp") * 16 + lax.axis_index("zero")
    gather_rows(block_ref, all_ref, z_sem, near_sem)
    upper = lax.broadcasted_iota(jnp.int32, (8, 1), 0) < 4
    for kind in range(2):
        for two in range(all_ref.shape[0] // 2):
            even = all_ref[2 * two, kind].astype(jnp.float32)
            odd = all_ref[2 * two + 1, kind].astype(jnp.float32)
            at = slice(8 * two, 8 * two + 8)
            pooled_ref[kind, 0, at, :] = jnp.where(upper, even, pltpu.roll(odd, 4, 0))
            pooled_ref[kind, 1, at, :] = jnp.where(upper, pltpu.roll(even, 4, 0), odd)
    contrastive_math(pooled_ref, false_ref, pair_ref, loss_ref, grad_ref)
    first = pl.multiple_of(me // 2 * 8, 8)
    swap = lax.rem(me, 2) == 1
    for kind in range(2):
        for role in range(2):
            rows = grad_ref[kind, role, pl.ds(first, 8), :]
            own_ref[kind, role] = jnp.where(swap, pltpu.roll(rows, 4, 0), rows)


def contrastive_math(pooled_ref, false_ref, pair_ref, loss_ref, grad_ref):
    pairs = false_ref.shape[0]
    high = lax.Precision.HIGHEST
    columns = lax.broadcasted_iota(jnp.int32, (pairs, pairs), 1)
    hit = columns == pair_ref[...]
    kept = (false_ref[...] == 0) | hit
    hits = hit.astype(jnp.float32)
    valid = (pair_ref[...] >= 0).astype(jnp.float32)
    inverse = 1.0 / jnp.maximum(jnp.sum(valid, axis=0, keepdims=True), 1.0)
    weight = valid * inverse
    named = jnp.sum(hits, axis=1, keepdims=True)
    totals = jnp.zeros((pairs, 1), jnp.float32)
    for first, width in enumerate(WIDTHS):
        span = -(-width // 128) * 128
        inside = lax.broadcasted_iota(jnp.int32, (1, span), 1) < width
        units, scales, logs = [], [], []
        for kind in range(2):
            pair_units, pair_scales = [], []
            for role in range(2):
                rows = jnp.where(inside, pooled_ref[kind, role, :, 0:span], 0.0)
                scale = lax.rsqrt(jnp.sum(rows * rows, axis=1, keepdims=True) + NORM_EPS)
                pair_units.append(rows * scale)
                pair_scales.append(scale)
            sims = lax.dot_general(
                pair_units[0],
                pair_units[1],
                (((1,), (1,)), ((), ())),
                precision=high,
                preferred_element_type=jnp.float32,
            )
            sims = jnp.where(kept, sims / SOFTMAX_TEMP, MASKED)
            shifted = sims - jnp.max(sims, axis=1, keepdims=True)
            logs.append(shifted - jnp.log(jnp.sum(jnp.exp(shifted), axis=1, keepdims=True)))
            units.append(pair_units)
            scales.append(pair_scales)
        shallow, deep = logs
        p_shallow, p_deep = jnp.exp(shallow), jnp.exp(deep)
        gap = p_deep * (deep - shallow)
        spread = jnp.sum(gap, axis=1, keepdims=True)
        totals = totals + spread - jnp.sum(jnp.where(hit, shallow + deep, 0.0), axis=1, keepdims=True)
        d_sims = (
            p_shallow * (named + 1.0) - hits - p_deep,
            gap + p_deep * (named - spread) - hits,
        )
        for kind in range(2):
            d_cos = jnp.where(kept, d_sims[kind] * weight, 0.0) / SOFTMAX_TEMP
            for role in range(2):
                unit = units[kind][role]
                d_unit = lax.dot_general(
                    d_cos,
                    units[kind][1 - role],
                    (((1 - role,), (0,)), ((), ())),
                    precision=high,
                    preferred_element_type=jnp.float32,
                )
                along = jnp.sum(d_unit * unit, axis=1, keepdims=True)
                d_rows = scales[kind][role] * (d_unit - unit * along)
                if first == 0:
                    grad_ref[kind, role] = d_rows
                else:
                    grad_ref[kind, role, :, 0:span] = grad_ref[kind, role, :, 0:span] + d_rows
    loss_ref[...] = jnp.broadcast_to(
        jnp.sum(totals * valid, axis=0, keepdims=True) * inverse, loss_ref.shape
    )


def contrastive(block, false_all, pair_all, collective_id):
    vmem = pl.BlockSpec(memory_space=pltpu.VMEM)
    pairs = false_all.shape[0]
    dma = pltpu.SemaphoreType.DMA
    whole = pltpu.VMEM((2, 2, pairs, D), jnp.float32)
    loss, grads = pl.pallas_call(
        contrastive_kernel,
        out_shape=(
            jax.ShapeDtypeStruct((8, 128), jnp.float32),
            jax.ShapeDtypeStruct((2, 2, 8, D), jnp.float32),
        ),
        in_specs=[vmem] * 3,
        out_specs=(vmem, vmem),
        scratch_shapes=[
            pltpu.VMEM((32,) + block.shape, block.dtype),
            whole,
            whole,
            dma((2, 4)),
            dma((2, 4, 8)),
        ],
        compiler_params=pltpu.CompilerParams(
            collective_id=collective_id, has_side_effects=True, vmem_limit_bytes=32 * 1024 * 1024
        ),
        cost_estimate=pl.CostEstimate(flops=10**9, bytes_accessed=3_000_000, transcendentals=10**6),
        name="contrastive",
    )(block, false_all, pair_all.reshape(-1, 1))
    return loss[0, 0], grads


PAIRS_OF_HEADS = HEADS // 2


def by_side(rows):
    lane = lax.broadcasted_iota(jnp.int32, (1, 2 * HD), 1)
    zero = jnp.zeros_like(rows)
    return jnp.concatenate([jnp.where(lane < HD, rows, zero), jnp.where(lane < HD, zero, rows)])


def join_sides(stacked):
    lane = lax.broadcasted_iota(jnp.int32, (1, 2 * HD), 1)
    return jnp.where(lane < HD, stacked[:SEQ], stacked[SEQ:])


def contract(left, right, left_dim, right_dim):
    return lax.dot_general(
        left, right, (((left_dim,), (right_dim,)), ((), ())), preferred_element_type=jnp.float32
    )


def thirds(packed_ref):
    for pair in range(PAIRS_OF_HEADS):
        at = pair * 2 * HD
        yield [packed_ref[0, :, t * D + at : t * D + at + 2 * HD] for t in range(3)]


def probabilities(scores, valid):
    scores = jnp.where(valid, scores * HD ** (-0.5), MASKED)
    raised = jnp.exp(scores - jnp.max(scores, axis=1, keepdims=True))
    return raised * (1.0 / jnp.sum(raised, axis=1, keepdims=True))


def attention_kernel(mask_ref, packed_ref, context_ref):
    valid = mask_ref[0] > 0.0
    parts = list(thirds(packed_ref))
    scores = [contract(by_side(queries), keys, 1, 1) for queries, keys, _ in parts]
    probs = [probabilities(now, valid).astype(jnp.bfloat16) for now in scores]
    for pair in range(PAIRS_OF_HEADS):
        mixed = contract(probs[pair], parts[pair][2], 1, 0)
        at = pair * 2 * HD
        context_ref[0, :, at : at + 2 * HD] = join_sides(mixed).astype(jnp.bfloat16)


def attention_back_kernel(mask_ref, packed_ref, grad_ref, out_ref):
    valid = mask_ref[0] > 0.0
    parts = list(thirds(packed_ref))
    queries = [by_side(part[0]) for part in parts]
    grads = [
        by_side(grad_ref[0, :, pair * 2 * HD : (pair + 1) * 2 * HD])
        for pair in range(PAIRS_OF_HEADS)
    ]
    scores = [contract(now, part[1], 1, 1) for now, part in zip(queries, parts)]
    d_probs = [contract(now, part[2], 1, 1) for now, part in zip(grads, parts)]
    probs = [probabilities(now, valid) for now in scores]
    d_scores = []
    for now, d_now in zip(probs, d_probs):
        shared = jnp.sum(d_now * now, axis=1, keepdims=True)
        d_scores.append(jnp.where(valid, now * (d_now - shared), 0.0).astype(jnp.bfloat16))
    for pair in range(PAIRS_OF_HEADS):
        d_queries = join_sides(contract(d_scores[pair], parts[pair][1], 1, 0)) * HD ** (-0.5)
        d_keys = contract(d_scores[pair], queries[pair], 0, 0) * HD ** (-0.5)
        d_values = contract(probs[pair].astype(jnp.bfloat16), grads[pair], 0, 0)
        for third, now in enumerate((d_queries, d_keys, d_values)):
            at = third * D + pair * 2 * HD
            out_ref[0, :, at : at + 2 * HD] = now.astype(jnp.bfloat16)


def attention_call(kernel, mask, operands, features, name):
    count = operands[0].shape[0]

    def spec(last):
        return pl.BlockSpec((1, SEQ, last), lambda i: (i, 0, 0))

    return pl.pallas_call(
        kernel,
        grid=(count,),
        out_shape=jax.ShapeDtypeStruct((count, SEQ, features), jnp.bfloat16),
        in_specs=[pl.BlockSpec((1, 1, SEQ), lambda i: (i, 0, 0))]
        + [spec(operand.shape[2]) for operand in operands],
        out_specs=spec(features),
        compiler_params=pltpu.CompilerParams(vmem_limit_bytes=32 * 1024 * 1024),
        cost_estimate=pl.CostEstimate(
            flops=10**9, bytes_accessed=count * SEQ * D * 10, transcendentals=10**6
        ),
        name=name,
    )(mask, *operands)


GELU_SCALE = 0.7978845608028654


def feed_back_kernel(middle_ref, down_ref, up_weights, down_weights, bias_ref, *outs):
    active_ref, d_up_ref, d_first_ref, total_ref = outs
    middle, d_down = middle_ref[...], down_ref[...]
    tile = FF // 4
    d_first = jnp.zeros(d_first_ref.shape, jnp.float32)
    for start in range(0, FF, tile):
        at = slice(start, start + tile)
        upward = contract(middle, up_weights[:, at], 1, 0) + bias_ref[:, at]
        d_active = contract(d_down, down_weights[:, at], 1, 0).astype(jnp.bfloat16)
        square = upward * upward
        bent = jnp.tanh(GELU_SCALE * (upward + 0.044715 * (square * upward)))
        share = 0.5 * (1.0 + bent)
        inner = GELU_SCALE * (1.0 + 3.0 * 0.044715 * square)
        slope = share + 0.5 * upward * (1.0 - bent * bent) * inner
        active_ref[:, at] = (upward * share).astype(jnp.bfloat16)
        d_up = (d_active.astype(jnp.float32) * slope).astype(jnp.bfloat16)
        d_up_ref[:, at] = d_up
        d_first = d_first + contract(d_up, up_weights[:, at], 1, 1)
        found = jnp.sum(d_up.astype(jnp.float32), axis=0, keepdims=True)
        before = jnp.where(pl.program_id(0) == 0, 0.0, total_ref[:, at])
        total_ref[:, at] = before + found
    d_first_ref[...] = d_first


def feed_back(middle, d_down, weights, up_bias):
    tokens = middle.shape[0]
    rows = 256
    half = jnp.bfloat16

    def by_rows(columns):
        return pl.BlockSpec((rows, columns), lambda i: (i, 0))

    def matrix(which):
        return pl.BlockSpec((D, FF), lambda i: (0, which))

    whole = pl.BlockSpec((1, FF), lambda i: (0, 0))
    return pl.pallas_call(
        feed_back_kernel,
        grid=(tokens // rows,),
        out_shape=(
            jax.ShapeDtypeStruct((tokens, FF), half),
            jax.ShapeDtypeStruct((tokens, FF), half),
            jax.ShapeDtypeStruct((tokens, D), jnp.float32),
            jax.ShapeDtypeStruct((1, FF), jnp.float32),
        ),
        in_specs=[by_rows(D), by_rows(D), matrix(1), matrix(2), whole],
        out_specs=(by_rows(FF), by_rows(FF), by_rows(D), whole),
        compiler_params=pltpu.CompilerParams(vmem_limit_bytes=40 * 1024 * 1024),
        cost_estimate=pl.CostEstimate(
            flops=6 * tokens * D * FF, bytes_accessed=24 * tokens * D, transcendentals=tokens * FF
        ),
        name="feed_back",
    )(middle, d_down, weights, weights, up_bias.reshape(1, FF))


LAYER_ROWS = 8 + FF // D


def layer_vectors(rows):
    up = 5 + FF // D
    return [rows[i] for i in range(5)] + [rows[5:up].reshape(FF)] + [rows[up + i] for i in range(3)]


def layer_norm(values, gain, shift):
    center = values - jnp.mean(values, axis=-1, keepdims=True)
    spread = jnp.mean(center * center, axis=-1, keepdims=True)
    return center * lax.rsqrt(spread + NORM_EPS) * gain + shift


def embed_tokens(rows, vectors):
    return layer_norm(low_back(rows) + vectors[None, :SEQ], vectors[SEQ], vectors[SEQ + 1])


def norm_forward(values, gain, shift):
    center = values - jnp.mean(values, axis=-1, keepdims=True)
    inverse = lax.rsqrt(jnp.mean(center * center, axis=-1, keepdims=True) + NORM_EPS)
    normal = center * inverse
    return normal * gain + shift, normal, inverse


def norm_back(grad, normal, inverse, gain):
    scaled = grad * gain
    mean = jnp.mean(scaled, axis=-1, keepdims=True)
    along = jnp.mean(scaled * normal, axis=-1, keepdims=True)
    return (
        (scaled - mean - normal * along) * inverse,
        jnp.sum(grad * normal, axis=(0, 1)),
        jnp.sum(grad, axis=(0, 1)),
    )


def gelu(value):
    bent = jnp.tanh(GELU_SCALE * (value + 0.044715 * value * value * value))
    return 0.5 * value * (1.0 + bent)


EDGES = (0, 3 * D, 4 * D, 4 * D + FF, 4 * D + 2 * FF)


def four_matrices(weights):
    return [weights[:, first:last] for first, last in zip(EDGES, EDGES[1:])]


def layer_forward(hidden, weights, vectors, mask):
    in_weights, out_weights, up_weights, down_weights = four_matrices(weights)
    q_bias, v_bias, o_bias, gain_one, shift_one, up_bias, down_bias, gain_two, second_shift = (
        layer_vectors(vectors)
    )
    half = jnp.bfloat16
    entry = lax.optimization_barrier(hidden.astype(half))
    bias = jnp.concatenate([q_bias, jnp.zeros_like(q_bias), v_bias])
    packed = (matmul(entry, in_weights) + bias).astype(half)
    context = attention_call(attention_kernel, mask, [packed], D, "attention")
    attended = matmul(context, out_weights) + o_bias
    first, normal_one, inverse_one = norm_forward(hidden + attended, gain_one, shift_one)
    middle = lax.optimization_barrier(first.astype(half))
    upward = matmul(middle, up_weights) + up_bias
    active = lax.optimization_barrier(gelu(upward).astype(half))
    downward = einsum_plain("nsf,df->nsd", active, down_weights) + down_bias
    output, normal_two, inverse_two = norm_forward(first + downward, gain_two, second_shift)
    kept = (
        entry, packed, context, middle,
        normal_one, inverse_one, normal_two, inverse_two,
    )
    return output, kept


def layer_backward(kept, weights, vectors, mask, grad, midway):
    in_weights, out_weights, _, _ = four_matrices(weights)
    entry, packed, context, middle = kept[:4]
    normal_one, inverse_one, normal_two, inverse_two = kept[4:]
    gain_one, gain_two = layer_vectors(vectors)[3], layer_vectors(vectors)[7]
    half = jnp.bfloat16

    def total(value):
        return jnp.sum(value.astype(jnp.float32), axis=(0, 1))

    d_second, d_gain_two, d_shift_two = norm_back(grad, normal_two, inverse_two, gain_two)
    d_down = lax.optimization_barrier(d_second.astype(half))
    flat_middle, flat_down = middle.reshape(-1, D), d_down.reshape(-1, D)
    active, d_up, d_first, d_up_bias = feed_back(
        flat_middle, flat_down, weights, layer_vectors(vectors)[5]
    )
    feed_pairs = [(flat_middle, d_up), (flat_down, active)]
    d_first = midway(feed_pairs, d_second + d_first.reshape(d_second.shape))
    d_middle, d_gain_one, d_shift_one = norm_back(d_first, normal_one, inverse_one, gain_one)
    d_attended = lax.optimization_barrier(d_middle.astype(half))
    d_context = jnp.einsum(
        "nsd,ed->nse", d_attended, out_weights, preferred_element_type=jnp.float32
    ).astype(half)
    d_packed = attention_call(
        attention_back_kernel, mask, [packed, d_context], 3 * D, "attention_back"
    )
    d_hidden = d_middle + jnp.einsum(
        "nsp,dp->nsd", d_packed, in_weights, preferred_element_type=jnp.float32
    )
    packed_total = total(d_packed)
    pieces = [
        packed_total[:D], packed_total[2 * D :], total(d_attended), d_gain_one, d_shift_one,
        d_up_bias, total(d_down), d_gain_two, d_shift_two,
    ]
    d_vectors, at = jnp.zeros((LAYER_ROWS, D), jnp.float32), 0
    for piece in pieces:
        rows = piece.reshape(-1, D)
        d_vectors = d_vectors + jnp.pad(rows, ((at, LAYER_ROWS - at - rows.shape[0]), (0, 0)))
        at = at + rows.shape[0]
    flat = [
        (left.reshape(-1, left.shape[2]), right.reshape(-1, right.shape[2]))
        for left, right in ((entry, d_packed), (context, d_attended))
    ]
    return d_hidden, flat + feed_pairs, d_vectors


def weight_gradient(left, right):
    return lax.dot_general(
        left, right, (((0,), (0,)), ((), ())), preferred_element_type=jnp.float32
    ).astype(jnp.bfloat16)


def pool_rows(hidden, key_mask, seq_lengths):
    share = key_mask.astype(jnp.float32) / seq_lengths.astype(jnp.float32)[:, None]
    return jnp.sum(hidden * share[:, :, None], axis=1)


def normalized_rows(rows):
    return rows * lax.rsqrt(jnp.sum(rows * rows, axis=-1, keepdims=True) + NORM_EPS)


def contrastive_terms(shallow_anchor, deep_anchor, shallow_pos, deep_pos, false_neg, pair_index):
    columns = lax.broadcasted_iota(jnp.int32, false_neg.shape, 1)
    hit = columns == pair_index[:, None]
    kept_cols = (false_neg == 0) | hit
    valid_rows = (pair_index >= 0).astype(jnp.float32)
    totals = jnp.zeros(pair_index.shape, jnp.float32)
    for current_width in (D, D * 2 // 3, D // 3, D // 6, D // 12):
        log_probs = []
        for anchor_vectors, positive_rows in (
            (shallow_anchor, shallow_pos),
            (deep_anchor, deep_pos),
        ):
            similarity_scores = (
                jnp.dot(
                    normalized_rows(anchor_vectors[:, :current_width]),
                    normalized_rows(positive_rows[:, :current_width]).T,
                    precision=lax.Precision.HIGHEST,
                )
                / SOFTMAX_TEMP
            )
            similarity_scores = jnp.where(kept_cols, similarity_scores, MASKED)
            log_probs.append(jax.nn.log_softmax(similarity_scores, axis=-1))
        for log_now in log_probs:
            totals = totals - jnp.sum(jnp.where(hit, log_now, 0.0), axis=-1)
        totals = totals + jnp.sum(jnp.exp(log_probs[1]) * (log_probs[1] - log_probs[0]), axis=-1)
    return jnp.sum(totals * valid_rows)


def adam_update(master, gradient, first, second, step_rate):
    first_new = BETA_ONE * first + (1.0 - BETA_ONE) * gradient
    second_new = BETA_TWO * second + (1.0 - BETA_TWO) * gradient * gradient
    first_hat = first_new / (1.0 - BETA_ONE**ADAM_STEP)
    second_hat = second_new / (1.0 - BETA_TWO**ADAM_STEP)
    master_new = master - step_rate * (
        first_hat / (jnp.sqrt(second_hat) + ADAM_EPS) + WEIGHT_DECAY * master
    )
    return (master_new, first_new, second_new)


def pad_rows(flat, multiple):
    rows = -(-flat.shape[0] // (128 * multiple)) * multiple
    return jnp.pad(flat, (0, rows * 128 - flat.shape[0])).reshape(rows, 128)


def one_hot(index, size, dtype=jnp.bfloat16):
    return (index[:, None] == lax.broadcasted_iota(jnp.int32, (1, size), 1)).astype(dtype)


def token_plan(ids, shard_rows):
    places = lax.broadcasted_iota(jnp.int32, ids.shape, 0)
    same = ids[:, None] == ids[None, :]
    leader = jnp.min(jnp.where(same, places[None, :], ids.shape[0]), axis=1)
    leads = leader == places
    owner = ids // shard_rows
    low_id = owner * shard_rows
    ahead = leads[None, :] & (ids[None, :] >= low_id[:, None]) & (ids[None, :] < ids[:, None])
    place = jnp.sum(ahead.astype(jnp.int32), axis=1)
    return owner, place, ids - low_id


def round_slots(owner, place, local_row, round_index, room, nz):
    inside = (place >= round_index * room) & (place < (round_index + 1) * room)
    slot = jnp.where(inside, owner * room + place - round_index * room, -1)
    slots = lax.broadcasted_iota(jnp.int32, (1, nz * room), 1)
    asked = jnp.max(jnp.where(slot[:, None] == slots, local_row[:, None], -1), axis=0)
    return slot, asked


def body(
    token_ids,
    lengths,
    false_neg,
    pair_index,
    word_table,
    vectors,
    attn_w,
    ffn_w,
    word_first,
    vector_first,
    attn_first,
    ffn_first,
    word_second,
    vector_second,
    attn_second,
    ffn_second,
):
    ndp = lax.axis_size("dp")
    nz = lax.axis_size("zero")
    n = ndp * nz
    by_hand = (ndp, nz) == (2, 16) and token_ids.shape[0] * ndp * nz <= 256
    my_dp = lax.axis_index("dp")
    my_zero = lax.axis_index("zero")
    me = my_dp * nz + my_zero
    pair_rows = token_ids.shape[0]
    total_pairs = pair_rows * n
    flat_ids = token_ids.reshape(-1, SEQ)
    seq_rows = flat_ids.shape[0]
    tokens = seq_rows * SEQ
    seq_lengths = lengths.reshape(-1)
    key_mask = lax.broadcasted_iota(jnp.int32, flat_ids.shape, 1) < seq_lengths[:, None]
    shard_rows = word_table.shape[0]
    vec_len = vectors.shape[0]

    room = -(-(tokens * 9 // 8) // (nz * 8)) * 8
    ids = flat_ids.reshape(-1)

    def packet_of(asked, rounds_here):
        last = jnp.concatenate([pair_index, rounds_here[None].astype(jnp.int32)])
        lines = nz + false_neg.size // 128
        return jnp.concatenate(
            [
                jnp.pad(asked.reshape(nz, room), ((0, 0), (0, 128 - room)), constant_values=-1),
                false_neg.reshape(-1, 128),
                jnp.zeros((7 - lines % 8, 128), jnp.int32),
                jnp.pad(last, (0, 128 - last.shape[0]))[None],
            ]
        )

    def gather_layer(layer_index):
        both = jnp.concatenate(
            [attn_w[layer_index].astype(jnp.bfloat16), ffn_w[layer_index].astype(jnp.bfloat16)],
            axis=1,
        )
        return lax.all_gather(both, "zero", axis=0, tiled=True)

    if by_hand:
        packet = pad_rows(jnp.concatenate([false_neg.reshape(-1), pair_index]), 8)
        place, slot, packets, asked_mine, vec_parts, received, *gathered = exchange_start(
            ids,
            packet.astype(jnp.bfloat16),
            pad_rows(vectors.astype(jnp.bfloat16), 16),
            attn_w,
            ffn_w,
            word_table,
            room,
            0,
        )
        layer_weights = [part.reshape(D, -1) for part in gathered]
        rounds = jnp.max(asked_mine[:, 0, 127])
        asked_mine = asked_mine[:, 0, :room]
        packets = packets.reshape(n, -1).astype(jnp.int32)
        false_all = packets[:, : false_neg.size].reshape(total_pairs, total_pairs)
        pair_all = packets[:, false_neg.size : false_neg.size + pair_rows].reshape(total_pairs)
        place, slot = place.reshape(-1), slot.reshape(-1)
    else:
        owner, place, local_row = token_plan(ids, shard_rows)
        slot, asked = round_slots(owner, place, local_row, 0, room, nz)
        packets, vec_parts = exchange(
            [
                packet_of(asked, jnp.max(place) // room + 1),
                pad_rows(vectors.astype(jnp.bfloat16), 16),
            ],
            ["all", "zero"],
            ndp,
            nz,
            0,
            "gather_requests",
        )
        layer_weights = [gather_layer(layer_index) for layer_index in range(LAYERS)]
        asked_mine = lax.dynamic_index_in_dim(packets[:, :nz, :room], my_zero, 1, keepdims=False)
        false_all = packets[:, nz : nz + false_neg.size // 128].reshape(total_pairs, total_pairs)
        pair_all = packets[:, -1, :pair_rows].reshape(total_pairs)
        rounds = jnp.max(packets[:, -1, pair_rows])
    vec_all = vec_parts.reshape(nz, -1)[:, :vec_len].reshape(-1).astype(jnp.float32)

    asked_near = lax.dynamic_slice_in_dim(asked_mine, my_dp * nz, nz, 0)

    def rows_for(wanted):
        picked = one_hot(wanted.reshape(-1), shard_rows, jnp.float32)
        return jnp.dot(picked, word_table, precision=lax.Precision.HIGHEST).astype(jnp.bfloat16)

    def rows_from(slot_now, received):
        return matmul(one_hot(slot_now, nz * room), received.reshape(nz * room, D)).astype(
            jnp.bfloat16
        )

    if not by_hand:
        (received,) = exchange(
            [rows_for(asked_near).reshape(nz, room, D)], ["zero_p"], ndp, nz, 1, "send_rows"
        )
    rows = rows_from(slot, received)

    def round_of(round_index):
        owner = ids // shard_rows
        local_row = ids - owner * shard_rows
        return round_slots(owner, place, local_row, round_index, room, nz)

    def more_rows(state):
        round_index, rows_now = state
        slot_now, asked_now = round_of(round_index)
        wanted = lax.all_to_all(asked_now.reshape(nz, room), "zero", 0, 0, tiled=True)
        got = lax.all_to_all(rows_for(wanted).reshape(nz, room, D), "zero", 0, 0, tiled=True)
        return round_index + 1, rows_now + rows_from(slot_now, got)

    def further(step, *value):
        return lax.while_loop(lambda state: state[0] < rounds, step, (jnp.int32(1), *value))[1:]

    (rows,) = further(more_rows, rows)
    rows = rows.reshape(seq_rows, SEQ, D).astype(jnp.float32)

    vec_rows = vec_all.reshape(-1, D)
    edges = [0] + [SEQ + 2 + i * LAYER_ROWS for i in range(LAYERS + 1)]
    vec_parts = [vec_rows[first:last] for first, last in zip(edges, edges[1:])]
    embedded, embed_back = jax.vjp(embed_tokens, rows, vec_parts[0])
    hidden = embedded
    mask = key_mask.astype(jnp.float32)[:, None, :]
    saved = []
    pooled = []
    for layer_index in range(LAYERS):
        weights = layer_weights[layer_index]
        hidden, kept = layer_forward(hidden, weights, vec_parts[1 + layer_index], mask)
        saved.append(kept)
        pooled.append(pool_rows(hidden, key_mask, seq_lengths).astype(jnp.bfloat16))

    if by_hand and pair_rows == 4:
        block = jnp.stack(pooled).reshape(2, pair_rows, 2, D).transpose(0, 2, 1, 3)
        loss, pooled_grads = contrastive(block.reshape(2, 2 * pair_rows, D), false_all, pair_all, 2)
        pooled_grads = pooled_grads[:, :, :pair_rows]
    else:
        (pooled_all,) = exchange(
            [jnp.stack(pooled).reshape(-1, 128)], ["all"], ndp, nz, 2, "gather_pooled"
        )
        pooled_all = pooled_all.reshape(n, 2, pair_rows, 2, D).astype(jnp.float32)
        pooled_all = pooled_all.transpose(1, 3, 0, 2, 4).reshape(2, 2, total_pairs, D)

        def whole_loss(pooled_now):
            summed = contrastive_terms(
                pooled_now[0, 0],
                pooled_now[1, 0],
                pooled_now[0, 1],
                pooled_now[1, 1],
                false_all,
                pair_all,
            )
            valid_total = jnp.sum((pair_all >= 0).astype(jnp.float32))
            return summed / jnp.maximum(valid_total, 1.0)

        loss, pooled_grads = jax.value_and_grad(whole_loss)(pooled_all)
        pooled_grads = lax.dynamic_slice_in_dim(pooled_grads, me * pair_rows, pair_rows, 2)
    pooled_grads = pooled_grads.transpose(0, 2, 1, 3).reshape(2, seq_rows, D)
    shallow_back, deep_back = pooled_grads[0], pooled_grads[1]
    share = key_mask.astype(jnp.float32) / seq_lengths.astype(jnp.float32)[:, None]
    grad_hidden = jnp.zeros_like(embedded)
    weight_parts, layer_pairs = [], []
    vec_grads = [None] * LAYERS
    for layer_index in range(LAYERS - 1, -1, -1):
        if layer_index == LAYERS - 1:
            grad_hidden = grad_hidden + deep_back[:, None, :] * share[:, :, None]
        if layer_index == 0:
            grad_hidden = grad_hidden + shallow_back[:, None, :] * share[:, :, None]
        by_scatter = []

        def scatter(pairs, after):
            both = jnp.concatenate([weight_gradient(*pair) for pair in pairs], axis=1)
            both, after = lax.optimization_barrier((both, after))
            by_scatter.append(lax.psum_scatter(both, "zero", scatter_dimension=0, tiled=True))
            return after

        early = by_hand and layer_index == LAYERS - 1
        grad_hidden, pairs, vec_grads[layer_index] = layer_backward(
            saved[layer_index],
            layer_weights[layer_index],
            vec_parts[1 + layer_index],
            mask,
            grad_hidden,
            scatter if early else lambda pairs, after: after,
        )
        if not by_hand:
            grad_hidden = scatter(pairs, grad_hidden)
        layer_pairs.insert(0, pairs)
        weight_parts = by_scatter + weight_parts
    rows_grad, embed_grads = embed_back(grad_hidden)
    vec_grad = jnp.concatenate([embed_grads] + vec_grads, axis=0)
    down_local = jnp.stack([part[5 + FF // D] for part in vec_grads])

    rows_grad = rows_grad.reshape(tokens, D).astype(jnp.bfloat16)

    def slot_sums(slot_now):
        picked = one_hot(slot_now, nz * room)
        return lax.dot_general(
            picked, rows_grad, (((0,), (0,)), ((), ())), preferred_element_type=jnp.float32
        ).astype(jnp.bfloat16)

    def into_rows(wanted, sums):
        return lax.dot_general(
            one_hot(wanted.reshape(-1), shard_rows),
            sums.reshape(-1, D),
            (((0,), (0,)), ((), ())),
            preferred_element_type=jnp.float32,
        )

    down_each = down_local.reshape(LAYERS, nz, -1).transpose(1, 0, 2).reshape(nz, -1)
    down_len = down_each.shape[1]
    vec_blocks = jnp.concatenate([vec_grad.reshape(nz, vec_len), down_each], axis=1)
    lines = -(-vec_blocks.shape[1] // 1024) * 8
    vec_blocks = jnp.pad(vec_blocks, ((0, 0), (0, lines * 128 - vec_blocks.shape[1])))
    sums = slot_sums(slot).reshape(nz, room, D)

    def more_sums(state):
        round_index, grad_now, square_now = state
        slot_now, asked_now = round_of(round_index)
        wanted = lax.all_to_all(asked_now.reshape(nz, room), "zero", 0, 0, tiled=True)
        got = lax.all_to_all(slot_sums(slot_now).reshape(nz, room, D), "zero", 0, 0, tiled=True)
        wanted = lax.all_gather(wanted, "dp", axis=0, tiled=True)
        got = lax.all_gather(got, "dp", axis=0, tiled=True)
        grad_next = grad_now + into_rows(wanted, got)
        grown = jnp.sum(grad_next * grad_next) - jnp.sum(grad_now * grad_now)
        return round_index + 1, grad_next, square_now + lax.psum(grown, "zero")

    if by_hand:
        attn_shard, ffn_shard, word_grad, vec_sum, squares = exchange_gradients(
            layer_pairs[0] + layer_pairs[1][:2],
            vec_blocks.reshape(4, 2, 2, lines, 128),
            sums,
            weight_parts[0],
            asked_mine.reshape(ndp, 1, nz * room),
            shard_rows,
            vec_len,
            3,
        )
        vec_sum = vec_sum.reshape(-1)
        square_total = squares[0, 0]
    else:
        sums_all, vec_shares = exchange(
            [sums, vec_blocks.reshape(nz, lines, 128)],
            ["all_p", "all_p"],
            ndp,
            nz,
            3,
            "send_gradients",
        )
        vec_sum = jnp.sum(vec_shares.reshape(n, -1), axis=0)
        (weight_all,) = exchange([jnp.stack(weight_parts)], ["dp"], ndp, nz, 4, "sum_replicas")
        weight_sum = jnp.sum(weight_all.astype(jnp.float32), axis=0)
        attn_shard = weight_sum[:, :, : 4 * D]
        ffn_shard = weight_sum[:, :, 4 * D :]
        word_grad = into_rows(asked_mine, sums_all)
    vec_shard = vec_sum[:vec_len]
    down_shard = vec_sum[vec_len : vec_len + down_len].reshape(LAYERS, -1)

    if not by_hand:
        square_local = jnp.sum(word_grad * word_grad) + jnp.sum(vec_shard * vec_shard)
        square_local = square_local + jnp.sum(attn_shard * attn_shard)
        square_local = square_local + jnp.sum(ffn_shard * ffn_shard)
        (squares,) = exchange(
            [jnp.broadcast_to(square_local, (8, 128))], ["zero"], ndp, nz, 5, "gather_squares"
        )
        square_total = jnp.sum(squares[:, 0, 0])
    word_grad, square_total = further(more_sums, word_grad, square_total)
    grad_norm = jnp.sqrt(square_total)
    factor = jnp.minimum(1.0, CLIP_NORM / (grad_norm + 1e-06))
    word_new, word_first_new, word_second_new = adam_update(
        word_table, word_grad * factor, word_first, word_second, LEARN_RATE
    )
    vector_new, vector_first_new, vector_second_new = adam_update(
        vectors, vec_shard * factor, vector_first, vector_second, VECTOR_RATE
    )
    attn_new, attn_first_new, attn_second_new = adam_update(
        attn_w, attn_shard * factor, attn_first, attn_second, LEARN_RATE
    )
    ffn_new, ffn_first_new, ffn_second_new = adam_update(
        ffn_w, ffn_shard * factor, ffn_first, ffn_second, LEARN_RATE
    )
    return (
        loss,
        grad_norm,
        word_new,
        vector_new,
        attn_new,
        ffn_new,
        word_new.astype(jnp.bfloat16),
        vector_new.astype(jnp.bfloat16),
        attn_new.astype(jnp.bfloat16),
        ffn_new.astype(jnp.bfloat16),
        word_first_new,
        vector_first_new,
        attn_first_new,
        ffn_first_new,
        word_second_new,
        vector_second_new,
        attn_second_new,
        ffn_second_new,
        down_shard * factor,
    )


def solution(mesh):
    placed = (
        P(("dp", "zero"), None, None),
        P(("dp", "zero"), None),
        P(("dp", "zero"), None),
        P(("dp", "zero")),
        P("zero", None),
        P("zero"),
        P(None, "zero", None),
        P(None, "zero", None),
        P("zero", None),
        P("zero"),
        P(None, "zero", None),
        P(None, "zero", None),
        P("zero", None),
        P("zero"),
        P(None, "zero", None),
        P(None, "zero", None),
    )
    return jax.shard_map(
        body,
        mesh=mesh,
        in_specs=placed,
        out_specs=(
            P(),
            P(),
            P("zero", None),
            P("zero"),
            P(None, "zero", None),
            P(None, "zero", None),
            P("zero", None),
            P("zero"),
            P(None, "zero", None),
            P(None, "zero", None),
            P("zero", None),
            P("zero"),
            P(None, "zero", None),
            P(None, "zero", None),
            P("zero", None),
            P("zero"),
            P(None, "zero", None),
            P(None, "zero", None),
            P(None, "zero"),
        ),
        check_vma=False,
    )
```

```python
import functools

import jax
import jax.numpy as jnp
from jax import lax
from jax.experimental import pallas as pl
from jax.experimental.pallas import tpu as pltpu
from jax.sharding import PartitionSpec as P

D = 512
HEADS = 8
HD = 64
FF = 2048
SEQ = 128
LAYERS = 2
ADAM_STEP = 5


SOFTMAX_TEMP = 0.05
CLIP_NORM = 1.0
LEARN_RATE = 0.02
VECTOR_RATE = 0.15
BETA_ONE = 0.5
BETA_TWO = 0.5
WEIGHT_DECAY = 0.01
ADAM_EPS = 1e-08
NORM_EPS = 1e-06
MASKED = -1000000000.0

MESH = pl.DeviceIdType.MESH


def build_low():

    def rounder(value):
        return lax.optimization_barrier(value.astype(jnp.bfloat16)).astype(jnp.float32)

    def keep_fwd(value):
        return (rounder(value), None)

    def pass_bwd(kept, grad):
        return (grad,)

    wrapped = jax.custom_vjp(rounder)
    wrapped.defvjp(keep_fwd, pass_bwd)
    return wrapped


def build_low_back():

    def identity_fn(value):
        return value

    def keep_fwd(value):
        return (value, None)

    def round_bwd(kept, grad):
        return (low(grad),)

    wrapped = jax.custom_vjp(identity_fn)
    wrapped.defvjp(keep_fwd, round_bwd)
    return wrapped


def low(value):
    return build_low()(value)


def low_back(value):
    return build_low_back()(value)


def rounded(value):
    return low(low_back(value))


def matmul(left, right):
    return jnp.dot(left, right, preferred_element_type=jnp.float32)


def einsum_plain(form, left, right):
    return jnp.einsum(form, left, right, preferred_element_type=jnp.float32)


def exchange_kernel(modes, ndp, nz, *refs):
    count = len(modes)
    ins = refs[:count]
    outs = refs[count : 2 * count]
    sems = refs[2 * count :]
    d = lax.axis_index("dp")
    z = lax.axis_index("zero")
    me = d * nz + z
    n = ndp * nz

    def peer_of(group, k):
        if group == "dp":
            pd = lax.rem(d + k, ndp)
            return pd, z, pd
        if group == "zero":
            pz = lax.rem(z + k, nz)
            return d, pz, pz
        p = lax.rem(me + k, n)
        return p // nz, lax.rem(p, nz), p

    groups = {m.split("_")[0] for m in modes}
    sizes = {"all": n, "zero": nz, "dp": ndp}
    mine = {"all": me, "zero": z, "dp": d}
    barrier = pltpu.get_barrier_semaphore()
    meet = ["all"] if "all" in groups else sorted(groups)
    total = 0
    for group in meet:
        total += sizes[group] - 1

        def greet(k, carry, group=group):
            pd, pz, _ = peer_of(group, k)
            pl.semaphore_signal(barrier, inc=1, device_id=(pd, pz), device_id_type=MESH)
            return carry

        lax.fori_loop(1, sizes[group], greet, 0)
    pl.semaphore_wait(barrier, total)

    def make(a, k):
        mode = modes[a]
        group = mode.split("_")[0]
        pd, pz, _ = peer_of(group, k)
        src = ins[a].at[pz] if mode.endswith("_p") else ins[a]
        return pltpu.make_async_remote_copy(
            src_ref=src,
            dst_ref=outs[a].at[mine[group]],
            send_sem=sems[2 * a].at[k],
            recv_sem=sems[2 * a + 1].at[k],
            device_id=(pd, pz),
            device_id_type=MESH,
        )

    for a, mode in enumerate(modes):
        group = mode.split("_")[0]

        def begin(k, carry, a=a):
            make(a, k).start()
            return carry

        lax.fori_loop(1, sizes[group], begin, 0)
    for a, mode in enumerate(modes):
        group = mode.split("_")[0]
        if mode.endswith("_p"):
            outs[a][mine[group]] = ins[a][z]
        else:
            outs[a][mine[group]] = ins[a][...]
    for a, mode in enumerate(modes):
        group = mode.split("_")[0]

        def finish(k, carry, a=a):
            make(a, k).wait()
            return carry

        lax.fori_loop(1, sizes[group], finish, 0)


def exchange(arrays, modes, ndp, nz, collective_id, name):
    sizes = {"all": ndp * nz, "zero": nz, "dp": ndp}
    outs = []
    scratch = []
    moved = 0
    for array, mode in zip(arrays, modes):
        size = sizes[mode.split("_")[0]]
        block = array.shape[1:] if mode.endswith("_p") else array.shape
        outs.append(jax.ShapeDtypeStruct((size,) + block, array.dtype))
        scratch += [pltpu.SemaphoreType.DMA((size,)), pltpu.SemaphoreType.DMA((size,))]
        one = array.dtype.itemsize
        for s in block:
            one *= s
        moved += one * size
    vmem = pl.BlockSpec(memory_space=pltpu.VMEM)
    return pl.pallas_call(
        functools.partial(exchange_kernel, tuple(modes), ndp, nz),
        out_shape=tuple(outs),
        in_specs=[vmem] * len(arrays),
        out_specs=tuple([vmem] * len(arrays)),
        scratch_shapes=scratch,
        compiler_params=pltpu.CompilerParams(
            collective_id=collective_id, has_side_effects=True, vmem_limit_bytes=48 * 1024 * 1024
        ),
        cost_estimate=pl.CostEstimate(flops=0, bytes_accessed=20 * moved, transcendentals=0),
        name=name,
    )(*arrays)


CHUNK = 1024
LAG_Z = 3
REST_EACH = 4
HALVED = (2,)


def gradient_kernel(chunks, matrices, vec_len, *refs):
    take = iter(refs)
    pairs = [(next(take), next(take)) for _ in range(matrices)]
    vec_ref, sums_ref, near_ref, asked_ref = [next(take) for _ in range(4)]
    attn_out, ffn_out, word_out, vec_out, stats_out = [next(take) for _ in range(5)]
    held = [None if chunk[1] is None else next(take) for chunk in chunks]
    bufs = [[next(take) for _ in range(6 if chunk[4] else 5)] for chunk in chunks]
    near_buf, rows_ref, sum_ref, square_ref, squares_ref = [next(take) for _ in range(5)]
    left_buf, right_buf, fetch_sem, near_held, local_sem = [next(take) for _ in range(5)]
    send_a, recv_a, send_y, recv_y, send_z, recv_z, send_x, recv_x = [next(take) for _ in range(8)]
    send_h, recv_h = next(take), next(take)
    row_send, row_recv, pass_send, pass_recv, near_sem, square_sem = [
        next(take) for _ in range(6)
    ]

    d = lax.axis_index("dp")
    z = lax.axis_index("zero")
    core = lax.rem(z, 2)
    col = lax.rem(z // 2, 2)
    line = z // 4
    sibling = z + 1 - 2 * core
    across = z + 2 - 4 * col
    attn_width = attn_out.shape[2]

    def along(k):
        return lax.rem(line + k, 4) * 4 + lax.rem(z, 4)

    barrier = pltpu.get_barrier_semaphore()

    def greet(k, carry):
        pl.semaphore_signal(
            barrier, inc=1, device_id=(d, lax.rem(z + k, 16)), device_id_type=MESH
        )
        return carry

    lax.fori_loop(1, 16, greet, 0)
    pl.semaphore_signal(barrier, inc=1, device_id=(1 - d, z), device_id_type=MESH)
    pl.semaphore_wait(barrier, 16)

    def remote(src, dst, send, recv, to):
        return pltpu.make_async_remote_copy(
            src_ref=src,
            dst_ref=dst,
            send_sem=send,
            recv_sem=recv,
            device_id=to,
            device_id_type=MESH,
        )

    def part_of(i):
        return vec_ref if held[i] is None else held[i]

    def halves(i):
        return chunks[i][4]

    def after_y(i):
        return bufs[i][1 + halves(i)]

    def half_rows(i, which):
        rows = bufs[i][0].shape[2] // 2
        return pl.ds(pl.multiple_of(which * rows, 16), rows)

    def copy_a(i):
        src = part_of(i).at[:, :, 1 - core]
        return remote(src, bufs[i][0], send_a.at[i], recv_a.at[i], (d, sibling))

    def copy_h(i):
        src = bufs[i][0].at[:, :, half_rows(i, 1 - d)]
        return remote(src, bufs[i][1], send_h.at[i], recv_h.at[i], (1 - d, z))

    def copy_y(i):
        src = bufs[i][halves(i)].at[:, 1 - col]
        return remote(src, after_y(i), send_y.at[i], recv_y.at[i], (d, across))

    def copy_z(i, k):
        src = after_y(i).at[lax.rem(line + k, 4)]
        into = bufs[i][-3].at[k - 1]
        return remote(src, into, send_z.at[i, k - 1], recv_z.at[i, k - 1], (d, along(k)))

    def copy_x(i):
        return remote(bufs[i][-2], bufs[i][-1], send_x.at[i], recv_x.at[i], (1 - d, z))

    def row_push(k):
        to = lax.rem(z + k, 16)
        return remote(sums_ref.at[to], rows_ref.at[d, z], row_send.at[k], row_recv.at[k], (d, to))

    def row_pass(k):
        at = lax.rem(z + 16 - k, 16)
        return remote(
            rows_ref.at[d, at], rows_ref.at[d, at], pass_send.at[k], pass_recv.at[k], (1 - d, z)
        )

    near = remote(near_ref, near_buf, near_sem.at[0], near_sem.at[1], (1 - d, z))

    total = len(chunks)

    def push(k, carry):
        row_push(k).start()
        return carry

    lax.fori_loop(1, 16, push, 0)
    near.start()
    near_copy = pltpu.make_async_copy(near_ref, near_held, local_sem.at[0])
    near_copy.start()
    own_copy = pltpu.make_async_copy(sums_ref.at[z], rows_ref.at[d, z], local_sem.at[1])
    own_copy.start()

    made = [i for i in range(total) if held[i] is not None]

    def fetches(i):
        _, matrix, start, width, _ = chunks[i]
        slot = made.index(i) % 2
        left, right = pairs[matrix]
        return (
            pltpu.make_async_copy(left, left_buf.at[slot], fetch_sem.at[0, slot]),
            pltpu.make_async_copy(
                right.at[:, pl.ds(start, width)],
                right_buf.at[slot, :, pl.ds(0, width)],
                fetch_sem.at[1, slot],
            ),
        )

    for copy in fetches(made[0]):
        copy.start()

    def compute(i):
        _, matrix, start, width, _ = chunks[i]
        if matrix is not None:
            place = made.index(i)
            slot = place % 2
            if place + 1 < len(made):
                for copy in fetches(made[place + 1]):
                    copy.start()
            for copy in fetches(i):
                copy.wait()

            def rows_of(j, carry):
                at = pl.ds(pl.multiple_of(j * 128, 128), 128)
                found = lax.dot_general(
                    left_buf[slot, :, at],
                    right_buf[slot, :, 0:width],
                    (((0,), (0,)), ((), ())),
                    preferred_element_type=jnp.float32,
                )
                held[i][j] = found.astype(jnp.bfloat16).reshape(2, 2, 32, width)
                return carry

            lax.fori_loop(0, 4, rows_of, 0)
        copy_a(i).start()

    def add_into(buf, count, place, mine):
        def add_block(b, carry):
            at = place(b)
            value = mine(b).astype(jnp.float32) + buf[at].astype(jnp.float32)
            buf[at] = value.astype(buf.dtype)
            return carry

        lax.fori_loop(0, count, add_block, 0)

    def stage_a(i):
        copy_a(i).wait_recv()
        add_into(
            bufs[i][0],
            8,
            lambda b: (b // 2, lax.rem(b, 2)),
            lambda b: part_of(i)[b // 2, lax.rem(b, 2), core],
        )
        (copy_h if halves(i) else copy_y)(i).start()

    def stage_h(i):
        copy_h(i).wait_recv()
        add_into(
            bufs[i][1],
            8,
            lambda b: (b // 2, lax.rem(b, 2)),
            lambda b: bufs[i][0][b // 2, lax.rem(b, 2), half_rows(i, d), :],
        )
        copy_y(i).start()

    def stage_y(i):
        copy_y(i).wait_recv()
        add_into(after_y(i), 4, lambda b: b, lambda b: bufs[i][halves(i)][b, col])
        for k in range(1, 4):
            copy_z(i, k).start()

    def stage_z(i):
        for k in range(1, 4):
            copy_z(i, k).wait_recv()
        value = after_y(i)[line].astype(jnp.float32)
        for k in range(3):
            value = value + bufs[i][-3][k].astype(jnp.float32)
        bufs[i][-2][...] = value.astype(bufs[i][-2].dtype)
        copy_x(i).start()

    def stage_x(i):
        target, _, start, width, _ = chunks[i]
        copy_x(i).wait_recv()
        mine, other = bufs[i][-2][...].astype(jnp.float32), bufs[i][-1][...].astype(jnp.float32)
        if target is None:
            vec_out[...] = mine + other
            return
        layer, first = target[0], target[1] + start
        out, first = (attn_out, first) if first < attn_width else (ffn_out, first - attn_width)
        if halves(i):
            out[layer, half_rows(i, d), first : first + width] = mine
            out[layer, half_rows(i, 1 - d), first : first + width] = other
        else:
            out[layer, :, first : first + width] = mine + other

    def steps_of(i):
        if halves(i):
            order = ((stage_a, 0), (stage_h, 1), (stage_y, 2), (stage_z, 2 + LAG_Z), (stage_x, 3 + LAG_Z))
        else:
            order = ((stage_a, 0), (stage_y, 1), (stage_z, 1 + LAG_Z), (stage_x, 2 + LAG_Z))
        return [(i + later, now) for now, later in order]

    def pass_on(k):
        row_push(k).wait_recv()
        row_pass(k).start()

    shard_rows, features = word_out.shape
    tiles = -(-shard_rows // 128)
    spots = rows_ref.shape[1] * rows_ref.shape[2]
    sum_ref[...] = jnp.zeros_like(sum_ref)

    def into_rows(plane, first, count):
        row = lax.broadcasted_iota(jnp.int32, (128, 1), 0) + first
        picked = (asked_ref[plane] == row).astype(jnp.bfloat16)
        return jnp.dot(
            picked, rows_ref[plane].reshape(spots, features), preferred_element_type=jnp.float32
        )[:count]

    def own_rows(tile):
        first, count = tile * 128, min(128, shard_rows - tile * 128)
        word_out[first : first + count, :] = into_rows(d, first, count)

    def all_arrived():
        def arrived(k, carry):
            ref = rows_ref.at[1 - d, lax.rem(z + 16 - k, 16)]
            remote(ref, ref, pass_send.at[k], pass_recv.at[k], (1 - d, z)).wait_recv()
            return carry

        lax.fori_loop(0, 16, arrived, 0)

    def other_rows(tile):
        first, count = tile * 128, min(128, shard_rows - tile * 128)
        value = word_out[first : first + count, :] + into_rows(1 - d, first, count)
        word_out[first : first + count, :] = value
        sum_ref[...] = sum_ref[...] + jnp.sum(value * value, axis=0, keepdims=True)

    rest = [functools.partial(own_rows, tile) for tile in range(tiles)]
    rest += [all_arrived] + [functools.partial(other_rows, tile) for tile in range(tiles)]

    compute(0)
    own_copy.wait()
    row_pass(0).start()
    passed = 1
    for t in range(total + LAG_Z + 3):
        if t + 1 < total:
            compute(t + 1)
        for i in range(total - 1, -1, -1):
            for at, now in steps_of(i):
                if at == t:
                    now(i)
        until = min(16, 1 + (t + 1) * 15 // (total - 2))
        for k in range(passed, until):
            pass_on(k)
        passed = until
        if t >= total - 2:
            for _ in range(min(len(rest), REST_EACH)):
                rest.pop(0)()
    while rest:
        rest.pop(0)()

    near.wait()
    near_copy.wait()
    ffn_out[1] = near_held[...].astype(jnp.float32) + near_buf[...].astype(jnp.float32)
    squares = sum_ref[...]
    square = jnp.sum(squares, axis=1, keepdims=True)
    for out in (attn_out, ffn_out):

        def of_rows(r, carry, out=out):
            at = pl.ds(pl.multiple_of(r * 8, 8), 8)
            for layer in range(out.shape[0]):
                value = out[layer, at, :]
                carry = carry + jnp.sum(value * value, axis=0, keepdims=True)
            return carry

        found = lax.fori_loop(
            0, out.shape[1] // 8, of_rows, jnp.zeros((1, out.shape[2]), jnp.float32)
        )
        square = square + jnp.sum(found, axis=1, keepdims=True)
    place = lax.broadcasted_iota(jnp.int32, vec_out.shape, 0) * 128 + lax.broadcasted_iota(
        jnp.int32, vec_out.shape, 1
    )
    value = jnp.where(place < vec_len, vec_out[...], 0.0)
    found = jnp.sum(value * value, axis=0, keepdims=True)
    square = square + jnp.sum(found, axis=1, keepdims=True)
    square_ref[...] = jnp.broadcast_to(square, square_ref.shape)

    def square_copy(k, slot):
        return remote(
            square_ref,
            squares_ref.at[slot],
            square_sem.at[0, k],
            square_sem.at[1, k],
            (d, lax.rem(z + k, 16)),
        )

    def send_square(k, carry):
        square_copy(k, z).start()
        return carry

    lax.fori_loop(1, 16, send_square, 0)
    squares_ref[z] = square_ref[...]

    for i in range(total):
        copy_a(i).wait_send()
        if halves(i):
            copy_h(i).wait_send()
        copy_y(i).wait_send()
        for k in range(1, 4):
            copy_z(i, k).wait_send()
        copy_x(i).wait_send()

    def finish(k, carry):
        row_push(k).wait_send()
        square_copy(k, lax.rem(z + 16 - k, 16)).wait_recv()
        square_copy(k, z).wait_send()
        return carry

    lax.fori_loop(1, 16, finish, 0)

    def finish_pass(k, carry):
        row_pass(k).wait_send()
        return carry

    lax.fori_loop(0, 16, finish_pass, 0)
    norm = squares_ref[0]
    for slot in range(1, 16):
        norm = norm + squares_ref[slot]
    stats_out[...] = jnp.broadcast_to(norm, stats_out.shape)


def exchange_gradients(pairs, vec_parts, sums, near, asked, shard_rows, vec_len, collective_id):
    spans = []
    for index, (_, right) in enumerate(pairs):
        layer, matrix = index // 4, index % 4
        columns = right.shape[1]
        width = columns // -(-columns // CHUNK)
        offset = sum(pairs[m][1].shape[1] for m in range(matrix))
        for start in range(0, columns, width):
            spans.append(((layer, offset), index, start, width, index in HALVED))
    plain = [chunk for chunk in spans if not chunk[4]]
    halved = [chunk for chunk in spans if chunk[4]]
    chunks = [(None, None, 0, 128, False)]
    while plain or halved:
        chunks += halved[:1] + plain[:1]
        halved, plain = halved[1:], plain[1:]
    half = jnp.bfloat16
    held, bufs = [], []
    for _, index, _, width, halves in chunks:
        kind = vec_parts.dtype if index is None else half
        r = vec_parts.shape[3] if index is None else 32
        if index is not None:
            held.append(pltpu.VMEM((4, 2, 2, r, width), kind))
        bufs.append(pltpu.VMEM((4, 2, r, width), kind))
        if halves:
            r = r // 2
            bufs.append(pltpu.VMEM((4, 2, r, width), kind))
        bufs += [
            pltpu.VMEM((4, r, width), kind),
            pltpu.VMEM((3, r, width), kind),
            pltpu.VMEM((r, width), kind),
            pltpu.VMEM((r, width), kind),
        ]
    features = sums.shape[2]
    dma = pltpu.SemaphoreType.DMA
    count = len(chunks)
    scratch = held + bufs
    scratch += [
        pltpu.VMEM(near.shape, half),
        pltpu.VMEM((2,) + sums.shape, half),
        pltpu.VMEM((1, features), jnp.float32),
        pltpu.VMEM((1, 128), jnp.float32),
        pltpu.VMEM((16, 1, 128), jnp.float32),
        pltpu.VMEM((2,) + pairs[0][0].shape, half),
        pltpu.VMEM((2, pairs[0][0].shape[0], max(chunk[3] for chunk in chunks)), half),
        dma((2, 2)),
        pltpu.VMEM(near.shape, half),
        dma((2,)),
    ]
    scratch += [dma((count,)) for _ in range(4)] + [dma((count, 3)) for _ in range(2)]
    scratch += [dma((count,)) for _ in range(4)]
    scratch += [dma((16,)) for _ in range(4)] + [dma((2,)), dma((2, 16))]
    rows = near.shape[0]
    outs = [
        jax.ShapeDtypeStruct((2, rows, 4 * D), jnp.float32),
        jax.ShapeDtypeStruct((2, rows, 2 * FF), jnp.float32),
        jax.ShapeDtypeStruct((shard_rows, features), jnp.float32),
        jax.ShapeDtypeStruct(vec_parts.shape[3:], jnp.float32),
        jax.ShapeDtypeStruct((8, 128), jnp.float32),
    ]
    vmem = pl.BlockSpec(memory_space=pltpu.VMEM)
    hbm = pl.BlockSpec(memory_space=pltpu.HBM)
    return pl.pallas_call(
        functools.partial(gradient_kernel, tuple(chunks), len(pairs), vec_len),
        out_shape=tuple(outs),
        in_specs=[hbm] * (2 * len(pairs)) + [vmem, hbm, hbm, vmem],
        out_specs=tuple([vmem] * len(outs)),
        scratch_shapes=scratch,
        compiler_params=pltpu.CompilerParams(
            collective_id=collective_id, has_side_effects=True, vmem_limit_bytes=58 * 1024 * 1024
        ),
        cost_estimate=pl.CostEstimate(flops=0, bytes_accessed=200_000_000, transcendentals=0),
        name="exchange_gradients",
    )(*[array for pair in pairs for array in pair], vec_parts, sums, near, asked)


SPLITS = 4
WINDOW = 2
LAG = 3


def start_kernel(shard_rows, room, *refs):
    column_ref, row_ref, packet_ref, vec_ref, attn_ref, ffn_ref, word_ref = refs[:7]
    place_out, slot_out, packet_out, asked_out, vec_out, rows_out, *weight_outs = refs[7:15]
    table, rows_held, asked, words, own, attn_held, ffn_held = refs[15:22]
    packet_sem, near_sem, far_sem, vec_sem, row_sem = refs[22:27]
    z_sem, y_sem, x_sem, d_sem, e_sem, own_sem, word_sem, self_sem = refs[27:]

    d = lax.axis_index("dp")
    z = lax.axis_index("zero")
    me = d * 16 + z
    core = lax.rem(z, 2)
    col = lax.rem(z // 2, 2)
    line = z // 4
    sibling = z + 1 - 2 * core
    across = z + 2 - 4 * col
    layers = attn_ref.shape[0]
    width = attn_ref.shape[2]
    whole = 3 * width
    unit = whole // 128 // SPLITS
    hand = unit * 5 // 12
    total = layers * SPLITS

    def everyone(k):
        p = lax.rem(me + k, 32)
        return (p // 16, lax.rem(p, 16))

    held_copies = [
        pltpu.make_async_copy(attn_ref, attn_held, word_sem.at[1]),
        pltpu.make_async_copy(ffn_ref, ffn_held, word_sem.at[2]),
    ]
    for copy in held_copies:
        copy.start()
    word_copy = pltpu.make_async_copy(word_ref, words, word_sem.at[0])
    word_copy.start()
    barrier = pltpu.get_barrier_semaphore()

    def greet(k, carry):
        pl.semaphore_signal(barrier, inc=1, device_id=everyone(k), device_id_type=MESH)
        return carry

    lax.fori_loop(1, 32, greet, 0)
    for copy in held_copies:
        copy.wait()

    def self_copy(layer):
        return pltpu.make_async_copy(own.at[layer], weight_outs[layer].at[z], self_sem.at[layer])

    for layer in range(layers):
        own[layer, :, 0:width] = attn_held[layer].astype(jnp.bfloat16)
        own[layer, :, width:whole] = ffn_held[layer].astype(jnp.bfloat16)
        self_copy(layer).start()
    for layer in range(layers):
        self_copy(layer).wait()
    pl.semaphore_wait(barrier, 31)

    def remote(src, dst, sems, at, to):
        return pltpu.make_async_remote_copy(
            src_ref=src,
            dst_ref=dst,
            send_sem=sems.at[(0,) + at],
            recv_sem=sems.at[(1,) + at],
            device_id=to,
            device_id_type=MESH,
        )

    def packet_copy(k, slot):
        return remote(packet_ref, packet_out.at[slot], packet_sem, (k,), everyone(k))

    def near_copy(k, slot):
        to = lax.rem(z + k, 16)
        return remote(asked.at[to], asked_out.at[slot], near_sem, (k,), (d, to))

    def far_copy(k, slot):
        to = lax.rem(z + k, 16)
        return remote(asked.at[to], asked_out.at[slot], far_sem, (k,), (1 - d, to))

    def vec_copy(k, slot):
        return remote(vec_ref, vec_out.at[slot], vec_sem, (k,), (d, lax.rem(z + k, 16)))

    def row_copy(k, slot):
        to = lax.rem(z + k, 16)
        return remote(rows_held.at[to], rows_out.at[slot], row_sem, (k,), (d, to))

    def shard(i):
        at = lax.rem(line + i % 4, 4) * 4 + lax.rem(z, 4)
        return at if i < 4 else at + 2 - 4 * col

    def piece(s):
        layer, p = s // SPLITS, s % SPLITS
        size = unit if p < SPLITS - 1 else whole // 128 - p * unit
        return layer, p * unit, size

    def columns_of(at, s, first, size):
        layer, base, _ = piece(s)
        return weight_outs[layer].at[
            at, :, pl.ds(pl.multiple_of((base + first) * 128, 128), size * 128)
        ]

    def stretch(at, s, ours):
        size = piece(s)[2]
        return columns_of(at, s, ours * hand, size - hand)

    def handed(at, s, ours):
        size = piece(s)[2]
        return columns_of(at, s, ours * (size - hand), hand)

    def both(ref, sems, at, to):
        return remote(ref, ref, sems, at, to)

    def z_copy(s, k, at):
        to = lax.rem(line + k, 4) * 4 + lax.rem(z, 4)
        return both(stretch(at, s, d), z_sem, (s, k - 1), (d, to))

    def y_copy(s, j, at):
        return both(stretch(at, s, d), y_sem, (s, j), (d, across))

    def x_copy(s, i, at, ours):
        return both(handed(at, s, ours), x_sem, (s, i), (1 - d, z))

    def d_copy(s, i, at):
        return both(stretch(at, s, d), d_sem, (s, i), (d, sibling))

    def e_copy(s, i, at):
        return both(handed(at, s, 1 - d), e_sem, (s, i), (d, sibling))

    def own_copy(layer, at):
        ref = weight_outs[layer].at[at]
        return both(ref, own_sem, (layer,), (d, sibling))

    def spread(s, i):
        at = shard(i)
        if i < 4:
            y_copy(s, i, at).start()
        if i > 0:
            x_copy(s, i, at, d).start()
            d_copy(s, i, at).start()

    def open_piece(s):
        for k in range(1, 4):
            z_copy(s, k, z).start()
        spread(s, 0)

    for s in range(WINDOW):
        open_piece(s)

    tokens = column_ref.shape[0]
    ids_row = row_ref[...]
    lane = lax.broadcasted_iota(jnp.int32, (1, tokens), 1).astype(jnp.float32)
    block = 128

    def lead_of(b, least):
        ids = column_ref[pl.ds(pl.multiple_of(b * block, block), block), :]
        there = lax.broadcasted_iota(jnp.int32, (block, 1), 0) + b * block
        found = jnp.where(ids == ids_row, there.astype(jnp.float32), 1e9)
        return jnp.minimum(least, jnp.min(found, axis=0, keepdims=True))

    least = lax.fori_loop(0, tokens // block, lead_of, jnp.full((1, tokens), 1e9, jnp.float32))
    lead_ids = jnp.where(least == lane, ids_row, -1)

    lane128 = lax.broadcasted_iota(jnp.int32, (1, 128), 1).astype(jnp.float32)

    def place_of(b, carry):
        most, best = carry
        at = pl.ds(pl.multiple_of(b * block, block), block)
        ids = column_ref[at, :]
        owner = jnp.floor((ids.astype(jnp.float32) + 0.5) * (1.0 / shard_rows))
        low_id = owner.astype(jnp.int32) * shard_rows
        ahead = (lead_ids >= low_id) & (lead_ids < ids)
        place = jnp.sum(jnp.where(ahead, 1.0, 0.0), axis=1, keepdims=True)
        place_out[at, :] = place.astype(jnp.int32)
        inside = place < room
        slot_out[at, :] = jnp.where(inside, owner * room + place, -1.0).astype(jnp.int32)
        slot = jnp.broadcast_to(jnp.where(inside, owner * 128.0 + place, -1.0), (block, 128))
        local = jnp.broadcast_to((ids - low_id).astype(jnp.float32), (block, 128))
        grown = []
        for o in range(16):
            found = jnp.where(slot == o * 128.0 + lane128, local, -1.0)
            found = jnp.max(found.reshape(block // 8, 8, 128), axis=0)
            grown.append(jnp.maximum(best[o], found))
        return jnp.maximum(most, jnp.max(place, axis=0, keepdims=True)), tuple(grown)

    most, best = lax.fori_loop(
        0,
        tokens // block,
        place_of,
        (jnp.zeros((1, 1), jnp.float32), (jnp.full((8, 128), -1.0, jnp.float32),) * 16),
    )
    rounds = jnp.ones((1, 1), jnp.float32)
    for r in range(1, -(-tokens // room)):
        rounds = rounds + (most >= r * room).astype(jnp.float32)
    for o in range(16):
        found = jnp.max(best[o], axis=0, keepdims=True)
        asked[o] = jnp.where(lane128 == 127.0, rounds, found).astype(jnp.int32)

    def send_near(k, carry):
        near_copy(k, me).start()
        return carry

    lax.fori_loop(1, 16, send_near, 0)

    def send_far(k, carry):
        far_copy(k, me).start()
        return carry

    lax.fori_loop(0, 16, send_far, 0)

    def send_packets(k, carry):
        packet_copy(k, me).start()
        return carry

    lax.fori_loop(1, 32, send_packets, 0)

    def send_vec(k, carry):
        vec_copy(k, z).start()
        return carry

    lax.fori_loop(1, 16, send_vec, 0)
    for layer in range(layers):
        own_copy(layer, z).start()
    vec_out[z] = vec_ref[...]
    asked_out[me] = asked[z]
    packet_out[me] = packet_ref[...]

    body_rows = shard_rows // 16 * 16
    step = 112 if body_rows % 112 == 0 else 16

    def to_half(i, carry):
        at = pl.multiple_of(i * step, 16)
        table[pl.ds(at, step), :] = words[pl.ds(at, step), :].astype(jnp.bfloat16)
        return carry

    word_copy.wait()
    lax.fori_loop(0, body_rows // step, to_half, 0)
    padded = table.shape[0]
    table[body_rows:padded, :] = jnp.zeros((padded - body_rows, table.shape[1]), jnp.bfloat16)
    if shard_rows > body_rows:
        table[body_rows:shard_rows, :] = words[body_rows:shard_rows, :].astype(jnp.bfloat16)

    def answer_one(k, carry):
        src = lax.rem(z + k, 16)
        rows_at = lax.broadcasted_iota(jnp.int32, (padded, 128), 0)
        picked = (rows_at == asked_out[d * 16 + src]).astype(jnp.bfloat16)
        found = lax.dot_general(
            picked, table[...], (((0,), (0,)), ((), ())), preferred_element_type=jnp.float32
        )
        rows_held[src] = found[:room, :].astype(jnp.bfloat16)
        return carry

    def packet_in(k, carry):
        near_copy(k, d * 16 + lax.rem(z + 16 - k, 16)).wait_recv()
        return carry

    def row_start(k, carry):
        row_copy(k, z).start()
        return carry

    def z_phase(s):
        for k in range(1, 4):
            z_copy(s, k, shard(4 - k)).wait_recv()
            spread(s, 4 - k)
        if s + WINDOW < total:
            open_piece(s + WINDOW)

    def y_phase(s):
        for j in range(4):
            y_copy(s, j, shard(4 + j)).wait_recv()
            spread(s, 4 + j)

    def x_phase(s):
        for i in range(1, 8):
            at = shard(i)
            x_copy(s, i, at, 1 - d).wait_recv()
            e_copy(s, i, at).start()

    done = 0
    for t in range(total + LAG):
        if t < total:
            z_phase(t)
        if t == 1:
            lax.fori_loop(1, 16, packet_in, 0)
        if t >= 1:
            until = min(16, done + 4)
            if until > done:
                lax.fori_loop(done, until, answer_one, 0)
            done = until
        if t == total - 1:
            lax.fori_loop(1, 16, row_start, 0)
            rows_out[z] = rows_held[z]
        if 0 <= t - 1 < total:
            y_phase(t - 1)
        if 0 <= t - LAG < total:
            x_phase(t - LAG)

    turn = 1 - 2 * core
    for layer in range(layers):
        own_copy(layer, z + turn).wait_recv()
        own_copy(layer, z).wait_send()
    for s in range(total):
        for i in range(1, 8):
            at = shard(i)
            d_copy(s, i, at + turn).wait_recv()
            d_copy(s, i, at).wait_send()
            e_copy(s, i, at + turn).wait_recv()
            e_copy(s, i, at).wait_send()
            x_copy(s, i, at, d).wait_send()
        for k in range(1, 4):
            z_copy(s, k, z).wait_send()
        for i in range(4):
            y_copy(s, i, shard(i)).wait_send()

    def finish(k, carry):
        back = lax.rem(z + 16 - k, 16)
        row_copy(k, back).wait_recv()
        row_copy(k, z).wait_send()
        vec_copy(k, back).wait_recv()
        vec_copy(k, z).wait_send()
        near_copy(k, me).wait_send()
        return carry

    lax.fori_loop(1, 16, finish, 0)

    def finish_packets(k, carry):
        packet_copy(k, lax.rem(me + 32 - k, 32)).wait_recv()
        packet_copy(k, me).wait_send()
        return carry

    lax.fori_loop(1, 32, finish_packets, 0)

    def finish_far(k, carry):
        far_copy(k, (1 - d) * 16 + lax.rem(z + 16 - k, 16)).wait_recv()
        far_copy(k, me).wait_send()
        return carry

    lax.fori_loop(0, 16, finish_far, 0)


def exchange_start(ids, packet, vec_rows, attn, ffn, word_table, room, collective_id):
    half = jnp.bfloat16
    shard_rows, features = word_table.shape
    padded = -(-shard_rows // 128) * 128
    layers, rows, width = attn.shape
    tokens = ids.shape[0]
    pieces = layers * SPLITS
    dma = pltpu.SemaphoreType.DMA
    vmem = pl.BlockSpec(memory_space=pltpu.VMEM)
    anywhere = pl.BlockSpec(memory_space=pltpu.HBM)
    return pl.pallas_call(
        functools.partial(start_kernel, shard_rows, room),
        out_shape=(
            jax.ShapeDtypeStruct((tokens, 1), jnp.int32),
            jax.ShapeDtypeStruct((tokens, 1), jnp.int32),
            jax.ShapeDtypeStruct((32,) + packet.shape, packet.dtype),
            jax.ShapeDtypeStruct((32, 1, 128), jnp.int32),
            jax.ShapeDtypeStruct((16,) + vec_rows.shape, vec_rows.dtype),
            jax.ShapeDtypeStruct((16, room, features), half),
        )
        + (jax.ShapeDtypeStruct((16, rows, 3 * width), half),) * layers,
        in_specs=[vmem] * 4 + [anywhere] * 3,
        out_specs=tuple([vmem] * 6 + [anywhere] * layers),
        scratch_shapes=[
            pltpu.VMEM((padded, features), half),
            pltpu.VMEM((16, room, features), half),
            pltpu.VMEM((16, 1, 128), jnp.int32),
            pltpu.VMEM(word_table.shape, word_table.dtype),
            pltpu.VMEM((layers, rows, 3 * width), half),
            pltpu.VMEM(attn.shape, attn.dtype),
            pltpu.VMEM(ffn.shape, ffn.dtype),
            dma((2, 32)),
            dma((2, 16)),
            dma((2, 16)),
            dma((2, 16)),
            dma((2, 16)),
            dma((2, pieces, 3)),
            dma((2, pieces, 4)),
            dma((2, pieces, 8)),
            dma((2, pieces, 8)),
            dma((2, pieces, 8)),
            dma((2, layers)),
            dma((3,)),
            dma((layers,)),
        ],
        compiler_params=pltpu.CompilerParams(
            collective_id=collective_id, has_side_effects=True, vmem_limit_bytes=52 * 1024 * 1024
        ),
        cost_estimate=pl.CostEstimate(flops=0, bytes_accessed=150_000_000, transcendentals=0),
        name="exchange_start",
    )(ids.reshape(-1, 1), ids.reshape(1, -1), packet, vec_rows, attn, ffn, word_table)


WIDTHS = (D, D * 2 // 3, D // 3, D // 6, D // 12)


def gather_rows(block_ref, all_ref, z_sem, near_sem):
    d = lax.axis_index("dp")
    z = lax.axis_index("zero")
    line, spot = z // 4, lax.rem(z, 4)

    def at_line(k):
        return lax.rem(line + k, 4) * 4 + spot

    def near_by(j):
        across = j // 4
        return lax.rem(d + across, 2), line * 4 + lax.rem(spot + j % 4, 4)

    barrier = pltpu.get_barrier_semaphore()
    for k in range(1, 4):
        pl.semaphore_signal(barrier, inc=1, device_id=(d, at_line(k)), device_id_type=MESH)
    for j in range(1, 8):
        pl.semaphore_signal(barrier, inc=1, device_id=near_by(j), device_id_type=MESH)
    pl.semaphore_wait(barrier, 10)

    def z_copy(k):
        return pltpu.make_async_remote_copy(
            src_ref=block_ref,
            dst_ref=all_ref.at[d * 16 + z],
            send_sem=z_sem.at[0, k],
            recv_sem=z_sem.at[1, k],
            device_id=(d, at_line(k)),
            device_id_type=MESH,
        )

    def z_arrival(k):
        ref = all_ref.at[d * 16 + at_line(4 - k)]
        return pltpu.make_async_remote_copy(
            src_ref=ref,
            dst_ref=ref,
            send_sem=z_sem.at[0, k],
            recv_sem=z_sem.at[1, k],
            device_id=(d, at_line(k)),
            device_id_type=MESH,
        )

    def near_copy(i, j, from_d, from_z):
        ref = all_ref.at[from_d * 16 + from_z]
        return pltpu.make_async_remote_copy(
            src_ref=ref,
            dst_ref=ref,
            send_sem=near_sem.at[0, i, j],
            recv_sem=near_sem.at[1, i, j],
            device_id=near_by(j),
            device_id_type=MESH,
        )

    for k in range(1, 4):
        z_copy(k).start()
    all_ref[d * 16 + z] = block_ref[...]
    for j in range(1, 8):
        near_copy(0, j, d, z).start()
    for k in range(1, 4):
        z_arrival(k).wait_recv()
        for j in range(1, 8):
            near_copy(4 - k, j, d, at_line(4 - k)).start()
    for i in range(4):
        for j in range(1, 8):
            back = lax.rem(line + i, 4) * 4 + lax.rem(spot + 4 - j % 4, 4)
            near_copy(i, j, lax.rem(d + j // 4, 2), back).wait_recv()
            near_copy(i, j, d, at_line(i)).wait_send()
    for k in range(1, 4):
        z_copy(k).wait_send()


def contrastive_kernel(
    block_ref, false_ref, pair_ref, loss_ref, own_ref, all_ref, pooled_ref, grad_ref, z_sem, near_sem
):
    me = lax.axis_index("dp") * 16 + lax.axis_index("zero")
    gather_rows(block_ref, all_ref, z_sem, near_sem)
    upper = lax.broadcasted_iota(jnp.int32, (8, 1), 0) < 4
    for kind in range(2):
        for two in range(all_ref.shape[0] // 2):
            even = all_ref[2 * two, kind].astype(jnp.float32)
            odd = all_ref[2 * two + 1, kind].astype(jnp.float32)
            at = slice(8 * two, 8 * two + 8)
            pooled_ref[kind, 0, at, :] = jnp.where(upper, even, pltpu.roll(odd, 4, 0))
            pooled_ref[kind, 1, at, :] = jnp.where(upper, pltpu.roll(even, 4, 0), odd)
    contrastive_math(pooled_ref, false_ref, pair_ref, loss_ref, grad_ref)
    first = pl.multiple_of(me // 2 * 8, 8)
    swap = lax.rem(me, 2) == 1
    for kind in range(2):
        for role in range(2):
            rows = grad_ref[kind, role, pl.ds(first, 8), :]
            own_ref[kind, role] = jnp.where(swap, pltpu.roll(rows, 4, 0), rows)


def contrastive_math(pooled_ref, false_ref, pair_ref, loss_ref, grad_ref):
    pairs = false_ref.shape[0]
    high = lax.Precision.HIGHEST
    columns = lax.broadcasted_iota(jnp.int32, (pairs, pairs), 1)
    hit = columns == pair_ref[...]
    kept = (false_ref[...] == 0) | hit
    hits = hit.astype(jnp.float32)
    valid = (pair_ref[...] >= 0).astype(jnp.float32)
    inverse = 1.0 / jnp.maximum(jnp.sum(valid, axis=0, keepdims=True), 1.0)
    weight = valid * inverse
    named = jnp.sum(hits, axis=1, keepdims=True)
    totals = jnp.zeros((pairs, 1), jnp.float32)
    for first, width in enumerate(WIDTHS):
        span = -(-width // 128) * 128
        inside = lax.broadcasted_iota(jnp.int32, (1, span), 1) < width
        units, scales, logs = [], [], []
        for kind in range(2):
            pair_units, pair_scales = [], []
            for role in range(2):
                rows = jnp.where(inside, pooled_ref[kind, role, :, 0:span], 0.0)
                scale = lax.rsqrt(jnp.sum(rows * rows, axis=1, keepdims=True) + NORM_EPS)
                pair_units.append(rows * scale)
                pair_scales.append(scale)
            sims = lax.dot_general(
                pair_units[0],
                pair_units[1],
                (((1,), (1,)), ((), ())),
                precision=high,
                preferred_element_type=jnp.float32,
            )
            sims = jnp.where(kept, sims / SOFTMAX_TEMP, MASKED)
            shifted = sims - jnp.max(sims, axis=1, keepdims=True)
            logs.append(shifted - jnp.log(jnp.sum(jnp.exp(shifted), axis=1, keepdims=True)))
            units.append(pair_units)
            scales.append(pair_scales)
        shallow, deep = logs
        p_shallow, p_deep = jnp.exp(shallow), jnp.exp(deep)
        gap = p_deep * (deep - shallow)
        spread = jnp.sum(gap, axis=1, keepdims=True)
        totals = totals + spread - jnp.sum(jnp.where(hit, shallow + deep, 0.0), axis=1, keepdims=True)
        d_sims = (
            p_shallow * (named + 1.0) - hits - p_deep,
            gap + p_deep * (named - spread) - hits,
        )
        for kind in range(2):
            d_cos = jnp.where(kept, d_sims[kind] * weight, 0.0) / SOFTMAX_TEMP
            for role in range(2):
                unit = units[kind][role]
                d_unit = lax.dot_general(
                    d_cos,
                    units[kind][1 - role],
                    (((1 - role,), (0,)), ((), ())),
                    precision=high,
                    preferred_element_type=jnp.float32,
                )
                along = jnp.sum(d_unit * unit, axis=1, keepdims=True)
                d_rows = scales[kind][role] * (d_unit - unit * along)
                if first == 0:
                    grad_ref[kind, role] = d_rows
                else:
                    grad_ref[kind, role, :, 0:span] = grad_ref[kind, role, :, 0:span] + d_rows
    loss_ref[...] = jnp.broadcast_to(
        jnp.sum(totals * valid, axis=0, keepdims=True) * inverse, loss_ref.shape
    )


def contrastive(block, false_all, pair_all, collective_id):
    vmem = pl.BlockSpec(memory_space=pltpu.VMEM)
    pairs = false_all.shape[0]
    dma = pltpu.SemaphoreType.DMA
    whole = pltpu.VMEM((2, 2, pairs, D), jnp.float32)
    loss, grads = pl.pallas_call(
        contrastive_kernel,
        out_shape=(
            jax.ShapeDtypeStruct((8, 128), jnp.float32),
            jax.ShapeDtypeStruct((2, 2, 8, D), jnp.float32),
        ),
        in_specs=[vmem] * 3,
        out_specs=(vmem, vmem),
        scratch_shapes=[
            pltpu.VMEM((32,) + block.shape, block.dtype),
            whole,
            whole,
            dma((2, 4)),
            dma((2, 4, 8)),
        ],
        compiler_params=pltpu.CompilerParams(
            collective_id=collective_id, has_side_effects=True, vmem_limit_bytes=20 * 1024 * 1024
        ),
        cost_estimate=pl.CostEstimate(flops=10**9, bytes_accessed=3_000_000, transcendentals=10**6),
        name="contrastive",
    )(block, false_all, pair_all.reshape(-1, 1))
    return loss[0, 0], grads


PAIRS_OF_HEADS = HEADS // 2


def by_side(rows):
    lane = lax.broadcasted_iota(jnp.int32, (1, 2 * HD), 1)
    zero = jnp.zeros_like(rows)
    return jnp.concatenate([jnp.where(lane < HD, rows, zero), jnp.where(lane < HD, zero, rows)])


def join_sides(stacked):
    lane = lax.broadcasted_iota(jnp.int32, (1, 2 * HD), 1)
    return jnp.where(lane < HD, stacked[:SEQ], stacked[SEQ:])


def contract(left, right, left_dim, right_dim):
    return lax.dot_general(
        left, right, (((left_dim,), (right_dim,)), ((), ())), preferred_element_type=jnp.float32
    )


def thirds(packed_ref):
    for pair in range(PAIRS_OF_HEADS):
        at = pair * 2 * HD
        yield [packed_ref[0, :, t * D + at : t * D + at + 2 * HD] for t in range(3)]


def probabilities(scores, valid):
    scores = jnp.where(valid, scores * HD ** (-0.5), MASKED)
    raised = jnp.exp(scores - jnp.max(scores, axis=1, keepdims=True))
    return raised * (1.0 / jnp.sum(raised, axis=1, keepdims=True))


def attention_kernel(mask_ref, packed_ref, context_ref):
    valid = mask_ref[0] > 0.0
    parts = list(thirds(packed_ref))
    scores = [contract(by_side(queries), keys, 1, 1) for queries, keys, _ in parts]
    probs = [probabilities(now, valid).astype(jnp.bfloat16) for now in scores]
    for pair in range(PAIRS_OF_HEADS):
        mixed = contract(probs[pair], parts[pair][2], 1, 0)
        at = pair * 2 * HD
        context_ref[0, :, at : at + 2 * HD] = join_sides(mixed).astype(jnp.bfloat16)


def attention_back_kernel(mask_ref, packed_ref, grad_ref, out_ref):
    valid = mask_ref[0] > 0.0
    parts = list(thirds(packed_ref))
    queries = [by_side(part[0]) for part in parts]
    grads = [
        by_side(grad_ref[0, :, pair * 2 * HD : (pair + 1) * 2 * HD])
        for pair in range(PAIRS_OF_HEADS)
    ]
    scores = [contract(now, part[1], 1, 1) for now, part in zip(queries, parts)]
    d_probs = [contract(now, part[2], 1, 1) for now, part in zip(grads, parts)]
    probs = [probabilities(now, valid) for now in scores]
    d_scores = []
    for now, d_now in zip(probs, d_probs):
        shared = jnp.sum(d_now * now, axis=1, keepdims=True)
        d_scores.append(jnp.where(valid, now * (d_now - shared), 0.0).astype(jnp.bfloat16))
    for pair in range(PAIRS_OF_HEADS):
        d_queries = join_sides(contract(d_scores[pair], parts[pair][1], 1, 0)) * HD ** (-0.5)
        d_keys = contract(d_scores[pair], queries[pair], 0, 0) * HD ** (-0.5)
        d_values = contract(probs[pair].astype(jnp.bfloat16), grads[pair], 0, 0)
        for third, now in enumerate((d_queries, d_keys, d_values)):
            at = third * D + pair * 2 * HD
            out_ref[0, :, at : at + 2 * HD] = now.astype(jnp.bfloat16)


def attention_call(kernel, mask, operands, features, name):
    count = operands[0].shape[0]

    def spec(last):
        return pl.BlockSpec((1, SEQ, last), lambda i: (i, 0, 0))

    return pl.pallas_call(
        kernel,
        grid=(count,),
        out_shape=jax.ShapeDtypeStruct((count, SEQ, features), jnp.bfloat16),
        in_specs=[pl.BlockSpec((1, 1, SEQ), lambda i: (i, 0, 0))]
        + [spec(operand.shape[2]) for operand in operands],
        out_specs=spec(features),
        compiler_params=pltpu.CompilerParams(vmem_limit_bytes=14 * 1024 * 1024),
        cost_estimate=pl.CostEstimate(
            flops=10**9, bytes_accessed=count * SEQ * D * 10, transcendentals=10**6
        ),
        name=name,
    )(mask, *operands)


GELU_SCALE = 0.7978845608028654


def feed_back_kernel(middle_ref, down_ref, up_weights, down_weights, bias_ref, *outs):
    active_ref, d_up_ref, d_first_ref, total_ref = outs
    middle, d_down = middle_ref[...], down_ref[...]
    tile = FF // 4
    d_first = jnp.zeros(d_first_ref.shape, jnp.float32)
    for start in range(0, FF, tile):
        at = slice(start, start + tile)
        upward = contract(middle, up_weights[:, at], 1, 0) + bias_ref[:, at]
        d_active = contract(d_down, down_weights[:, at], 1, 0).astype(jnp.bfloat16)
        square = upward * upward
        bent = jnp.tanh(GELU_SCALE * (upward + 0.044715 * (square * upward)))
        share = 0.5 * (1.0 + bent)
        inner = GELU_SCALE * (1.0 + 3.0 * 0.044715 * square)
        slope = share + 0.5 * upward * (1.0 - bent * bent) * inner
        active_ref[:, at] = (upward * share).astype(jnp.bfloat16)
        d_up = (d_active.astype(jnp.float32) * slope).astype(jnp.bfloat16)
        d_up_ref[:, at] = d_up
        d_first = d_first + contract(d_up, up_weights[:, at], 1, 1)
        found = jnp.sum(d_up.astype(jnp.float32), axis=0, keepdims=True)
        before = jnp.where(pl.program_id(0) == 0, 0.0, total_ref[:, at])
        total_ref[:, at] = before + found
    d_first_ref[...] = d_first


def feed_back(middle, d_down, weights, up_bias):
    tokens = middle.shape[0]
    rows = 256
    half = jnp.bfloat16

    def by_rows(columns):
        return pl.BlockSpec((rows, columns), lambda i: (i, 0))

    def matrix(which):
        return pl.BlockSpec((D, FF), lambda i: (0, which))

    whole = pl.BlockSpec((1, FF), lambda i: (0, 0))
    return pl.pallas_call(
        feed_back_kernel,
        grid=(tokens // rows,),
        out_shape=(
            jax.ShapeDtypeStruct((tokens, FF), half),
            jax.ShapeDtypeStruct((tokens, FF), half),
            jax.ShapeDtypeStruct((tokens, D), jnp.float32),
            jax.ShapeDtypeStruct((1, FF), jnp.float32),
        ),
        in_specs=[by_rows(D), by_rows(D), matrix(1), matrix(2), whole],
        out_specs=(by_rows(FF), by_rows(FF), by_rows(D), whole),
        compiler_params=pltpu.CompilerParams(vmem_limit_bytes=26 * 1024 * 1024),
        cost_estimate=pl.CostEstimate(
            flops=6 * tokens * D * FF, bytes_accessed=24 * tokens * D, transcendentals=tokens * FF
        ),
        name="feed_back",
    )(middle, d_down, weights, weights, up_bias.reshape(1, FF))


LAYER_ROWS = 8 + FF // D


def layer_vectors(rows):
    up = 5 + FF // D
    return [rows[i] for i in range(5)] + [rows[5:up].reshape(FF)] + [rows[up + i] for i in range(3)]


def layer_norm(values, gain, shift):
    center = values - jnp.mean(values, axis=-1, keepdims=True)
    spread = jnp.mean(center * center, axis=-1, keepdims=True)
    return center * lax.rsqrt(spread + NORM_EPS) * gain + shift


def embed_tokens(rows, vectors):
    return layer_norm(low_back(rows) + vectors[None, :SEQ], vectors[SEQ], vectors[SEQ + 1])


def norm_forward(values, gain, shift):
    center = values - jnp.mean(values, axis=-1, keepdims=True)
    inverse = lax.rsqrt(jnp.mean(center * center, axis=-1, keepdims=True) + NORM_EPS)
    normal = center * inverse
    return normal * gain + shift, normal, inverse


def norm_back(grad, normal, inverse, gain):
    scaled = grad * gain
    mean = jnp.mean(scaled, axis=-1, keepdims=True)
    along = jnp.mean(scaled * normal, axis=-1, keepdims=True)
    return (
        (scaled - mean - normal * along) * inverse,
        jnp.sum(grad * normal, axis=(0, 1)),
        jnp.sum(grad, axis=(0, 1)),
    )


def gelu(value):
    bent = jnp.tanh(GELU_SCALE * (value + 0.044715 * value * value * value))
    return 0.5 * value * (1.0 + bent)


EDGES = (0, 3 * D, 4 * D, 4 * D + FF, 4 * D + 2 * FF)


def four_matrices(weights):
    return [weights[:, first:last] for first, last in zip(EDGES, EDGES[1:])]


def layer_forward(hidden, weights, vectors, mask):
    in_weights, out_weights, up_weights, down_weights = four_matrices(weights)
    q_bias, v_bias, o_bias, gain_one, shift_one, up_bias, down_bias, gain_two, second_shift = (
        layer_vectors(vectors)
    )
    half = jnp.bfloat16
    entry = lax.optimization_barrier(hidden.astype(half))
    bias = jnp.concatenate([q_bias, jnp.zeros_like(q_bias), v_bias])
    packed = (matmul(entry, in_weights) + bias).astype(half)
    context = attention_call(attention_kernel, mask, [packed], D, "attention")
    attended = matmul(context, out_weights) + o_bias
    first, normal_one, inverse_one = norm_forward(hidden + attended, gain_one, shift_one)
    middle = lax.optimization_barrier(first.astype(half))
    upward = matmul(middle, up_weights) + up_bias
    active = lax.optimization_barrier(gelu(upward).astype(half))
    downward = einsum_plain("nsf,df->nsd", active, down_weights) + down_bias
    output, normal_two, inverse_two = norm_forward(first + downward, gain_two, second_shift)
    kept = (
        entry, packed, context, middle,
        normal_one, inverse_one, normal_two, inverse_two,
    )
    return output, kept


def layer_backward(kept, weights, vectors, mask, grad, midway):
    in_weights, out_weights, _, _ = four_matrices(weights)
    entry, packed, context, middle = kept[:4]
    normal_one, inverse_one, normal_two, inverse_two = kept[4:]
    gain_one, gain_two = layer_vectors(vectors)[3], layer_vectors(vectors)[7]
    half = jnp.bfloat16

    def total(value):
        return jnp.sum(value.astype(jnp.float32), axis=(0, 1))

    d_second, d_gain_two, d_shift_two = norm_back(grad, normal_two, inverse_two, gain_two)
    d_down = lax.optimization_barrier(d_second.astype(half))
    flat_middle, flat_down = middle.reshape(-1, D), d_down.reshape(-1, D)
    active, d_up, d_first, d_up_bias = feed_back(
        flat_middle, flat_down, weights, layer_vectors(vectors)[5]
    )
    feed_pairs = [(flat_middle, d_up), (flat_down, active)]
    d_first = midway(feed_pairs, d_second + d_first.reshape(d_second.shape))
    d_middle, d_gain_one, d_shift_one = norm_back(d_first, normal_one, inverse_one, gain_one)
    d_attended = lax.optimization_barrier(d_middle.astype(half))
    d_context = jnp.einsum(
        "nsd,ed->nse", d_attended, out_weights, preferred_element_type=jnp.float32
    ).astype(half)
    d_packed = attention_call(
        attention_back_kernel, mask, [packed, d_context], 3 * D, "attention_back"
    )
    d_hidden = d_middle + jnp.einsum(
        "nsp,dp->nsd", d_packed, in_weights, preferred_element_type=jnp.float32
    )
    packed_total = total(d_packed)
    pieces = [
        packed_total[:D], packed_total[2 * D :], total(d_attended), d_gain_one, d_shift_one,
        d_up_bias, total(d_down), d_gain_two, d_shift_two,
    ]
    d_vectors, at = jnp.zeros((LAYER_ROWS, D), jnp.float32), 0
    for piece in pieces:
        rows = piece.reshape(-1, D)
        d_vectors = d_vectors + jnp.pad(rows, ((at, LAYER_ROWS - at - rows.shape[0]), (0, 0)))
        at = at + rows.shape[0]
    flat = [
        (left.reshape(-1, left.shape[2]), right.reshape(-1, right.shape[2]))
        for left, right in ((entry, d_packed), (context, d_attended))
    ]
    return d_hidden, flat + feed_pairs, d_vectors


def weight_gradient(left, right):
    return lax.dot_general(
        left, right, (((0,), (0,)), ((), ())), preferred_element_type=jnp.float32
    ).astype(jnp.bfloat16)


def pool_rows(hidden, key_mask, seq_lengths):
    share = key_mask.astype(jnp.float32) / seq_lengths.astype(jnp.float32)[:, None]
    return jnp.sum(hidden * share[:, :, None], axis=1)


def normalized_rows(rows):
    return rows * lax.rsqrt(jnp.sum(rows * rows, axis=-1, keepdims=True) + NORM_EPS)


def contrastive_terms(shallow_anchor, deep_anchor, shallow_pos, deep_pos, false_neg, pair_index):
    columns = lax.broadcasted_iota(jnp.int32, false_neg.shape, 1)
    hit = columns == pair_index[:, None]
    kept_cols = (false_neg == 0) | hit
    valid_rows = (pair_index >= 0).astype(jnp.float32)
    totals = jnp.zeros(pair_index.shape, jnp.float32)
    for current_width in (D, D * 2 // 3, D // 3, D // 6, D // 12):
        log_probs = []
        for anchor_vectors, positive_rows in (
            (shallow_anchor, shallow_pos),
            (deep_anchor, deep_pos),
        ):
            similarity_scores = (
                jnp.dot(
                    normalized_rows(anchor_vectors[:, :current_width]),
                    normalized_rows(positive_rows[:, :current_width]).T,
                    precision=lax.Precision.HIGHEST,
                )
                / SOFTMAX_TEMP
            )
            similarity_scores = jnp.where(kept_cols, similarity_scores, MASKED)
            log_probs.append(jax.nn.log_softmax(similarity_scores, axis=-1))
        for log_now in log_probs:
            totals = totals - jnp.sum(jnp.where(hit, log_now, 0.0), axis=-1)
        totals = totals + jnp.sum(jnp.exp(log_probs[1]) * (log_probs[1] - log_probs[0]), axis=-1)
    return jnp.sum(totals * valid_rows)


def adam_update(master, gradient, first, second, step_rate):
    first_new = BETA_ONE * first + (1.0 - BETA_ONE) * gradient
    second_new = BETA_TWO * second + (1.0 - BETA_TWO) * gradient * gradient
    first_hat = first_new / (1.0 - BETA_ONE**ADAM_STEP)
    second_hat = second_new / (1.0 - BETA_TWO**ADAM_STEP)
    master_new = master - step_rate * (
        first_hat / (jnp.sqrt(second_hat) + ADAM_EPS) + WEIGHT_DECAY * master
    )
    return (master_new, first_new, second_new)


def pad_rows(flat, multiple):
    rows = -(-flat.shape[0] // (128 * multiple)) * multiple
    return jnp.pad(flat, (0, rows * 128 - flat.shape[0])).reshape(rows, 128)


def one_hot(index, size, dtype=jnp.bfloat16):
    return (index[:, None] == lax.broadcasted_iota(jnp.int32, (1, size), 1)).astype(dtype)


def token_plan(ids, shard_rows):
    places = lax.broadcasted_iota(jnp.int32, ids.shape, 0)
    same = ids[:, None] == ids[None, :]
    leader = jnp.min(jnp.where(same, places[None, :], ids.shape[0]), axis=1)
    leads = leader == places
    owner = ids // shard_rows
    low_id = owner * shard_rows
    ahead = leads[None, :] & (ids[None, :] >= low_id[:, None]) & (ids[None, :] < ids[:, None])
    place = jnp.sum(ahead.astype(jnp.int32), axis=1)
    return owner, place, ids - low_id


def round_slots(owner, place, local_row, round_index, room, nz):
    inside = (place >= round_index * room) & (place < (round_index + 1) * room)
    slot = jnp.where(inside, owner * room + place - round_index * room, -1)
    slots = lax.broadcasted_iota(jnp.int32, (1, nz * room), 1)
    asked = jnp.max(jnp.where(slot[:, None] == slots, local_row[:, None], -1), axis=0)
    return slot, asked


def body(
    token_ids,
    lengths,
    false_neg,
    pair_index,
    word_table,
    vectors,
    attn_w,
    ffn_w,
    word_first,
    vector_first,
    attn_first,
    ffn_first,
    word_second,
    vector_second,
    attn_second,
    ffn_second,
):
    ndp = lax.axis_size("dp")
    nz = lax.axis_size("zero")
    n = ndp * nz
    by_hand = (ndp, nz) == (2, 16) and token_ids.shape[0] * ndp * nz <= 256
    my_dp = lax.axis_index("dp")
    my_zero = lax.axis_index("zero")
    me = my_dp * nz + my_zero
    pair_rows = token_ids.shape[0]
    total_pairs = pair_rows * n
    flat_ids = token_ids.reshape(-1, SEQ)
    seq_rows = flat_ids.shape[0]
    tokens = seq_rows * SEQ
    seq_lengths = lengths.reshape(-1)
    key_mask = lax.broadcasted_iota(jnp.int32, flat_ids.shape, 1) < seq_lengths[:, None]
    shard_rows = word_table.shape[0]
    vec_len = vectors.shape[0]

    room = -(-(tokens * 9 // 8) // (nz * 8)) * 8
    ids = flat_ids.reshape(-1)

    def packet_of(asked, rounds_here):
        last = jnp.concatenate([pair_index, rounds_here[None].astype(jnp.int32)])
        lines = nz + false_neg.size // 128
        return jnp.concatenate(
            [
                jnp.pad(asked.reshape(nz, room), ((0, 0), (0, 128 - room)), constant_values=-1),
                false_neg.reshape(-1, 128),
                jnp.zeros((7 - lines % 8, 128), jnp.int32),
                jnp.pad(last, (0, 128 - last.shape[0]))[None],
            ]
        )

    def gather_layer(layer_index):
        both = jnp.concatenate(
            [attn_w[layer_index].astype(jnp.bfloat16), ffn_w[layer_index].astype(jnp.bfloat16)],
            axis=1,
        )
        return lax.all_gather(both, "zero", axis=0, tiled=True)

    if by_hand:
        packet = pad_rows(jnp.concatenate([false_neg.reshape(-1), pair_index]), 8)
        place, slot, packets, asked_mine, vec_parts, received, *gathered = exchange_start(
            ids,
            packet.astype(jnp.bfloat16),
            pad_rows(vectors.astype(jnp.bfloat16), 16),
            attn_w,
            ffn_w,
            word_table,
            room,
            0,
        )
        layer_weights = [part.reshape(D, -1) for part in gathered]
        rounds = jnp.max(asked_mine[:, 0, 127])
        asked_mine = asked_mine[:, 0, :room]
        packets = packets.reshape(n, -1).astype(jnp.int32)
        false_all = packets[:, : false_neg.size].reshape(total_pairs, total_pairs)
        pair_all = packets[:, false_neg.size : false_neg.size + pair_rows].reshape(total_pairs)
        place, slot = place.reshape(-1), slot.reshape(-1)
    else:
        owner, place, local_row = token_plan(ids, shard_rows)
        slot, asked = round_slots(owner, place, local_row, 0, room, nz)
        packets, vec_parts = exchange(
            [
                packet_of(asked, jnp.max(place) // room + 1),
                pad_rows(vectors.astype(jnp.bfloat16), 16),
            ],
            ["all", "zero"],
            ndp,
            nz,
            0,
            "gather_requests",
        )
        layer_weights = [gather_layer(layer_index) for layer_index in range(LAYERS)]
        asked_mine = lax.dynamic_index_in_dim(packets[:, :nz, :room], my_zero, 1, keepdims=False)
        false_all = packets[:, nz : nz + false_neg.size // 128].reshape(total_pairs, total_pairs)
        pair_all = packets[:, -1, :pair_rows].reshape(total_pairs)
        rounds = jnp.max(packets[:, -1, pair_rows])
    vec_all = vec_parts.reshape(nz, -1)[:, :vec_len].reshape(-1).astype(jnp.float32)

    asked_near = lax.dynamic_slice_in_dim(asked_mine, my_dp * nz, nz, 0)

    def rows_for(wanted):
        picked = one_hot(wanted.reshape(-1), shard_rows, jnp.float32)
        return jnp.dot(picked, word_table, precision=lax.Precision.HIGHEST).astype(jnp.bfloat16)

    def rows_from(slot_now, received):
        return matmul(one_hot(slot_now, nz * room), received.reshape(nz * room, D)).astype(
            jnp.bfloat16
        )

    if not by_hand:
        (received,) = exchange(
            [rows_for(asked_near).reshape(nz, room, D)], ["zero_p"], ndp, nz, 1, "send_rows"
        )
    rows = rows_from(slot, received)

    def round_of(round_index):
        owner = lax.div(ids, jnp.int32(shard_rows))
        local_row = ids - owner * shard_rows
        return round_slots(owner, place, local_row, round_index, room, nz)

    def more_rows(state):
        round_index, rows_now = state
        slot_now, asked_now = round_of(round_index)
        wanted = lax.all_to_all(asked_now.reshape(nz, room), "zero", 0, 0, tiled=True)
        got = lax.all_to_all(rows_for(wanted).reshape(nz, room, D), "zero", 0, 0, tiled=True)
        return round_index + 1, rows_now + rows_from(slot_now, got)

    def further(step, *value):
        return lax.while_loop(lambda state: state[0] < rounds, step, (jnp.int32(1), *value))[1:]

    (rows,) = further(more_rows, rows)
    rows = rows.reshape(seq_rows, SEQ, D).astype(jnp.float32)

    vec_rows = vec_all.reshape(-1, D)
    edges = [0] + [SEQ + 2 + i * LAYER_ROWS for i in range(LAYERS + 1)]
    vec_parts = [vec_rows[first:last] for first, last in zip(edges, edges[1:])]
    embedded, embed_back = jax.vjp(embed_tokens, rows, vec_parts[0])
    hidden = embedded
    mask = key_mask.astype(jnp.float32)[:, None, :]
    saved = []
    pooled = []
    for layer_index in range(LAYERS):
        weights = layer_weights[layer_index]
        hidden, kept = layer_forward(hidden, weights, vec_parts[1 + layer_index], mask)
        saved.append(kept)
        pooled.append(pool_rows(hidden, key_mask, seq_lengths).astype(jnp.bfloat16))

    if by_hand and pair_rows == 4:
        block = jnp.stack(pooled).reshape(2, pair_rows, 2, D).transpose(0, 2, 1, 3)
        loss, pooled_grads = contrastive(block.reshape(2, 2 * pair_rows, D), false_all, pair_all, 2)
        pooled_grads = pooled_grads[:, :, :pair_rows]
    else:
        (pooled_all,) = exchange(
            [jnp.stack(pooled).reshape(-1, 128)], ["all"], ndp, nz, 2, "gather_pooled"
        )
        pooled_all = pooled_all.reshape(n, 2, pair_rows, 2, D).astype(jnp.float32)
        pooled_all = pooled_all.transpose(1, 3, 0, 2, 4).reshape(2, 2, total_pairs, D)

        def whole_loss(pooled_now):
            summed = contrastive_terms(
                pooled_now[0, 0],
                pooled_now[1, 0],
                pooled_now[0, 1],
                pooled_now[1, 1],
                false_all,
                pair_all,
            )
            valid_total = jnp.sum((pair_all >= 0).astype(jnp.float32))
            return summed / jnp.maximum(valid_total, 1.0)

        loss, pooled_grads = jax.value_and_grad(whole_loss)(pooled_all)
        pooled_grads = lax.dynamic_slice_in_dim(pooled_grads, me * pair_rows, pair_rows, 2)
    pooled_grads = pooled_grads.transpose(0, 2, 1, 3).reshape(2, seq_rows, D)
    shallow_back, deep_back = pooled_grads[0], pooled_grads[1]
    share = key_mask.astype(jnp.float32) / seq_lengths.astype(jnp.float32)[:, None]
    grad_hidden = jnp.zeros_like(embedded)
    weight_parts, layer_pairs = [], []
    vec_grads = [None] * LAYERS
    for layer_index in range(LAYERS - 1, -1, -1):
        if layer_index == LAYERS - 1:
            grad_hidden = grad_hidden + deep_back[:, None, :] * share[:, :, None]
        if layer_index == 0:
            grad_hidden = grad_hidden + shallow_back[:, None, :] * share[:, :, None]
        by_scatter = []

        def scatter(pairs, after):
            both = jnp.concatenate([weight_gradient(*pair) for pair in pairs], axis=1)
            both, after = lax.optimization_barrier((both, after))
            by_scatter.append(lax.psum_scatter(both, "zero", scatter_dimension=0, tiled=True))
            return after

        early = by_hand and layer_index == LAYERS - 1
        grad_hidden, pairs, vec_grads[layer_index] = layer_backward(
            saved[layer_index],
            layer_weights[layer_index],
            vec_parts[1 + layer_index],
            mask,
            grad_hidden,
            scatter if early else lambda pairs, after: after,
        )
        if not by_hand:
            grad_hidden = scatter(pairs, grad_hidden)
        layer_pairs.insert(0, pairs)
        weight_parts = by_scatter + weight_parts
    rows_grad, embed_grads = embed_back(grad_hidden)
    vec_grad = jnp.concatenate([embed_grads] + vec_grads, axis=0)
    down_local = jnp.stack([part[5 + FF // D] for part in vec_grads])

    rows_grad = rows_grad.reshape(tokens, D).astype(jnp.bfloat16)

    def slot_sums(slot_now):
        picked = one_hot(slot_now, nz * room)
        return lax.dot_general(
            picked, rows_grad, (((0,), (0,)), ((), ())), preferred_element_type=jnp.float32
        ).astype(jnp.bfloat16)

    def into_rows(wanted, sums):
        return lax.dot_general(
            one_hot(wanted.reshape(-1), shard_rows),
            sums.reshape(-1, D),
            (((0,), (0,)), ((), ())),
            preferred_element_type=jnp.float32,
        )

    down_each = down_local.reshape(LAYERS, nz, -1).transpose(1, 0, 2).reshape(nz, -1)
    down_len = down_each.shape[1]
    vec_blocks = jnp.concatenate([vec_grad.reshape(nz, vec_len), down_each], axis=1)
    lines = -(-vec_blocks.shape[1] // 1024) * 8
    vec_blocks = jnp.pad(vec_blocks, ((0, 0), (0, lines * 128 - vec_blocks.shape[1])))
    sums = slot_sums(slot).reshape(nz, room, D)

    def more_sums(state):
        round_index, grad_now, square_now = state
        slot_now, asked_now = round_of(round_index)
        wanted = lax.all_to_all(asked_now.reshape(nz, room), "zero", 0, 0, tiled=True)
        got = lax.all_to_all(slot_sums(slot_now).reshape(nz, room, D), "zero", 0, 0, tiled=True)
        wanted = lax.all_gather(wanted, "dp", axis=0, tiled=True)
        got = lax.all_gather(got, "dp", axis=0, tiled=True)
        more = into_rows(wanted, got)
        grown = lax.psum(jnp.sum(more * (2.0 * grad_now + more)), "zero")
        return round_index + 1, grad_now + more, square_now + grown

    if by_hand:
        attn_shard, ffn_shard, word_grad, vec_sum, squares = exchange_gradients(
            layer_pairs[0] + layer_pairs[1][:2],
            vec_blocks.reshape(4, 2, 2, lines, 128),
            sums,
            weight_parts[0],
            asked_mine.reshape(ndp, 1, nz * room),
            shard_rows,
            vec_len,
            3,
        )
        vec_sum = vec_sum.reshape(-1)
        square_total = squares[0, 0]
    else:
        sums_all, vec_shares = exchange(
            [sums, vec_blocks.reshape(nz, lines, 128)],
            ["all_p", "all_p"],
            ndp,
            nz,
            3,
            "send_gradients",
        )
        vec_sum = jnp.sum(vec_shares.reshape(n, -1), axis=0)
        (weight_all,) = exchange([jnp.stack(weight_parts)], ["dp"], ndp, nz, 4, "sum_replicas")
        weight_sum = jnp.sum(weight_all.astype(jnp.float32), axis=0)
        attn_shard = weight_sum[:, :, : 4 * D]
        ffn_shard = weight_sum[:, :, 4 * D :]
        word_grad = into_rows(asked_mine, sums_all)
    vec_shard = vec_sum[:vec_len]
    down_shard = vec_sum[vec_len : vec_len + down_len].reshape(LAYERS, -1)

    if not by_hand:
        square_local = jnp.sum(word_grad * word_grad) + jnp.sum(vec_shard * vec_shard)
        square_local = square_local + jnp.sum(attn_shard * attn_shard)
        square_local = square_local + jnp.sum(ffn_shard * ffn_shard)
        (squares,) = exchange(
            [jnp.broadcast_to(square_local, (8, 128))], ["zero"], ndp, nz, 5, "gather_squares"
        )
        square_total = jnp.sum(squares[:, 0, 0])
    word_grad, square_total = further(more_sums, word_grad, square_total)
    grad_norm = jnp.sqrt(square_total)
    factor = jnp.minimum(1.0, CLIP_NORM / (grad_norm + 1e-06))
    word_new, word_first_new, word_second_new = adam_update(
        word_table, word_grad * factor, word_first, word_second, LEARN_RATE
    )
    vector_new, vector_first_new, vector_second_new = adam_update(
        vectors, vec_shard * factor, vector_first, vector_second, VECTOR_RATE
    )
    attn_new, attn_first_new, attn_second_new = adam_update(
        attn_w, attn_shard * factor, attn_first, attn_second, LEARN_RATE
    )
    ffn_new, ffn_first_new, ffn_second_new = adam_update(
        ffn_w, ffn_shard * factor, ffn_first, ffn_second, LEARN_RATE
    )
    return (
        loss,
        grad_norm,
        word_new,
        vector_new,
        attn_new,
        ffn_new,
        word_new.astype(jnp.bfloat16),
        vector_new.astype(jnp.bfloat16),
        attn_new.astype(jnp.bfloat16),
        ffn_new.astype(jnp.bfloat16),
        word_first_new,
        vector_first_new,
        attn_first_new,
        ffn_first_new,
        word_second_new,
        vector_second_new,
        attn_second_new,
        ffn_second_new,
        down_shard * factor,
    )


def solution(mesh):
    placed = (
        P(("dp", "zero"), None, None),
        P(("dp", "zero"), None),
        P(("dp", "zero"), None),
        P(("dp", "zero")),
        P("zero", None),
        P("zero"),
        P(None, "zero", None),
        P(None, "zero", None),
        P("zero", None),
        P("zero"),
        P(None, "zero", None),
        P(None, "zero", None),
        P("zero", None),
        P("zero"),
        P(None, "zero", None),
        P(None, "zero", None),
    )
    return jax.shard_map(
        body,
        mesh=mesh,
        in_specs=placed,
        out_specs=(
            P(),
            P(),
            P("zero", None),
            P("zero"),
            P(None, "zero", None),
            P(None, "zero", None),
            P("zero", None),
            P("zero"),
            P(None, "zero", None),
            P(None, "zero", None),
            P("zero", None),
            P("zero"),
            P(None, "zero", None),
            P(None, "zero", None),
            P("zero", None),
            P("zero"),
            P(None, "zero", None),
            P(None, "zero", None),
            P(None, "zero"),
        ),
        check_vma=False,
    )
```

```python
import functools

import jax
import jax.numpy as jnp
from jax import lax
from jax.experimental import pallas as pl
from jax.experimental.pallas import tpu as pltpu
from jax.sharding import PartitionSpec as P

D = 512
HEADS = 8
HD = 64
FF = 2048
SEQ = 128
LAYERS = 2
ADAM_STEP = 5


SOFTMAX_TEMP = 0.05
CLIP_NORM = 1.0
LEARN_RATE = 0.02
VECTOR_RATE = 0.15
BETA_ONE = 0.5
BETA_TWO = 0.5
WEIGHT_DECAY = 0.01
ADAM_EPS = 1e-08
NORM_EPS = 1e-06
MASKED = -1000000000.0

MESH = pl.DeviceIdType.MESH


def build_low():

    def rounder(value):
        return lax.optimization_barrier(value.astype(jnp.bfloat16)).astype(jnp.float32)

    def keep_fwd(value):
        return (rounder(value), None)

    def pass_bwd(kept, grad):
        return (grad,)

    wrapped = jax.custom_vjp(rounder)
    wrapped.defvjp(keep_fwd, pass_bwd)
    return wrapped


def build_low_back():

    def identity_fn(value):
        return value

    def keep_fwd(value):
        return (value, None)

    def round_bwd(kept, grad):
        return (low(grad),)

    wrapped = jax.custom_vjp(identity_fn)
    wrapped.defvjp(keep_fwd, round_bwd)
    return wrapped


def low(value):
    return build_low()(value)


def low_back(value):
    return build_low_back()(value)


def rounded(value):
    return low(low_back(value))


def matmul(left, right):
    return jnp.dot(left, right, preferred_element_type=jnp.float32)


def einsum_plain(form, left, right):
    return jnp.einsum(form, left, right, preferred_element_type=jnp.float32)


def exchange_kernel(modes, ndp, nz, *refs):
    count = len(modes)
    ins = refs[:count]
    outs = refs[count : 2 * count]
    sems = refs[2 * count :]
    d = lax.axis_index("dp")
    z = lax.axis_index("zero")
    me = d * nz + z
    n = ndp * nz

    def peer_of(group, k):
        if group == "dp":
            pd = lax.rem(d + k, ndp)
            return pd, z, pd
        if group == "zero":
            pz = lax.rem(z + k, nz)
            return d, pz, pz
        p = lax.rem(me + k, n)
        return p // nz, lax.rem(p, nz), p

    groups = {m.split("_")[0] for m in modes}
    sizes = {"all": n, "zero": nz, "dp": ndp}
    mine = {"all": me, "zero": z, "dp": d}
    barrier = pltpu.get_barrier_semaphore()
    meet = ["all"] if "all" in groups else sorted(groups)
    total = 0
    for group in meet:
        total += sizes[group] - 1

        def greet(k, carry, group=group):
            pd, pz, _ = peer_of(group, k)
            pl.semaphore_signal(barrier, inc=1, device_id=(pd, pz), device_id_type=MESH)
            return carry

        lax.fori_loop(1, sizes[group], greet, 0)
    pl.semaphore_wait(barrier, total)

    def make(a, k):
        mode = modes[a]
        group = mode.split("_")[0]
        pd, pz, _ = peer_of(group, k)
        src = ins[a].at[pz] if mode.endswith("_p") else ins[a]
        return pltpu.make_async_remote_copy(
            src_ref=src,
            dst_ref=outs[a].at[mine[group]],
            send_sem=sems[2 * a].at[k],
            recv_sem=sems[2 * a + 1].at[k],
            device_id=(pd, pz),
            device_id_type=MESH,
        )

    for a, mode in enumerate(modes):
        group = mode.split("_")[0]

        def begin(k, carry, a=a):
            make(a, k).start()
            return carry

        lax.fori_loop(1, sizes[group], begin, 0)
    for a, mode in enumerate(modes):
        group = mode.split("_")[0]
        if mode.endswith("_p"):
            outs[a][mine[group]] = ins[a][z]
        else:
            outs[a][mine[group]] = ins[a][...]
    for a, mode in enumerate(modes):
        group = mode.split("_")[0]

        def finish(k, carry, a=a):
            make(a, k).wait()
            return carry

        lax.fori_loop(1, sizes[group], finish, 0)


def exchange(arrays, modes, ndp, nz, collective_id, name):
    sizes = {"all": ndp * nz, "zero": nz, "dp": ndp}
    outs = []
    scratch = []
    moved = 0
    for array, mode in zip(arrays, modes):
        size = sizes[mode.split("_")[0]]
        block = array.shape[1:] if mode.endswith("_p") else array.shape
        outs.append(jax.ShapeDtypeStruct((size,) + block, array.dtype))
        scratch += [pltpu.SemaphoreType.DMA((size,)), pltpu.SemaphoreType.DMA((size,))]
        one = array.dtype.itemsize
        for s in block:
            one *= s
        moved += one * size
    vmem = pl.BlockSpec(memory_space=pltpu.VMEM)
    return pl.pallas_call(
        functools.partial(exchange_kernel, tuple(modes), ndp, nz),
        out_shape=tuple(outs),
        in_specs=[vmem] * len(arrays),
        out_specs=tuple([vmem] * len(arrays)),
        scratch_shapes=scratch,
        compiler_params=pltpu.CompilerParams(
            collective_id=collective_id, has_side_effects=True, vmem_limit_bytes=48 * 1024 * 1024
        ),
        cost_estimate=pl.CostEstimate(flops=0, bytes_accessed=20 * moved, transcendentals=0),
        name=name,
    )(*arrays)


CHUNK = 1024
LAG_Z = 3
REST_EACH = 4
HALVED = (2,)


def gradient_kernel(chunks, matrices, vec_len, *refs):
    take = iter(refs)
    pairs = [(next(take), next(take)) for _ in range(matrices)]
    vec_ref, sums_ref, near_ref, asked_ref = [next(take) for _ in range(4)]
    attn_out, ffn_out, word_out, vec_out, stats_out = [next(take) for _ in range(5)]
    held = [None if chunk[1] is None else next(take) for chunk in chunks]
    bufs = [[next(take) for _ in range(6 if chunk[4] else 5)] for chunk in chunks]
    near_buf, rows_ref, sum_ref, square_ref, squares_ref = [next(take) for _ in range(5)]
    left_buf, right_buf, fetch_sem, near_held, local_sem = [next(take) for _ in range(5)]
    send_a, recv_a, send_y, recv_y, send_z, recv_z, send_x, recv_x = [next(take) for _ in range(8)]
    send_h, recv_h = next(take), next(take)
    row_send, row_recv, pass_send, pass_recv, near_sem, square_sem = [
        next(take) for _ in range(6)
    ]

    d = lax.axis_index("dp")
    z = lax.axis_index("zero")
    core = lax.rem(z, 2)
    col = lax.rem(z // 2, 2)
    line = z // 4
    sibling = z + 1 - 2 * core
    across = z + 2 - 4 * col
    attn_width = attn_out.shape[2]

    def along(k):
        return lax.rem(line + k, 4) * 4 + lax.rem(z, 4)

    barrier = pltpu.get_barrier_semaphore()

    def greet(k, carry):
        pl.semaphore_signal(
            barrier, inc=1, device_id=(d, lax.rem(z + k, 16)), device_id_type=MESH
        )
        return carry

    lax.fori_loop(1, 16, greet, 0)
    pl.semaphore_signal(barrier, inc=1, device_id=(1 - d, z), device_id_type=MESH)
    pl.semaphore_wait(barrier, 16)

    def remote(src, dst, send, recv, to):
        return pltpu.make_async_remote_copy(
            src_ref=src,
            dst_ref=dst,
            send_sem=send,
            recv_sem=recv,
            device_id=to,
            device_id_type=MESH,
        )

    def part_of(i):
        return vec_ref if held[i] is None else held[i]

    def halves(i):
        return chunks[i][4]

    def after_y(i):
        return bufs[i][1 + halves(i)]

    def half_rows(i, which):
        rows = bufs[i][0].shape[2] // 2
        return pl.ds(pl.multiple_of(which * rows, 16), rows)

    def copy_a(i):
        src = part_of(i).at[:, :, 1 - core]
        return remote(src, bufs[i][0], send_a.at[i], recv_a.at[i], (d, sibling))

    def copy_h(i):
        src = bufs[i][0].at[:, :, half_rows(i, 1 - d)]
        return remote(src, bufs[i][1], send_h.at[i], recv_h.at[i], (1 - d, z))

    def copy_y(i):
        src = bufs[i][halves(i)].at[:, 1 - col]
        return remote(src, after_y(i), send_y.at[i], recv_y.at[i], (d, across))

    def copy_z(i, k):
        src = after_y(i).at[lax.rem(line + k, 4)]
        into = bufs[i][-3].at[k - 1]
        return remote(src, into, send_z.at[i, k - 1], recv_z.at[i, k - 1], (d, along(k)))

    def copy_x(i):
        return remote(bufs[i][-2], bufs[i][-1], send_x.at[i], recv_x.at[i], (1 - d, z))

    def row_push(k):
        to = lax.rem(z + k, 16)
        return remote(sums_ref.at[to], rows_ref.at[d, z], row_send.at[k], row_recv.at[k], (d, to))

    def row_pass(k):
        at = lax.rem(z + 16 - k, 16)
        return remote(
            rows_ref.at[d, at], rows_ref.at[d, at], pass_send.at[k], pass_recv.at[k], (1 - d, z)
        )

    near = remote(near_ref, near_buf, near_sem.at[0], near_sem.at[1], (1 - d, z))

    total = len(chunks)

    def push(k, carry):
        row_push(k).start()
        return carry

    lax.fori_loop(1, 16, push, 0)
    near.start()
    near_copy = pltpu.make_async_copy(near_ref, near_held, local_sem.at[0])
    near_copy.start()
    own_copy = pltpu.make_async_copy(sums_ref.at[z], rows_ref.at[d, z], local_sem.at[1])
    own_copy.start()

    made = [i for i in range(total) if held[i] is not None]

    def fetches(i):
        _, matrix, start, width, _ = chunks[i]
        slot = made.index(i) % 2
        left, right = pairs[matrix]
        return (
            pltpu.make_async_copy(left, left_buf.at[slot], fetch_sem.at[0, slot]),
            pltpu.make_async_copy(
                right.at[:, pl.ds(start, width)],
                right_buf.at[slot, :, pl.ds(0, width)],
                fetch_sem.at[1, slot],
            ),
        )

    for copy in fetches(made[0]):
        copy.start()

    def compute(i):
        _, matrix, start, width, _ = chunks[i]
        if matrix is not None:
            place = made.index(i)
            slot = place % 2
            if place + 1 < len(made):
                for copy in fetches(made[place + 1]):
                    copy.start()
            for copy in fetches(i):
                copy.wait()

            def rows_of(j, carry):
                at = pl.ds(pl.multiple_of(j * 128, 128), 128)
                found = lax.dot_general(
                    left_buf[slot, :, at],
                    right_buf[slot, :, 0:width],
                    (((0,), (0,)), ((), ())),
                    preferred_element_type=jnp.float32,
                )
                held[i][j] = found.astype(jnp.bfloat16).reshape(2, 2, 32, width)
                return carry

            lax.fori_loop(0, 4, rows_of, 0)
        copy_a(i).start()

    def add_into(buf, count, place, mine):
        def add_block(b, carry):
            at = place(b)
            value = mine(b).astype(jnp.float32) + buf[at].astype(jnp.float32)
            buf[at] = value.astype(buf.dtype)
            return carry

        lax.fori_loop(0, count, add_block, 0)

    def stage_a(i):
        copy_a(i).wait_recv()
        add_into(
            bufs[i][0],
            8,
            lambda b: (b // 2, lax.rem(b, 2)),
            lambda b: part_of(i)[b // 2, lax.rem(b, 2), core],
        )
        (copy_h if halves(i) else copy_y)(i).start()

    def stage_h(i):
        copy_h(i).wait_recv()
        add_into(
            bufs[i][1],
            8,
            lambda b: (b // 2, lax.rem(b, 2)),
            lambda b: bufs[i][0][b // 2, lax.rem(b, 2), half_rows(i, d), :],
        )
        copy_y(i).start()

    def stage_y(i):
        copy_y(i).wait_recv()
        add_into(after_y(i), 4, lambda b: b, lambda b: bufs[i][halves(i)][b, col])
        for k in range(1, 4):
            copy_z(i, k).start()

    def stage_z(i):
        for k in range(1, 4):
            copy_z(i, k).wait_recv()
        value = after_y(i)[line].astype(jnp.float32)
        for k in range(3):
            value = value + bufs[i][-3][k].astype(jnp.float32)
        bufs[i][-2][...] = value.astype(bufs[i][-2].dtype)
        copy_x(i).start()

    def stage_x(i):
        target, _, start, width, _ = chunks[i]
        copy_x(i).wait_recv()
        mine, other = bufs[i][-2][...].astype(jnp.float32), bufs[i][-1][...].astype(jnp.float32)
        if target is None:
            vec_out[...] = mine + other
            return
        layer, first = target[0], target[1] + start
        out, first = (attn_out, first) if first < attn_width else (ffn_out, first - attn_width)
        if halves(i):
            out[layer, half_rows(i, d), first : first + width] = mine
            out[layer, half_rows(i, 1 - d), first : first + width] = other
        else:
            out[layer, :, first : first + width] = mine + other

    def steps_of(i):
        if halves(i):
            order = ((stage_a, 0), (stage_h, 1), (stage_y, 2), (stage_z, 2 + LAG_Z), (stage_x, 3 + LAG_Z))
        else:
            order = ((stage_a, 0), (stage_y, 1), (stage_z, 1 + LAG_Z), (stage_x, 2 + LAG_Z))
        return [(i + later, now) for now, later in order]

    def pass_on(k):
        row_push(k).wait_recv()
        row_pass(k).start()

    shard_rows, features = word_out.shape
    tiles = -(-shard_rows // 128)
    spots = rows_ref.shape[1] * rows_ref.shape[2]
    sum_ref[...] = jnp.zeros_like(sum_ref)

    def into_rows(plane, first, count):
        row = lax.broadcasted_iota(jnp.int32, (128, 1), 0) + first
        picked = (asked_ref[plane] == row).astype(jnp.bfloat16)
        return jnp.dot(
            picked, rows_ref[plane].reshape(spots, features), preferred_element_type=jnp.float32
        )[:count]

    def own_rows(tile):
        first, count = tile * 128, min(128, shard_rows - tile * 128)
        word_out[first : first + count, :] = into_rows(d, first, count)

    def all_arrived():
        def arrived(k, carry):
            ref = rows_ref.at[1 - d, lax.rem(z + 16 - k, 16)]
            remote(ref, ref, pass_send.at[k], pass_recv.at[k], (1 - d, z)).wait_recv()
            return carry

        lax.fori_loop(0, 16, arrived, 0)

    def other_rows(tile):
        first, count = tile * 128, min(128, shard_rows - tile * 128)
        value = word_out[first : first + count, :] + into_rows(1 - d, first, count)
        word_out[first : first + count, :] = value
        sum_ref[...] = sum_ref[...] + jnp.sum(value * value, axis=0, keepdims=True)

    rest = [functools.partial(own_rows, tile) for tile in range(tiles)]
    rest += [all_arrived] + [functools.partial(other_rows, tile) for tile in range(tiles)]

    compute(0)
    own_copy.wait()
    row_pass(0).start()
    passed = 1
    for t in range(total + LAG_Z + 3):
        if t + 1 < total:
            compute(t + 1)
        for i in range(total - 1, -1, -1):
            for at, now in steps_of(i):
                if at == t:
                    now(i)
        until = min(16, 1 + (t + 1) * 15 // (total - 2))
        for k in range(passed, until):
            pass_on(k)
        passed = until
        if t >= total - 2:
            for _ in range(min(len(rest), REST_EACH)):
                rest.pop(0)()
    while rest:
        rest.pop(0)()

    near.wait()
    near_copy.wait()
    ffn_out[1] = near_held[...].astype(jnp.float32) + near_buf[...].astype(jnp.float32)
    squares = sum_ref[...]
    square = jnp.sum(squares, axis=1, keepdims=True)
    for out in (attn_out, ffn_out):

        def of_rows(r, carry, out=out):
            at = pl.ds(pl.multiple_of(r * 8, 8), 8)
            for layer in range(out.shape[0]):
                value = out[layer, at, :]
                carry = carry + jnp.sum(value * value, axis=0, keepdims=True)
            return carry

        found = lax.fori_loop(
            0, out.shape[1] // 8, of_rows, jnp.zeros((1, out.shape[2]), jnp.float32)
        )
        square = square + jnp.sum(found, axis=1, keepdims=True)
    place = lax.broadcasted_iota(jnp.int32, vec_out.shape, 0) * 128 + lax.broadcasted_iota(
        jnp.int32, vec_out.shape, 1
    )
    value = jnp.where(place < vec_len, vec_out[...], 0.0)
    found = jnp.sum(value * value, axis=0, keepdims=True)
    square = square + jnp.sum(found, axis=1, keepdims=True)
    square_ref[...] = jnp.broadcast_to(square, square_ref.shape)

    def square_copy(k, slot):
        return remote(
            square_ref,
            squares_ref.at[slot],
            square_sem.at[0, k],
            square_sem.at[1, k],
            (d, lax.rem(z + k, 16)),
        )

    def send_square(k, carry):
        square_copy(k, z).start()
        return carry

    lax.fori_loop(1, 16, send_square, 0)
    squares_ref[z] = square_ref[...]

    for i in range(total):
        copy_a(i).wait_send()
        if halves(i):
            copy_h(i).wait_send()
        copy_y(i).wait_send()
        for k in range(1, 4):
            copy_z(i, k).wait_send()
        copy_x(i).wait_send()

    def finish(k, carry):
        row_push(k).wait_send()
        square_copy(k, lax.rem(z + 16 - k, 16)).wait_recv()
        square_copy(k, z).wait_send()
        return carry

    lax.fori_loop(1, 16, finish, 0)

    def finish_pass(k, carry):
        row_pass(k).wait_send()
        return carry

    lax.fori_loop(0, 16, finish_pass, 0)
    norm = squares_ref[0]
    for slot in range(1, 16):
        norm = norm + squares_ref[slot]
    stats_out[...] = jnp.broadcast_to(norm, stats_out.shape)


def exchange_gradients(pairs, vec_parts, sums, near, asked, shard_rows, vec_len, collective_id):
    spans = []
    for index, (_, right) in enumerate(pairs):
        layer, matrix = index // 4, index % 4
        columns = right.shape[1]
        width = columns // -(-columns // CHUNK)
        offset = sum(pairs[m][1].shape[1] for m in range(matrix))
        for start in range(0, columns, width):
            spans.append(((layer, offset), index, start, width, index in HALVED))
    plain = [chunk for chunk in spans if not chunk[4]]
    halved = [chunk for chunk in spans if chunk[4]]
    chunks = [(None, None, 0, 128, False)]
    while plain or halved:
        chunks += halved[:1] + plain[:1]
        halved, plain = halved[1:], plain[1:]
    half = jnp.bfloat16
    held, bufs = [], []
    for _, index, _, width, halves in chunks:
        kind = vec_parts.dtype if index is None else half
        r = vec_parts.shape[3] if index is None else 32
        if index is not None:
            held.append(pltpu.VMEM((4, 2, 2, r, width), kind))
        bufs.append(pltpu.VMEM((4, 2, r, width), kind))
        if halves:
            r = r // 2
            bufs.append(pltpu.VMEM((4, 2, r, width), kind))
        bufs += [
            pltpu.VMEM((4, r, width), kind),
            pltpu.VMEM((3, r, width), kind),
            pltpu.VMEM((r, width), kind),
            pltpu.VMEM((r, width), kind),
        ]
    features = sums.shape[2]
    dma = pltpu.SemaphoreType.DMA
    count = len(chunks)
    scratch = held + bufs
    scratch += [
        pltpu.VMEM(near.shape, half),
        pltpu.VMEM((2,) + sums.shape, half),
        pltpu.VMEM((1, features), jnp.float32),
        pltpu.VMEM((1, 128), jnp.float32),
        pltpu.VMEM((16, 1, 128), jnp.float32),
        pltpu.VMEM((2,) + pairs[0][0].shape, half),
        pltpu.VMEM((2, pairs[0][0].shape[0], max(chunk[3] for chunk in chunks)), half),
        dma((2, 2)),
        pltpu.VMEM(near.shape, half),
        dma((2,)),
    ]
    scratch += [dma((count,)) for _ in range(4)] + [dma((count, 3)) for _ in range(2)]
    scratch += [dma((count,)) for _ in range(4)]
    scratch += [dma((16,)) for _ in range(4)] + [dma((2,)), dma((2, 16))]
    rows = near.shape[0]
    outs = [
        jax.ShapeDtypeStruct((2, rows, 4 * D), jnp.float32),
        jax.ShapeDtypeStruct((2, rows, 2 * FF), jnp.float32),
        jax.ShapeDtypeStruct((shard_rows, features), jnp.float32),
        jax.ShapeDtypeStruct(vec_parts.shape[3:], jnp.float32),
        jax.ShapeDtypeStruct((8, 128), jnp.float32),
    ]
    vmem = pl.BlockSpec(memory_space=pltpu.VMEM)
    hbm = pl.BlockSpec(memory_space=pltpu.HBM)
    return pl.pallas_call(
        functools.partial(gradient_kernel, tuple(chunks), len(pairs), vec_len),
        out_shape=tuple(outs),
        in_specs=[hbm] * (2 * len(pairs)) + [vmem, hbm, hbm, vmem],
        out_specs=tuple([vmem] * len(outs)),
        scratch_shapes=scratch,
        compiler_params=pltpu.CompilerParams(
            collective_id=collective_id, has_side_effects=True, vmem_limit_bytes=58 * 1024 * 1024
        ),
        cost_estimate=pl.CostEstimate(flops=0, bytes_accessed=200_000_000, transcendentals=0),
        name="exchange_gradients",
    )(*[array for pair in pairs for array in pair], vec_parts, sums, near, asked)


SPLITS = 4
WINDOW = 2
LAG = 3


def start_kernel(shard_rows, room, *refs):
    column_ref, row_ref, packet_ref, vec_ref, attn_ref, ffn_ref, word_ref = refs[:7]
    place_out, slot_out, packet_out, asked_out, vec_out, rows_out, *weight_outs = refs[7:15]
    table, rows_held, asked, words, own, attn_held, ffn_held = refs[15:22]
    packet_sem, near_sem, far_sem, vec_sem, row_sem = refs[22:27]
    z_sem, y_sem, x_sem, d_sem, e_sem, own_sem, word_sem, self_sem = refs[27:]

    d = lax.axis_index("dp")
    z = lax.axis_index("zero")
    me = d * 16 + z
    core = lax.rem(z, 2)
    col = lax.rem(z // 2, 2)
    line = z // 4
    sibling = z + 1 - 2 * core
    across = z + 2 - 4 * col
    layers = attn_ref.shape[0]
    width = attn_ref.shape[2]
    whole = 3 * width
    unit = whole // 128 // SPLITS
    hand = unit * 5 // 12
    total = layers * SPLITS

    def everyone(k):
        p = lax.rem(me + k, 32)
        return (p // 16, lax.rem(p, 16))

    held_copies = [
        pltpu.make_async_copy(attn_ref, attn_held, word_sem.at[1]),
        pltpu.make_async_copy(ffn_ref, ffn_held, word_sem.at[2]),
    ]
    for copy in held_copies:
        copy.start()
    word_copy = pltpu.make_async_copy(word_ref, words, word_sem.at[0])
    word_copy.start()
    barrier = pltpu.get_barrier_semaphore()

    def greet(k, carry):
        pl.semaphore_signal(barrier, inc=1, device_id=everyone(k), device_id_type=MESH)
        return carry

    lax.fori_loop(1, 32, greet, 0)
    for copy in held_copies:
        copy.wait()

    def self_copy(layer):
        return pltpu.make_async_copy(own.at[layer], weight_outs[layer].at[z], self_sem.at[layer])

    for layer in range(layers):
        own[layer, :, 0:width] = attn_held[layer].astype(jnp.bfloat16)
        own[layer, :, width:whole] = ffn_held[layer].astype(jnp.bfloat16)
        self_copy(layer).start()
    for layer in range(layers):
        self_copy(layer).wait()
    pl.semaphore_wait(barrier, 31)

    def remote(src, dst, sems, at, to):
        return pltpu.make_async_remote_copy(
            src_ref=src,
            dst_ref=dst,
            send_sem=sems.at[(0,) + at],
            recv_sem=sems.at[(1,) + at],
            device_id=to,
            device_id_type=MESH,
        )

    def packet_copy(k, slot):
        return remote(packet_ref, packet_out.at[slot], packet_sem, (k,), everyone(k))

    def near_copy(k, slot):
        to = lax.rem(z + k, 16)
        return remote(asked.at[to], asked_out.at[slot], near_sem, (k,), (d, to))

    def far_copy(k, slot):
        to = lax.rem(z + k, 16)
        return remote(asked.at[to], asked_out.at[slot], far_sem, (k,), (1 - d, to))

    def vec_copy(k, slot):
        return remote(vec_ref, vec_out.at[slot], vec_sem, (k,), (d, lax.rem(z + k, 16)))

    def row_copy(k, slot):
        to = lax.rem(z + k, 16)
        return remote(rows_held.at[to], rows_out.at[slot], row_sem, (k,), (d, to))

    def shard(i):
        at = lax.rem(line + i % 4, 4) * 4 + lax.rem(z, 4)
        return at if i < 4 else at + 2 - 4 * col

    def piece(s):
        layer, p = s // SPLITS, s % SPLITS
        size = unit if p < SPLITS - 1 else whole // 128 - p * unit
        return layer, p * unit, size

    def columns_of(at, s, first, size):
        layer, base, _ = piece(s)
        return weight_outs[layer].at[
            at, :, pl.ds(pl.multiple_of((base + first) * 128, 128), size * 128)
        ]

    def stretch(at, s, ours):
        size = piece(s)[2]
        return columns_of(at, s, ours * hand, size - hand)

    def handed(at, s, ours):
        size = piece(s)[2]
        return columns_of(at, s, ours * (size - hand), hand)

    def both(ref, sems, at, to):
        return remote(ref, ref, sems, at, to)

    def z_copy(s, k, at):
        to = lax.rem(line + k, 4) * 4 + lax.rem(z, 4)
        return both(stretch(at, s, d), z_sem, (s, k - 1), (d, to))

    def y_copy(s, j, at):
        return both(stretch(at, s, d), y_sem, (s, j), (d, across))

    def x_copy(s, i, at, ours):
        return both(handed(at, s, ours), x_sem, (s, i), (1 - d, z))

    def d_copy(s, i, at):
        return both(stretch(at, s, d), d_sem, (s, i), (d, sibling))

    def e_copy(s, i, at):
        return both(handed(at, s, 1 - d), e_sem, (s, i), (d, sibling))

    def own_copy(layer, at):
        ref = weight_outs[layer].at[at]
        return both(ref, own_sem, (layer,), (d, sibling))

    def spread(s, i):
        at = shard(i)
        if i < 4:
            y_copy(s, i, at).start()
        if i > 0:
            x_copy(s, i, at, d).start()
            d_copy(s, i, at).start()

    def open_piece(s):
        for k in range(1, 4):
            z_copy(s, k, z).start()
        spread(s, 0)

    for s in range(WINDOW):
        open_piece(s)

    tokens = column_ref.shape[0]
    ids_row = row_ref[...]
    lane = lax.broadcasted_iota(jnp.int32, (1, tokens), 1).astype(jnp.float32)
    block = 128

    def lead_of(b, least):
        ids = column_ref[pl.ds(pl.multiple_of(b * block, block), block), :]
        there = lax.broadcasted_iota(jnp.int32, (block, 1), 0) + b * block
        found = jnp.where(ids == ids_row, there.astype(jnp.float32), 1e9)
        return jnp.minimum(least, jnp.min(found, axis=0, keepdims=True))

    least = lax.fori_loop(0, tokens // block, lead_of, jnp.full((1, tokens), 1e9, jnp.float32))
    lead_ids = jnp.where(least == lane, ids_row, -1)

    lane128 = lax.broadcasted_iota(jnp.int32, (1, 128), 1).astype(jnp.float32)

    def place_of(b, carry):
        most, best = carry
        at = pl.ds(pl.multiple_of(b * block, block), block)
        ids = column_ref[at, :]
        owner = jnp.floor((ids.astype(jnp.float32) + 0.5) * (1.0 / shard_rows))
        low_id = owner.astype(jnp.int32) * shard_rows
        ahead = (lead_ids >= low_id) & (lead_ids < ids)
        place = jnp.sum(jnp.where(ahead, 1.0, 0.0), axis=1, keepdims=True)
        place_out[at, :] = place.astype(jnp.int32)
        inside = place < room
        slot_out[at, :] = jnp.where(inside, owner * room + place, -1.0).astype(jnp.int32)
        slot = jnp.broadcast_to(jnp.where(inside, owner * 128.0 + place, -1.0), (block, 128))
        local = jnp.broadcast_to((ids - low_id).astype(jnp.float32), (block, 128))
        grown = []
        for o in range(16):
            found = jnp.where(slot == o * 128.0 + lane128, local, -1.0)
            found = jnp.max(found.reshape(block // 8, 8, 128), axis=0)
            grown.append(jnp.maximum(best[o], found))
        return jnp.maximum(most, jnp.max(place, axis=0, keepdims=True)), tuple(grown)

    most, best = lax.fori_loop(
        0,
        tokens // block,
        place_of,
        (jnp.zeros((1, 1), jnp.float32), (jnp.full((8, 128), -1.0, jnp.float32),) * 16),
    )
    rounds = jnp.ones((1, 1), jnp.float32)
    for r in range(1, -(-tokens // room)):
        rounds = rounds + (most >= r * room).astype(jnp.float32)
    for o in range(16):
        found = jnp.max(best[o], axis=0, keepdims=True)
        asked[o] = jnp.where(lane128 == 127.0, rounds, found).astype(jnp.int32)

    def send_near(k, carry):
        near_copy(k, me).start()
        return carry

    lax.fori_loop(1, 16, send_near, 0)

    def send_far(k, carry):
        far_copy(k, me).start()
        return carry

    lax.fori_loop(0, 16, send_far, 0)

    def send_packets(k, carry):
        packet_copy(k, me).start()
        return carry

    lax.fori_loop(1, 32, send_packets, 0)

    def send_vec(k, carry):
        vec_copy(k, z).start()
        return carry

    lax.fori_loop(1, 16, send_vec, 0)
    for layer in range(layers):
        own_copy(layer, z).start()
    vec_out[z] = vec_ref[...]
    asked_out[me] = asked[z]
    packet_out[me] = packet_ref[...]

    body_rows = shard_rows // 16 * 16
    step = 112 if body_rows % 112 == 0 else 16

    def to_half(i, carry):
        at = pl.multiple_of(i * step, 16)
        table[pl.ds(at, step), :] = words[pl.ds(at, step), :].astype(jnp.bfloat16)
        return carry

    word_copy.wait()
    lax.fori_loop(0, body_rows // step, to_half, 0)
    padded = table.shape[0]
    table[body_rows:padded, :] = jnp.zeros((padded - body_rows, table.shape[1]), jnp.bfloat16)
    if shard_rows > body_rows:
        table[body_rows:shard_rows, :] = words[body_rows:shard_rows, :].astype(jnp.bfloat16)

    def answer_one(k, carry):
        src = lax.rem(z + k, 16)
        rows_at = lax.broadcasted_iota(jnp.int32, (padded, 128), 0)
        picked = (rows_at == asked_out[d * 16 + src]).astype(jnp.bfloat16)
        found = lax.dot_general(
            picked, table[...], (((0,), (0,)), ((), ())), preferred_element_type=jnp.float32
        )
        rows_held[src] = found[:room, :].astype(jnp.bfloat16)
        return carry

    def packet_in(k, carry):
        near_copy(k, d * 16 + lax.rem(z + 16 - k, 16)).wait_recv()
        return carry

    def row_start(k, carry):
        row_copy(k, z).start()
        return carry

    def z_phase(s):
        for k in range(1, 4):
            z_copy(s, k, shard(4 - k)).wait_recv()
            spread(s, 4 - k)
        if s + WINDOW < total:
            open_piece(s + WINDOW)

    def y_phase(s):
        for j in range(4):
            y_copy(s, j, shard(4 + j)).wait_recv()
            spread(s, 4 + j)

    def x_phase(s):
        for i in range(1, 8):
            at = shard(i)
            x_copy(s, i, at, 1 - d).wait_recv()
            e_copy(s, i, at).start()

    done = 0
    for t in range(total + LAG):
        if t < total:
            z_phase(t)
        if t == 1:
            lax.fori_loop(1, 16, packet_in, 0)
        if t >= 1:
            until = min(16, done + 4)
            if until > done:
                lax.fori_loop(done, until, answer_one, 0)
            done = until
        if t == total - 1:
            lax.fori_loop(1, 16, row_start, 0)
            rows_out[z] = rows_held[z]
        if 0 <= t - 1 < total:
            y_phase(t - 1)
        if 0 <= t - LAG < total:
            x_phase(t - LAG)

    turn = 1 - 2 * core
    for layer in range(layers):
        own_copy(layer, z + turn).wait_recv()
        own_copy(layer, z).wait_send()
    for s in range(total):
        for i in range(1, 8):
            at = shard(i)
            d_copy(s, i, at + turn).wait_recv()
            d_copy(s, i, at).wait_send()
            e_copy(s, i, at + turn).wait_recv()
            e_copy(s, i, at).wait_send()
            x_copy(s, i, at, d).wait_send()
        for k in range(1, 4):
            z_copy(s, k, z).wait_send()
        for i in range(4):
            y_copy(s, i, shard(i)).wait_send()

    def finish(k, carry):
        back = lax.rem(z + 16 - k, 16)
        row_copy(k, back).wait_recv()
        row_copy(k, z).wait_send()
        vec_copy(k, back).wait_recv()
        vec_copy(k, z).wait_send()
        near_copy(k, me).wait_send()
        return carry

    lax.fori_loop(1, 16, finish, 0)

    def finish_packets(k, carry):
        packet_copy(k, lax.rem(me + 32 - k, 32)).wait_recv()
        packet_copy(k, me).wait_send()
        return carry

    lax.fori_loop(1, 32, finish_packets, 0)

    def finish_far(k, carry):
        far_copy(k, (1 - d) * 16 + lax.rem(z + 16 - k, 16)).wait_recv()
        far_copy(k, me).wait_send()
        return carry

    lax.fori_loop(0, 16, finish_far, 0)


def exchange_start(ids, packet, vec_rows, attn, ffn, word_table, room, collective_id):
    half = jnp.bfloat16
    shard_rows, features = word_table.shape
    padded = -(-shard_rows // 128) * 128
    layers, rows, width = attn.shape
    tokens = ids.shape[0]
    pieces = layers * SPLITS
    dma = pltpu.SemaphoreType.DMA
    vmem = pl.BlockSpec(memory_space=pltpu.VMEM)
    anywhere = pl.BlockSpec(memory_space=pltpu.HBM)
    return pl.pallas_call(
        functools.partial(start_kernel, shard_rows, room),
        out_shape=(
            jax.ShapeDtypeStruct((tokens, 1), jnp.int32),
            jax.ShapeDtypeStruct((tokens, 1), jnp.int32),
            jax.ShapeDtypeStruct((32,) + packet.shape, packet.dtype),
            jax.ShapeDtypeStruct((32, 1, 128), jnp.int32),
            jax.ShapeDtypeStruct((16,) + vec_rows.shape, vec_rows.dtype),
            jax.ShapeDtypeStruct((16, room, features), half),
        )
        + (jax.ShapeDtypeStruct((16, rows, 3 * width), half),) * layers,
        in_specs=[vmem] * 4 + [anywhere] * 3,
        out_specs=tuple([vmem] * 6 + [anywhere] * layers),
        scratch_shapes=[
            pltpu.VMEM((padded, features), half),
            pltpu.VMEM((16, room, features), half),
            pltpu.VMEM((16, 1, 128), jnp.int32),
            pltpu.VMEM(word_table.shape, word_table.dtype),
            pltpu.VMEM((layers, rows, 3 * width), half),
            pltpu.VMEM(attn.shape, attn.dtype),
            pltpu.VMEM(ffn.shape, ffn.dtype),
            dma((2, 32)),
            dma((2, 16)),
            dma((2, 16)),
            dma((2, 16)),
            dma((2, 16)),
            dma((2, pieces, 3)),
            dma((2, pieces, 4)),
            dma((2, pieces, 8)),
            dma((2, pieces, 8)),
            dma((2, pieces, 8)),
            dma((2, layers)),
            dma((3,)),
            dma((layers,)),
        ],
        compiler_params=pltpu.CompilerParams(
            collective_id=collective_id, has_side_effects=True, vmem_limit_bytes=52 * 1024 * 1024
        ),
        cost_estimate=pl.CostEstimate(flops=0, bytes_accessed=150_000_000, transcendentals=0),
        name="exchange_start",
    )(ids.reshape(-1, 1), ids.reshape(1, -1), packet, vec_rows, attn, ffn, word_table)


WIDTHS = (D, D * 2 // 3, D // 3, D // 6, D // 12)


def gather_rows(block_ref, all_ref, z_sem, near_sem):
    d = lax.axis_index("dp")
    z = lax.axis_index("zero")
    line, spot = z // 4, lax.rem(z, 4)

    def at_line(k):
        return lax.rem(line + k, 4) * 4 + spot

    def near_by(j):
        across = j // 4
        return lax.rem(d + across, 2), line * 4 + lax.rem(spot + j % 4, 4)

    barrier = pltpu.get_barrier_semaphore()
    for k in range(1, 4):
        pl.semaphore_signal(barrier, inc=1, device_id=(d, at_line(k)), device_id_type=MESH)
    for j in range(1, 8):
        pl.semaphore_signal(barrier, inc=1, device_id=near_by(j), device_id_type=MESH)
    pl.semaphore_wait(barrier, 10)

    def z_copy(k):
        return pltpu.make_async_remote_copy(
            src_ref=block_ref,
            dst_ref=all_ref.at[d * 16 + z],
            send_sem=z_sem.at[0, k],
            recv_sem=z_sem.at[1, k],
            device_id=(d, at_line(k)),
            device_id_type=MESH,
        )

    def z_arrival(k):
        ref = all_ref.at[d * 16 + at_line(4 - k)]
        return pltpu.make_async_remote_copy(
            src_ref=ref,
            dst_ref=ref,
            send_sem=z_sem.at[0, k],
            recv_sem=z_sem.at[1, k],
            device_id=(d, at_line(k)),
            device_id_type=MESH,
        )

    def near_copy(i, j, from_d, from_z):
        ref = all_ref.at[from_d * 16 + from_z]
        return pltpu.make_async_remote_copy(
            src_ref=ref,
            dst_ref=ref,
            send_sem=near_sem.at[0, i, j],
            recv_sem=near_sem.at[1, i, j],
            device_id=near_by(j),
            device_id_type=MESH,
        )

    for k in range(1, 4):
        z_copy(k).start()
    all_ref[d * 16 + z] = block_ref[...]
    for j in range(1, 8):
        near_copy(0, j, d, z).start()
    for k in range(1, 4):
        z_arrival(k).wait_recv()
        for j in range(1, 8):
            near_copy(4 - k, j, d, at_line(4 - k)).start()
    for i in range(4):
        for j in range(1, 8):
            back = lax.rem(line + i, 4) * 4 + lax.rem(spot + 4 - j % 4, 4)
            near_copy(i, j, lax.rem(d + j // 4, 2), back).wait_recv()
            near_copy(i, j, d, at_line(i)).wait_send()
    for k in range(1, 4):
        z_copy(k).wait_send()


def contrastive_kernel(
    block_ref, false_ref, pair_ref, loss_ref, own_ref, all_ref, pooled_ref, grad_ref, z_sem, near_sem
):
    me = lax.axis_index("dp") * 16 + lax.axis_index("zero")
    gather_rows(block_ref, all_ref, z_sem, near_sem)
    upper = lax.broadcasted_iota(jnp.int32, (8, 1), 0) < 4
    for kind in range(2):
        for two in range(all_ref.shape[0] // 2):
            even = all_ref[2 * two, kind].astype(jnp.float32)
            odd = all_ref[2 * two + 1, kind].astype(jnp.float32)
            at = slice(8 * two, 8 * two + 8)
            pooled_ref[kind, 0, at, :] = jnp.where(upper, even, pltpu.roll(odd, 4, 0))
            pooled_ref[kind, 1, at, :] = jnp.where(upper, pltpu.roll(even, 4, 0), odd)
    contrastive_math(pooled_ref, false_ref, pair_ref, loss_ref, grad_ref)
    first = pl.multiple_of(me // 2 * 8, 8)
    swap = lax.rem(me, 2) == 1
    for kind in range(2):
        for role in range(2):
            rows = grad_ref[kind, role, pl.ds(first, 8), :]
            own_ref[kind, role] = jnp.where(swap, pltpu.roll(rows, 4, 0), rows)


def contrastive_math(pooled_ref, false_ref, pair_ref, loss_ref, grad_ref):
    pairs = false_ref.shape[0]
    high = lax.Precision.HIGHEST
    columns = lax.broadcasted_iota(jnp.int32, (pairs, pairs), 1)
    hit = columns == pair_ref[...]
    kept = (false_ref[...] == 0) | hit
    hits = hit.astype(jnp.float32)
    valid = (pair_ref[...] >= 0).astype(jnp.float32)
    inverse = 1.0 / jnp.maximum(jnp.sum(valid, axis=0, keepdims=True), 1.0)
    weight = valid * inverse
    named = jnp.sum(hits, axis=1, keepdims=True)
    totals = jnp.zeros((pairs, 1), jnp.float32)
    for first, width in enumerate(WIDTHS):
        span = -(-width // 128) * 128
        inside = lax.broadcasted_iota(jnp.int32, (1, span), 1) < width
        units, scales, logs = [], [], []
        for kind in range(2):
            pair_units, pair_scales = [], []
            for role in range(2):
                rows = jnp.where(inside, pooled_ref[kind, role, :, 0:span], 0.0)
                scale = lax.rsqrt(jnp.sum(rows * rows, axis=1, keepdims=True) + NORM_EPS)
                pair_units.append(rows * scale)
                pair_scales.append(scale)
            sims = lax.dot_general(
                pair_units[0],
                pair_units[1],
                (((1,), (1,)), ((), ())),
                precision=high,
                preferred_element_type=jnp.float32,
            )
            sims = jnp.where(kept, sims / SOFTMAX_TEMP, MASKED)
            shifted = sims - jnp.max(sims, axis=1, keepdims=True)
            logs.append(shifted - jnp.log(jnp.sum(jnp.exp(shifted), axis=1, keepdims=True)))
            units.append(pair_units)
            scales.append(pair_scales)
        shallow, deep = logs
        p_shallow, p_deep = jnp.exp(shallow), jnp.exp(deep)
        gap = p_deep * (deep - shallow)
        spread = jnp.sum(gap, axis=1, keepdims=True)
        totals = totals + spread - jnp.sum(jnp.where(hit, shallow + deep, 0.0), axis=1, keepdims=True)
        d_sims = (
            p_shallow * (named + 1.0) - hits - p_deep,
            gap + p_deep * (named - spread) - hits,
        )
        for kind in range(2):
            d_cos = jnp.where(kept, d_sims[kind] * weight, 0.0) / SOFTMAX_TEMP
            for role in range(2):
                unit = units[kind][role]
                d_unit = lax.dot_general(
                    d_cos,
                    units[kind][1 - role],
                    (((1 - role,), (0,)), ((), ())),
                    precision=high,
                    preferred_element_type=jnp.float32,
                )
                along = jnp.sum(d_unit * unit, axis=1, keepdims=True)
                d_rows = scales[kind][role] * (d_unit - unit * along)
                if first == 0:
                    grad_ref[kind, role] = d_rows
                else:
                    grad_ref[kind, role, :, 0:span] = grad_ref[kind, role, :, 0:span] + d_rows
    loss_ref[...] = jnp.broadcast_to(
        jnp.sum(totals * valid, axis=0, keepdims=True) * inverse, loss_ref.shape
    )


def contrastive(block, false_all, pair_all, collective_id):
    vmem = pl.BlockSpec(memory_space=pltpu.VMEM)
    pairs = false_all.shape[0]
    dma = pltpu.SemaphoreType.DMA
    whole = pltpu.VMEM((2, 2, pairs, D), jnp.float32)
    loss, grads = pl.pallas_call(
        contrastive_kernel,
        out_shape=(
            jax.ShapeDtypeStruct((8, 128), jnp.float32),
            jax.ShapeDtypeStruct((2, 2, 8, D), jnp.float32),
        ),
        in_specs=[vmem] * 3,
        out_specs=(vmem, vmem),
        scratch_shapes=[
            pltpu.VMEM((32,) + block.shape, block.dtype),
            whole,
            whole,
            dma((2, 4)),
            dma((2, 4, 8)),
        ],
        compiler_params=pltpu.CompilerParams(
            collective_id=collective_id, has_side_effects=True, vmem_limit_bytes=20 * 1024 * 1024
        ),
        cost_estimate=pl.CostEstimate(flops=10**9, bytes_accessed=3_000_000, transcendentals=10**6),
        name="contrastive",
    )(block, false_all, pair_all.reshape(-1, 1))
    return loss[0, 0], grads


PAIRS_OF_HEADS = HEADS // 2


def by_side(rows):
    lane = lax.broadcasted_iota(jnp.int32, (1, 2 * HD), 1)
    zero = jnp.zeros_like(rows)
    return jnp.concatenate([jnp.where(lane < HD, rows, zero), jnp.where(lane < HD, zero, rows)])


def join_sides(stacked):
    lane = lax.broadcasted_iota(jnp.int32, (1, 2 * HD), 1)
    return jnp.where(lane < HD, stacked[:SEQ], stacked[SEQ:])


def contract(left, right, left_dim, right_dim):
    return lax.dot_general(
        left, right, (((left_dim,), (right_dim,)), ((), ())), preferred_element_type=jnp.float32
    )


def thirds(packed_ref):
    for pair in range(PAIRS_OF_HEADS):
        at = pair * 2 * HD
        yield [packed_ref[0, :, t * D + at : t * D + at + 2 * HD] for t in range(3)]


def probabilities(scores, valid):
    scores = jnp.where(valid, scores * HD ** (-0.5), MASKED)
    raised = jnp.exp(scores - jnp.max(scores, axis=1, keepdims=True))
    return raised * (1.0 / jnp.sum(raised, axis=1, keepdims=True))


def attention_kernel(mask_ref, packed_ref, context_ref):
    valid = mask_ref[0] > 0.0
    parts = list(thirds(packed_ref))
    scores = [contract(by_side(queries), keys, 1, 1) for queries, keys, _ in parts]
    probs = [probabilities(now, valid).astype(jnp.bfloat16) for now in scores]
    for pair in range(PAIRS_OF_HEADS):
        mixed = contract(probs[pair], parts[pair][2], 1, 0)
        at = pair * 2 * HD
        context_ref[0, :, at : at + 2 * HD] = join_sides(mixed).astype(jnp.bfloat16)


def attention_back_kernel(mask_ref, packed_ref, grad_ref, out_ref):
    valid = mask_ref[0] > 0.0
    parts = list(thirds(packed_ref))
    queries = [by_side(part[0]) for part in parts]
    grads = [
        by_side(grad_ref[0, :, pair * 2 * HD : (pair + 1) * 2 * HD])
        for pair in range(PAIRS_OF_HEADS)
    ]
    scores = [contract(now, part[1], 1, 1) for now, part in zip(queries, parts)]
    d_probs = [contract(now, part[2], 1, 1) for now, part in zip(grads, parts)]
    probs = [probabilities(now, valid) for now in scores]
    d_scores = []
    for now, d_now in zip(probs, d_probs):
        shared = jnp.sum(d_now * now, axis=1, keepdims=True)
        d_scores.append(jnp.where(valid, now * (d_now - shared), 0.0).astype(jnp.bfloat16))
    for pair in range(PAIRS_OF_HEADS):
        d_queries = join_sides(contract(d_scores[pair], parts[pair][1], 1, 0)) * HD ** (-0.5)
        d_keys = contract(d_scores[pair], queries[pair], 0, 0) * HD ** (-0.5)
        d_values = contract(probs[pair].astype(jnp.bfloat16), grads[pair], 0, 0)
        for third, now in enumerate((d_queries, d_keys, d_values)):
            at = third * D + pair * 2 * HD
            out_ref[0, :, at : at + 2 * HD] = now.astype(jnp.bfloat16)


def attention_call(kernel, mask, operands, features, name):
    count = operands[0].shape[0]

    def spec(last):
        return pl.BlockSpec((1, SEQ, last), lambda i: (i, 0, 0))

    return pl.pallas_call(
        kernel,
        grid=(count,),
        out_shape=jax.ShapeDtypeStruct((count, SEQ, features), jnp.bfloat16),
        in_specs=[pl.BlockSpec((1, 1, SEQ), lambda i: (i, 0, 0))]
        + [spec(operand.shape[2]) for operand in operands],
        out_specs=spec(features),
        compiler_params=pltpu.CompilerParams(vmem_limit_bytes=14 * 1024 * 1024),
        cost_estimate=pl.CostEstimate(
            flops=10**9, bytes_accessed=count * SEQ * D * 10, transcendentals=10**6
        ),
        name=name,
    )(mask, *operands)


GELU_SCALE = 0.7978845608028654


def feed_back_kernel(middle_ref, down_ref, up_weights, down_weights, bias_ref, *outs):
    active_ref, d_up_ref, d_first_ref, total_ref = outs
    middle, d_down = middle_ref[...], down_ref[...]
    tile = FF // 4
    d_first = jnp.zeros(d_first_ref.shape, jnp.float32)
    for start in range(0, FF, tile):
        at = slice(start, start + tile)
        upward = contract(middle, up_weights[:, at], 1, 0) + bias_ref[:, at]
        d_active = contract(d_down, down_weights[:, at], 1, 0).astype(jnp.bfloat16)
        square = upward * upward
        bent = jnp.tanh(GELU_SCALE * (upward + 0.044715 * (square * upward)))
        share = 0.5 * (1.0 + bent)
        inner = GELU_SCALE * (1.0 + 3.0 * 0.044715 * square)
        slope = share + 0.5 * upward * (1.0 - bent * bent) * inner
        active_ref[:, at] = (upward * share).astype(jnp.bfloat16)
        d_up = (d_active.astype(jnp.float32) * slope).astype(jnp.bfloat16)
        d_up_ref[:, at] = d_up
        d_first = d_first + contract(d_up, up_weights[:, at], 1, 1)
        found = jnp.sum(d_up.astype(jnp.float32), axis=0, keepdims=True)
        before = jnp.where(pl.program_id(0) == 0, 0.0, total_ref[:, at])
        total_ref[:, at] = before + found
    d_first_ref[...] = d_first


def feed_back(middle, d_down, weights, up_bias):
    tokens = middle.shape[0]
    rows = 256
    half = jnp.bfloat16

    def by_rows(columns):
        return pl.BlockSpec((rows, columns), lambda i: (i, 0))

    def matrix(which):
        return pl.BlockSpec((D, FF), lambda i: (0, which))

    whole = pl.BlockSpec((1, FF), lambda i: (0, 0))
    return pl.pallas_call(
        feed_back_kernel,
        grid=(tokens // rows,),
        out_shape=(
            jax.ShapeDtypeStruct((tokens, FF), half),
            jax.ShapeDtypeStruct((tokens, FF), half),
            jax.ShapeDtypeStruct((tokens, D), jnp.float32),
            jax.ShapeDtypeStruct((1, FF), jnp.float32),
        ),
        in_specs=[by_rows(D), by_rows(D), matrix(1), matrix(2), whole],
        out_specs=(by_rows(FF), by_rows(FF), by_rows(D), whole),
        compiler_params=pltpu.CompilerParams(vmem_limit_bytes=26 * 1024 * 1024),
        cost_estimate=pl.CostEstimate(
            flops=6 * tokens * D * FF, bytes_accessed=24 * tokens * D, transcendentals=tokens * FF
        ),
        name="feed_back",
    )(middle, d_down, weights, weights, up_bias.reshape(1, FF))


def embed_back_kernel(grad_ref, normal_ref, inverse_ref, gain_ref, rows_ref, vec_ref):
    grad, normal = grad_ref[0], normal_ref[0]
    scaled = grad * gain_ref[...]
    mean = jnp.mean(scaled, axis=1, keepdims=True)
    along = jnp.mean(scaled * normal, axis=1, keepdims=True)
    values = (scaled - mean - normal * along) * inverse_ref[0]
    rows_ref[0] = values.astype(jnp.bfloat16)
    first = pl.program_id(0) == 0
    for start, stop, found in (
        (0, SEQ, values),
        (SEQ, SEQ + 1, jnp.sum(grad * normal, axis=0, keepdims=True)),
        (SEQ + 1, SEQ + 2, jnp.sum(grad, axis=0, keepdims=True)),
    ):
        before = jnp.where(first, 0.0, vec_ref[start:stop, :])
        vec_ref[start:stop, :] = before + found


def embed_back(grad, normal, inverse, gain):
    count = grad.shape[0]

    def by_sequence(last):
        return pl.BlockSpec((1, SEQ, last), lambda i: (i, 0, 0))

    def whole(rows):
        return pl.BlockSpec((rows, D), lambda i: (0, 0))

    return pl.pallas_call(
        embed_back_kernel,
        grid=(count,),
        out_shape=(
            jax.ShapeDtypeStruct((count, SEQ, D), jnp.bfloat16),
            jax.ShapeDtypeStruct((SEQ + 2, D), jnp.float32),
        ),
        in_specs=[by_sequence(D), by_sequence(D), by_sequence(1), whole(1)],
        out_specs=(by_sequence(D), whole(SEQ + 2)),
        compiler_params=pltpu.CompilerParams(vmem_limit_bytes=14 * 1024 * 1024),
        cost_estimate=pl.CostEstimate(
            flops=10 * count * SEQ * D, bytes_accessed=10 * count * SEQ * D, transcendentals=0
        ),
        name="embed_back",
    )(grad, normal, inverse, gain.reshape(1, D))


LAYER_ROWS = 8 + FF // D


def layer_vectors(rows):
    up = 5 + FF // D
    return [rows[i] for i in range(5)] + [rows[5:up].reshape(FF)] + [rows[up + i] for i in range(3)]


def layer_norm(values, gain, shift):
    center = values - jnp.mean(values, axis=-1, keepdims=True)
    spread = jnp.mean(center * center, axis=-1, keepdims=True)
    return center * lax.rsqrt(spread + NORM_EPS) * gain + shift


def norm_forward(values, gain, shift):
    center = values - jnp.mean(values, axis=-1, keepdims=True)
    inverse = lax.rsqrt(jnp.mean(center * center, axis=-1, keepdims=True) + NORM_EPS)
    normal = center * inverse
    return normal * gain + shift, normal, inverse


def norm_back(grad, normal, inverse, gain):
    scaled = grad * gain
    mean = jnp.mean(scaled, axis=-1, keepdims=True)
    along = jnp.mean(scaled * normal, axis=-1, keepdims=True)
    return (
        (scaled - mean - normal * along) * inverse,
        jnp.sum(grad * normal, axis=(0, 1)),
        jnp.sum(grad, axis=(0, 1)),
    )


def gelu(value):
    bent = jnp.tanh(GELU_SCALE * (value + 0.044715 * value * value * value))
    return 0.5 * value * (1.0 + bent)


EDGES = (0, 3 * D, 4 * D, 4 * D + FF, 4 * D + 2 * FF)


def four_matrices(weights):
    return [weights[:, first:last] for first, last in zip(EDGES, EDGES[1:])]


def layer_forward(hidden, weights, vectors, mask):
    in_weights, out_weights, up_weights, down_weights = four_matrices(weights)
    q_bias, v_bias, o_bias, gain_one, shift_one, up_bias, down_bias, gain_two, second_shift = (
        layer_vectors(vectors)
    )
    half = jnp.bfloat16
    entry = lax.optimization_barrier(hidden.astype(half))
    bias = jnp.concatenate([q_bias, jnp.zeros_like(q_bias), v_bias])
    packed = (matmul(entry, in_weights) + bias).astype(half)
    context = attention_call(attention_kernel, mask, [packed], D, "attention")
    attended = matmul(context, out_weights) + o_bias
    first, normal_one, inverse_one = norm_forward(hidden + attended, gain_one, shift_one)
    middle = lax.optimization_barrier(first.astype(half))
    upward = matmul(middle, up_weights) + up_bias
    active = lax.optimization_barrier(gelu(upward).astype(half))
    downward = einsum_plain("nsf,df->nsd", active, down_weights) + down_bias
    output, normal_two, inverse_two = norm_forward(first + downward, gain_two, second_shift)
    kept = (
        entry, packed, context, middle,
        normal_one, inverse_one, normal_two, inverse_two,
    )
    return output, kept


def layer_backward(kept, weights, vectors, mask, grad, midway):
    in_weights, out_weights, _, _ = four_matrices(weights)
    entry, packed, context, middle = kept[:4]
    normal_one, inverse_one, normal_two, inverse_two = kept[4:]
    gain_one, gain_two = layer_vectors(vectors)[3], layer_vectors(vectors)[7]
    half = jnp.bfloat16

    def total(value):
        return jnp.sum(value.astype(jnp.float32), axis=(0, 1))

    d_second, d_gain_two, d_shift_two = norm_back(grad, normal_two, inverse_two, gain_two)
    d_down = lax.optimization_barrier(d_second.astype(half))
    flat_middle, flat_down = middle.reshape(-1, D), d_down.reshape(-1, D)
    active, d_up, d_first, d_up_bias = feed_back(
        flat_middle, flat_down, weights, layer_vectors(vectors)[5]
    )
    feed_pairs = [(flat_middle, d_up), (flat_down, active)]
    d_first = midway(feed_pairs, d_second + d_first.reshape(d_second.shape))
    d_middle, d_gain_one, d_shift_one = norm_back(d_first, normal_one, inverse_one, gain_one)
    d_attended = lax.optimization_barrier(d_middle.astype(half))
    d_context = jnp.einsum(
        "nsd,ed->nse", d_attended, out_weights, preferred_element_type=jnp.float32
    ).astype(half)
    d_packed = attention_call(
        attention_back_kernel, mask, [packed, d_context], 3 * D, "attention_back"
    )
    d_hidden = d_middle + jnp.einsum(
        "nsp,dp->nsd", d_packed, in_weights, preferred_element_type=jnp.float32
    )
    packed_total = total(d_packed)
    pieces = [
        packed_total[:D], packed_total[2 * D :], total(d_attended), d_gain_one, d_shift_one,
        d_up_bias, total(d_down), d_gain_two, d_shift_two,
    ]
    d_vectors, at = jnp.zeros((LAYER_ROWS, D), jnp.float32), 0
    for piece in pieces:
        rows = piece.reshape(-1, D)
        d_vectors = d_vectors + jnp.pad(rows, ((at, LAYER_ROWS - at - rows.shape[0]), (0, 0)))
        at = at + rows.shape[0]
    flat = [
        (left.reshape(-1, left.shape[2]), right.reshape(-1, right.shape[2]))
        for left, right in ((entry, d_packed), (context, d_attended))
    ]
    return d_hidden, flat + feed_pairs, d_vectors


def weight_gradient(left, right):
    return lax.dot_general(
        left, right, (((0,), (0,)), ((), ())), preferred_element_type=jnp.float32
    ).astype(jnp.bfloat16)


def pool_rows(hidden, key_mask, seq_lengths):
    share = key_mask.astype(jnp.float32) / seq_lengths.astype(jnp.float32)[:, None]
    return jnp.sum(hidden * share[:, :, None], axis=1)


def normalized_rows(rows):
    return rows * lax.rsqrt(jnp.sum(rows * rows, axis=-1, keepdims=True) + NORM_EPS)


def contrastive_terms(shallow_anchor, deep_anchor, shallow_pos, deep_pos, false_neg, pair_index):
    columns = lax.broadcasted_iota(jnp.int32, false_neg.shape, 1)
    hit = columns == pair_index[:, None]
    kept_cols = (false_neg == 0) | hit
    valid_rows = (pair_index >= 0).astype(jnp.float32)
    totals = jnp.zeros(pair_index.shape, jnp.float32)
    for current_width in (D, D * 2 // 3, D // 3, D // 6, D // 12):
        log_probs = []
        for anchor_vectors, positive_rows in (
            (shallow_anchor, shallow_pos),
            (deep_anchor, deep_pos),
        ):
            similarity_scores = (
                jnp.dot(
                    normalized_rows(anchor_vectors[:, :current_width]),
                    normalized_rows(positive_rows[:, :current_width]).T,
                    precision=lax.Precision.HIGHEST,
                )
                / SOFTMAX_TEMP
            )
            similarity_scores = jnp.where(kept_cols, similarity_scores, MASKED)
            log_probs.append(jax.nn.log_softmax(similarity_scores, axis=-1))
        for log_now in log_probs:
            totals = totals - jnp.sum(jnp.where(hit, log_now, 0.0), axis=-1)
        totals = totals + jnp.sum(jnp.exp(log_probs[1]) * (log_probs[1] - log_probs[0]), axis=-1)
    return jnp.sum(totals * valid_rows)


def adam_update(master, gradient, first, second, step_rate):
    first_new = BETA_ONE * first + (1.0 - BETA_ONE) * gradient
    second_new = BETA_TWO * second + (1.0 - BETA_TWO) * gradient * gradient
    first_hat = first_new / (1.0 - BETA_ONE**ADAM_STEP)
    second_hat = second_new / (1.0 - BETA_TWO**ADAM_STEP)
    master_new = master - step_rate * (
        first_hat / (jnp.sqrt(second_hat) + ADAM_EPS) + WEIGHT_DECAY * master
    )
    return (master_new, first_new, second_new)


def pad_rows(flat, multiple):
    rows = -(-flat.shape[0] // (128 * multiple)) * multiple
    return jnp.pad(flat, (0, rows * 128 - flat.shape[0])).reshape(rows, 128)


def one_hot(index, size, dtype=jnp.bfloat16):
    return (index[:, None] == lax.broadcasted_iota(jnp.int32, (1, size), 1)).astype(dtype)


def token_plan(ids, shard_rows):
    places = lax.broadcasted_iota(jnp.int32, ids.shape, 0)
    same = ids[:, None] == ids[None, :]
    leader = jnp.min(jnp.where(same, places[None, :], ids.shape[0]), axis=1)
    leads = leader == places
    owner = ids // shard_rows
    low_id = owner * shard_rows
    ahead = leads[None, :] & (ids[None, :] >= low_id[:, None]) & (ids[None, :] < ids[:, None])
    place = jnp.sum(ahead.astype(jnp.int32), axis=1)
    return owner, place, ids - low_id


def round_slots(owner, place, local_row, round_index, room, nz):
    inside = (place >= round_index * room) & (place < (round_index + 1) * room)
    slot = jnp.where(inside, owner * room + place - round_index * room, -1)
    slots = lax.broadcasted_iota(jnp.int32, (1, nz * room), 1)
    asked = jnp.max(jnp.where(slot[:, None] == slots, local_row[:, None], -1), axis=0)
    return slot, asked


def body(
    token_ids,
    lengths,
    false_neg,
    pair_index,
    word_table,
    vectors,
    attn_w,
    ffn_w,
    word_first,
    vector_first,
    attn_first,
    ffn_first,
    word_second,
    vector_second,
    attn_second,
    ffn_second,
):
    ndp = lax.axis_size("dp")
    nz = lax.axis_size("zero")
    n = ndp * nz
    by_hand = (ndp, nz) == (2, 16) and token_ids.shape[0] * ndp * nz <= 256
    my_dp = lax.axis_index("dp")
    my_zero = lax.axis_index("zero")
    me = my_dp * nz + my_zero
    pair_rows = token_ids.shape[0]
    total_pairs = pair_rows * n
    flat_ids = token_ids.reshape(-1, SEQ)
    seq_rows = flat_ids.shape[0]
    tokens = seq_rows * SEQ
    seq_lengths = lengths.reshape(-1)
    key_mask = lax.broadcasted_iota(jnp.int32, flat_ids.shape, 1) < seq_lengths[:, None]
    shard_rows = word_table.shape[0]
    vec_len = vectors.shape[0]

    room = -(-(tokens * 9 // 8) // (nz * 8)) * 8
    ids = flat_ids.reshape(-1)

    def packet_of(asked, rounds_here):
        last = jnp.concatenate([pair_index, rounds_here[None].astype(jnp.int32)])
        lines = nz + false_neg.size // 128
        return jnp.concatenate(
            [
                jnp.pad(asked.reshape(nz, room), ((0, 0), (0, 128 - room)), constant_values=-1),
                false_neg.reshape(-1, 128),
                jnp.zeros((7 - lines % 8, 128), jnp.int32),
                jnp.pad(last, (0, 128 - last.shape[0]))[None],
            ]
        )

    def gather_layer(layer_index):
        both = jnp.concatenate(
            [attn_w[layer_index].astype(jnp.bfloat16), ffn_w[layer_index].astype(jnp.bfloat16)],
            axis=1,
        )
        return lax.all_gather(both, "zero", axis=0, tiled=True)

    if by_hand:
        packet = pad_rows(jnp.concatenate([false_neg.reshape(-1), pair_index]), 8)
        place, slot, packets, asked_mine, vec_parts, received, *gathered = exchange_start(
            ids,
            packet.astype(jnp.bfloat16),
            pad_rows(vectors.astype(jnp.bfloat16), 16),
            attn_w,
            ffn_w,
            word_table,
            room,
            0,
        )
        layer_weights = [part.reshape(D, -1) for part in gathered]
        rounds = jnp.max(asked_mine[:, 0, 127])
        asked_mine = asked_mine[:, 0, :room]
        packets = packets.reshape(n, -1).astype(jnp.int32)
        false_all = packets[:, : false_neg.size].reshape(total_pairs, total_pairs)
        pair_all = packets[:, false_neg.size : false_neg.size + pair_rows].reshape(total_pairs)
        place, slot = place.reshape(-1), slot.reshape(-1)
    else:
        owner, place, local_row = token_plan(ids, shard_rows)
        slot, asked = round_slots(owner, place, local_row, 0, room, nz)
        packets, vec_parts = exchange(
            [
                packet_of(asked, jnp.max(place) // room + 1),
                pad_rows(vectors.astype(jnp.bfloat16), 16),
            ],
            ["all", "zero"],
            ndp,
            nz,
            0,
            "gather_requests",
        )
        layer_weights = [gather_layer(layer_index) for layer_index in range(LAYERS)]
        asked_mine = lax.dynamic_index_in_dim(packets[:, :nz, :room], my_zero, 1, keepdims=False)
        false_all = packets[:, nz : nz + false_neg.size // 128].reshape(total_pairs, total_pairs)
        pair_all = packets[:, -1, :pair_rows].reshape(total_pairs)
        rounds = jnp.max(packets[:, -1, pair_rows])
    vec_all = vec_parts.reshape(nz, -1)[:, :vec_len].reshape(-1).astype(jnp.float32)

    asked_near = lax.dynamic_slice_in_dim(asked_mine, my_dp * nz, nz, 0)

    def rows_for(wanted):
        picked = one_hot(wanted.reshape(-1), shard_rows, jnp.float32)
        return jnp.dot(picked, word_table, precision=lax.Precision.HIGHEST).astype(jnp.bfloat16)

    def rows_from(slot_now, received):
        return matmul(one_hot(slot_now, nz * room), received.reshape(nz * room, D)).astype(
            jnp.bfloat16
        )

    if not by_hand:
        (received,) = exchange(
            [rows_for(asked_near).reshape(nz, room, D)], ["zero_p"], ndp, nz, 1, "send_rows"
        )
    rows = rows_from(slot, received)

    def round_of(round_index):
        owner = lax.div(ids, jnp.int32(shard_rows))
        local_row = ids - owner * shard_rows
        return round_slots(owner, place, local_row, round_index, room, nz)

    def more_rows(state):
        round_index, rows_now = state
        slot_now, asked_now = round_of(round_index)
        wanted = lax.all_to_all(asked_now.reshape(nz, room), "zero", 0, 0, tiled=True)
        got = lax.all_to_all(rows_for(wanted).reshape(nz, room, D), "zero", 0, 0, tiled=True)
        return round_index + 1, rows_now + rows_from(slot_now, got)

    def further(step, *value):
        return lax.while_loop(lambda state: state[0] < rounds, step, (jnp.int32(1), *value))[1:]

    (rows,) = further(more_rows, rows)
    rows = rows.reshape(seq_rows, SEQ, D).astype(jnp.float32)

    vec_rows = vec_all.reshape(-1, D)
    edges = [0] + [SEQ + 2 + i * LAYER_ROWS for i in range(LAYERS + 1)]
    vec_parts = [vec_rows[first:last] for first, last in zip(edges, edges[1:])]
    first_part = vec_parts[0]
    embedded, embed_normal, embed_inverse = norm_forward(
        rows + first_part[None, :SEQ], first_part[SEQ], first_part[SEQ + 1]
    )
    hidden = embedded
    mask = key_mask.astype(jnp.float32)[:, None, :]
    saved = []
    pooled = []
    for layer_index in range(LAYERS):
        weights = layer_weights[layer_index]
        hidden, kept = layer_forward(hidden, weights, vec_parts[1 + layer_index], mask)
        saved.append(kept)
        pooled.append(pool_rows(hidden, key_mask, seq_lengths).astype(jnp.bfloat16))

    if by_hand and pair_rows == 4:
        block = jnp.stack(pooled).reshape(2, pair_rows, 2, D).transpose(0, 2, 1, 3)
        loss, pooled_grads = contrastive(block.reshape(2, 2 * pair_rows, D), false_all, pair_all, 2)
        pooled_grads = pooled_grads[:, :, :pair_rows]
    else:
        (pooled_all,) = exchange(
            [jnp.stack(pooled).reshape(-1, 128)], ["all"], ndp, nz, 2, "gather_pooled"
        )
        pooled_all = pooled_all.reshape(n, 2, pair_rows, 2, D).astype(jnp.float32)
        pooled_all = pooled_all.transpose(1, 3, 0, 2, 4).reshape(2, 2, total_pairs, D)

        def whole_loss(pooled_now):
            summed = contrastive_terms(
                pooled_now[0, 0],
                pooled_now[1, 0],
                pooled_now[0, 1],
                pooled_now[1, 1],
                false_all,
                pair_all,
            )
            valid_total = jnp.sum((pair_all >= 0).astype(jnp.float32))
            return summed / jnp.maximum(valid_total, 1.0)

        loss, pooled_grads = jax.value_and_grad(whole_loss)(pooled_all)
        pooled_grads = lax.dynamic_slice_in_dim(pooled_grads, me * pair_rows, pair_rows, 2)
    pooled_grads = pooled_grads.transpose(0, 2, 1, 3).reshape(2, seq_rows, D)
    shallow_back, deep_back = pooled_grads[0], pooled_grads[1]
    share = key_mask.astype(jnp.float32) / seq_lengths.astype(jnp.float32)[:, None]
    grad_hidden = jnp.zeros_like(embedded)
    weight_parts, layer_pairs = [], []
    vec_grads = [None] * LAYERS
    for layer_index in range(LAYERS - 1, -1, -1):
        if layer_index == LAYERS - 1:
            grad_hidden = grad_hidden + deep_back[:, None, :] * share[:, :, None]
        if layer_index == 0:
            grad_hidden = grad_hidden + shallow_back[:, None, :] * share[:, :, None]
        by_scatter = []

        def scatter(pairs, after):
            both = jnp.concatenate([weight_gradient(*pair) for pair in pairs], axis=1)
            both, after = lax.optimization_barrier((both, after))
            by_scatter.append(lax.psum_scatter(both, "zero", scatter_dimension=0, tiled=True))
            return after

        early = by_hand and layer_index == LAYERS - 1
        grad_hidden, pairs, vec_grads[layer_index] = layer_backward(
            saved[layer_index],
            layer_weights[layer_index],
            vec_parts[1 + layer_index],
            mask,
            grad_hidden,
            scatter if early else lambda pairs, after: after,
        )
        if not by_hand:
            grad_hidden = scatter(pairs, grad_hidden)
        layer_pairs.insert(0, pairs)
        weight_parts = by_scatter + weight_parts
    rows_grad, embed_grads = embed_back(
        grad_hidden, embed_normal, embed_inverse, first_part[SEQ]
    )
    vec_grad = jnp.concatenate([embed_grads] + vec_grads, axis=0)
    down_local = jnp.stack([part[5 + FF // D] for part in vec_grads])

    rows_grad = rows_grad.reshape(tokens, D)

    def slot_sums(slot_now):
        picked = one_hot(slot_now, nz * room)
        return lax.dot_general(
            picked, rows_grad, (((0,), (0,)), ((), ())), preferred_element_type=jnp.float32
        ).astype(jnp.bfloat16)

    def into_rows(wanted, sums):
        return lax.dot_general(
            one_hot(wanted.reshape(-1), shard_rows),
            sums.reshape(-1, D),
            (((0,), (0,)), ((), ())),
            preferred_element_type=jnp.float32,
        )

    down_each = down_local.reshape(LAYERS, nz, -1).transpose(1, 0, 2).reshape(nz, -1)
    down_len = down_each.shape[1]
    vec_blocks = jnp.concatenate([vec_grad.reshape(nz, vec_len), down_each], axis=1)
    lines = -(-vec_blocks.shape[1] // 1024) * 8
    vec_blocks = jnp.pad(vec_blocks, ((0, 0), (0, lines * 128 - vec_blocks.shape[1])))
    sums = slot_sums(slot).reshape(nz, room, D)

    def more_sums(state):
        round_index, grad_now, square_now = state
        slot_now, asked_now = round_of(round_index)
        wanted = lax.all_to_all(asked_now.reshape(nz, room), "zero", 0, 0, tiled=True)
        got = lax.all_to_all(slot_sums(slot_now).reshape(nz, room, D), "zero", 0, 0, tiled=True)
        wanted = lax.all_gather(wanted, "dp", axis=0, tiled=True)
        got = lax.all_gather(got, "dp", axis=0, tiled=True)
        more = into_rows(wanted, got)
        grown = lax.psum(jnp.sum(more * (2.0 * grad_now + more)), "zero")
        return round_index + 1, grad_now + more, square_now + grown

    if by_hand:
        attn_shard, ffn_shard, word_grad, vec_sum, squares = exchange_gradients(
            layer_pairs[0] + layer_pairs[1][:2],
            vec_blocks.reshape(4, 2, 2, lines, 128),
            sums,
            weight_parts[0],
            asked_mine.reshape(ndp, 1, nz * room),
            shard_rows,
            vec_len,
            3,
        )
        vec_sum = vec_sum.reshape(-1)
        square_total = squares[0, 0]
    else:
        sums_all, vec_shares = exchange(
            [sums, vec_blocks.reshape(nz, lines, 128)],
            ["all_p", "all_p"],
            ndp,
            nz,
            3,
            "send_gradients",
        )
        vec_sum = jnp.sum(vec_shares.reshape(n, -1), axis=0)
        (weight_all,) = exchange([jnp.stack(weight_parts)], ["dp"], ndp, nz, 4, "sum_replicas")
        weight_sum = jnp.sum(weight_all.astype(jnp.float32), axis=0)
        attn_shard = weight_sum[:, :, : 4 * D]
        ffn_shard = weight_sum[:, :, 4 * D :]
        word_grad = into_rows(asked_mine, sums_all)
    vec_shard = vec_sum[:vec_len]
    down_shard = vec_sum[vec_len : vec_len + down_len].reshape(LAYERS, -1)

    if not by_hand:
        square_local = jnp.sum(word_grad * word_grad) + jnp.sum(vec_shard * vec_shard)
        square_local = square_local + jnp.sum(attn_shard * attn_shard)
        square_local = square_local + jnp.sum(ffn_shard * ffn_shard)
        (squares,) = exchange(
            [jnp.broadcast_to(square_local, (8, 128))], ["zero"], ndp, nz, 5, "gather_squares"
        )
        square_total = jnp.sum(squares[:, 0, 0])
    word_grad, square_total = further(more_sums, word_grad, square_total)
    grad_norm = jnp.sqrt(square_total)
    factor = jnp.minimum(1.0, CLIP_NORM / (grad_norm + 1e-06))
    word_new, word_first_new, word_second_new = adam_update(
        word_table, word_grad * factor, word_first, word_second, LEARN_RATE
    )
    vector_new, vector_first_new, vector_second_new = adam_update(
        vectors, vec_shard * factor, vector_first, vector_second, VECTOR_RATE
    )
    attn_new, attn_first_new, attn_second_new = adam_update(
        attn_w, attn_shard * factor, attn_first, attn_second, LEARN_RATE
    )
    ffn_new, ffn_first_new, ffn_second_new = adam_update(
        ffn_w, ffn_shard * factor, ffn_first, ffn_second, LEARN_RATE
    )
    return (
        loss,
        grad_norm,
        word_new,
        vector_new,
        attn_new,
        ffn_new,
        word_new.astype(jnp.bfloat16),
        vector_new.astype(jnp.bfloat16),
        attn_new.astype(jnp.bfloat16),
        ffn_new.astype(jnp.bfloat16),
        word_first_new,
        vector_first_new,
        attn_first_new,
        ffn_first_new,
        word_second_new,
        vector_second_new,
        attn_second_new,
        ffn_second_new,
        down_shard * factor,
    )


def solution(mesh):
    placed = (
        P(("dp", "zero"), None, None),
        P(("dp", "zero"), None),
        P(("dp", "zero"), None),
        P(("dp", "zero")),
        P("zero", None),
        P("zero"),
        P(None, "zero", None),
        P(None, "zero", None),
        P("zero", None),
        P("zero"),
        P(None, "zero", None),
        P(None, "zero", None),
        P("zero", None),
        P("zero"),
        P(None, "zero", None),
        P(None, "zero", None),
    )
    return jax.shard_map(
        body,
        mesh=mesh,
        in_specs=placed,
        out_specs=(
            P(),
            P(),
            P("zero", None),
            P("zero"),
            P(None, "zero", None),
            P(None, "zero", None),
            P("zero", None),
            P("zero"),
            P(None, "zero", None),
            P(None, "zero", None),
            P("zero", None),
            P("zero"),
            P(None, "zero", None),
            P(None, "zero", None),
            P("zero", None),
            P("zero"),
            P(None, "zero", None),
            P(None, "zero", None),
            P(None, "zero"),
        ),
        check_vma=False,
    )
```

```python
import functools

import jax
import jax.numpy as jnp
from jax import lax
from jax.experimental import pallas as pl
from jax.experimental.pallas import tpu as pltpu
from jax.sharding import PartitionSpec as P

D = 512
HEADS = 8
HD = 64
FF = 2048
SEQ = 128
LAYERS = 2
ADAM_STEP = 5


SOFTMAX_TEMP = 0.05
CLIP_NORM = 1.0
LEARN_RATE = 0.02
VECTOR_RATE = 0.15
BETA_ONE = 0.5
BETA_TWO = 0.5
WEIGHT_DECAY = 0.01
ADAM_EPS = 1e-08
NORM_EPS = 1e-06
MASKED = -1000000000.0

MESH = pl.DeviceIdType.MESH


def build_low():

    def rounder(value):
        return lax.optimization_barrier(value.astype(jnp.bfloat16)).astype(jnp.float32)

    def keep_fwd(value):
        return (rounder(value), None)

    def pass_bwd(kept, grad):
        return (grad,)

    wrapped = jax.custom_vjp(rounder)
    wrapped.defvjp(keep_fwd, pass_bwd)
    return wrapped


def build_low_back():

    def identity_fn(value):
        return value

    def keep_fwd(value):
        return (value, None)

    def round_bwd(kept, grad):
        return (low(grad),)

    wrapped = jax.custom_vjp(identity_fn)
    wrapped.defvjp(keep_fwd, round_bwd)
    return wrapped


def low(value):
    return build_low()(value)


def low_back(value):
    return build_low_back()(value)


def rounded(value):
    return low(low_back(value))


def matmul(left, right):
    return jnp.dot(left, right, preferred_element_type=jnp.float32)


def einsum_plain(form, left, right):
    return jnp.einsum(form, left, right, preferred_element_type=jnp.float32)


def exchange_kernel(modes, ndp, nz, *refs):
    count = len(modes)
    ins = refs[:count]
    outs = refs[count : 2 * count]
    sems = refs[2 * count :]
    d = lax.axis_index("dp")
    z = lax.axis_index("zero")
    me = d * nz + z
    n = ndp * nz

    def peer_of(group, k):
        if group == "dp":
            pd = lax.rem(d + k, ndp)
            return pd, z, pd
        if group == "zero":
            pz = lax.rem(z + k, nz)
            return d, pz, pz
        p = lax.rem(me + k, n)
        return p // nz, lax.rem(p, nz), p

    groups = {m.split("_")[0] for m in modes}
    sizes = {"all": n, "zero": nz, "dp": ndp}
    mine = {"all": me, "zero": z, "dp": d}
    barrier = pltpu.get_barrier_semaphore()
    meet = ["all"] if "all" in groups else sorted(groups)
    total = 0
    for group in meet:
        total += sizes[group] - 1

        def greet(k, carry, group=group):
            pd, pz, _ = peer_of(group, k)
            pl.semaphore_signal(barrier, inc=1, device_id=(pd, pz), device_id_type=MESH)
            return carry

        lax.fori_loop(1, sizes[group], greet, 0)
    pl.semaphore_wait(barrier, total)

    def make(a, k):
        mode = modes[a]
        group = mode.split("_")[0]
        pd, pz, _ = peer_of(group, k)
        src = ins[a].at[pz] if mode.endswith("_p") else ins[a]
        return pltpu.make_async_remote_copy(
            src_ref=src,
            dst_ref=outs[a].at[mine[group]],
            send_sem=sems[2 * a].at[k],
            recv_sem=sems[2 * a + 1].at[k],
            device_id=(pd, pz),
            device_id_type=MESH,
        )

    for a, mode in enumerate(modes):
        group = mode.split("_")[0]

        def begin(k, carry, a=a):
            make(a, k).start()
            return carry

        lax.fori_loop(1, sizes[group], begin, 0)
    for a, mode in enumerate(modes):
        group = mode.split("_")[0]
        if mode.endswith("_p"):
            outs[a][mine[group]] = ins[a][z]
        else:
            outs[a][mine[group]] = ins[a][...]
    for a, mode in enumerate(modes):
        group = mode.split("_")[0]

        def finish(k, carry, a=a):
            make(a, k).wait()
            return carry

        lax.fori_loop(1, sizes[group], finish, 0)


def exchange(arrays, modes, ndp, nz, collective_id, name):
    sizes = {"all": ndp * nz, "zero": nz, "dp": ndp}
    outs = []
    scratch = []
    moved = 0
    for array, mode in zip(arrays, modes):
        size = sizes[mode.split("_")[0]]
        block = array.shape[1:] if mode.endswith("_p") else array.shape
        outs.append(jax.ShapeDtypeStruct((size,) + block, array.dtype))
        scratch += [pltpu.SemaphoreType.DMA((size,)), pltpu.SemaphoreType.DMA((size,))]
        one = array.dtype.itemsize
        for s in block:
            one *= s
        moved += one * size
    vmem = pl.BlockSpec(memory_space=pltpu.VMEM)
    return pl.pallas_call(
        functools.partial(exchange_kernel, tuple(modes), ndp, nz),
        out_shape=tuple(outs),
        in_specs=[vmem] * len(arrays),
        out_specs=tuple([vmem] * len(arrays)),
        scratch_shapes=scratch,
        compiler_params=pltpu.CompilerParams(
            collective_id=collective_id, has_side_effects=True, vmem_limit_bytes=48 * 1024 * 1024
        ),
        cost_estimate=pl.CostEstimate(flops=0, bytes_accessed=20 * moved, transcendentals=0),
        name=name,
    )(*arrays)


CHUNK = 1024
LAG_Z = 3
REST_EACH = 4
HALVED = (2,)


def gradient_kernel(chunks, matrices, vec_len, *refs):
    take = iter(refs)
    pairs = [(next(take), next(take)) for _ in range(matrices)]
    vec_ref, sums_ref, near_ref, asked_ref = [next(take) for _ in range(4)]
    attn_out, ffn_out, word_out, vec_out, stats_out = [next(take) for _ in range(5)]
    held = [None if chunk[1] is None else next(take) for chunk in chunks]
    bufs = [[next(take) for _ in range(6 if chunk[4] else 5)] for chunk in chunks]
    near_buf, rows_ref, sum_ref, square_ref, squares_ref = [next(take) for _ in range(5)]
    left_buf, right_buf, fetch_sem, near_held, local_sem = [next(take) for _ in range(5)]
    send_a, recv_a, send_y, recv_y, send_z, recv_z, send_x, recv_x = [next(take) for _ in range(8)]
    send_h, recv_h = next(take), next(take)
    row_send, row_recv, pass_send, pass_recv, near_sem, square_sem = [
        next(take) for _ in range(6)
    ]

    d = lax.axis_index("dp")
    z = lax.axis_index("zero")
    core = lax.rem(z, 2)
    col = lax.rem(z // 2, 2)
    line = z // 4
    sibling = z + 1 - 2 * core
    across = z + 2 - 4 * col
    attn_width = attn_out.shape[2]

    def along(k):
        return lax.rem(line + k, 4) * 4 + lax.rem(z, 4)

    barrier = pltpu.get_barrier_semaphore()

    def greet(k, carry):
        pl.semaphore_signal(
            barrier, inc=1, device_id=(d, lax.rem(z + k, 16)), device_id_type=MESH
        )
        return carry

    lax.fori_loop(1, 16, greet, 0)
    pl.semaphore_signal(barrier, inc=1, device_id=(1 - d, z), device_id_type=MESH)
    pl.semaphore_wait(barrier, 16)

    def remote(src, dst, send, recv, to):
        return pltpu.make_async_remote_copy(
            src_ref=src,
            dst_ref=dst,
            send_sem=send,
            recv_sem=recv,
            device_id=to,
            device_id_type=MESH,
        )

    def part_of(i):
        return vec_ref if held[i] is None else held[i]

    def halves(i):
        return chunks[i][4]

    def after_y(i):
        return bufs[i][1 + halves(i)]

    def half_rows(i, which):
        rows = bufs[i][0].shape[2] // 2
        return pl.ds(pl.multiple_of(which * rows, 16), rows)

    def copy_a(i):
        src = part_of(i).at[:, :, 1 - core]
        return remote(src, bufs[i][0], send_a.at[i], recv_a.at[i], (d, sibling))

    def copy_h(i):
        src = bufs[i][0].at[:, :, half_rows(i, 1 - d)]
        return remote(src, bufs[i][1], send_h.at[i], recv_h.at[i], (1 - d, z))

    def copy_y(i):
        src = bufs[i][halves(i)].at[:, 1 - col]
        return remote(src, after_y(i), send_y.at[i], recv_y.at[i], (d, across))

    def copy_z(i, k):
        src = after_y(i).at[lax.rem(line + k, 4)]
        into = bufs[i][-3].at[k - 1]
        return remote(src, into, send_z.at[i, k - 1], recv_z.at[i, k - 1], (d, along(k)))

    def copy_x(i):
        return remote(bufs[i][-2], bufs[i][-1], send_x.at[i], recv_x.at[i], (1 - d, z))

    def row_push(k):
        to = lax.rem(z + k, 16)
        return remote(sums_ref.at[to], rows_ref.at[d, z], row_send.at[k], row_recv.at[k], (d, to))

    def row_pass(k):
        at = lax.rem(z + 16 - k, 16)
        return remote(
            rows_ref.at[d, at], rows_ref.at[d, at], pass_send.at[k], pass_recv.at[k], (1 - d, z)
        )

    near = remote(near_ref, near_buf, near_sem.at[0], near_sem.at[1], (1 - d, z))

    total = len(chunks)

    def push(k, carry):
        row_push(k).start()
        return carry

    lax.fori_loop(1, 16, push, 0)
    near.start()
    near_copy = pltpu.make_async_copy(near_ref, near_held, local_sem.at[0])
    near_copy.start()
    own_copy = pltpu.make_async_copy(sums_ref.at[z], rows_ref.at[d, z], local_sem.at[1])
    own_copy.start()

    made = [i for i in range(total) if held[i] is not None]

    def fetches(i):
        _, matrix, start, width, _ = chunks[i]
        slot = made.index(i) % 2
        left, right = pairs[matrix]
        return (
            pltpu.make_async_copy(left, left_buf.at[slot], fetch_sem.at[0, slot]),
            pltpu.make_async_copy(
                right.at[:, pl.ds(start, width)],
                right_buf.at[slot, :, pl.ds(0, width)],
                fetch_sem.at[1, slot],
            ),
        )

    for copy in fetches(made[0]):
        copy.start()

    def compute(i):
        _, matrix, start, width, _ = chunks[i]
        if matrix is not None:
            place = made.index(i)
            slot = place % 2
            if place + 1 < len(made):
                for copy in fetches(made[place + 1]):
                    copy.start()
            for copy in fetches(i):
                copy.wait()

            def rows_of(j, carry):
                at = pl.ds(pl.multiple_of(j * 128, 128), 128)
                found = lax.dot_general(
                    left_buf[slot, :, at],
                    right_buf[slot, :, 0:width],
                    (((0,), (0,)), ((), ())),
                    preferred_element_type=jnp.float32,
                )
                held[i][j] = found.astype(jnp.bfloat16).reshape(2, 2, 32, width)
                return carry

            lax.fori_loop(0, 4, rows_of, 0)
        copy_a(i).start()

    def add_into(buf, count, place, mine):
        def add_block(b, carry):
            at = place(b)
            value = mine(b).astype(jnp.float32) + buf[at].astype(jnp.float32)
            buf[at] = value.astype(buf.dtype)
            return carry

        lax.fori_loop(0, count, add_block, 0)

    def stage_a(i):
        copy_a(i).wait_recv()
        add_into(
            bufs[i][0],
            8,
            lambda b: (b // 2, lax.rem(b, 2)),
            lambda b: part_of(i)[b // 2, lax.rem(b, 2), core],
        )
        (copy_h if halves(i) else copy_y)(i).start()

    def stage_h(i):
        copy_h(i).wait_recv()
        add_into(
            bufs[i][1],
            8,
            lambda b: (b // 2, lax.rem(b, 2)),
            lambda b: bufs[i][0][b // 2, lax.rem(b, 2), half_rows(i, d), :],
        )
        copy_y(i).start()

    def stage_y(i):
        copy_y(i).wait_recv()
        add_into(after_y(i), 4, lambda b: b, lambda b: bufs[i][halves(i)][b, col])
        for k in range(1, 4):
            copy_z(i, k).start()

    def stage_z(i):
        for k in range(1, 4):
            copy_z(i, k).wait_recv()
        value = after_y(i)[line].astype(jnp.float32)
        for k in range(3):
            value = value + bufs[i][-3][k].astype(jnp.float32)
        bufs[i][-2][...] = value.astype(bufs[i][-2].dtype)
        copy_x(i).start()

    def stage_x(i):
        target, _, start, width, _ = chunks[i]
        copy_x(i).wait_recv()
        mine, other = bufs[i][-2][...].astype(jnp.float32), bufs[i][-1][...].astype(jnp.float32)
        if target is None:
            vec_out[...] = mine + other
            return
        layer, first = target[0], target[1] + start
        out, first = (attn_out, first) if first < attn_width else (ffn_out, first - attn_width)
        if halves(i):
            out[layer, half_rows(i, d), first : first + width] = mine
            out[layer, half_rows(i, 1 - d), first : first + width] = other
        else:
            out[layer, :, first : first + width] = mine + other

    def steps_of(i):
        if halves(i):
            order = ((stage_a, 0), (stage_h, 1), (stage_y, 2), (stage_z, 2 + LAG_Z), (stage_x, 3 + LAG_Z))
        else:
            order = ((stage_a, 0), (stage_y, 1), (stage_z, 1 + LAG_Z), (stage_x, 2 + LAG_Z))
        return [(i + later, now) for now, later in order]

    def pass_on(k):
        row_push(k).wait_recv()
        row_pass(k).start()

    shard_rows, features = word_out.shape
    tiles = -(-shard_rows // 128)
    spots = rows_ref.shape[1] * rows_ref.shape[2]
    sum_ref[...] = jnp.zeros_like(sum_ref)

    def into_rows(plane, first, count):
        row = lax.broadcasted_iota(jnp.int32, (128, 1), 0) + first
        picked = (asked_ref[plane] == row).astype(jnp.bfloat16)
        return jnp.dot(
            picked, rows_ref[plane].reshape(spots, features), preferred_element_type=jnp.float32
        )[:count]

    def own_rows(tile):
        first, count = tile * 128, min(128, shard_rows - tile * 128)
        word_out[first : first + count, :] = into_rows(d, first, count)

    def all_arrived():
        def arrived(k, carry):
            ref = rows_ref.at[1 - d, lax.rem(z + 16 - k, 16)]
            remote(ref, ref, pass_send.at[k], pass_recv.at[k], (1 - d, z)).wait_recv()
            return carry

        lax.fori_loop(0, 16, arrived, 0)

    def other_rows(tile):
        first, count = tile * 128, min(128, shard_rows - tile * 128)
        value = word_out[first : first + count, :] + into_rows(1 - d, first, count)
        word_out[first : first + count, :] = value
        sum_ref[...] = sum_ref[...] + jnp.sum(value * value, axis=0, keepdims=True)

    rest = [functools.partial(own_rows, tile) for tile in range(tiles)]
    rest += [all_arrived] + [functools.partial(other_rows, tile) for tile in range(tiles)]

    compute(0)
    own_copy.wait()
    row_pass(0).start()
    passed = 1
    for t in range(total + LAG_Z + 3):
        if t + 1 < total:
            compute(t + 1)
        for i in range(total - 1, -1, -1):
            for at, now in steps_of(i):
                if at == t:
                    now(i)
        until = min(16, 1 + (t + 1) * 15 // (total - 2))
        for k in range(passed, until):
            pass_on(k)
        passed = until
        if t >= total - 2:
            for _ in range(min(len(rest), REST_EACH)):
                rest.pop(0)()
    while rest:
        rest.pop(0)()

    near.wait()
    near_copy.wait()
    ffn_out[1] = near_held[...].astype(jnp.float32) + near_buf[...].astype(jnp.float32)
    squares = sum_ref[...]
    square = jnp.sum(squares, axis=1, keepdims=True)
    for out in (attn_out, ffn_out):

        def of_rows(r, carry, out=out):
            at = pl.ds(pl.multiple_of(r * 8, 8), 8)
            for layer in range(out.shape[0]):
                value = out[layer, at, :]
                carry = carry + jnp.sum(value * value, axis=0, keepdims=True)
            return carry

        found = lax.fori_loop(
            0, out.shape[1] // 8, of_rows, jnp.zeros((1, out.shape[2]), jnp.float32)
        )
        square = square + jnp.sum(found, axis=1, keepdims=True)
    place = lax.broadcasted_iota(jnp.int32, vec_out.shape, 0) * 128 + lax.broadcasted_iota(
        jnp.int32, vec_out.shape, 1
    )
    value = jnp.where(place < vec_len, vec_out[...], 0.0)
    found = jnp.sum(value * value, axis=0, keepdims=True)
    square = square + jnp.sum(found, axis=1, keepdims=True)
    square_ref[...] = jnp.broadcast_to(square, square_ref.shape)

    def square_copy(k, slot):
        return remote(
            square_ref,
            squares_ref.at[slot],
            square_sem.at[0, k],
            square_sem.at[1, k],
            (d, lax.rem(z + k, 16)),
        )

    def send_square(k, carry):
        square_copy(k, z).start()
        return carry

    lax.fori_loop(1, 16, send_square, 0)
    squares_ref[z] = square_ref[...]

    for i in range(total):
        copy_a(i).wait_send()
        if halves(i):
            copy_h(i).wait_send()
        copy_y(i).wait_send()
        for k in range(1, 4):
            copy_z(i, k).wait_send()
        copy_x(i).wait_send()

    def finish(k, carry):
        row_push(k).wait_send()
        square_copy(k, lax.rem(z + 16 - k, 16)).wait_recv()
        square_copy(k, z).wait_send()
        return carry

    lax.fori_loop(1, 16, finish, 0)

    def finish_pass(k, carry):
        row_pass(k).wait_send()
        return carry

    lax.fori_loop(0, 16, finish_pass, 0)
    norm = squares_ref[0]
    for slot in range(1, 16):
        norm = norm + squares_ref[slot]
    stats_out[...] = jnp.broadcast_to(norm, stats_out.shape)


def exchange_gradients(pairs, vec_parts, sums, near, asked, shard_rows, vec_len, collective_id):
    spans = []
    for index, (_, right) in enumerate(pairs):
        layer, matrix = index // 4, index % 4
        columns = right.shape[1]
        width = columns // -(-columns // CHUNK)
        offset = sum(pairs[m][1].shape[1] for m in range(matrix))
        for start in range(0, columns, width):
            spans.append(((layer, offset), index, start, width, index in HALVED))
    plain = [chunk for chunk in spans if not chunk[4]]
    halved = [chunk for chunk in spans if chunk[4]]
    chunks = [(None, None, 0, 128, False)]
    while plain or halved:
        chunks += halved[:1] + plain[:1]
        halved, plain = halved[1:], plain[1:]
    half = jnp.bfloat16
    held, bufs = [], []
    for _, index, _, width, halves in chunks:
        kind = vec_parts.dtype if index is None else half
        r = vec_parts.shape[3] if index is None else 32
        if index is not None:
            held.append(pltpu.VMEM((4, 2, 2, r, width), kind))
        bufs.append(pltpu.VMEM((4, 2, r, width), kind))
        if halves:
            r = r // 2
            bufs.append(pltpu.VMEM((4, 2, r, width), kind))
        bufs += [
            pltpu.VMEM((4, r, width), kind),
            pltpu.VMEM((3, r, width), kind),
            pltpu.VMEM((r, width), kind),
            pltpu.VMEM((r, width), kind),
        ]
    features = sums.shape[2]
    dma = pltpu.SemaphoreType.DMA
    count = len(chunks)
    scratch = held + bufs
    scratch += [
        pltpu.VMEM(near.shape, half),
        pltpu.VMEM((2,) + sums.shape, half),
        pltpu.VMEM((1, features), jnp.float32),
        pltpu.VMEM((1, 128), jnp.float32),
        pltpu.VMEM((16, 1, 128), jnp.float32),
        pltpu.VMEM((2,) + pairs[0][0].shape, half),
        pltpu.VMEM((2, pairs[0][0].shape[0], max(chunk[3] for chunk in chunks)), half),
        dma((2, 2)),
        pltpu.VMEM(near.shape, half),
        dma((2,)),
    ]
    scratch += [dma((count,)) for _ in range(4)] + [dma((count, 3)) for _ in range(2)]
    scratch += [dma((count,)) for _ in range(4)]
    scratch += [dma((16,)) for _ in range(4)] + [dma((2,)), dma((2, 16))]
    rows = near.shape[0]
    outs = [
        jax.ShapeDtypeStruct((2, rows, 4 * D), jnp.float32),
        jax.ShapeDtypeStruct((2, rows, 2 * FF), jnp.float32),
        jax.ShapeDtypeStruct((shard_rows, features), jnp.float32),
        jax.ShapeDtypeStruct(vec_parts.shape[3:], jnp.float32),
        jax.ShapeDtypeStruct((8, 128), jnp.float32),
    ]
    vmem = pl.BlockSpec(memory_space=pltpu.VMEM)
    hbm = pl.BlockSpec(memory_space=pltpu.HBM)
    return pl.pallas_call(
        functools.partial(gradient_kernel, tuple(chunks), len(pairs), vec_len),
        out_shape=tuple(outs),
        in_specs=[hbm] * (2 * len(pairs)) + [vmem, hbm, hbm, vmem],
        out_specs=tuple([vmem] * len(outs)),
        scratch_shapes=scratch,
        compiler_params=pltpu.CompilerParams(
            collective_id=collective_id, has_side_effects=True, vmem_limit_bytes=58 * 1024 * 1024
        ),
        cost_estimate=pl.CostEstimate(flops=0, bytes_accessed=200_000_000, transcendentals=0),
        name="exchange_gradients",
    )(*[array for pair in pairs for array in pair], vec_parts, sums, near, asked)


SPLITS = 4
WINDOW = 2
LAG = 3


def start_kernel(shard_rows, room, *refs):
    column_ref, row_ref, packet_ref, vec_ref, attn_ref, ffn_ref, word_ref = refs[:7]
    place_out, slot_out, packet_out, asked_out, vec_out, rows_out, *weight_outs = refs[7:15]
    table, rows_held, asked, words, own, attn_held, ffn_held = refs[15:22]
    packet_sem, near_sem, far_sem, vec_sem, row_sem = refs[22:27]
    z_sem, y_sem, x_sem, d_sem, e_sem, own_sem, word_sem, self_sem = refs[27:]

    d = lax.axis_index("dp")
    z = lax.axis_index("zero")
    me = d * 16 + z
    core = lax.rem(z, 2)
    col = lax.rem(z // 2, 2)
    line = z // 4
    sibling = z + 1 - 2 * core
    across = z + 2 - 4 * col
    layers = attn_ref.shape[0]
    width = attn_ref.shape[2]
    whole = 3 * width
    unit = whole // 128 // SPLITS
    hand = unit * 5 // 12
    total = layers * SPLITS

    def everyone(k):
        p = lax.rem(me + k, 32)
        return (p // 16, lax.rem(p, 16))

    held_copies = [
        pltpu.make_async_copy(attn_ref, attn_held, word_sem.at[1]),
        pltpu.make_async_copy(ffn_ref, ffn_held, word_sem.at[2]),
    ]
    for copy in held_copies:
        copy.start()
    word_copy = pltpu.make_async_copy(word_ref, words, word_sem.at[0])
    word_copy.start()
    barrier = pltpu.get_barrier_semaphore()

    def greet(k, carry):
        pl.semaphore_signal(barrier, inc=1, device_id=everyone(k), device_id_type=MESH)
        return carry

    lax.fori_loop(1, 32, greet, 0)
    for copy in held_copies:
        copy.wait()

    def self_copy(layer):
        return pltpu.make_async_copy(own.at[layer], weight_outs[layer].at[z], self_sem.at[layer])

    for layer in range(layers):
        own[layer, :, 0:width] = attn_held[layer].astype(jnp.bfloat16)
        own[layer, :, width:whole] = ffn_held[layer].astype(jnp.bfloat16)
        self_copy(layer).start()
    for layer in range(layers):
        self_copy(layer).wait()
    pl.semaphore_wait(barrier, 31)

    def remote(src, dst, sems, at, to):
        return pltpu.make_async_remote_copy(
            src_ref=src,
            dst_ref=dst,
            send_sem=sems.at[(0,) + at],
            recv_sem=sems.at[(1,) + at],
            device_id=to,
            device_id_type=MESH,
        )

    def packet_copy(k, slot):
        return remote(packet_ref, packet_out.at[slot], packet_sem, (k,), everyone(k))

    def near_copy(k, slot):
        to = lax.rem(z + k, 16)
        return remote(asked.at[to], asked_out.at[slot], near_sem, (k,), (d, to))

    def far_copy(k, slot):
        to = lax.rem(z + k, 16)
        return remote(asked.at[to], asked_out.at[slot], far_sem, (k,), (1 - d, to))

    def vec_copy(k, slot):
        return remote(vec_ref, vec_out.at[slot], vec_sem, (k,), (d, lax.rem(z + k, 16)))

    def row_copy(k, slot):
        to = lax.rem(z + k, 16)
        return remote(rows_held.at[to], rows_out.at[slot], row_sem, (k,), (d, to))

    def shard(i):
        at = lax.rem(line + i % 4, 4) * 4 + lax.rem(z, 4)
        return at if i < 4 else at + 2 - 4 * col

    def piece(s):
        layer, p = s // SPLITS, s % SPLITS
        size = unit if p < SPLITS - 1 else whole // 128 - p * unit
        return layer, p * unit, size

    def columns_of(at, s, first, size):
        layer, base, _ = piece(s)
        return weight_outs[layer].at[
            at, :, pl.ds(pl.multiple_of((base + first) * 128, 128), size * 128)
        ]

    def stretch(at, s, ours):
        size = piece(s)[2]
        return columns_of(at, s, ours * hand, size - hand)

    def handed(at, s, ours):
        size = piece(s)[2]
        return columns_of(at, s, ours * (size - hand), hand)

    def both(ref, sems, at, to):
        return remote(ref, ref, sems, at, to)

    def z_copy(s, k, at):
        to = lax.rem(line + k, 4) * 4 + lax.rem(z, 4)
        return both(stretch(at, s, d), z_sem, (s, k - 1), (d, to))

    def y_copy(s, j, at):
        return both(stretch(at, s, d), y_sem, (s, j), (d, across))

    def x_copy(s, i, at, ours):
        return both(handed(at, s, ours), x_sem, (s, i), (1 - d, z))

    def d_copy(s, i, at):
        return both(stretch(at, s, d), d_sem, (s, i), (d, sibling))

    def e_copy(s, i, at):
        return both(handed(at, s, 1 - d), e_sem, (s, i), (d, sibling))

    def own_copy(layer, at):
        ref = weight_outs[layer].at[at]
        return both(ref, own_sem, (layer,), (d, sibling))

    def spread(s, i):
        at = shard(i)
        if i < 4:
            y_copy(s, i, at).start()
        if i > 0:
            x_copy(s, i, at, d).start()
            d_copy(s, i, at).start()

    def open_piece(s):
        for k in range(1, 4):
            z_copy(s, k, z).start()
        spread(s, 0)

    for s in range(WINDOW):
        open_piece(s)

    tokens = column_ref.shape[0]
    ids_row = row_ref[...]
    lane = lax.broadcasted_iota(jnp.int32, (1, tokens), 1).astype(jnp.float32)
    block = 128

    def lead_of(b, least):
        ids = column_ref[pl.ds(pl.multiple_of(b * block, block), block), :]
        there = lax.broadcasted_iota(jnp.int32, (block, 1), 0) + b * block
        found = jnp.where(ids == ids_row, there.astype(jnp.float32), 1e9)
        return jnp.minimum(least, jnp.min(found, axis=0, keepdims=True))

    least = lax.fori_loop(0, tokens // block, lead_of, jnp.full((1, tokens), 1e9, jnp.float32))
    lead_ids = jnp.where(least == lane, ids_row, -1)

    lane128 = lax.broadcasted_iota(jnp.int32, (1, 128), 1).astype(jnp.float32)

    def place_of(b, carry):
        most, best = carry
        at = pl.ds(pl.multiple_of(b * block, block), block)
        ids = column_ref[at, :]
        owner = jnp.floor((ids.astype(jnp.float32) + 0.5) * (1.0 / shard_rows))
        low_id = owner.astype(jnp.int32) * shard_rows
        ahead = (lead_ids >= low_id) & (lead_ids < ids)
        place = jnp.sum(jnp.where(ahead, 1.0, 0.0), axis=1, keepdims=True)
        place_out[at, :] = place.astype(jnp.int32)
        inside = place < room
        slot_out[at, :] = jnp.where(inside, owner * room + place, -1.0).astype(jnp.int32)
        slot = jnp.broadcast_to(jnp.where(inside, owner * 128.0 + place, -1.0), (block, 128))
        local = jnp.broadcast_to((ids - low_id).astype(jnp.float32), (block, 128))
        grown = []
        for o in range(16):
            found = jnp.where(slot == o * 128.0 + lane128, local, -1.0)
            found = jnp.max(found.reshape(block // 8, 8, 128), axis=0)
            grown.append(jnp.maximum(best[o], found))
        return jnp.maximum(most, jnp.max(place, axis=0, keepdims=True)), tuple(grown)

    most, best = lax.fori_loop(
        0,
        tokens // block,
        place_of,
        (jnp.zeros((1, 1), jnp.float32), (jnp.full((8, 128), -1.0, jnp.float32),) * 16),
    )
    rounds = jnp.ones((1, 1), jnp.float32)
    for r in range(1, -(-tokens // room)):
        rounds = rounds + (most >= r * room).astype(jnp.float32)
    for o in range(16):
        found = jnp.max(best[o], axis=0, keepdims=True)
        asked[o] = jnp.where(lane128 == 127.0, rounds, found).astype(jnp.int32)

    def send_near(k, carry):
        near_copy(k, me).start()
        return carry

    lax.fori_loop(1, 16, send_near, 0)

    def send_far(k, carry):
        far_copy(k, me).start()
        return carry

    lax.fori_loop(0, 16, send_far, 0)

    def send_packets(k, carry):
        packet_copy(k, me).start()
        return carry

    lax.fori_loop(1, 32, send_packets, 0)

    def send_vec(k, carry):
        vec_copy(k, z).start()
        return carry

    lax.fori_loop(1, 16, send_vec, 0)
    for layer in range(layers):
        own_copy(layer, z).start()
    vec_out[z] = vec_ref[...]
    asked_out[me] = asked[z]
    packet_out[me] = packet_ref[...]

    body_rows = shard_rows // 16 * 16
    step = 112 if body_rows % 112 == 0 else 16

    def to_half(i, carry):
        at = pl.multiple_of(i * step, 16)
        table[pl.ds(at, step), :] = words[pl.ds(at, step), :].astype(jnp.bfloat16)
        return carry

    word_copy.wait()
    lax.fori_loop(0, body_rows // step, to_half, 0)
    padded = table.shape[0]
    table[body_rows:padded, :] = jnp.zeros((padded - body_rows, table.shape[1]), jnp.bfloat16)
    if shard_rows > body_rows:
        table[body_rows:shard_rows, :] = words[body_rows:shard_rows, :].astype(jnp.bfloat16)

    def answer_one(k, carry):
        src = lax.rem(z + k, 16)
        rows_at = lax.broadcasted_iota(jnp.int32, (padded, 128), 0)
        picked = (rows_at == asked_out[d * 16 + src]).astype(jnp.bfloat16)
        found = lax.dot_general(
            picked, table[...], (((0,), (0,)), ((), ())), preferred_element_type=jnp.float32
        )
        rows_held[src] = found[:room, :].astype(jnp.bfloat16)
        return carry

    def packet_in(k, carry):
        near_copy(k, d * 16 + lax.rem(z + 16 - k, 16)).wait_recv()
        return carry

    def row_start(k, carry):
        row_copy(k, z).start()
        return carry

    def z_phase(s):
        for k in range(1, 4):
            z_copy(s, k, shard(4 - k)).wait_recv()
            spread(s, 4 - k)
        if s + WINDOW < total:
            open_piece(s + WINDOW)

    def y_phase(s):
        for j in range(4):
            y_copy(s, j, shard(4 + j)).wait_recv()
            spread(s, 4 + j)

    def x_phase(s):
        for i in range(1, 8):
            at = shard(i)
            x_copy(s, i, at, 1 - d).wait_recv()
            e_copy(s, i, at).start()

    done = 0
    for t in range(total + LAG):
        if t < total:
            z_phase(t)
        if t == 1:
            lax.fori_loop(1, 16, packet_in, 0)
        if t >= 1:
            until = min(16, done + 4)
            if until > done:
                lax.fori_loop(done, until, answer_one, 0)
            done = until
        if t == total - 1:
            lax.fori_loop(1, 16, row_start, 0)
            rows_out[z] = rows_held[z]
        if 0 <= t - 1 < total:
            y_phase(t - 1)
        if 0 <= t - LAG < total:
            x_phase(t - LAG)

    turn = 1 - 2 * core
    for layer in range(layers):
        own_copy(layer, z + turn).wait_recv()
        own_copy(layer, z).wait_send()
    for s in range(total):
        for i in range(1, 8):
            at = shard(i)
            d_copy(s, i, at + turn).wait_recv()
            d_copy(s, i, at).wait_send()
            e_copy(s, i, at + turn).wait_recv()
            e_copy(s, i, at).wait_send()
            x_copy(s, i, at, d).wait_send()
        for k in range(1, 4):
            z_copy(s, k, z).wait_send()
        for i in range(4):
            y_copy(s, i, shard(i)).wait_send()

    def finish(k, carry):
        back = lax.rem(z + 16 - k, 16)
        row_copy(k, back).wait_recv()
        row_copy(k, z).wait_send()
        vec_copy(k, back).wait_recv()
        vec_copy(k, z).wait_send()
        near_copy(k, me).wait_send()
        return carry

    lax.fori_loop(1, 16, finish, 0)

    def finish_packets(k, carry):
        packet_copy(k, lax.rem(me + 32 - k, 32)).wait_recv()
        packet_copy(k, me).wait_send()
        return carry

    lax.fori_loop(1, 32, finish_packets, 0)

    def finish_far(k, carry):
        far_copy(k, (1 - d) * 16 + lax.rem(z + 16 - k, 16)).wait_recv()
        far_copy(k, me).wait_send()
        return carry

    lax.fori_loop(0, 16, finish_far, 0)


def exchange_start(ids, packet, vec_rows, attn, ffn, word_table, room, collective_id):
    half = jnp.bfloat16
    shard_rows, features = word_table.shape
    padded = -(-shard_rows // 128) * 128
    layers, rows, width = attn.shape
    tokens = ids.shape[0]
    pieces = layers * SPLITS
    dma = pltpu.SemaphoreType.DMA
    vmem = pl.BlockSpec(memory_space=pltpu.VMEM)
    anywhere = pl.BlockSpec(memory_space=pltpu.HBM)
    return pl.pallas_call(
        functools.partial(start_kernel, shard_rows, room),
        out_shape=(
            jax.ShapeDtypeStruct((tokens, 1), jnp.int32),
            jax.ShapeDtypeStruct((tokens, 1), jnp.int32),
            jax.ShapeDtypeStruct((32,) + packet.shape, packet.dtype),
            jax.ShapeDtypeStruct((32, 1, 128), jnp.int32),
            jax.ShapeDtypeStruct((16,) + vec_rows.shape, vec_rows.dtype),
            jax.ShapeDtypeStruct((16, room, features), half),
        )
        + (jax.ShapeDtypeStruct((16, rows, 3 * width), half),) * layers,
        in_specs=[vmem] * 4 + [anywhere] * 3,
        out_specs=tuple([vmem] * 6 + [anywhere] * layers),
        scratch_shapes=[
            pltpu.VMEM((padded, features), half),
            pltpu.VMEM((16, room, features), half),
            pltpu.VMEM((16, 1, 128), jnp.int32),
            pltpu.VMEM(word_table.shape, word_table.dtype),
            pltpu.VMEM((layers, rows, 3 * width), half),
            pltpu.VMEM(attn.shape, attn.dtype),
            pltpu.VMEM(ffn.shape, ffn.dtype),
            dma((2, 32)),
            dma((2, 16)),
            dma((2, 16)),
            dma((2, 16)),
            dma((2, 16)),
            dma((2, pieces, 3)),
            dma((2, pieces, 4)),
            dma((2, pieces, 8)),
            dma((2, pieces, 8)),
            dma((2, pieces, 8)),
            dma((2, layers)),
            dma((3,)),
            dma((layers,)),
        ],
        compiler_params=pltpu.CompilerParams(
            collective_id=collective_id, has_side_effects=True, vmem_limit_bytes=52 * 1024 * 1024
        ),
        cost_estimate=pl.CostEstimate(flops=0, bytes_accessed=150_000_000, transcendentals=0),
        name="exchange_start",
    )(ids.reshape(-1, 1), ids.reshape(1, -1), packet, vec_rows, attn, ffn, word_table)


WIDTHS = (D, D * 2 // 3, D // 3, D // 6, D // 12)


def gather_rows(block_ref, all_ref, z_sem, near_sem):
    d = lax.axis_index("dp")
    z = lax.axis_index("zero")
    line, spot = z // 4, lax.rem(z, 4)

    def at_line(k):
        return lax.rem(line + k, 4) * 4 + spot

    def near_by(j):
        across = j // 4
        return lax.rem(d + across, 2), line * 4 + lax.rem(spot + j % 4, 4)

    barrier = pltpu.get_barrier_semaphore()
    for k in range(1, 4):
        pl.semaphore_signal(barrier, inc=1, device_id=(d, at_line(k)), device_id_type=MESH)
    for j in range(1, 8):
        pl.semaphore_signal(barrier, inc=1, device_id=near_by(j), device_id_type=MESH)
    pl.semaphore_wait(barrier, 10)

    def z_copy(k):
        return pltpu.make_async_remote_copy(
            src_ref=block_ref,
            dst_ref=all_ref.at[d * 16 + z],
            send_sem=z_sem.at[0, k],
            recv_sem=z_sem.at[1, k],
            device_id=(d, at_line(k)),
            device_id_type=MESH,
        )

    def z_arrival(k):
        ref = all_ref.at[d * 16 + at_line(4 - k)]
        return pltpu.make_async_remote_copy(
            src_ref=ref,
            dst_ref=ref,
            send_sem=z_sem.at[0, k],
            recv_sem=z_sem.at[1, k],
            device_id=(d, at_line(k)),
            device_id_type=MESH,
        )

    def near_copy(i, j, from_d, from_z):
        ref = all_ref.at[from_d * 16 + from_z]
        return pltpu.make_async_remote_copy(
            src_ref=ref,
            dst_ref=ref,
            send_sem=near_sem.at[0, i, j],
            recv_sem=near_sem.at[1, i, j],
            device_id=near_by(j),
            device_id_type=MESH,
        )

    for k in range(1, 4):
        z_copy(k).start()
    all_ref[d * 16 + z] = block_ref[...]
    for j in range(1, 8):
        near_copy(0, j, d, z).start()
    for k in range(1, 4):
        z_arrival(k).wait_recv()
        for j in range(1, 8):
            near_copy(4 - k, j, d, at_line(4 - k)).start()
    for i in range(4):
        for j in range(1, 8):
            back = lax.rem(line + i, 4) * 4 + lax.rem(spot + 4 - j % 4, 4)
            near_copy(i, j, lax.rem(d + j // 4, 2), back).wait_recv()
            near_copy(i, j, d, at_line(i)).wait_send()
    for k in range(1, 4):
        z_copy(k).wait_send()


def contrastive_kernel(
    block_ref, false_ref, pair_ref, loss_ref, own_ref, all_ref, pooled_ref, grad_ref, z_sem, near_sem
):
    me = lax.axis_index("dp") * 16 + lax.axis_index("zero")
    gather_rows(block_ref, all_ref, z_sem, near_sem)
    upper = lax.broadcasted_iota(jnp.int32, (8, 1), 0) < 4
    for kind in range(2):
        for two in range(all_ref.shape[0] // 2):
            even = all_ref[2 * two, kind].astype(jnp.float32)
            odd = all_ref[2 * two + 1, kind].astype(jnp.float32)
            at = slice(8 * two, 8 * two + 8)
            pooled_ref[kind, 0, at, :] = jnp.where(upper, even, pltpu.roll(odd, 4, 0))
            pooled_ref[kind, 1, at, :] = jnp.where(upper, pltpu.roll(even, 4, 0), odd)
    contrastive_math(pooled_ref, false_ref, pair_ref, loss_ref, grad_ref)
    first = pl.multiple_of(me // 2 * 8, 8)
    swap = lax.rem(me, 2) == 1
    for kind in range(2):
        for role in range(2):
            rows = grad_ref[kind, role, pl.ds(first, 8), :]
            own_ref[kind, role] = jnp.where(swap, pltpu.roll(rows, 4, 0), rows)


def contrastive_math(pooled_ref, false_ref, pair_ref, loss_ref, grad_ref):
    pairs = false_ref.shape[0]
    high = lax.Precision.HIGHEST
    columns = lax.broadcasted_iota(jnp.int32, (pairs, pairs), 1)
    hit = columns == pair_ref[...]
    kept = (false_ref[...] == 0) | hit
    hits = hit.astype(jnp.float32)
    valid = (pair_ref[...] >= 0).astype(jnp.float32)
    inverse = 1.0 / jnp.maximum(jnp.sum(valid, axis=0, keepdims=True), 1.0)
    weight = valid * inverse
    named = jnp.sum(hits, axis=1, keepdims=True)
    totals = jnp.zeros((pairs, 1), jnp.float32)
    for first, width in enumerate(WIDTHS):
        span = -(-width // 128) * 128
        inside = lax.broadcasted_iota(jnp.int32, (1, span), 1) < width
        units, scales, logs = [], [], []
        for kind in range(2):
            pair_units, pair_scales = [], []
            for role in range(2):
                rows = jnp.where(inside, pooled_ref[kind, role, :, 0:span], 0.0)
                scale = lax.rsqrt(jnp.sum(rows * rows, axis=1, keepdims=True) + NORM_EPS)
                pair_units.append(rows * scale)
                pair_scales.append(scale)
            sims = lax.dot_general(
                pair_units[0],
                pair_units[1],
                (((1,), (1,)), ((), ())),
                precision=high,
                preferred_element_type=jnp.float32,
            )
            sims = jnp.where(kept, sims / SOFTMAX_TEMP, MASKED)
            shifted = sims - jnp.max(sims, axis=1, keepdims=True)
            logs.append(shifted - jnp.log(jnp.sum(jnp.exp(shifted), axis=1, keepdims=True)))
            units.append(pair_units)
            scales.append(pair_scales)
        shallow, deep = logs
        p_shallow, p_deep = jnp.exp(shallow), jnp.exp(deep)
        gap = p_deep * (deep - shallow)
        spread = jnp.sum(gap, axis=1, keepdims=True)
        totals = totals + spread - jnp.sum(jnp.where(hit, shallow + deep, 0.0), axis=1, keepdims=True)
        d_sims = (
            p_shallow * (named + 1.0) - hits - p_deep,
            gap + p_deep * (named - spread) - hits,
        )
        for kind in range(2):
            d_cos = jnp.where(kept, d_sims[kind] * weight, 0.0) / SOFTMAX_TEMP
            for role in range(2):
                unit = units[kind][role]
                d_unit = lax.dot_general(
                    d_cos,
                    units[kind][1 - role],
                    (((1 - role,), (0,)), ((), ())),
                    precision=high,
                    preferred_element_type=jnp.float32,
                )
                along = jnp.sum(d_unit * unit, axis=1, keepdims=True)
                d_rows = scales[kind][role] * (d_unit - unit * along)
                if first == 0:
                    grad_ref[kind, role] = d_rows
                else:
                    grad_ref[kind, role, :, 0:span] = grad_ref[kind, role, :, 0:span] + d_rows
    loss_ref[...] = jnp.broadcast_to(
        jnp.sum(totals * valid, axis=0, keepdims=True) * inverse, loss_ref.shape
    )


def contrastive(block, false_all, pair_all, collective_id):
    vmem = pl.BlockSpec(memory_space=pltpu.VMEM)
    pairs = false_all.shape[0]
    dma = pltpu.SemaphoreType.DMA
    whole = pltpu.VMEM((2, 2, pairs, D), jnp.float32)
    loss, grads = pl.pallas_call(
        contrastive_kernel,
        out_shape=(
            jax.ShapeDtypeStruct((8, 128), jnp.float32),
            jax.ShapeDtypeStruct((2, 2, 8, D), jnp.float32),
        ),
        in_specs=[vmem] * 3,
        out_specs=(vmem, vmem),
        scratch_shapes=[
            pltpu.VMEM((32,) + block.shape, block.dtype),
            whole,
            whole,
            dma((2, 4)),
            dma((2, 4, 8)),
        ],
        compiler_params=pltpu.CompilerParams(
            collective_id=collective_id, has_side_effects=True, vmem_limit_bytes=20 * 1024 * 1024
        ),
        cost_estimate=pl.CostEstimate(flops=10**9, bytes_accessed=3_000_000, transcendentals=10**6),
        name="contrastive",
    )(block, false_all, pair_all.reshape(-1, 1))
    return loss[0, 0], grads


PAIRS_OF_HEADS = HEADS // 2


def by_side(rows):
    lane = lax.broadcasted_iota(jnp.int32, (1, 2 * HD), 1)
    zero = jnp.zeros_like(rows)
    return jnp.concatenate([jnp.where(lane < HD, rows, zero), jnp.where(lane < HD, zero, rows)])


def join_sides(stacked):
    lane = lax.broadcasted_iota(jnp.int32, (1, 2 * HD), 1)
    return jnp.where(lane < HD, stacked[:SEQ], stacked[SEQ:])


def contract(left, right, left_dim, right_dim):
    return lax.dot_general(
        left, right, (((left_dim,), (right_dim,)), ((), ())), preferred_element_type=jnp.float32
    )


def thirds(packed_ref):
    for pair in range(PAIRS_OF_HEADS):
        at = pair * 2 * HD
        yield [packed_ref[0, :, t * D + at : t * D + at + 2 * HD] for t in range(3)]


def probabilities(scores, valid):
    scores = jnp.where(valid, scores * HD ** (-0.5), MASKED)
    raised = jnp.exp(scores - jnp.max(scores, axis=1, keepdims=True))
    return raised * (1.0 / jnp.sum(raised, axis=1, keepdims=True))


def attention_kernel(mask_ref, packed_ref, context_ref):
    valid = mask_ref[0] > 0.0
    parts = list(thirds(packed_ref))
    scores = [contract(by_side(queries), keys, 1, 1) for queries, keys, _ in parts]
    probs = [probabilities(now, valid).astype(jnp.bfloat16) for now in scores]
    for pair in range(PAIRS_OF_HEADS):
        mixed = contract(probs[pair], parts[pair][2], 1, 0)
        at = pair * 2 * HD
        context_ref[0, :, at : at + 2 * HD] = join_sides(mixed).astype(jnp.bfloat16)


def attention_back_kernel(mask_ref, packed_ref, grad_ref, out_ref):
    valid = mask_ref[0] > 0.0
    parts = list(thirds(packed_ref))
    queries = [by_side(part[0]) for part in parts]
    grads = [
        by_side(grad_ref[0, :, pair * 2 * HD : (pair + 1) * 2 * HD])
        for pair in range(PAIRS_OF_HEADS)
    ]
    scores = [contract(now, part[1], 1, 1) for now, part in zip(queries, parts)]
    d_probs = [contract(now, part[2], 1, 1) for now, part in zip(grads, parts)]
    probs = [probabilities(now, valid) for now in scores]
    d_scores = []
    for now, d_now in zip(probs, d_probs):
        shared = jnp.sum(d_now * now, axis=1, keepdims=True)
        d_scores.append(jnp.where(valid, now * (d_now - shared), 0.0).astype(jnp.bfloat16))
    for pair in range(PAIRS_OF_HEADS):
        d_queries = join_sides(contract(d_scores[pair], parts[pair][1], 1, 0)) * HD ** (-0.5)
        d_keys = contract(d_scores[pair], queries[pair], 0, 0) * HD ** (-0.5)
        d_values = contract(probs[pair].astype(jnp.bfloat16), grads[pair], 0, 0)
        for third, now in enumerate((d_queries, d_keys, d_values)):
            at = third * D + pair * 2 * HD
            out_ref[0, :, at : at + 2 * HD] = now.astype(jnp.bfloat16)


def attention_call(kernel, mask, operands, features, name):
    count = operands[0].shape[0]

    def spec(last):
        return pl.BlockSpec((1, SEQ, last), lambda i: (i, 0, 0))

    return pl.pallas_call(
        kernel,
        grid=(count,),
        out_shape=jax.ShapeDtypeStruct((count, SEQ, features), jnp.bfloat16),
        in_specs=[pl.BlockSpec((1, 1, SEQ), lambda i: (i, 0, 0))]
        + [spec(operand.shape[2]) for operand in operands],
        out_specs=spec(features),
        compiler_params=pltpu.CompilerParams(vmem_limit_bytes=14 * 1024 * 1024),
        cost_estimate=pl.CostEstimate(
            flops=10**9, bytes_accessed=count * SEQ * D * 10, transcendentals=10**6
        ),
        name=name,
    )(mask, *operands)


GELU_SCALE = 0.7978845608028654


def feed_back_kernel(middle_ref, down_ref, up_weights, down_weights, bias_ref, *outs):
    active_ref, d_up_ref, d_first_ref, total_ref = outs
    middle, d_down = middle_ref[...], down_ref[...]
    tile = FF // 4
    d_first = jnp.zeros(d_first_ref.shape, jnp.float32)
    for start in range(0, FF, tile):
        at = slice(start, start + tile)
        upward = contract(middle, up_weights[:, at], 1, 0) + bias_ref[:, at]
        d_active = contract(d_down, down_weights[:, at], 1, 0).astype(jnp.bfloat16)
        square = upward * upward
        bent = jnp.tanh(GELU_SCALE * (upward + 0.044715 * (square * upward)))
        share = 0.5 * (1.0 + bent)
        inner = GELU_SCALE * (1.0 + 3.0 * 0.044715 * square)
        slope = share + 0.5 * upward * (1.0 - bent * bent) * inner
        active_ref[:, at] = (upward * share).astype(jnp.bfloat16)
        d_up = (d_active.astype(jnp.float32) * slope).astype(jnp.bfloat16)
        d_up_ref[:, at] = d_up
        d_first = d_first + contract(d_up, up_weights[:, at], 1, 1)
        found = jnp.sum(d_up.astype(jnp.float32), axis=0, keepdims=True)
        before = jnp.where(pl.program_id(0) == 0, 0.0, total_ref[:, at])
        total_ref[:, at] = before + found
    d_first_ref[...] = d_first


def feed_back(middle, d_down, weights, up_bias):
    tokens = middle.shape[0]
    rows = 256
    half = jnp.bfloat16

    def by_rows(columns):
        return pl.BlockSpec((rows, columns), lambda i: (i, 0))

    def matrix(which):
        return pl.BlockSpec((D, FF), lambda i: (0, which))

    whole = pl.BlockSpec((1, FF), lambda i: (0, 0))
    return pl.pallas_call(
        feed_back_kernel,
        grid=(tokens // rows,),
        out_shape=(
            jax.ShapeDtypeStruct((tokens, FF), half),
            jax.ShapeDtypeStruct((tokens, FF), half),
            jax.ShapeDtypeStruct((tokens, D), jnp.float32),
            jax.ShapeDtypeStruct((1, FF), jnp.float32),
        ),
        in_specs=[by_rows(D), by_rows(D), matrix(1), matrix(2), whole],
        out_specs=(by_rows(FF), by_rows(FF), by_rows(D), whole),
        compiler_params=pltpu.CompilerParams(vmem_limit_bytes=26 * 1024 * 1024),
        cost_estimate=pl.CostEstimate(
            flops=6 * tokens * D * FF, bytes_accessed=24 * tokens * D, transcendentals=tokens * FF
        ),
        name="feed_back",
    )(middle, d_down, weights, weights, up_bias.reshape(1, FF))


def products_kernel(left_one, right_one, left_two, right_two, out_ref):
    step = pl.program_id(0)
    half_way = pl.num_programs(0) // 2

    def fill(left, right):
        def rows_of(j, carry):
            at = pl.ds(pl.multiple_of(j * 128, 128), 128)
            out_ref[at, :] = contract(left[:, at], right[...], 0, 0).astype(jnp.bfloat16)
            return carry

        lax.fori_loop(0, D // 128, rows_of, 0)

    @pl.when(step < half_way)
    def _():
        fill(left_one, right_one)

    @pl.when(step >= half_way)
    def _():
        fill(left_two, right_two)


def products(pairs):
    (left_one, right_one), (left_two, right_two) = pairs
    tokens = left_one.shape[0]
    columns = FF // 2
    left = pl.BlockSpec((tokens, D), lambda i: (0, 0))
    return pl.pallas_call(
        products_kernel,
        grid=(4,),
        out_shape=jax.ShapeDtypeStruct((D, 2 * FF), jnp.bfloat16),
        in_specs=[
            left,
            pl.BlockSpec((tokens, columns), lambda i: (0, jnp.minimum(i, 1))),
            left,
            pl.BlockSpec((tokens, columns), lambda i: (0, jnp.maximum(i - 2, 0))),
        ],
        out_specs=pl.BlockSpec((D, columns), lambda i: (0, i)),
        compiler_params=pltpu.CompilerParams(vmem_limit_bytes=24 * 1024 * 1024),
        cost_estimate=pl.CostEstimate(
            flops=4 * tokens * D * FF, bytes_accessed=4 * D * FF + 8 * tokens * FF, transcendentals=0
        ),
        name="products",
    )(left_one, right_one, left_two, right_two)


def embed_back_kernel(grad_ref, normal_ref, inverse_ref, gain_ref, rows_ref, vec_ref):
    grad, normal = grad_ref[0], normal_ref[0]
    scaled = grad * gain_ref[...]
    mean = jnp.mean(scaled, axis=1, keepdims=True)
    along = jnp.mean(scaled * normal, axis=1, keepdims=True)
    values = (scaled - mean - normal * along) * inverse_ref[0]
    rows_ref[0] = values.astype(jnp.bfloat16)
    first = pl.program_id(0) == 0
    for start, stop, found in (
        (0, SEQ, values),
        (SEQ, SEQ + 1, jnp.sum(grad * normal, axis=0, keepdims=True)),
        (SEQ + 1, SEQ + 2, jnp.sum(grad, axis=0, keepdims=True)),
    ):
        before = jnp.where(first, 0.0, vec_ref[start:stop, :])
        vec_ref[start:stop, :] = before + found


def embed_back(grad, normal, inverse, gain):
    count = grad.shape[0]

    def by_sequence(last):
        return pl.BlockSpec((1, SEQ, last), lambda i: (i, 0, 0))

    def whole(rows):
        return pl.BlockSpec((rows, D), lambda i: (0, 0))

    return pl.pallas_call(
        embed_back_kernel,
        grid=(count,),
        out_shape=(
            jax.ShapeDtypeStruct((count, SEQ, D), jnp.bfloat16),
            jax.ShapeDtypeStruct((SEQ + 2, D), jnp.float32),
        ),
        in_specs=[by_sequence(D), by_sequence(D), by_sequence(1), whole(1)],
        out_specs=(by_sequence(D), whole(SEQ + 2)),
        compiler_params=pltpu.CompilerParams(vmem_limit_bytes=14 * 1024 * 1024),
        cost_estimate=pl.CostEstimate(
            flops=10 * count * SEQ * D, bytes_accessed=10 * count * SEQ * D, transcendentals=0
        ),
        name="embed_back",
    )(grad, normal, inverse, gain.reshape(1, D))


LAYER_ROWS = 8 + FF // D


def layer_vectors(rows):
    up = 5 + FF // D
    return [rows[i] for i in range(5)] + [rows[5:up].reshape(FF)] + [rows[up + i] for i in range(3)]


def layer_norm(values, gain, shift):
    center = values - jnp.mean(values, axis=-1, keepdims=True)
    spread = jnp.mean(center * center, axis=-1, keepdims=True)
    return center * lax.rsqrt(spread + NORM_EPS) * gain + shift


def norm_forward(values, gain, shift):
    center = values - jnp.mean(values, axis=-1, keepdims=True)
    inverse = lax.rsqrt(jnp.mean(center * center, axis=-1, keepdims=True) + NORM_EPS)
    normal = center * inverse
    return normal * gain + shift, normal, inverse


def norm_back(grad, normal, inverse, gain):
    scaled = grad * gain
    mean = jnp.mean(scaled, axis=-1, keepdims=True)
    along = jnp.mean(scaled * normal, axis=-1, keepdims=True)
    return (
        (scaled - mean - normal * along) * inverse,
        jnp.sum(grad * normal, axis=(0, 1)),
        jnp.sum(grad, axis=(0, 1)),
    )


def gelu(value):
    bent = jnp.tanh(GELU_SCALE * (value + 0.044715 * value * value * value))
    return 0.5 * value * (1.0 + bent)


EDGES = (0, 3 * D, 4 * D, 4 * D + FF, 4 * D + 2 * FF)


def four_matrices(weights):
    return [weights[:, first:last] for first, last in zip(EDGES, EDGES[1:])]


def layer_forward(hidden, weights, vectors, mask):
    in_weights, out_weights, up_weights, down_weights = four_matrices(weights)
    q_bias, v_bias, o_bias, gain_one, shift_one, up_bias, down_bias, gain_two, second_shift = (
        layer_vectors(vectors)
    )
    half = jnp.bfloat16
    entry = lax.optimization_barrier(hidden.astype(half))
    bias = jnp.concatenate([q_bias, jnp.zeros_like(q_bias), v_bias])
    packed = (matmul(entry, in_weights) + bias).astype(half)
    context = attention_call(attention_kernel, mask, [packed], D, "attention")
    attended = matmul(context, out_weights) + o_bias
    first, normal_one, inverse_one = norm_forward(hidden + attended, gain_one, shift_one)
    middle = lax.optimization_barrier(first.astype(half))
    upward = matmul(middle, up_weights) + up_bias
    active = lax.optimization_barrier(gelu(upward).astype(half))
    downward = einsum_plain("nsf,df->nsd", active, down_weights) + down_bias
    output, normal_two, inverse_two = norm_forward(first + downward, gain_two, second_shift)
    kept = (
        entry, packed, context, middle,
        normal_one, inverse_one, normal_two, inverse_two,
    )
    return output, kept


def layer_backward(kept, weights, vectors, mask, grad, midway):
    in_weights, out_weights, _, _ = four_matrices(weights)
    entry, packed, context, middle = kept[:4]
    normal_one, inverse_one, normal_two, inverse_two = kept[4:]
    gain_one, gain_two = layer_vectors(vectors)[3], layer_vectors(vectors)[7]
    half = jnp.bfloat16

    def total(value):
        return jnp.sum(value.astype(jnp.float32), axis=(0, 1))

    d_second, d_gain_two, d_shift_two = norm_back(grad, normal_two, inverse_two, gain_two)
    d_down = lax.optimization_barrier(d_second.astype(half))
    flat_middle, flat_down = middle.reshape(-1, D), d_down.reshape(-1, D)
    active, d_up, d_first, d_up_bias = feed_back(
        flat_middle, flat_down, weights, layer_vectors(vectors)[5]
    )
    feed_pairs = [(flat_middle, d_up), (flat_down, active)]
    d_first = midway(feed_pairs, d_second + d_first.reshape(d_second.shape))
    d_middle, d_gain_one, d_shift_one = norm_back(d_first, normal_one, inverse_one, gain_one)
    d_attended = lax.optimization_barrier(d_middle.astype(half))
    d_context = jnp.einsum(
        "nsd,ed->nse", d_attended, out_weights, preferred_element_type=jnp.float32
    ).astype(half)
    d_packed = attention_call(
        attention_back_kernel, mask, [packed, d_context], 3 * D, "attention_back"
    )
    d_hidden = d_middle + jnp.einsum(
        "nsp,dp->nsd", d_packed, in_weights, preferred_element_type=jnp.float32
    )
    packed_total = total(d_packed)
    pieces = [
        packed_total[:D], packed_total[2 * D :], total(d_attended), d_gain_one, d_shift_one,
        d_up_bias, total(d_down), d_gain_two, d_shift_two,
    ]
    d_vectors, at = jnp.zeros((LAYER_ROWS, D), jnp.float32), 0
    for piece in pieces:
        rows = piece.reshape(-1, D)
        d_vectors = d_vectors + jnp.pad(rows, ((at, LAYER_ROWS - at - rows.shape[0]), (0, 0)))
        at = at + rows.shape[0]
    flat = [
        (left.reshape(-1, left.shape[2]), right.reshape(-1, right.shape[2]))
        for left, right in ((entry, d_packed), (context, d_attended))
    ]
    return d_hidden, flat + feed_pairs, d_vectors


def weight_gradient(left, right):
    return lax.dot_general(
        left, right, (((0,), (0,)), ((), ())), preferred_element_type=jnp.float32
    ).astype(jnp.bfloat16)


def pool_rows(hidden, key_mask, seq_lengths):
    share = key_mask.astype(jnp.float32) / seq_lengths.astype(jnp.float32)[:, None]
    return jnp.sum(hidden * share[:, :, None], axis=1)


def normalized_rows(rows):
    return rows * lax.rsqrt(jnp.sum(rows * rows, axis=-1, keepdims=True) + NORM_EPS)


def contrastive_terms(shallow_anchor, deep_anchor, shallow_pos, deep_pos, false_neg, pair_index):
    columns = lax.broadcasted_iota(jnp.int32, false_neg.shape, 1)
    hit = columns == pair_index[:, None]
    kept_cols = (false_neg == 0) | hit
    valid_rows = (pair_index >= 0).astype(jnp.float32)
    totals = jnp.zeros(pair_index.shape, jnp.float32)
    for current_width in (D, D * 2 // 3, D // 3, D // 6, D // 12):
        log_probs = []
        for anchor_vectors, positive_rows in (
            (shallow_anchor, shallow_pos),
            (deep_anchor, deep_pos),
        ):
            similarity_scores = (
                jnp.dot(
                    normalized_rows(anchor_vectors[:, :current_width]),
                    normalized_rows(positive_rows[:, :current_width]).T,
                    precision=lax.Precision.HIGHEST,
                )
                / SOFTMAX_TEMP
            )
            similarity_scores = jnp.where(kept_cols, similarity_scores, MASKED)
            log_probs.append(jax.nn.log_softmax(similarity_scores, axis=-1))
        for log_now in log_probs:
            totals = totals - jnp.sum(jnp.where(hit, log_now, 0.0), axis=-1)
        totals = totals + jnp.sum(jnp.exp(log_probs[1]) * (log_probs[1] - log_probs[0]), axis=-1)
    return jnp.sum(totals * valid_rows)


def adam_update(master, gradient, first, second, step_rate):
    first_new = BETA_ONE * first + (1.0 - BETA_ONE) * gradient
    second_new = BETA_TWO * second + (1.0 - BETA_TWO) * gradient * gradient
    first_hat = first_new / (1.0 - BETA_ONE**ADAM_STEP)
    second_hat = second_new / (1.0 - BETA_TWO**ADAM_STEP)
    master_new = master - step_rate * (
        first_hat / (jnp.sqrt(second_hat) + ADAM_EPS) + WEIGHT_DECAY * master
    )
    return (master_new, first_new, second_new)


def pad_rows(flat, multiple):
    rows = -(-flat.shape[0] // (128 * multiple)) * multiple
    return jnp.pad(flat, (0, rows * 128 - flat.shape[0])).reshape(rows, 128)


def one_hot(index, size, dtype=jnp.bfloat16):
    return (index[:, None] == lax.broadcasted_iota(jnp.int32, (1, size), 1)).astype(dtype)


def token_plan(ids, shard_rows):
    places = lax.broadcasted_iota(jnp.int32, ids.shape, 0)
    same = ids[:, None] == ids[None, :]
    leader = jnp.min(jnp.where(same, places[None, :], ids.shape[0]), axis=1)
    leads = leader == places
    owner = ids // shard_rows
    low_id = owner * shard_rows
    ahead = leads[None, :] & (ids[None, :] >= low_id[:, None]) & (ids[None, :] < ids[:, None])
    place = jnp.sum(ahead.astype(jnp.int32), axis=1)
    return owner, place, ids - low_id


def round_slots(owner, place, local_row, round_index, room, nz):
    inside = (place >= round_index * room) & (place < (round_index + 1) * room)
    slot = jnp.where(inside, owner * room + place - round_index * room, -1)
    slots = lax.broadcasted_iota(jnp.int32, (1, nz * room), 1)
    asked = jnp.max(jnp.where(slot[:, None] == slots, local_row[:, None], -1), axis=0)
    return slot, asked


def body(
    token_ids,
    lengths,
    false_neg,
    pair_index,
    word_table,
    vectors,
    attn_w,
    ffn_w,
    word_first,
    vector_first,
    attn_first,
    ffn_first,
    word_second,
    vector_second,
    attn_second,
    ffn_second,
):
    ndp = lax.axis_size("dp")
    nz = lax.axis_size("zero")
    n = ndp * nz
    by_hand = (ndp, nz) == (2, 16) and token_ids.shape[0] * ndp * nz <= 256
    my_dp = lax.axis_index("dp")
    my_zero = lax.axis_index("zero")
    me = my_dp * nz + my_zero
    pair_rows = token_ids.shape[0]
    total_pairs = pair_rows * n
    flat_ids = token_ids.reshape(-1, SEQ)
    seq_rows = flat_ids.shape[0]
    tokens = seq_rows * SEQ
    seq_lengths = lengths.reshape(-1)
    key_mask = lax.broadcasted_iota(jnp.int32, flat_ids.shape, 1) < seq_lengths[:, None]
    shard_rows = word_table.shape[0]
    vec_len = vectors.shape[0]

    room = -(-(tokens * 9 // 8) // (nz * 8)) * 8
    ids = flat_ids.reshape(-1)

    def packet_of(asked, rounds_here):
        last = jnp.concatenate([pair_index, rounds_here[None].astype(jnp.int32)])
        lines = nz + false_neg.size // 128
        return jnp.concatenate(
            [
                jnp.pad(asked.reshape(nz, room), ((0, 0), (0, 128 - room)), constant_values=-1),
                false_neg.reshape(-1, 128),
                jnp.zeros((7 - lines % 8, 128), jnp.int32),
                jnp.pad(last, (0, 128 - last.shape[0]))[None],
            ]
        )

    def gather_layer(layer_index):
        both = jnp.concatenate(
            [attn_w[layer_index].astype(jnp.bfloat16), ffn_w[layer_index].astype(jnp.bfloat16)],
            axis=1,
        )
        return lax.all_gather(both, "zero", axis=0, tiled=True)

    if by_hand:
        packet = pad_rows(jnp.concatenate([false_neg.reshape(-1), pair_index]), 8)
        place, slot, packets, asked_mine, vec_parts, received, *gathered = exchange_start(
            ids,
            packet.astype(jnp.bfloat16),
            pad_rows(vectors.astype(jnp.bfloat16), 16),
            attn_w,
            ffn_w,
            word_table,
            room,
            0,
        )
        layer_weights = [part.reshape(D, -1) for part in gathered]
        rounds = jnp.max(asked_mine[:, 0, 127])
        asked_mine = asked_mine[:, 0, :room]
        packets = packets.reshape(n, -1).astype(jnp.int32)
        false_all = packets[:, : false_neg.size].reshape(total_pairs, total_pairs)
        pair_all = packets[:, false_neg.size : false_neg.size + pair_rows].reshape(total_pairs)
        place, slot = place.reshape(-1), slot.reshape(-1)
    else:
        owner, place, local_row = token_plan(ids, shard_rows)
        slot, asked = round_slots(owner, place, local_row, 0, room, nz)
        packets, vec_parts = exchange(
            [
                packet_of(asked, jnp.max(place) // room + 1),
                pad_rows(vectors.astype(jnp.bfloat16), 16),
            ],
            ["all", "zero"],
            ndp,
            nz,
            0,
            "gather_requests",
        )
        layer_weights = [gather_layer(layer_index) for layer_index in range(LAYERS)]
        asked_mine = lax.dynamic_index_in_dim(packets[:, :nz, :room], my_zero, 1, keepdims=False)
        false_all = packets[:, nz : nz + false_neg.size // 128].reshape(total_pairs, total_pairs)
        pair_all = packets[:, -1, :pair_rows].reshape(total_pairs)
        rounds = jnp.max(packets[:, -1, pair_rows])
    vec_all = vec_parts.reshape(nz, -1)[:, :vec_len].reshape(-1).astype(jnp.float32)

    asked_near = lax.dynamic_slice_in_dim(asked_mine, my_dp * nz, nz, 0)

    def rows_for(wanted):
        picked = one_hot(wanted.reshape(-1), shard_rows, jnp.float32)
        return jnp.dot(picked, word_table, precision=lax.Precision.HIGHEST).astype(jnp.bfloat16)

    def rows_from(slot_now, received):
        return matmul(one_hot(slot_now, nz * room), received.reshape(nz * room, D)).astype(
            jnp.bfloat16
        )

    if not by_hand:
        (received,) = exchange(
            [rows_for(asked_near).reshape(nz, room, D)], ["zero_p"], ndp, nz, 1, "send_rows"
        )
    rows = rows_from(slot, received)

    def round_of(round_index):
        owner = lax.div(ids, jnp.int32(shard_rows))
        local_row = ids - owner * shard_rows
        return round_slots(owner, place, local_row, round_index, room, nz)

    def more_rows(state):
        round_index, rows_now = state
        slot_now, asked_now = round_of(round_index)
        wanted = lax.all_to_all(asked_now.reshape(nz, room), "zero", 0, 0, tiled=True)
        got = lax.all_to_all(rows_for(wanted).reshape(nz, room, D), "zero", 0, 0, tiled=True)
        return round_index + 1, rows_now + rows_from(slot_now, got)

    def further(step, *value):
        return lax.while_loop(lambda state: state[0] < rounds, step, (jnp.int32(1), *value))[1:]

    (rows,) = further(more_rows, rows)
    rows = rows.reshape(seq_rows, SEQ, D).astype(jnp.float32)

    vec_rows = vec_all.reshape(-1, D)
    edges = [0] + [SEQ + 2 + i * LAYER_ROWS for i in range(LAYERS + 1)]
    vec_parts = [vec_rows[first:last] for first, last in zip(edges, edges[1:])]
    first_part = vec_parts[0]
    embedded, embed_normal, embed_inverse = norm_forward(
        rows + first_part[None, :SEQ], first_part[SEQ], first_part[SEQ + 1]
    )
    hidden = embedded
    mask = key_mask.astype(jnp.float32)[:, None, :]
    saved = []
    pooled = []
    for layer_index in range(LAYERS):
        weights = layer_weights[layer_index]
        hidden, kept = layer_forward(hidden, weights, vec_parts[1 + layer_index], mask)
        saved.append(kept)
        pooled.append(pool_rows(hidden, key_mask, seq_lengths).astype(jnp.bfloat16))

    if by_hand and pair_rows == 4:
        block = jnp.stack(pooled).reshape(2, pair_rows, 2, D).transpose(0, 2, 1, 3)
        loss, pooled_grads = contrastive(block.reshape(2, 2 * pair_rows, D), false_all, pair_all, 2)
        pooled_grads = pooled_grads[:, :, :pair_rows]
    else:
        (pooled_all,) = exchange(
            [jnp.stack(pooled).reshape(-1, 128)], ["all"], ndp, nz, 2, "gather_pooled"
        )
        pooled_all = pooled_all.reshape(n, 2, pair_rows, 2, D).astype(jnp.float32)
        pooled_all = pooled_all.transpose(1, 3, 0, 2, 4).reshape(2, 2, total_pairs, D)

        def whole_loss(pooled_now):
            summed = contrastive_terms(
                pooled_now[0, 0],
                pooled_now[1, 0],
                pooled_now[0, 1],
                pooled_now[1, 1],
                false_all,
                pair_all,
            )
            valid_total = jnp.sum((pair_all >= 0).astype(jnp.float32))
            return summed / jnp.maximum(valid_total, 1.0)

        loss, pooled_grads = jax.value_and_grad(whole_loss)(pooled_all)
        pooled_grads = lax.dynamic_slice_in_dim(pooled_grads, me * pair_rows, pair_rows, 2)
    pooled_grads = pooled_grads.transpose(0, 2, 1, 3).reshape(2, seq_rows, D)
    shallow_back, deep_back = pooled_grads[0], pooled_grads[1]
    share = key_mask.astype(jnp.float32) / seq_lengths.astype(jnp.float32)[:, None]
    grad_hidden = jnp.zeros_like(embedded)
    weight_parts, layer_pairs = [], []
    vec_grads = [None] * LAYERS
    for layer_index in range(LAYERS - 1, -1, -1):
        if layer_index == LAYERS - 1:
            grad_hidden = grad_hidden + deep_back[:, None, :] * share[:, :, None]
        if layer_index == 0:
            grad_hidden = grad_hidden + shallow_back[:, None, :] * share[:, :, None]
        by_scatter = []

        def scatter(pairs, after):
            if by_hand:
                both = products(pairs)
            else:
                both = jnp.concatenate([weight_gradient(*pair) for pair in pairs], axis=1)
            both, after = lax.optimization_barrier((both, after))
            by_scatter.append(lax.psum_scatter(both, "zero", scatter_dimension=0, tiled=True))
            return after

        early = by_hand and layer_index == LAYERS - 1
        grad_hidden, pairs, vec_grads[layer_index] = layer_backward(
            saved[layer_index],
            layer_weights[layer_index],
            vec_parts[1 + layer_index],
            mask,
            grad_hidden,
            scatter if early else lambda pairs, after: after,
        )
        if not by_hand:
            grad_hidden = scatter(pairs, grad_hidden)
        layer_pairs.insert(0, pairs)
        weight_parts = by_scatter + weight_parts
    rows_grad, embed_grads = embed_back(
        grad_hidden, embed_normal, embed_inverse, first_part[SEQ]
    )
    vec_grad = jnp.concatenate([embed_grads] + vec_grads, axis=0)
    down_local = jnp.stack([part[5 + FF // D] for part in vec_grads])

    rows_grad = rows_grad.reshape(tokens, D)

    def slot_sums(slot_now):
        picked = one_hot(slot_now, nz * room)
        return lax.dot_general(
            picked, rows_grad, (((0,), (0,)), ((), ())), preferred_element_type=jnp.float32
        ).astype(jnp.bfloat16)

    def into_rows(wanted, sums):
        return lax.dot_general(
            one_hot(wanted.reshape(-1), shard_rows),
            sums.reshape(-1, D),
            (((0,), (0,)), ((), ())),
            preferred_element_type=jnp.float32,
        )

    down_each = down_local.reshape(LAYERS, nz, -1).transpose(1, 0, 2).reshape(nz, -1)
    down_len = down_each.shape[1]
    vec_blocks = jnp.concatenate([vec_grad.reshape(nz, vec_len), down_each], axis=1)
    lines = -(-vec_blocks.shape[1] // 1024) * 8
    vec_blocks = jnp.pad(vec_blocks, ((0, 0), (0, lines * 128 - vec_blocks.shape[1])))
    sums = slot_sums(slot).reshape(nz, room, D)

    def more_sums(state):
        round_index, grad_now, square_now = state
        slot_now, asked_now = round_of(round_index)
        wanted = lax.all_to_all(asked_now.reshape(nz, room), "zero", 0, 0, tiled=True)
        got = lax.all_to_all(slot_sums(slot_now).reshape(nz, room, D), "zero", 0, 0, tiled=True)
        wanted = lax.all_gather(wanted, "dp", axis=0, tiled=True)
        got = lax.all_gather(got, "dp", axis=0, tiled=True)
        more = into_rows(wanted, got)
        grown = lax.psum(jnp.sum(more * (2.0 * grad_now + more)), "zero")
        return round_index + 1, grad_now + more, square_now + grown

    if by_hand:
        attn_shard, ffn_shard, word_grad, vec_sum, squares = exchange_gradients(
            layer_pairs[0] + layer_pairs[1][:2],
            vec_blocks.reshape(4, 2, 2, lines, 128),
            sums,
            weight_parts[0],
            asked_mine.reshape(ndp, 1, nz * room),
            shard_rows,
            vec_len,
            3,
        )
        vec_sum = vec_sum.reshape(-1)
        square_total = squares[0, 0]
    else:
        sums_all, vec_shares = exchange(
            [sums, vec_blocks.reshape(nz, lines, 128)],
            ["all_p", "all_p"],
            ndp,
            nz,
            3,
            "send_gradients",
        )
        vec_sum = jnp.sum(vec_shares.reshape(n, -1), axis=0)
        (weight_all,) = exchange([jnp.stack(weight_parts)], ["dp"], ndp, nz, 4, "sum_replicas")
        weight_sum = jnp.sum(weight_all.astype(jnp.float32), axis=0)
        attn_shard = weight_sum[:, :, : 4 * D]
        ffn_shard = weight_sum[:, :, 4 * D :]
        word_grad = into_rows(asked_mine, sums_all)
    vec_shard = vec_sum[:vec_len]
    down_shard = vec_sum[vec_len : vec_len + down_len].reshape(LAYERS, -1)

    if not by_hand:
        square_local = jnp.sum(word_grad * word_grad) + jnp.sum(vec_shard * vec_shard)
        square_local = square_local + jnp.sum(attn_shard * attn_shard)
        square_local = square_local + jnp.sum(ffn_shard * ffn_shard)
        (squares,) = exchange(
            [jnp.broadcast_to(square_local, (8, 128))], ["zero"], ndp, nz, 5, "gather_squares"
        )
        square_total = jnp.sum(squares[:, 0, 0])
    word_grad, square_total = further(more_sums, word_grad, square_total)
    grad_norm = jnp.sqrt(square_total)
    factor = jnp.minimum(1.0, CLIP_NORM / (grad_norm + 1e-06))
    word_new, word_first_new, word_second_new = adam_update(
        word_table, word_grad * factor, word_first, word_second, LEARN_RATE
    )
    vector_new, vector_first_new, vector_second_new = adam_update(
        vectors, vec_shard * factor, vector_first, vector_second, VECTOR_RATE
    )
    attn_new, attn_first_new, attn_second_new = adam_update(
        attn_w, attn_shard * factor, attn_first, attn_second, LEARN_RATE
    )
    ffn_new, ffn_first_new, ffn_second_new = adam_update(
        ffn_w, ffn_shard * factor, ffn_first, ffn_second, LEARN_RATE
    )
    return (
        loss,
        grad_norm,
        word_new,
        vector_new,
        attn_new,
        ffn_new,
        word_new.astype(jnp.bfloat16),
        vector_new.astype(jnp.bfloat16),
        attn_new.astype(jnp.bfloat16),
        ffn_new.astype(jnp.bfloat16),
        word_first_new,
        vector_first_new,
        attn_first_new,
        ffn_first_new,
        word_second_new,
        vector_second_new,
        attn_second_new,
        ffn_second_new,
        down_shard * factor,
    )


def solution(mesh):
    placed = (
        P(("dp", "zero"), None, None),
        P(("dp", "zero"), None),
        P(("dp", "zero"), None),
        P(("dp", "zero")),
        P("zero", None),
        P("zero"),
        P(None, "zero", None),
        P(None, "zero", None),
        P("zero", None),
        P("zero"),
        P(None, "zero", None),
        P(None, "zero", None),
        P("zero", None),
        P("zero"),
        P(None, "zero", None),
        P(None, "zero", None),
    )
    return jax.shard_map(
        body,
        mesh=mesh,
        in_specs=placed,
        out_specs=(
            P(),
            P(),
            P("zero", None),
            P("zero"),
            P(None, "zero", None),
            P(None, "zero", None),
            P("zero", None),
            P("zero"),
            P(None, "zero", None),
            P(None, "zero", None),
            P("zero", None),
            P("zero"),
            P(None, "zero", None),
            P(None, "zero", None),
            P("zero", None),
            P("zero"),
            P(None, "zero", None),
            P(None, "zero", None),
            P(None, "zero"),
        ),
        check_vma=False,
    )
```
